32 devices in a mesh: dp: 16 (over z, x, core), mp: 2 (over y).
Axes of the slice: x: 2, y: 2, z: 4, core: 2. Of those that a mesh axis runs over, the one named last changes fastest.
Arguments:
- tokens: bfloat16 [16384, 1024], P(('dp', 'mp')), may hold values from -6 to 6
- lengths: int32 [16], P('dp'), may hold values from 512 to 1024, as said below
- first_gain: float32 [1024], replicated, may hold values from 0.5 to 1.5
- first_shift: float32 [1024], replicated, may hold values from -1 to 1
- heads_weight: bfloat16 [3, 1024, 1024], P(None, None, 'mp'), may hold values from -0.1875 to 0.1875
- relative_bias: float32 [16, 32], P('mp'), may hold values from -4 to 4
- mixer_weight: bfloat16 [1024, 1024], P('mp'), may hold values from -0.5 to 0.5
- second_gain: float32 [1024], replicated, may hold values from 0.5 to 1.5
- second_shift: float32 [1024], replicated, may hold values from -1 to 1
- expand_weight: bfloat16 [1024, 4096], P(None, 'mp'), may hold values from -0.1875 to 0.1875
- expand_bias: bfloat16 [4096], P('mp'), may hold values from -3 to 3
- reduce_weight: bfloat16 [4096, 1024], P('mp'), may hold values from -0.09375 to 0.09375
- reduce_bias: float32 [1024], replicated, may hold values from -1.5 to 1.5
- cotangent: bfloat16 [16384, 1024], P(('dp', 'mp')), may hold values from -6 to 6
Outputs:
- block_out: bfloat16 [16384, 1024], P(('dp', 'mp'))
- tokens_grad: bfloat16 [16384, 1024], P(('dp', 'mp'))
- first_gain_grad: float32 [1024], replicated
- first_shift_grad: float32 [1024], replicated
- heads_weight_grad: float32 [3, 1024, 1024], P(None, None, 'mp')
- relative_bias_grad: float32 [16, 32], P('mp')
- mixer_weight_grad: float32 [1024, 1024], P('mp')
- second_gain_grad: float32 [1024], replicated
- second_shift_grad: float32 [1024], replicated
- expand_weight_grad: float32 [1024, 4096], P(None, 'mp')
- expand_bias_grad: float32 [4096], P('mp')
- reduce_weight_grad: float32 [4096, 1024], P('mp')
- reduce_bias_grad: float32 [1024], replicated
The draws below stay inside these ranges and needn't reach their ends.
Inputs may be any that keep to these rules, and one draw needn't show every extreme that they name: Each sequence holds lengths valid tokens followed by padding slots; some sequence fills all 1024 slots.
All inputs are finite; a program needn't handle non-finite values.
Results may differ from the reference program's by a relative error of at most 0.025.
Values may be sent and summed in bfloat16 or wider, within the bound.
No kernel may reach another device: no remote copies, remote signals or barrier semaphores. Data moves between devices by JAX's collectives and lax.ppermute only.
A program may use at most 320 MiB of HBM per device.

```python
import math
import jax
import jax.numpy as jnp
import numpy as np
from jax import lax

D = 1024
H = 16
DH = 64
FF = 4096
NB = 32
MAXDIST = 128
TOK_DEV = 1024
SEQS = 16
TOKENS = 16384


def draw_lengths(key, part):
    key_length = jax.random.fold_in(key, 11)
    key_full = jax.random.fold_in(key, 23)
    drawn = jax.random.randint(key_length, (SEQS,), TOK_DEV // 2, TOK_DEV + 1)
    chosen = jax.random.randint(key_full, (), 0, SEQS)
    return jnp.where(jnp.arange(SEQS) == chosen, TOK_DEV, drawn).astype(jnp.int32)


def block_scale(stream_key, dims, cuts, low, top_value):
    loudness, own = 1.0, jax.random.fold_in(stream_key, 6)
    for dim, shards_of in cuts:
        draws = jnp.exp(jax.random.uniform(jax.random.fold_in(own, dim), (shards_of,), jnp.float32, low / len(cuts), top_value / len(cuts)))
        loudness = loudness * jnp.repeat(draws, dims[dim] // shards_of).reshape([-1 if axis == dim else 1 for axis in range(len(dims))])
    return loudness


def gaussian(own_key, shape, width, most, cuts=(), held_as=jnp.bfloat16):
    values = jax.random.normal(own_key, shape, jnp.float32) * width
    if len(cuts) > 0:
        values = block_scale(own_key, shape, cuts, -0.22, 0.18) * values
    return jnp.clip(values, min=-most, max=most).astype(held_as)


def setup_inputs(seed: int = 0) -> dict:
    seeds = jax.random.split(jax.random.key(seed), 15)
    tokens = gaussian(seeds[0], (TOKENS, D), 1.0, 6.0, ((0, 32),))
    lengths = draw_lengths(jax.random.fold_in(seeds[14], 71), 0)
    first_gain = jnp.clip(1.0 + 0.1 * jax.random.normal(seeds[2], (D,), jnp.float32), 0.5, 1.5)
    first_shift = gaussian(seeds[3], (D,), 0.2, 1.0, (), jnp.float32)
    heads_weight = gaussian(seeds[4], (3, D, D), D ** -0.5, 0.1875, ((2, 2),))
    relative_bias = gaussian(seeds[5], (H, NB), 1.0, 4.0, ((0, 2),), jnp.float32)
    mixer_weight = gaussian(seeds[6], (D, D), (D // 8) ** -0.5, 0.5, ((0, 2),))
    second_gain = jnp.clip(1.0 + 0.1 * jax.random.normal(seeds[7], (D,), jnp.float32), 0.5, 1.5)
    second_shift = gaussian(seeds[8], (D,), 0.2, 1.0, (), jnp.float32)
    expand_weight = gaussian(seeds[9], (D, FF), D ** -0.5, 0.1875, ((1, 2),))
    expand_bias = gaussian(seeds[10], (FF,), 0.5, 3.0, ((0, 2),))
    reduce_weight = gaussian(seeds[11], (FF, D), FF ** -0.5, 0.09375, ((0, 2),))
    reduce_bias = gaussian(seeds[12], (D,), 0.3, 1.5, (), jnp.float32)
    cotangent = gaussian(seeds[13], (TOKENS, D), 1.0, 6.0, ((0, 32),))
    return {"tokens": tokens, "lengths": lengths, "first_gain": first_gain, "first_shift": first_shift, "heads_weight": heads_weight, "relative_bias": relative_bias, "mixer_weight": mixer_weight, "second_gain": second_gain, "second_shift": second_shift, "expand_weight": expand_weight, "expand_bias": expand_bias, "reduce_weight": reduce_weight, "reduce_bias": reduce_bias, "cotangent": cotangent}


EPS = 1e-05
NEG = -1e+30
HIGHEST = lax.Precision.HIGHEST

@jax.custom_vjp
def low(v):
    return lax.optimization_barrier(v.astype(jnp.bfloat16)).astype(jnp.float32)

@jax.custom_vjp
def low_back(v):
    return v

def low_keep(v):
    return (low(v), None)

def low_pass(kept, grad):
    return (grad,)

def back_keep(v):
    return (v, None)

def back_low(kept, grad):
    return (low(grad),)
low.defvjp(low_keep, low_pass)
low_back.defvjp(back_keep, back_low)

def bucket_table(count, buckets, reach):
    exact = buckets // 2
    entries = []
    for position in range(count):
        if position < exact:
            entries.append(position)
        else:
            level = exact + int(math.log(position / exact) / math.log(reach / exact) * (buckets - exact))
            entries.append(min(buckets - 1, level))
    return np.array(entries, dtype=np.int32)

def layer_norm(values, gain, shift):
    center = lax.optimization_barrier(jnp.mean(values, axis=-1, keepdims=True))
    centered = values - center
    spread = lax.optimization_barrier(jnp.mean(centered * centered, axis=-1, keepdims=True))
    return centered * lax.rsqrt(spread + EPS) * gain + shift

def forward(params, sequence, length):
    first_gain, first_shift, heads_weight, relative_bias, mixer_weight, second_gain, second_shift, expand_weight, expand_bias, reduce_weight, reduce_bias = params
    rows = sequence.shape[0]
    first = low(layer_norm(sequence, first_gain, first_shift))
    projected = jnp.einsum('td,cde->cte', first, heads_weight, precision=HIGHEST)
    projected = low_back(low(projected))
    queries = projected[0].reshape(rows, H, DH)
    keys = projected[1].reshape(rows, H, DH)
    values = projected[2].reshape(rows, H, DH)
    places = np.arange(rows)
    table = bucket_table(rows, NB, MAXDIST)
    index = table[np.maximum(places[:, None] - places[None, :], 0)]
    bias = relative_bias[:, index]
    raw = jnp.einsum('thd,shd->hts', queries, keys, precision=HIGHEST) * DH ** (-0.5) + bias
    raw = low_back(raw)
    causal = jnp.asarray(places[None, :] <= places[:, None])
    allowed = causal & (jnp.arange(rows)[None, :] < length)
    scores = jnp.where(allowed[None], raw, NEG)
    top = lax.optimization_barrier(jnp.max(scores, axis=2, keepdims=True))
    raised = jnp.exp(scores - top)
    weights = low(raised / lax.optimization_barrier(jnp.sum(raised, axis=2, keepdims=True)))
    mixed = jnp.einsum('hts,shd->thd', weights, values, precision=HIGHEST).reshape(rows, H * DH)
    mixed = low_back(low(mixed))
    attended = low_back(jnp.dot(mixed, mixer_weight, precision=HIGHEST))
    middle = sequence + attended
    second = low(layer_norm(middle, second_gain, second_shift))
    expanded = low_back(jnp.dot(second, expand_weight, precision=HIGHEST) + expand_bias)
    active = low(jax.nn.gelu(expanded, approximate=True))
    return middle + jnp.dot(active, reduce_weight, precision=HIGHEST) + reduce_bias

def reference(tokens, lengths, first_gain, first_shift, heads_weight, relative_bias, mixer_weight, second_gain, second_shift, expand_weight, expand_bias, reduce_weight, reduce_bias, cotangent):
    params = (first_gain, first_shift, heads_weight.astype(jnp.float32), relative_bias, mixer_weight.astype(jnp.float32), second_gain, second_shift, expand_weight.astype(jnp.float32), expand_bias.astype(jnp.float32), reduce_weight.astype(jnp.float32), reduce_bias)
    inputs = tokens.astype(jnp.float32).reshape(SEQS, TOK_DEV, D)
    targets = cotangent.astype(jnp.float32).reshape(SEQS, TOK_DEV, D)

    def one_sequence(totals, item):
        sequence, target, length = item
        valid = (jnp.arange(TOK_DEV) < length).astype(jnp.float32)[:, None]
        output, pull = jax.vjp(lambda weights, values: forward(weights, values, length), params, sequence)
        param_grads, input_grad = pull(target * valid)
        totals = jax.tree.map(jnp.add, totals, param_grads)
        return (totals, (output.astype(jnp.bfloat16), input_grad.astype(jnp.bfloat16)))
    zeros = jax.tree.map(jnp.zeros_like, params)
    totals, (outputs, input_grads) = lax.scan(one_sequence, zeros, (inputs, targets, lengths))
    return (outputs.reshape(TOKENS, D), input_grads.reshape(TOKENS, D), totals[0], totals[1], totals[2], totals[3], totals[4], totals[5], totals[6], totals[7], totals[8], totals[9], totals[10])
```

```python
import functools
import math

import jax
import jax.numpy as jnp
import numpy as np
from jax import lax
from jax.experimental import pallas as pl
from jax.experimental.pallas import tpu as pltpu
from jax.sharding import PartitionSpec as P

EPS = 1e-05
DH=64; MAXDIST=128; NEG=-1e30; BLK=256
F32=jnp.float32; BF16=jnp.bfloat16
HIGHEST=lax.Precision.HIGHEST

def bucket_table(count, buckets, reach):
    exact = buckets // 2
    entries = []
    for position in range(count):
        if position < exact:
            entries.append(position)
        else:
            level = exact + int(math.log(position / exact) / math.log(reach / exact) * (buckets - exact))
            entries.append(min(buckets - 1, level))
    return np.array(entries, dtype=np.int32)

def bias_tables(buckets):
    W=2*BLK
    tab=bucket_table(W,buckets,MAXDIST)
    oh=np.zeros((buckets,4,W),np.float32); neg=np.zeros((1,4,W),np.float32)
    for y in range(W):
        x = y if y < BLK else y-W
        if x<=0 and -x<BLK: oh[tab[-x],0,y]=1
        else: neg[0,0,y]=NEG
        d=BLK-x
        if 0<=d<W: oh[tab[d],1,y]=1
        if 0<=x: oh[tab[x],2,y]=1
        else: neg[0,2,y]=NEG
        d=BLK+x
        if 0<=d<W: oh[tab[d],3,y]=1
    return oh.reshape(buckets,4*W), neg.reshape(1,4*W)

def bias_rows(relative_bias):
    heads,buckets=relative_bias.shape
    oh,neg=bias_tables(buckets)
    rel=relative_bias-relative_bias[:,buckets-1:]
    rows=jnp.dot(rel,jnp.asarray(oh),precision=HIGHEST)+jnp.asarray(neg)
    return rows.reshape(heads//2,2,4*2*BLK)

def split3(x):
    hi=x.astype(BF16); rest=x-hi.astype(F32); mid=rest.astype(BF16)
    lo=(rest-mid.astype(F32)).astype(BF16)
    return hi.astype(F32),mid.astype(F32),lo.astype(F32)

def toeplitz(row):
    wide=jnp.broadcast_to(row,(BLK,2*BLK))
    return pltpu.roll(wide,0,1,stride=1,stride_axis=0)[:,:BLK]

def halves(ref, off, half, lead=()):
    lo=ref[(*lead, pl.ds(pl.multiple_of(off,half),half), slice(None))]
    hi=ref[(*lead, pl.ds(pl.multiple_of(half-off,half),half), slice(None))]
    return lo,hi

def fwd_kernel(sp, q_ref,k_ref,v_ref,b_ref,o_ref,lse_ref,qs,ks,vs):
    T=q_ref.shape[1]; half=T//2; off=pl.multiple_of(sp[0],half); length=sp[1]
    lane=lax.broadcasted_iota(jnp.int32,(1,128),1)
    W=2*BLK
    for part in range(2):
        start=pl.multiple_of(off if part==0 else half-off, half)
        rows=pl.ds(start,half)
        q=q_ref[0,rows,:].astype(F32); k=k_ref[0,rows,:].astype(F32); v=v_ref[0,rows,:].astype(F32)
        pos=lax.broadcasted_iota(jnp.int32,(half,1),0)+part*half
        gone=jnp.where(pos<length,0.0,NEG).astype(F32)
        for h in range(2):
            mine=(lane//DH)==h
            spare=lane==(DH*(1-h))
            dst=slice(part*half,(part+1)*half)
            qs[h,dst,:]=jnp.where(mine,q*DH**-0.5,jnp.where(spare,1.0,0.0)).astype(BF16)
            ks[h,dst,:]=jnp.where(mine,k,jnp.where(spare,gone,0.0)).astype(BF16)
            vs[h,dst,:]=jnp.where(mine,v,1.0).astype(BF16)
    for h in range(2):
        mine=(lane//DH)==h
        t0=toeplitz(b_ref[0,h:h+1,0:W]); t1=toeplitz(b_ref[0,h:h+1,W:2*W])
        for i in range(T//BLK):
            kc=(i+1)*BLK
            s=lax.dot_general(qs[h,i*BLK:kc,:],ks[h,:kc,:],(((1,),(1,)),((),())),preferred_element_type=F32)
            parts=[]
            if i>=2: parts.append(s[:,:kc-2*BLK])
            if i>=1: parts.append(s[:,kc-2*BLK:kc-BLK]+t1)
            parts.append(s[:,kc-BLK:]+t0)
            top=functools.reduce(jnp.maximum,[jnp.max(x,axis=1,keepdims=True) for x in parts])
            p=jnp.concatenate([jnp.exp(x-top).astype(BF16) for x in parts],axis=1)
            o=jnp.dot(p,vs[h,:kc,:],preferred_element_type=F32)
            total=o[:,DH*(1-h):DH*(1-h)+1]
            o=o/total
            lse=top+jnp.log(total)
            rows=pl.ds(pl.multiple_of((i*BLK+off)%T,BLK),BLK)
            if h==0:
                o_ref[rows,:]=o.astype(BF16)
                lse_ref[0,rows,:]=jnp.broadcast_to(lse,(BLK,128))
            else:
                o_ref[rows,:]=jnp.where(mine,o,o_ref[rows,:].astype(F32)).astype(BF16)
                lse_ref[0,rows,:]=jnp.where(mine,lse,lse_ref[0,rows,:])

def attend_forward(sp,projected,rows,interpret=False):
    _,T,HD=projected.shape; pairs=HD//128
    return pl.pallas_call(
        fwd_kernel,
        grid_spec=pltpu.PrefetchScalarGridSpec(
            num_scalar_prefetch=1,grid=(pairs,),
            in_specs=[pl.BlockSpec((1,T,128),lambda p,s,c=c:(c,0,p)) for c in range(3)]
              +[pl.BlockSpec((1,2,rows.shape[2]),lambda p,s:(p,0,0))],
            out_specs=[pl.BlockSpec((T,128),lambda p,s:(0,p)),pl.BlockSpec((1,T,128),lambda p,s:(p,0,0))],
            scratch_shapes=[pltpu.VMEM((2,T,128),BF16)]*3),
        out_shape=[jax.ShapeDtypeStruct((T,HD),BF16),jax.ShapeDtypeStruct((pairs,T,128),F32)],
        name="attend_forward",
    )(sp,projected,projected,projected,rows)

def diagonal_sums(acc, offset):
    W=2*BLK
    wide=jnp.concatenate([acc,jnp.zeros_like(acc)],axis=1)
    n=BLK
    while n>1:
        n//=2
        top=wide[:n]; bottom=wide[n:2*n]
        wide=top+pltpu.roll(bottom,W-n,1)
    return pltpu.roll(wide,offset,1) if offset else wide

def bwd_kernel(sp, q_ref,k_ref,v_ref,do_ref,o_ref,lse_ref,b_ref,g_ref,d_ref,qs,ks,vs,dos,dq,acc0,acc1, *, variant):
    T=q_ref.shape[1]; half=T//2; off=pl.multiple_of(sp[0],half); length=sp[1]
    lane=lax.broadcasted_iota(jnp.int32,(1,128),1)
    W=2*BLK
    n=T//BLK
    for part in range(2):
        start=pl.multiple_of(off if part==0 else half-off, half)
        rows=pl.ds(start,half)
        dst=slice(part*half,(part+1)*half)
        q=q_ref[0,rows,:].astype(F32); k=k_ref[0,rows,:].astype(F32); v=v_ref[0,rows,:].astype(F32)
        do=do_ref[rows,:].astype(F32)
        prod=do*o_ref[rows,:].astype(F32)
        lse=lse_ref[0,rows,:]
        pos=lax.broadcasted_iota(jnp.int32,(half,1),0)+part*half
        gone=jnp.where(pos<length,0.0,NEG).astype(F32)
        for h in range(2):
            mine=(lane//DH)==h
            s0=DH*(1-h)
            delta=jnp.sum(jnp.where(mine,prod,0.0),axis=1,keepdims=True)
            dh,dm,dl=split3(delta)
            lh,lm,ll=split3(lse[:,DH*h:DH*h+1])
            def lanes(base,vals):
                out=0.0
                for t,val in enumerate(vals): out=jnp.where(lane==s0+t,val,out)
                return jnp.where(mine,base,out).astype(BF16)
            qs[h,dst,:]=lanes(q*DH**-0.5,(1.0,-lh,-lm,-ll))
            ks[h,dst,:]=lanes(k,(gone,1.0,1.0,1.0))
            vs[h,dst,:]=lanes(v,(1.0,1.0,1.0))
            dos[h,dst,:]=lanes(do,(-dh,-dm,-dl))
    for h in range(2):
        mine=(lane//DH)==h
        t0=toeplitz(b_ref[0,h:h+1,2*W:3*W]); t1=toeplitz(b_ref[0,h:h+1,3*W:])
        for j in range(n):
            cols=slice(j*BLK,T)
            rj=slice(j*BLK,(j+1)*BLK)
            s=lax.dot_general(ks[h,rj,:],qs[h,cols,:],(((1,),(1,)),((),())),preferred_element_type=F32)
            dp=lax.dot_general(vs[h,rj,:],dos[h,cols,:],(((1,),(1,)),((),())),preferred_element_type=F32)
            ps=[];dss=[]
            for b in range(n-j):
                c=slice(b*BLK,(b+1)*BLK)
                x=s[:,c]
                if b==0: x=x+t0
                if b==1: x=x+t1
                p=jnp.exp(x)
                ds=p*dp[:,c]
                if b==0:
                    if j==0: acc0[...]=ds
                    else: acc0[...]+=ds
                if b==1:
                    if j==0: acc1[...]=ds
                    else: acc1[...]+=ds
                ps.append(p.astype(BF16)); dss.append(ds.astype(BF16))
            p=jnp.concatenate(ps,axis=1); ds=jnp.concatenate(dss,axis=1)
            dv=jnp.dot(p,dos[h,cols,:],preferred_element_type=F32)
            dk=jnp.dot(ds,qs[h,cols,:],preferred_element_type=F32)
            kk=jnp.where(mine,ks[h,rj,:].astype(F32),1.0).astype(BF16)
            dqj=lax.dot_general(ds,kk,(((0,),(0,)),((),())),preferred_element_type=F32)
            if j==0: dq[h,:,:]=dqj
            else: dq[h,cols,:]+=dqj
            rows=pl.ds(pl.multiple_of((j*BLK+off)%T,BLK),BLK)
            if h==0:
                g_ref[1,rows,:]=dk.astype(BF16); g_ref[2,rows,:]=dv.astype(BF16)
            else:
                g_ref[1,rows,:]=jnp.where(mine,dk,g_ref[1,rows,:].astype(F32)).astype(BF16)
                g_ref[2,rows,:]=jnp.where(mine,dv,g_ref[2,rows,:].astype(F32)).astype(BF16)
        near=diagonal_sums(acc0[...],0)
        near1=diagonal_sums(acc1[...],BLK)
        d_ref[0,h:h+1,:]=near+near1
        total=jnp.sum(dq[h,:,:],axis=0,keepdims=True)[:,DH*(1-h):DH*(1-h)+1]
        d_ref[0,2+h:3+h,:]=jnp.broadcast_to(total,(1,W))
    first=(lane//DH)==0
    for part in range(2):
        start=pl.multiple_of(off if part==0 else half-off, half)
        dst=slice(part*half,(part+1)*half)
        g_ref[0,pl.ds(start,half),:]=(jnp.where(first,dq[0,dst,:],dq[1,dst,:])*DH**-0.5).astype(BF16)

def attend_backward(sp,projected,grad_mixed,mixed,lse,rows,variant=0):
    _,T,HD=projected.shape; pairs=HD//128
    flat=pl.BlockSpec((T,128),lambda p,s:(0,p))
    return pl.pallas_call(
        functools.partial(bwd_kernel,variant=variant),
        grid_spec=pltpu.PrefetchScalarGridSpec(
            num_scalar_prefetch=1,grid=(pairs,),
            in_specs=[pl.BlockSpec((1,T,128),lambda p,s,c=c:(c,0,p)) for c in range(3)]
              +[flat,flat,pl.BlockSpec((1,T,128),lambda p,s:(p,0,0)),pl.BlockSpec((1,2,rows.shape[2]),lambda p,s:(p,0,0))],
            out_specs=[pl.BlockSpec((3,T,128),lambda p,s:(0,0,p)),pl.BlockSpec((1,4,2*BLK),lambda p,s:(p,0,0))],
            scratch_shapes=[pltpu.VMEM((2,T,128),BF16)]*4+[pltpu.VMEM((2,T,128),F32)]+[pltpu.VMEM((BLK,BLK),F32)]*2),
        out_shape=[jax.ShapeDtypeStruct((3,T,HD),BF16),jax.ShapeDtypeStruct((pairs,4,2*BLK),F32)],
        name="attend_backward",
    )(sp,projected,projected,projected,grad_mixed,mixed,lse,rows)

def bias_grad(sums, buckets):
    pairs=sums.shape[0]; W=2*BLK
    tab=bucket_table(W,buckets,MAXDIST)
    assert tab[BLK]==buckets-1
    m=np.zeros((W,buckets),np.float32)
    for d in range(W):
        if tab[d]<buckets-1:
            m[d,tab[d]]=1; m[d,buckets-1]=-1
    near=sums[:,0:2].reshape(pairs*2,W); total=sums[:,2:4,0].reshape(pairs*2,1)
    last=np.zeros((1,buckets),np.float32); last[0,-1]=1
    return jnp.dot(near,jnp.asarray(m),precision=HIGHEST)+total*jnp.asarray(last)


def normalize(values):
    center = jnp.mean(values, axis=-1, keepdims=True)
    centered = values - center
    inverse = lax.rsqrt(jnp.mean(centered * centered, axis=-1, keepdims=True) + EPS)
    return (centered * inverse, inverse)


def norm_back(grad_norm, normed, inverse):
    return inverse * (
        grad_norm
        - jnp.mean(grad_norm, axis=-1, keepdims=True)
        - normed * jnp.mean(grad_norm * normed, axis=-1, keepdims=True)
    )


def gelu_back(expanded, grad_active):
    pull = jax.vjp(lambda value: jax.nn.gelu(value, approximate=True), expanded)[1]
    return pull(grad_active)[0]


def dot(a, b, ca, cb):
    return lax.dot_general(a, b, (((ca,), (cb,)), ((), ())), preferred_element_type=F32)


def swap(x):
    return lax.ppermute(x, "mp", [(0, 1), (1, 0)])


def gather_rows(x, members):
    if members == 2:
        return jnp.concatenate([x, swap(x)], axis=0)
    return lax.all_gather(x, "mp", axis=0, tiled=True)


def scatter_rows(x, members):
    if members == 2:
        own = x.shape[0] // 2
        return x[:own] + swap(x[own:].astype(BF16)).astype(F32)
    return lax.psum_scatter(x.astype(BF16), "mp", scatter_dimension=0, tiled=True).astype(F32)


def per_device(
    tokens,
    lengths,
    first_gain,
    first_shift,
    heads_weight,
    relative_bias,
    mixer_weight,
    second_gain,
    second_shift,
    expand_weight,
    expand_bias,
    reduce_weight,
    reduce_bias,
    cotangent,
):
    members = lax.axis_size("mp")
    member = lax.axis_index("mp")
    length = lengths[0]
    own = tokens.shape[0]
    whole = own * members
    buckets = relative_bias.shape[1]
    turn = member * own if members == 2 else 0
    sp = jnp.stack([jnp.asarray(turn, jnp.int32), length.astype(jnp.int32)])
    places = member * own + jnp.arange(own)
    if members == 2:
        places_all = (jnp.arange(whole) + member * own) % whole
    else:
        places_all = jnp.arange(whole)
    rows = bias_rows(relative_bias)

    source_all = gather_rows(tokens, members)
    first_norm_all, first_inverse_all = normalize(source_all.astype(F32))
    first_all = (first_norm_all * first_gain + first_shift).astype(BF16)
    projected = jnp.einsum(
        "td,cde->cte", first_all, heads_weight, preferred_element_type=F32
    ).astype(BF16)
    mixed_low, logsum = attend_forward(sp, projected, rows)
    target_all = gather_rows(cotangent, members)
    target_all = jnp.where((places_all < length)[:, None], target_all, jnp.zeros_like(target_all))
    source = tokens.astype(F32)
    attended = scatter_rows(dot(mixed_low, mixer_weight, 1, 0), members)
    middle = source + attended
    second_norm, second_inverse = normalize(middle)
    second_low = (second_norm * second_gain + second_shift).astype(BF16)
    second_all = gather_rows(second_low, members)
    expanded = dot(second_all, expand_weight, 1, 0) + expand_bias
    active_low = jax.nn.gelu(expanded, approximate=True).astype(BF16)
    grad_active = dot(target_all, reduce_weight, 1, 1)
    grad_expanded = gelu_back(expanded, grad_active).astype(BF16)
    grad_second = scatter_rows(dot(grad_expanded, expand_weight, 1, 1), members)
    reduced = scatter_rows(dot(active_low, reduce_weight, 1, 0), members)
    reduce_grad = dot(active_low, target_all, 0, 0)
    expand_grad = dot(second_all, grad_expanded, 0, 0)
    expand_bias_grad = jnp.sum(grad_expanded.astype(F32), axis=0)
    block_out = (middle + reduced + reduce_bias).astype(BF16)
    target_wide = jnp.where((places < length)[:, None], cotangent, jnp.zeros_like(cotangent)).astype(F32)
    grad_middle = target_wide + norm_back(grad_second * second_gain, second_norm, second_inverse)
    attended_all = gather_rows(grad_middle.astype(BF16), members)
    mixer_grad = dot(mixed_low, attended_all, 0, 0)
    grad_mixed = dot(attended_all, mixer_weight, 1, 1).astype(BF16)
    grad_projected, sums = attend_backward(sp, projected, grad_mixed, mixed_low, logsum, rows)
    bias_part = bias_grad(sums, buckets)
    heads_grad = jnp.einsum("td,cte->cde", first_all, grad_projected, preferred_element_type=F32)
    grad_first = scatter_rows(
        jnp.einsum("cte,cde->td", grad_projected, heads_weight, preferred_element_type=F32), members
    )
    first_norm, first_inverse = normalize(source)
    tokens_grad = (
        grad_middle + norm_back(grad_first * first_gain, first_norm, first_inverse)
    ).astype(BF16)
    first_gain_grad, first_shift_grad, second_gain_grad, second_shift_grad, reduce_bias_grad = (
        lax.psum(
            (
                jnp.sum(grad_first * first_norm, axis=0),
                jnp.sum(grad_first, axis=0),
                jnp.sum(grad_second * second_norm, axis=0),
                jnp.sum(grad_second, axis=0),
                jnp.sum(target_wide, axis=0),
            ),
            ("dp", "mp"),
        )
    )
    heads_grad, bias_part, mixer_grad, expand_grad, expand_bias_grad, reduce_grad = (
        lax.psum(heads_grad.astype(BF16), "dp").astype(F32),
        lax.psum(bias_part.astype(BF16), "dp").astype(F32),
        lax.psum(mixer_grad.astype(BF16), "dp").astype(F32),
        lax.psum(expand_grad.astype(BF16), "dp").astype(F32),
        lax.psum(expand_bias_grad.astype(BF16), "dp").astype(F32),
        lax.psum(reduce_grad.astype(BF16), "dp").astype(F32),
    )
    return (
        block_out,
        tokens_grad,
        first_gain_grad,
        first_shift_grad,
        heads_grad,
        bias_part,
        mixer_grad,
        second_gain_grad,
        second_shift_grad,
        expand_grad,
        expand_bias_grad,
        reduce_grad,
        reduce_bias_grad,
    )


def solution(mesh):
    return jax.shard_map(
        per_device,
        mesh=mesh,
        in_specs=(
            P(("dp", "mp"), None),
            P("dp"),
            P(),
            P(),
            P(None, None, "mp"),
            P("mp", None),
            P("mp", None),
            P(),
            P(),
            P(None, "mp"),
            P("mp"),
            P("mp", None),
            P(),
            P(("dp", "mp"), None),
        ),
        out_specs=(
            P(("dp", "mp"), None),
            P(("dp", "mp"), None),
            P(),
            P(),
            P(None, None, "mp"),
            P("mp", None),
            P("mp", None),
            P(),
            P(),
            P(None, "mp"),
            P("mp"),
            P("mp", None),
            P(),
        ),
        check_vma=False,
    )
```

```python
import functools
import math

import jax
import jax.numpy as jnp
import numpy as np
from jax import lax
from jax.experimental import pallas as pl
from jax.experimental.pallas import tpu as pltpu
from jax.sharding import PartitionSpec as P

EPS = 1e-05
DH=64; MAXDIST=128; NEG=-1e30; BLK=256
F32=jnp.float32; BF16=jnp.bfloat16
HIGHEST=lax.Precision.HIGHEST

def bucket_table(count, buckets, reach):
    exact = buckets // 2
    entries = []
    for position in range(count):
        if position < exact:
            entries.append(position)
        else:
            level = exact + int(math.log(position / exact) / math.log(reach / exact) * (buckets - exact))
            entries.append(min(buckets - 1, level))
    return np.array(entries, dtype=np.int32)

def bias_tables(buckets):
    W=2*BLK
    tab=bucket_table(W,buckets,MAXDIST)
    oh=np.zeros((buckets,4,W),np.float32); neg=np.zeros((1,4,W),np.float32)
    for y in range(W):
        x = y if y < BLK else y-W
        if x<=0 and -x<BLK: oh[tab[-x],0,y]=1
        else: neg[0,0,y]=NEG
        d=BLK-x
        if 0<=d<W: oh[tab[d],1,y]=1
        if 0<=x: oh[tab[x],2,y]=1
        else: neg[0,2,y]=NEG
        d=BLK+x
        if 0<=d<W: oh[tab[d],3,y]=1
    return oh.reshape(buckets,4*W), neg.reshape(1,4*W)

def bias_rows(relative_bias):
    heads,buckets=relative_bias.shape
    oh,neg=bias_tables(buckets)
    rel=relative_bias-relative_bias[:,buckets-1:]
    rows=jnp.dot(rel,jnp.asarray(oh),precision=HIGHEST)+jnp.asarray(neg)
    return rows.reshape(heads//2,2,4*2*BLK)

def split3(x):
    hi=x.astype(BF16); rest=x-hi.astype(F32); mid=rest.astype(BF16)
    lo=(rest-mid.astype(F32)).astype(BF16)
    return hi.astype(F32),mid.astype(F32),lo.astype(F32)

def toeplitz(row):
    wide=jnp.broadcast_to(row,(BLK,2*BLK))
    return pltpu.roll(wide,0,1,stride=1,stride_axis=0)[:,:BLK]


def fwd_kernel(sp, a_ref,c_ref,b_ref,o_ref,lse_ref,qs,ks,vs):
    half=a_ref.shape[1]; T=2*half; flip=sp[0]; length=sp[1]
    lane=lax.broadcasted_iota(jnp.int32,(1,128),1)
    W=2*BLK
    for a,ref in enumerate((a_ref,c_ref)):
        start=pl.multiple_of((a^flip)*half,half)
        dst=pl.ds(start,half)
        q=ref[0].astype(F32); k=ref[1].astype(F32); v=ref[2].astype(F32)
        pos=lax.broadcasted_iota(jnp.int32,(half,1),0)+start
        gone=jnp.where(pos<length,0.0,NEG).astype(F32)
        for h in range(2):
            mine=(lane//DH)==h
            spare=lane==(DH*(1-h))
            qs[h,dst,:]=jnp.where(mine,q*DH**-0.5,jnp.where(spare,1.0,0.0)).astype(BF16)
            ks[h,dst,:]=jnp.where(mine,k,jnp.where(spare,gone,0.0)).astype(BF16)
            vs[h,dst,:]=jnp.where(mine,v,1.0).astype(BF16)
    for h in range(2):
        mine=(lane//DH)==h
        t0=toeplitz(b_ref[0,h:h+1,0:W]); t1=toeplitz(b_ref[0,h:h+1,W:2*W])
        for i in range(T//BLK):
            kc=(i+1)*BLK
            s=lax.dot_general(qs[h,i*BLK:kc,:],ks[h,:kc,:],(((1,),(1,)),((),())),preferred_element_type=F32)
            parts=[]
            if i>=2: parts.append(s[:,:kc-2*BLK])
            if i>=1: parts.append(s[:,kc-2*BLK:kc-BLK]+t1)
            parts.append(s[:,kc-BLK:]+t0)
            top=functools.reduce(jnp.maximum,[jnp.max(x,axis=1,keepdims=True) for x in parts])
            p=jnp.concatenate([jnp.exp(x-top).astype(BF16) for x in parts],axis=1)
            o=jnp.dot(p,vs[h,:kc,:],preferred_element_type=F32)
            total=o[:,DH*(1-h):DH*(1-h)+1]
            o=o/total
            lse=top+jnp.log(total)
            rows=pl.ds(pl.multiple_of((i*BLK+flip*half)%T,BLK),BLK)
            here=slice(i*BLK,kc)
            if h==0:
                o_ref[rows,:]=o.astype(BF16)
                lse_ref[0,here,:]=jnp.broadcast_to(lse,(BLK,128))
            else:
                o_ref[rows,:]=jnp.where(mine,o,o_ref[rows,:].astype(F32)).astype(BF16)
                lse_ref[0,here,:]=jnp.where(mine,lse,lse_ref[0,here,:])

def attend_forward(sp,projected0,projected1,rows):
    _,half,HD=projected0.shape; pairs=HD//128; T=2*half
    part=pl.BlockSpec((3,half,128),lambda p,s:(0,0,p))
    return pl.pallas_call(
        fwd_kernel,
        grid_spec=pltpu.PrefetchScalarGridSpec(
            num_scalar_prefetch=1,grid=(pairs,),
            in_specs=[part,part,pl.BlockSpec((1,2,rows.shape[2]),lambda p,s:(p,0,0))],
            out_specs=[pl.BlockSpec((T,128),lambda p,s:(0,p)),pl.BlockSpec((1,T,128),lambda p,s:(p,0,0))],
            scratch_shapes=[pltpu.VMEM((2,T,128),BF16)]*3),
        out_shape=[jax.ShapeDtypeStruct((T,HD),BF16),jax.ShapeDtypeStruct((pairs,T,128),F32)],
        cost_estimate=cost(8*T*T*HD,8*T*HD+512*pairs*T),
        name="attend_forward",
    )(sp,projected0,projected1,rows)

def diagonal_sums(acc, offset):
    W=2*BLK
    wide=jnp.concatenate([acc,jnp.zeros_like(acc)],axis=1)
    n=BLK
    while n>1:
        n//=2
        top=wide[:n]; bottom=wide[n:2*n]
        wide=top+pltpu.roll(bottom,W-n,1)
    return pltpu.roll(wide,offset,1) if offset else wide

def bwd_kernel(sp, a_ref,c_ref,d0_ref,d1_ref,o_ref,lse_ref,b_ref,g_ref,d_ref,qs,ks,vs,dos,dq,acc0,acc1):
    half=a_ref.shape[1]; T=2*half; flip=sp[0]; length=sp[1]
    lane=lax.broadcasted_iota(jnp.int32,(1,128),1)
    W=2*BLK
    n=T//BLK
    for a,(ref,do_ref) in enumerate(((a_ref,d0_ref),(c_ref,d1_ref))):
        start=pl.multiple_of((a^flip)*half,half)
        dst=pl.ds(start,half)
        q=ref[0].astype(F32); k=ref[1].astype(F32); v=ref[2].astype(F32)
        do=do_ref[...].astype(F32)
        prod=do*o_ref[a*half:(a+1)*half,:].astype(F32)
        lse=lse_ref[0,dst,:]
        pos=lax.broadcasted_iota(jnp.int32,(half,1),0)+start
        gone=jnp.where(pos<length,0.0,NEG).astype(F32)
        for h in range(2):
            mine=(lane//DH)==h
            s0=DH*(1-h)
            delta=jnp.sum(jnp.where(mine,prod,0.0),axis=1,keepdims=True)
            dh,dm,dl=split3(delta)
            lh,lm,ll=split3(lse[:,DH*h:DH*h+1])
            def lanes(base,vals):
                out=0.0
                for t,val in enumerate(vals): out=jnp.where(lane==s0+t,val,out)
                return jnp.where(mine,base,out).astype(BF16)
            qs[h,dst,:]=lanes(q*DH**-0.5,(1.0,-lh,-lm,-ll))
            ks[h,dst,:]=lanes(k,(gone,1.0,1.0,1.0))
            vs[h,dst,:]=lanes(v,(1.0,1.0,1.0))
            dos[h,dst,:]=lanes(do,(-dh,-dm,-dl))
    for h in range(2):
        mine=(lane//DH)==h
        t0=toeplitz(b_ref[0,h:h+1,2*W:3*W]); t1=toeplitz(b_ref[0,h:h+1,3*W:])
        for j in range(n):
            cols=slice(j*BLK,T)
            rj=slice(j*BLK,(j+1)*BLK)
            s=lax.dot_general(ks[h,rj,:],qs[h,cols,:],(((1,),(1,)),((),())),preferred_element_type=F32)
            dp=lax.dot_general(vs[h,rj,:],dos[h,cols,:],(((1,),(1,)),((),())),preferred_element_type=F32)
            ps=[];dss=[]
            for b in range(n-j):
                c=slice(b*BLK,(b+1)*BLK)
                x=s[:,c]
                if b==0: x=x+t0
                if b==1: x=x+t1
                p=jnp.exp(x)
                ds=p*dp[:,c]
                if b==0:
                    if j==0: acc0[...]=ds
                    else: acc0[...]+=ds
                if b==1:
                    if j==0: acc1[...]=ds
                    else: acc1[...]+=ds
                ps.append(p.astype(BF16)); dss.append(ds.astype(BF16))
            p=jnp.concatenate(ps,axis=1); ds=jnp.concatenate(dss,axis=1)
            dv=jnp.dot(p,dos[h,cols,:],preferred_element_type=F32)
            dk=jnp.dot(ds,qs[h,cols,:],preferred_element_type=F32)
            kk=jnp.where(mine,ks[h,rj,:].astype(F32),1.0).astype(BF16)
            dqj=lax.dot_general(ds,kk,(((0,),(0,)),((),())),preferred_element_type=F32)
            if j==0: dq[h,:,:]=dqj
            else: dq[h,cols,:]+=dqj
            rows=pl.ds(pl.multiple_of((j*BLK+flip*half)%T,BLK),BLK)
            if h==0:
                g_ref[1,rows,:]=dk.astype(BF16); g_ref[2,rows,:]=dv.astype(BF16)
            else:
                g_ref[1,rows,:]=jnp.where(mine,dk,g_ref[1,rows,:].astype(F32)).astype(BF16)
                g_ref[2,rows,:]=jnp.where(mine,dv,g_ref[2,rows,:].astype(F32)).astype(BF16)
        near=diagonal_sums(acc0[...],0)
        near1=diagonal_sums(acc1[...],BLK)
        d_ref[0,h:h+1,:]=near+near1
        total=jnp.sum(dq[h,:,:],axis=0,keepdims=True)[:,DH*(1-h):DH*(1-h)+1]
        d_ref[0,2+h:3+h,:]=jnp.broadcast_to(total,(1,W))
    first=(lane//DH)==0
    for a in range(2):
        dst=pl.ds(pl.multiple_of((a^flip)*half,half),half)
        g_ref[0,a*half:(a+1)*half,:]=(jnp.where(first,dq[0,dst,:],dq[1,dst,:])*DH**-0.5).astype(BF16)

def attend_backward(sp,projected0,projected1,grad0,grad1,mixed,lse,rows):
    _,half,HD=projected0.shape; pairs=HD//128; T=2*half
    part=pl.BlockSpec((3,half,128),lambda p,s:(0,0,p))
    grad=pl.BlockSpec((half,128),lambda p,s:(0,p))
    return pl.pallas_call(
        bwd_kernel,
        grid_spec=pltpu.PrefetchScalarGridSpec(
            num_scalar_prefetch=1,grid=(pairs,),
            in_specs=[part,part,grad,grad,pl.BlockSpec((T,128),lambda p,s:(0,p)),
              pl.BlockSpec((1,T,128),lambda p,s:(p,0,0)),pl.BlockSpec((1,2,rows.shape[2]),lambda p,s:(p,0,0))],
            out_specs=[pl.BlockSpec((3,T,128),lambda p,s:(0,0,p)),pl.BlockSpec((1,4,2*BLK),lambda p,s:(p,0,0))],
            scratch_shapes=[pltpu.VMEM((2,T,128),BF16)]*4+[pltpu.VMEM((2,T,128),F32)]+[pltpu.VMEM((BLK,BLK),F32)]*2),
        out_shape=[jax.ShapeDtypeStruct((3,T,HD),BF16),jax.ShapeDtypeStruct((pairs,4,2*BLK),F32)],
        cost_estimate=cost(20*T*T*HD,16*T*HD+512*pairs*T),
        name="attend_backward",
    )(sp,projected0,projected1,grad0,grad1,mixed,lse,rows)

def bias_grad(sums, buckets):
    pairs=sums.shape[0]; W=2*BLK
    tab=bucket_table(W,buckets,MAXDIST)
    assert tab[BLK]==buckets-1
    m=np.zeros((W,buckets),np.float32)
    for d in range(W):
        if tab[d]<buckets-1:
            m[d,tab[d]]=1; m[d,buckets-1]=-1
    near=sums[:,0:2].reshape(pairs*2,W); total=sums[:,2:4,0].reshape(pairs*2,1)
    last=np.zeros((1,buckets),np.float32); last[0,-1]=1
    return jnp.dot(near,jnp.asarray(m),precision=HIGHEST)+total*jnp.asarray(last)


HALF_TANH = math.sqrt(2.0 / math.pi)


def dot(a, b, ca, cb):
    return lax.dot_general(a, b, (((ca,), (cb,)), ((), ())), preferred_element_type=F32)


def fixed(shape):
    return pl.BlockSpec(shape, lambda *_: (0,) * len(shape))


def cost(flops, moved):
    return pl.CostEstimate(flops=int(flops), transcendentals=0, bytes_accessed=int(moved))


def row_norm(values):
    center = jnp.mean(values, axis=-1, keepdims=True)
    centered = values - center
    inverse = lax.rsqrt(jnp.mean(centered * centered, axis=-1, keepdims=True) + EPS)
    return centered * inverse, inverse


def project_kernel(x_ref, gain_ref, shift_ref, w_ref, low_ref, out_ref):
    normed, _ = row_norm(x_ref[...].astype(F32))
    low = (normed * gain_ref[...] + shift_ref[...]).astype(BF16)
    low_ref[...] = low
    for c in range(3):
        out_ref[c] = dot(low, w_ref[c], 1, 0).astype(BF16)


def project(x, gain, shift, weight):
    rows, model = x.shape
    width = weight.shape[2]
    step = min(256, rows)
    return pl.pallas_call(
        project_kernel,
        grid=(rows // step,),
        in_specs=[pl.BlockSpec((step, model), lambda i: (i, 0)), fixed((1, model)), fixed((1, model)), fixed(weight.shape)],
        out_specs=[pl.BlockSpec((step, model), lambda i: (i, 0)), pl.BlockSpec((3, step, width), lambda i: (0, i, 0))],
        out_shape=[jax.ShapeDtypeStruct((rows, model), BF16), jax.ShapeDtypeStruct((3, rows, width), BF16)],
        cost_estimate=cost(6 * rows * model * width, 2 * (2 * rows * model + weight.size + 3 * rows * width)),
        name="project",
    )(x, gain, shift, weight)


def mix_kernel(own_blocks, x0_ref, x1_ref, m_ref, p_ref, w0_ref, w1_ref, gain_ref, shift_ref, mid_ref, low_ref):
    i = pl.program_id(0)
    attended = dot(m_ref[...], w0_ref[...], 1, 0) + dot(p_ref[...], w1_ref[...], 1, 0)

    def rows(x_ref):
        return x_ref[...].astype(F32) + attended

    def rest(middle):
        normed, _ = row_norm(middle)
        low_ref[...] = (normed * gain_ref[...] + shift_ref[...]).astype(BF16)

    @pl.when(i < own_blocks)
    def _():
        middle = rows(x0_ref)
        mid_ref[...] = middle
        rest(middle)

    @pl.when(i >= own_blocks)
    def _():
        rest(rows(x1_ref))


def mix(tokens, other, mixed, mixed_other, weight, weight_other, gain, shift):
    own, model = tokens.shape
    width = mixed.shape[1]
    step = 256
    n = own // step
    return pl.pallas_call(
        functools.partial(mix_kernel, n),
        grid=(2 * n,),
        in_specs=[
            pl.BlockSpec((step, model), lambda i: (jnp.minimum(i, n - 1), 0)),
            pl.BlockSpec((step, model), lambda i: (jnp.maximum(i - n, 0), 0)),
            pl.BlockSpec((step, width), lambda i: (i, 0)),
            pl.BlockSpec((step, width), lambda i: ((i + n) % (2 * n), 0)),
            fixed(weight.shape), fixed(weight.shape), fixed((1, model)), fixed((1, model)),
        ],
        out_specs=[
            pl.BlockSpec((step, model), lambda i: (jnp.minimum(i, n - 1), 0)),
            pl.BlockSpec((step, model), lambda i: (i, 0)),
        ],
        out_shape=[jax.ShapeDtypeStruct((own, model), F32), jax.ShapeDtypeStruct((2 * own, model), BF16)],
        cost_estimate=cost(8 * own * model * width, 2 * (4 * own * model + 4 * own * width + 2 * weight.size) + 4 * own * model),
        name="mix",
    )(tokens, other, mixed, mixed_other, weight, weight_other, gain, shift)


def expand_kernel(x_ref, g_ref, w_ref, b_ref, act_ref, ge_ref, gs_ref, bias_ref, acc_ref):
    i = pl.program_id(0)
    x = x_ref[...]
    width = w_ref.shape[1]
    sub = 256
    total = None
    for s in range(width // sub):
        cols = slice(s * sub, (s + 1) * sub)
        u = dot(x, w_ref[:, cols], 1, 0) + b_ref[:, cols].astype(F32)
        square = u * u
        t = jnp.tanh(HALF_TANH * u * (1.0 + 0.044715 * square))
        half = 0.5 + 0.5 * t
        act_ref[:, cols] = (u * half).astype(BF16)
        slope = half + 0.5 * u * (1.0 - t * t) * (HALF_TANH * (1.0 + 3 * 0.044715 * square))
        grad = g_ref[:, cols].astype(F32) * slope
        low = grad.astype(BF16)
        ge_ref[:, cols] = low
        bias_ref[:, cols] = jnp.sum(grad, axis=0, keepdims=True)
        part = dot(low, w_ref[:, cols], 1, 1)
        total = part if total is None else total + part

    @pl.when(i == 0)
    def _():
        acc_ref[...] = total

    @pl.when(i > 0)
    def _():
        acc_ref[...] += total

    @pl.when(i == pl.num_programs(0) - 1)
    def _():
        gs_ref[...] = acc_ref[...].astype(gs_ref.dtype)


def expand(x, block, rows, grad_active, weight, bias, dtype):
    model = x.shape[1]
    hidden = weight.shape[1]
    step = min(512, hidden)
    return pl.pallas_call(
        expand_kernel,
        grid=(hidden // step,),
        in_specs=[
            pl.BlockSpec((rows, model), lambda i: (block, 0)),
            pl.BlockSpec((rows, step), lambda i: (0, i)),
            pl.BlockSpec((model, step), lambda i: (0, i)),
            pl.BlockSpec((1, step), lambda i: (0, i)),
        ],
        out_specs=[
            pl.BlockSpec((rows, step), lambda i: (0, i)),
            pl.BlockSpec((rows, step), lambda i: (0, i)),
            fixed((rows, model)),
            pl.BlockSpec((1, step), lambda i: (0, i)),
        ],
        out_shape=[
            jax.ShapeDtypeStruct((rows, hidden), BF16),
            jax.ShapeDtypeStruct((rows, hidden), BF16),
            jax.ShapeDtypeStruct((rows, model), dtype),
            jax.ShapeDtypeStruct((1, hidden), F32),
        ],
        scratch_shapes=[pltpu.VMEM((rows, model), F32)],
        cost_estimate=cost(4 * rows * model * hidden, 2 * (2 * rows * model + 3 * rows * hidden + weight.size)),
        name="expand",
    )(x, grad_active, weight, bias)


STAGES = ((1, 2, 4, 8), (1, 4, 8, 2))


def place_of(index, stages):
    bit = [(index // s) % 2 for s in stages]
    return bit[0] * 4 + bit[1] * 2 + bit[2]


def trade(x, bit):
    size = lax.axis_size("dp")
    return lax.ppermute(x, "dp", [(i, i ^ bit) for i in range(size)])


def add_low(a, b):
    return (a.astype(F32) + b.astype(F32)).astype(BF16)


def chunk_specs(tail):
    zeros = (0,) * len(tail)
    return [
        pl.BlockSpec((1, *tail), lambda g, s: (jnp.minimum(g, 3), *zeros)),
        pl.BlockSpec((1, *tail), lambda g, s: (jnp.maximum(g - 4, 0), *zeros)),
    ]


def chunk_at(slot):
    return lambda g, s: ((g + 4) % 8) ^ s[slot]


def store_chunk(value, slot, send_ref, keep_ref):
    g = pl.program_id(0)

    @pl.when(g < 4)
    def _():
        send_ref[(0, *slot)] = value

    @pl.when(g >= 4)
    def _():
        keep_ref[(0, *slot)] = value


def chunk_shapes(tail):
    return [jax.ShapeDtypeStruct((4, *tail), BF16)] * 2


def reduce_grad_kernel(s_ref, a0_ref, a1_ref, t0_ref, t1_ref, send_ref, keep_ref):
    value = dot(a0_ref[...], t0_ref[...], 0, 0) + dot(a1_ref[...], t1_ref[...], 0, 0)
    store_chunk(value.astype(BF16), (), send_ref, keep_ref)


def reduce_grad_chunks(places, slot, act0, act1, t0, t1):
    rows, hidden = act0.shape
    model = t0.shape[1]
    width = hidden // 8
    at = chunk_at(slot)
    block = pl.BlockSpec((rows, width), lambda g, s: (0, at(g, s)))
    whole = pl.BlockSpec((rows, model), lambda g, s: (0, 0))
    return pl.pallas_call(
        reduce_grad_kernel,
        grid_spec=pltpu.PrefetchScalarGridSpec(
            num_scalar_prefetch=1, grid=(8,), in_specs=[block, block, whole, whole], out_specs=chunk_specs((width, model)),
        ),
        out_shape=chunk_shapes((width, model)),
        cost_estimate=cost(4 * rows * model * hidden, 4 * rows * (model + hidden) + 2 * model * hidden),
        name="reduce_grad",
    )(places, act0, act1, t0, t1)


def expand_grad_kernel(s_ref, x_ref, g0_ref, g1_ref, send_ref, keep_ref, turned_ref):
    rows = g0_ref.shape[0]

    @pl.when(pl.program_id(0) == 0)
    def _():
        turned_ref[...] = x_ref[...].T

    value = dot(turned_ref[:, :rows], g0_ref[...], 1, 0) + dot(turned_ref[:, rows:], g1_ref[...], 1, 0)
    store_chunk(value.astype(BF16), (), send_ref, keep_ref)


def expand_grad_chunks(places, slot, x, g0, g1):
    rows, hidden = g0.shape
    model = x.shape[1]
    width = hidden // 8
    at = chunk_at(slot)
    block = pl.BlockSpec((rows, width), lambda g, s: (0, at(g, s)))
    return pl.pallas_call(
        expand_grad_kernel,
        grid_spec=pltpu.PrefetchScalarGridSpec(
            num_scalar_prefetch=1, grid=(8,),
            in_specs=[pl.BlockSpec(x.shape, lambda g, s: (0, 0)), block, block],
            out_specs=chunk_specs((model, width)),
            scratch_shapes=[pltpu.VMEM((model, x.shape[0]), BF16)],
        ),
        out_shape=chunk_shapes((model, width)),
        cost_estimate=cost(4 * rows * model * hidden, 4 * rows * (model + hidden) + 2 * model * hidden),
        name="expand_grad",
    )(places, x, g0, g1)


def heads_grad_kernel(s_ref, l0_ref, l1_ref, g_ref, send_ref, keep_ref):
    rows = l0_ref.shape[0]
    for c in range(2):
        value = dot(l0_ref[...], g_ref[c, :rows], 0, 0) + dot(l1_ref[...], g_ref[c, rows:], 0, 0)
        store_chunk(value.astype(BF16), (c,), send_ref, keep_ref)


def heads_grad_chunks(places, slot, low0, low1, grad):
    rows, model = low0.shape
    width = grad.shape[2]
    at = chunk_at(slot)
    block = pl.BlockSpec((rows, model // 8), lambda g, s: (0, at(g, s)))
    tail = (2, model // 8, width)
    return pl.pallas_call(
        heads_grad_kernel,
        grid_spec=pltpu.PrefetchScalarGridSpec(
            num_scalar_prefetch=1, grid=(8,),
            in_specs=[block, block, pl.BlockSpec((2, 2 * rows, width), lambda g, s: (0, 0, 0))],
            out_specs=chunk_specs(tail),
        ),
        out_shape=chunk_shapes(tail),
        cost_estimate=cost(8 * rows * model * width, 4 * rows * (model + 2 * width) + 4 * model * width),
        name="heads_grad",
    )(places, low0, low1, grad)


def values_grad_kernel(s_ref, l0_ref, l1_ref, g_ref, a0_ref, a1_ref, m_ref, send_ref, keep_ref):
    rows = l0_ref.shape[0]
    value = dot(l0_ref[...], g_ref[0, :rows], 0, 0) + dot(l1_ref[...], g_ref[0, rows:], 0, 0)
    store_chunk(value.astype(BF16), (0,), send_ref, keep_ref)
    value = dot(a0_ref[...], m_ref[:rows], 0, 0) + dot(a1_ref[...], m_ref[rows:], 0, 0)
    store_chunk(value.astype(BF16), (1,), send_ref, keep_ref)


def values_grad_chunks(places, slot, low0, low1, grad, att0, att1, mixed):
    rows, model = low0.shape
    width = grad.shape[2]
    at = chunk_at(slot)
    block = pl.BlockSpec((rows, model // 8), lambda g, s: (0, at(g, s)))
    tail = (2, model // 8, width)
    return pl.pallas_call(
        values_grad_kernel,
        grid_spec=pltpu.PrefetchScalarGridSpec(
            num_scalar_prefetch=1, grid=(8,),
            in_specs=[block, block, pl.BlockSpec((1, 2 * rows, width), lambda g, s: (2, 0, 0)), block, block,
                      pl.BlockSpec((2 * rows, width), lambda g, s: (0, 0))],
            out_specs=chunk_specs(tail),
        ),
        out_shape=chunk_shapes(tail),
        cost_estimate=cost(8 * rows * model * width, 4 * rows * (2 * model + 2 * width) + 4 * model * width),
        name="values_grad",
    )(places, low0, low1, grad, att0, att1, mixed)


def sum_chunks(send, keep, stages):
    got = trade(send, stages[0])
    out, stay = add_low(keep[2:], got[2:]), add_low(keep[:2], got[:2])
    got = trade(out, stages[1])
    out, stay = add_low(stay[1:], got[1:]), add_low(stay[:1], got[:1])
    got = trade(out, stages[2])
    stay = add_low(stay, got)
    stay = add_low(stay, trade(stay, stages[3]))
    first = jnp.concatenate([stay, trade(stay, stages[2])], axis=0)
    second = trade(first, stages[1])
    return first, second, trade(first, stages[0]), trade(second, stages[0])


def spread_kernel(put, s_ref, *refs):
    g = pl.program_id(0)
    pieces, outs = refs[-4 - put.outs:-put.outs], refs[-put.outs:]
    for a in range(4):
        @pl.when(g // 2 == a)
        def _(a=a):
            put(pieces[a], outs)


def spread(places, slot, pieces, put, tail, out_specs, out_shape, given=None, name=None):
    zeros = (0,) * len(tail)
    at = lambda g, s: g ^ s[slot]
    in_specs = [
        pl.BlockSpec((1, *tail), lambda g, s, a=a: (jnp.clip(g - 2 * a, 0, 1), *zeros)) for a in range(4)
    ]
    args = list(pieces)
    aliases = {}
    if given is not None:
        in_specs.insert(0, pl.BlockSpec(memory_space=pl.ANY))
        args.insert(0, given)
        aliases = {1: 0}
    return pl.pallas_call(
        functools.partial(spread_kernel, put),
        grid_spec=pltpu.PrefetchScalarGridSpec(
            num_scalar_prefetch=1, grid=(8,), in_specs=in_specs, out_specs=[spec(at) for spec in out_specs],
        ),
        out_shape=out_shape,
        input_output_aliases=aliases,
        cost_estimate=cost(0, 6 * 8 * math.prod(tail)),
        name=name,
    )(places, *args)


def put_rows(piece, outs):
    outs[0][...] = piece[0].astype(F32)


put_rows.outs = 1


def put_values(piece, outs):
    outs[0][0] = piece[0, 0].astype(F32)
    outs[1][...] = piece[0, 1].astype(F32).T


put_values.outs = 2


def normalize(values):
    return row_norm(values)


def norm_back(grad_norm, normed, inverse):
    return inverse * (
        grad_norm
        - jnp.mean(grad_norm, axis=-1, keepdims=True)
        - normed * jnp.mean(grad_norm * normed, axis=-1, keepdims=True)
    )


def gelu_back(expanded, grad_active):
    pull = jax.vjp(lambda value: jax.nn.gelu(value, approximate=True), expanded)[1]
    return pull(grad_active)[0]


def swap(x):
    return lax.ppermute(x, "mp", [(0, 1), (1, 0)])


def keep_valid(x, places, length):
    return jnp.where((places < length)[:, None], x, jnp.zeros_like(x))


def paired(
    tokens, lengths, first_gain, first_shift, heads_weight, relative_bias, mixer_weight, second_gain,
    second_shift, expand_weight, expand_bias, reduce_weight, reduce_bias, cotangent,
):
    member = lax.axis_index("mp")
    index = lax.axis_index("dp")
    length = lengths[0]
    own, model = tokens.shape
    buckets = relative_bias.shape[1]
    width = heads_weight.shape[2]
    sp = jnp.stack([member.astype(jnp.int32), length.astype(jnp.int32)])
    chunk_place = jnp.stack([place_of(index, s).astype(jnp.int32) for s in STAGES])
    places = member * own + jnp.arange(own)
    places_other = (1 - member) * own + jnp.arange(own)
    rows = bias_rows(relative_bias)
    line = lambda v: v.reshape(1, -1)

    other = swap(tokens)
    low0, projected0 = project(tokens, line(first_gain), line(first_shift), heads_weight)
    target0 = keep_valid(cotangent, places, length)
    cotangent_late, other = lax.optimization_barrier((cotangent, other))
    mixer_late, _ = lax.optimization_barrier((mixer_weight, other))
    cotangent_other = swap(cotangent_late)
    mixer_other = swap(mixer_late)
    low1, projected1 = project(other, line(first_gain), line(first_shift), heads_weight)
    mixed, logsum = attend_forward(sp, projected0, projected1, rows)
    mixed_other = swap(mixed)
    target1 = keep_valid(cotangent_other, places_other, length)
    active_grad0 = dot(target0, reduce_weight, 1, 1).astype(BF16)
    active_grad1 = dot(target1, reduce_weight, 1, 1).astype(BF16)
    middle, second = mix(tokens, other, mixed, mixed_other, mixer_weight, mixer_other, line(second_gain), line(second_shift))
    act1, ge1, gs1, eb1 = expand(second, 1, own, active_grad1, expand_weight, line(expand_bias), BF16)
    gs_got = swap(gs1)
    act0, ge0, gs0, eb0 = expand(second, 0, own, active_grad0, expand_weight, line(expand_bias), F32)

    reduce_sums = sum_chunks(*reduce_grad_chunks(chunk_place, 0, act0, act1, target0, target1), STAGES[0])
    expand_sums = sum_chunks(*expand_grad_chunks(chunk_place, 1, second, ge0, ge1), STAGES[1])

    second_norm, second_inverse = normalize(middle)
    grad_second = gs0 + gs_got.astype(F32)
    target_wide = target0.astype(F32)
    grad_middle = target_wide + norm_back(grad_second * second_gain, second_norm, second_inverse)
    attended0 = grad_middle.astype(BF16)
    attended1 = swap(attended0)
    grad_mixed0 = dot(attended0, mixer_weight, 1, 1).astype(BF16)
    grad_mixed1 = dot(attended1, mixer_weight, 1, 1).astype(BF16)

    reduced_got = swap(dot(act1, reduce_weight, 1, 0).astype(BF16))
    block_out = (middle + dot(act0, reduce_weight, 1, 0) + reduced_got.astype(F32) + reduce_bias).astype(BF16)

    grad_projected, sums = attend_backward(sp, projected0, projected1, grad_mixed0, grad_mixed1, mixed, logsum, rows)
    first_part1 = sum(dot(grad_projected[c, own:], heads_weight[c], 1, 1) for c in range(3)).astype(BF16)
    first_got = swap(first_part1)
    query_sums = sum_chunks(*heads_grad_chunks(chunk_place, 0, low0, low1, grad_projected), STAGES[0])
    value_sums = sum_chunks(
        *values_grad_chunks(chunk_place, 1, low0, low1, grad_projected, attended0, attended1, mixed), STAGES[1]
    )
    first_part0 = sum(dot(grad_projected[c, :own], heads_weight[c], 1, 1) for c in range(3))
    grad_first = first_part0 + first_got.astype(F32)
    first_norm, first_inverse = normalize(tokens.astype(F32))
    tokens_grad = (
        grad_middle + norm_back(grad_first * first_gain, first_norm, first_inverse)
    ).astype(BF16)

    both = jnp.stack([
        jnp.sum(grad_first * first_norm, axis=0),
        jnp.sum(grad_first, axis=0),
        jnp.sum(grad_second * second_norm, axis=0),
        jnp.sum(grad_second, axis=0),
        jnp.sum(target_wide, axis=0),
    ])
    both = both + swap(both)
    hidden = expand_bias.shape[0]
    bias_part = bias_grad(sums, buckets)
    pack = jnp.concatenate([both.reshape(-1), (eb0 + eb1).reshape(-1), bias_part.reshape(-1)]).reshape(-1, 128)
    for bit in (1, 2, 4, 8):
        pack = pack + trade(pack, bit)
    pack = pack.reshape(-1)
    both = pack[: 5 * model].reshape(5, model)
    expand_bias_grad = pack[5 * model : 5 * model + hidden]
    bias_part = pack[5 * model + hidden :].reshape(relative_bias.shape)

    chunk = (hidden // 8, model)
    (reduce_grad,) = spread(
        chunk_place, 0, reduce_sums, put_rows, chunk,
        [lambda at: pl.BlockSpec(chunk, lambda g, s: (at(g, s), 0))],
        [jax.ShapeDtypeStruct(reduce_weight.shape, F32)], name="spread_reduce",
    )
    turned = (model, hidden // 8)
    (expand_grad,) = spread(
        chunk_place, 1, expand_sums, put_rows, turned,
        [lambda at: pl.BlockSpec(turned, lambda g, s: (0, at(g, s)))],
        [jax.ShapeDtypeStruct(expand_weight.shape, F32)], name="spread_expand",
    )
    piece = (2, model // 8, width)
    (heads_grad,) = spread(
        chunk_place, 0, query_sums, put_rows, piece,
        [lambda at: pl.BlockSpec(piece, lambda g, s: (0, at(g, s), 0))],
        [jax.ShapeDtypeStruct(heads_weight.shape, F32)], name="spread_queries",
    )
    heads_grad, mixer_grad = spread(
        chunk_place, 1, value_sums, put_values, piece,
        [
            lambda at: pl.BlockSpec((1, model // 8, width), lambda g, s: (2, at(g, s), 0)),
            lambda at: pl.BlockSpec((width, model // 8), lambda g, s: (0, at(g, s))),
        ],
        [jax.ShapeDtypeStruct(heads_weight.shape, F32), jax.ShapeDtypeStruct(mixer_weight.shape, F32)],
        given=heads_grad, name="spread_values",
    )
    return (
        block_out, tokens_grad, both[0], both[1], heads_grad, bias_part, mixer_grad, both[2], both[3],
        expand_grad, expand_bias_grad, reduce_grad, both[4],
    )


def gathered(
    tokens, lengths, first_gain, first_shift, heads_weight, relative_bias, mixer_weight, second_gain,
    second_shift, expand_weight, expand_bias, reduce_weight, reduce_bias, cotangent,
):
    def gather(x):
        return lax.all_gather(x, "mp", axis=0, tiled=True)

    def scatter(x):
        return lax.psum_scatter(x.astype(BF16), "mp", scatter_dimension=0, tiled=True).astype(F32)

    members = lax.axis_size("mp")
    length = lengths[0]
    own = tokens.shape[0]
    whole = own * members
    half = whole // 2
    buckets = relative_bias.shape[1]
    sp = jnp.stack([jnp.zeros((), jnp.int32), length.astype(jnp.int32)])
    places = lax.axis_index("mp") * own + jnp.arange(own)
    rows = bias_rows(relative_bias)
    source_all = gather(tokens)
    first_all, projected = project(source_all, first_gain.reshape(1, -1), first_shift.reshape(1, -1), heads_weight)
    projected0, projected1 = projected[:, :half], projected[:, half:]
    mixed, logsum = attend_forward(sp, projected0, projected1, rows)
    source = tokens.astype(F32)
    middle = source + scatter(dot(mixed, mixer_weight, 1, 0))
    second_norm, second_inverse = normalize(middle)
    second_all = gather((second_norm * second_gain + second_shift).astype(BF16))
    target = keep_valid(cotangent, places, length)
    target_wide = target.astype(F32)
    target_all = gather(target)
    expanded = dot(second_all, expand_weight, 1, 0) + expand_bias
    active_low = jax.nn.gelu(expanded, approximate=True).astype(BF16)
    grad_expanded = gelu_back(expanded, dot(target_all, reduce_weight, 1, 1)).astype(BF16)
    grad_second = scatter(dot(grad_expanded, expand_weight, 1, 1))
    reduced = scatter(dot(active_low, reduce_weight, 1, 0))
    reduce_grad = dot(active_low, target_all, 0, 0)
    expand_grad = dot(second_all, grad_expanded, 0, 0)
    expand_bias_grad = jnp.sum(grad_expanded.astype(F32), axis=0)
    block_out = (middle + reduced + reduce_bias).astype(BF16)
    grad_middle = target_wide + norm_back(grad_second * second_gain, second_norm, second_inverse)
    attended_all = gather(grad_middle.astype(BF16))
    mixer_grad = dot(mixed, attended_all, 0, 0)
    grad_mixed = dot(attended_all, mixer_weight, 1, 1).astype(BF16)
    grad_projected, sums = attend_backward(
        sp, projected0, projected1, grad_mixed[:half], grad_mixed[half:], mixed, logsum, rows
    )
    bias_part = bias_grad(sums, buckets)
    heads_grad = jnp.einsum("td,cte->cde", first_all, grad_projected, preferred_element_type=F32)
    grad_first = scatter(jnp.einsum("cte,cde->td", grad_projected, heads_weight, preferred_element_type=F32))
    first_norm, first_inverse = normalize(source)
    tokens_grad = (
        grad_middle + norm_back(grad_first * first_gain, first_norm, first_inverse)
    ).astype(BF16)
    first_gain_grad, first_shift_grad, second_gain_grad, second_shift_grad, reduce_bias_grad = (
        lax.psum(
            (
                jnp.sum(grad_first * first_norm, axis=0),
                jnp.sum(grad_first, axis=0),
                jnp.sum(grad_second * second_norm, axis=0),
                jnp.sum(grad_second, axis=0),
                jnp.sum(target_wide, axis=0),
            ),
            ("dp", "mp"),
        )
    )
    heads_grad, bias_part, mixer_grad, expand_grad, expand_bias_grad, reduce_grad = (
        lax.psum(x.astype(BF16), "dp").astype(F32)
        for x in (heads_grad, bias_part, mixer_grad, expand_grad, expand_bias_grad, reduce_grad)
    )
    return (
        block_out, tokens_grad, first_gain_grad, first_shift_grad, heads_grad, bias_part, mixer_grad,
        second_gain_grad, second_shift_grad, expand_grad, expand_bias_grad, reduce_grad, reduce_bias_grad,
    )


def per_device(*args):
    if lax.axis_size("mp") == 2 and lax.axis_size("dp") == 16:
        return paired(*args)
    return gathered(*args)


def solution(mesh):
    return jax.shard_map(
        per_device,
        mesh=mesh,
        in_specs=(
            P(("dp", "mp"), None),
            P("dp"),
            P(),
            P(),
            P(None, None, "mp"),
            P("mp", None),
            P("mp", None),
            P(),
            P(),
            P(None, "mp"),
            P("mp"),
            P("mp", None),
            P(),
            P(("dp", "mp"), None),
        ),
        out_specs=(
            P(("dp", "mp"), None),
            P(("dp", "mp"), None),
            P(),
            P(),
            P(None, None, "mp"),
            P("mp", None),
            P("mp", None),
            P(),
            P(),
            P(None, "mp"),
            P("mp"),
            P("mp", None),
            P(),
        ),
        check_vma=False,
    )
```

```python
import functools
import math

import jax
import jax.numpy as jnp
import numpy as np
from jax import lax
from jax.experimental import pallas as pl
from jax.experimental.pallas import tpu as pltpu
from jax.sharding import PartitionSpec as P

EPS = 1e-05
DH=64; MAXDIST=128; NEG=-1e30; BLK=256
F32=jnp.float32; BF16=jnp.bfloat16
HIGHEST=lax.Precision.HIGHEST

def bucket_table(count, buckets, reach):
    exact = buckets // 2
    entries = []
    for position in range(count):
        if position < exact:
            entries.append(position)
        else:
            level = exact + int(math.log(position / exact) / math.log(reach / exact) * (buckets - exact))
            entries.append(min(buckets - 1, level))
    return np.array(entries, dtype=np.int32)

def bias_tables(buckets):
    W=2*BLK
    tab=bucket_table(W,buckets,MAXDIST)
    oh=np.zeros((buckets,4,W),np.float32); neg=np.zeros((1,4,W),np.float32)
    for y in range(W):
        x = y if y < BLK else y-W
        if x<=0 and -x<BLK: oh[tab[-x],0,y]=1
        else: neg[0,0,y]=NEG
        d=BLK-x
        if 0<=d<W: oh[tab[d],1,y]=1
        if 0<=x: oh[tab[x],2,y]=1
        else: neg[0,2,y]=NEG
        d=BLK+x
        if 0<=d<W: oh[tab[d],3,y]=1
    return oh.reshape(buckets,4*W), neg.reshape(1,4*W)

def bias_rows(relative_bias):
    heads,buckets=relative_bias.shape
    oh,neg=bias_tables(buckets)
    rel=relative_bias-relative_bias[:,buckets-1:]
    rows=jnp.dot(rel,jnp.asarray(oh),precision=HIGHEST)+jnp.asarray(neg)
    return rows.reshape(heads//2,2,4*2*BLK)

def split3(x):
    hi=x.astype(BF16); rest=x-hi.astype(F32); mid=rest.astype(BF16)
    lo=(rest-mid.astype(F32)).astype(BF16)
    return hi.astype(F32),mid.astype(F32),lo.astype(F32)

def toeplitz(row):
    wide=jnp.broadcast_to(row,(BLK,2*BLK))
    return pltpu.roll(wide,0,1,stride=1,stride_axis=0)[:,:BLK]


def fwd_kernel(sp, a_ref,c_ref,b_ref,o_ref,lse_ref,qs,ks,vs):
    half=a_ref.shape[1]; T=2*half; flip=sp[0]; length=sp[1]
    lane=lax.broadcasted_iota(jnp.int32,(1,128),1)
    W=2*BLK
    for a,ref in enumerate((a_ref,c_ref)):
        start=pl.multiple_of((a^flip)*half,half)
        dst=pl.ds(start,half)
        q=ref[0].astype(F32); k=ref[1].astype(F32); v=ref[2].astype(F32)
        pos=lax.broadcasted_iota(jnp.int32,(half,1),0)+start
        gone=jnp.where(pos<length,0.0,NEG).astype(F32)
        for h in range(2):
            mine=(lane//DH)==h
            spare=lane==(DH*(1-h))
            qs[h,dst,:]=jnp.where(mine,q*DH**-0.5,jnp.where(spare,1.0,0.0)).astype(BF16)
            ks[h,dst,:]=jnp.where(mine,k,jnp.where(spare,gone,0.0)).astype(BF16)
            vs[h,dst,:]=jnp.where(mine,v,1.0).astype(BF16)
    for h in range(2):
        mine=(lane//DH)==h
        t0=toeplitz(b_ref[0,h:h+1,0:W]); t1=toeplitz(b_ref[0,h:h+1,W:2*W])
        for i in range(T//BLK):
            kc=(i+1)*BLK
            s=lax.dot_general(qs[h,i*BLK:kc,:],ks[h,:kc,:],(((1,),(1,)),((),())),preferred_element_type=F32)
            parts=[]
            if i>=2: parts.append(s[:,:kc-2*BLK])
            if i>=1: parts.append(s[:,kc-2*BLK:kc-BLK]+t1)
            parts.append(s[:,kc-BLK:]+t0)
            top=functools.reduce(jnp.maximum,[jnp.max(x,axis=1,keepdims=True) for x in parts])
            p=jnp.concatenate([jnp.exp(x-top).astype(BF16) for x in parts],axis=1)
            o=jnp.dot(p,vs[h,:kc,:],preferred_element_type=F32)
            total=o[:,DH*(1-h):DH*(1-h)+1]
            o=o/total
            lse=top+jnp.log(total)
            rows=pl.ds(pl.multiple_of((i*BLK+flip*half)%T,BLK),BLK)
            here=slice(i*BLK,kc)
            if h==0:
                o_ref[rows,:]=o.astype(BF16)
                lse_ref[0,here,:]=jnp.broadcast_to(lse,(BLK,128))
            else:
                o_ref[rows,:]=jnp.where(mine,o,o_ref[rows,:].astype(F32)).astype(BF16)
                lse_ref[0,here,:]=jnp.where(mine,lse,lse_ref[0,here,:])

def attend_forward(sp,projected0,projected1,rows):
    _,half,HD=projected0.shape; pairs=HD//128; T=2*half
    part=pl.BlockSpec((3,half,128),lambda p,s:(0,0,p))
    return pl.pallas_call(
        fwd_kernel,
        grid_spec=pltpu.PrefetchScalarGridSpec(
            num_scalar_prefetch=1,grid=(pairs,),
            in_specs=[part,part,pl.BlockSpec((1,2,rows.shape[2]),lambda p,s:(p,0,0))],
            out_specs=[pl.BlockSpec((T,128),lambda p,s:(0,p)),pl.BlockSpec((1,T,128),lambda p,s:(p,0,0))],
            scratch_shapes=[pltpu.VMEM((2,T,128),BF16)]*3),
        out_shape=[jax.ShapeDtypeStruct((T,HD),BF16),jax.ShapeDtypeStruct((pairs,T,128),F32)],
        cost_estimate=cost(8*T*T*HD,8*T*HD+512*pairs*T),
        name="attend_forward",
    )(sp,projected0,projected1,rows)

def diagonal_sums(acc, offset):
    W=2*BLK
    wide=jnp.concatenate([acc,jnp.zeros_like(acc)],axis=1)
    n=BLK
    while n>1:
        n//=2
        top=wide[:n]; bottom=wide[n:2*n]
        wide=top+pltpu.roll(bottom,W-n,1)
    return pltpu.roll(wide,offset,1) if offset else wide

def bwd_kernel(sp, a_ref,c_ref,d0_ref,d1_ref,o_ref,lse_ref,b_ref,g_ref,d_ref,qs,ks,vs,dos,dq,acc0,acc1):
    half=a_ref.shape[1]; T=2*half; flip=sp[0]; length=sp[1]
    lane=lax.broadcasted_iota(jnp.int32,(1,128),1)
    W=2*BLK
    n=T//BLK
    for a,(ref,do_ref) in enumerate(((a_ref,d0_ref),(c_ref,d1_ref))):
        start=pl.multiple_of((a^flip)*half,half)
        dst=pl.ds(start,half)
        q=ref[0].astype(F32); k=ref[1].astype(F32); v=ref[2].astype(F32)
        do=do_ref[...].astype(F32)
        prod=do*o_ref[a*half:(a+1)*half,:].astype(F32)
        lse=lse_ref[0,dst,:]
        pos=lax.broadcasted_iota(jnp.int32,(half,1),0)+start
        gone=jnp.where(pos<length,0.0,NEG).astype(F32)
        for h in range(2):
            mine=(lane//DH)==h
            s0=DH*(1-h)
            delta=jnp.sum(jnp.where(mine,prod,0.0),axis=1,keepdims=True)
            dh,dm,dl=split3(delta)
            lh,lm,ll=split3(lse[:,DH*h:DH*h+1])
            def lanes(base,vals):
                out=0.0
                for t,val in enumerate(vals): out=jnp.where(lane==s0+t,val,out)
                return jnp.where(mine,base,out).astype(BF16)
            qs[h,dst,:]=lanes(q*DH**-0.5,(1.0,-lh,-lm,-ll))
            ks[h,dst,:]=lanes(k,(gone,1.0,1.0,1.0))
            vs[h,dst,:]=lanes(v,(1.0,1.0,1.0))
            dos[h,dst,:]=lanes(do,(-dh,-dm,-dl))
    for h in range(2):
        mine=(lane//DH)==h
        t0=toeplitz(b_ref[0,h:h+1,2*W:3*W]); t1=toeplitz(b_ref[0,h:h+1,3*W:])
        for j in range(n):
            cols=slice(j*BLK,T)
            rj=slice(j*BLK,(j+1)*BLK)
            s=lax.dot_general(ks[h,rj,:],qs[h,cols,:],(((1,),(1,)),((),())),preferred_element_type=F32)
            dp=lax.dot_general(vs[h,rj,:],dos[h,cols,:],(((1,),(1,)),((),())),preferred_element_type=F32)
            ps=[];dss=[]
            for b in range(n-j):
                c=slice(b*BLK,(b+1)*BLK)
                x=s[:,c]
                if b==0: x=x+t0
                if b==1: x=x+t1
                p=jnp.exp(x)
                ds=p*dp[:,c]
                if b==0:
                    if j==0: acc0[...]=ds
                    else: acc0[...]+=ds
                if b==1:
                    if j==0: acc1[...]=ds
                    else: acc1[...]+=ds
                ps.append(p.astype(BF16)); dss.append(ds.astype(BF16))
            p=jnp.concatenate(ps,axis=1); ds=jnp.concatenate(dss,axis=1)
            dv=jnp.dot(p,dos[h,cols,:],preferred_element_type=F32)
            dk=jnp.dot(ds,qs[h,cols,:],preferred_element_type=F32)
            kk=jnp.where(mine,ks[h,rj,:].astype(F32),1.0).astype(BF16)
            dqj=lax.dot_general(ds,kk,(((0,),(0,)),((),())),preferred_element_type=F32)
            if j==0: dq[h,:,:]=dqj
            else: dq[h,cols,:]+=dqj
            rows=pl.ds(pl.multiple_of((j*BLK+flip*half)%T,BLK),BLK)
            if h==0:
                g_ref[1,rows,:]=dk.astype(BF16); g_ref[2,rows,:]=dv.astype(BF16)
            else:
                g_ref[1,rows,:]=jnp.where(mine,dk,g_ref[1,rows,:].astype(F32)).astype(BF16)
                g_ref[2,rows,:]=jnp.where(mine,dv,g_ref[2,rows,:].astype(F32)).astype(BF16)
        near=diagonal_sums(acc0[...],0)
        near1=diagonal_sums(acc1[...],BLK)
        d_ref[0,h:h+1,:]=near+near1
        total=jnp.sum(dq[h,:,:],axis=0,keepdims=True)[:,DH*(1-h):DH*(1-h)+1]
        d_ref[0,2+h:3+h,:]=jnp.broadcast_to(total,(1,W))
    first=(lane//DH)==0
    for a in range(2):
        dst=pl.ds(pl.multiple_of((a^flip)*half,half),half)
        g_ref[0,a*half:(a+1)*half,:]=(jnp.where(first,dq[0,dst,:],dq[1,dst,:])*DH**-0.5).astype(BF16)

def attend_backward(sp,projected0,projected1,grad0,grad1,mixed,lse,rows,start=0,count=None,given=None):
    _,half,HD=projected0.shape; pairs=HD//128; T=2*half
    count=pairs if count is None else count
    part=pl.BlockSpec((3,half,128),lambda p,s:(0,0,p+start))
    grad=pl.BlockSpec((half,128),lambda p,s:(0,p+start))
    in_specs=[part,part,grad,grad,pl.BlockSpec((T,128),lambda p,s:(0,p+start)),
              pl.BlockSpec((1,T,128),lambda p,s:(p+start,0,0)),pl.BlockSpec((1,2,rows.shape[2]),lambda p,s:(p+start,0,0))]
    args=[sp,projected0,projected1,grad0,grad1,mixed,lse,rows]
    kernel=bwd_kernel
    if given is not None:
        in_specs.append(pl.BlockSpec(memory_space=pl.ANY)); args.append(given)
        kernel=lambda *refs: bwd_kernel(*refs[:8],*refs[9:])
    return pl.pallas_call(
        kernel,
        grid_spec=pltpu.PrefetchScalarGridSpec(
            num_scalar_prefetch=1,grid=(count,),
            in_specs=in_specs,
            out_specs=[pl.BlockSpec((3,T,128),lambda p,s:(0,0,p+start)),pl.BlockSpec((1,4,2*BLK),lambda p,s:(p,0,0))],
            scratch_shapes=[pltpu.VMEM((2,T,128),BF16)]*4+[pltpu.VMEM((2,T,128),F32)]+[pltpu.VMEM((BLK,BLK),F32)]*2),
        out_shape=[jax.ShapeDtypeStruct((3,T,HD),BF16),jax.ShapeDtypeStruct((count,4,2*BLK),F32)],
        input_output_aliases={} if given is None else {8:0},
        cost_estimate=cost(20*T*T*128*count,(16*T*128+512*T)*count),
        name="attend_backward",
    )(*args)

def bias_grad(sums, buckets):
    pairs=sums.shape[0]; W=2*BLK
    tab=bucket_table(W,buckets,MAXDIST)
    assert tab[BLK]==buckets-1
    m=np.zeros((W,buckets),np.float32)
    for d in range(W):
        if tab[d]<buckets-1:
            m[d,tab[d]]=1; m[d,buckets-1]=-1
    near=sums[:,0:2].reshape(pairs*2,W); total=sums[:,2:4,0].reshape(pairs*2,1)
    last=np.zeros((1,buckets),np.float32); last[0,-1]=1
    return jnp.dot(near,jnp.asarray(m),precision=HIGHEST)+total*jnp.asarray(last)


HALF_TANH = math.sqrt(2.0 / math.pi)


def dot(a, b, ca, cb):
    return lax.dot_general(a, b, (((ca,), (cb,)), ((), ())), preferred_element_type=F32)


def fixed(shape):
    return pl.BlockSpec(shape, lambda *_: (0,) * len(shape))


def cost(flops, moved):
    return pl.CostEstimate(flops=int(flops), transcendentals=0, bytes_accessed=int(moved))


def row_norm(values):
    center = jnp.mean(values, axis=-1, keepdims=True)
    centered = values - center
    inverse = lax.rsqrt(jnp.mean(centered * centered, axis=-1, keepdims=True) + EPS)
    return centered * inverse, inverse


def project_kernel(x_ref, gain_ref, shift_ref, w_ref, low_ref, out_ref):
    normed, _ = row_norm(x_ref[...].astype(F32))
    low = (normed * gain_ref[...] + shift_ref[...]).astype(BF16)
    low_ref[...] = low
    for c in range(3):
        out_ref[c] = dot(low, w_ref[c], 1, 0).astype(BF16)


def project(x, gain, shift, weight):
    rows, model = x.shape
    width = weight.shape[2]
    step = min(256, rows)
    return pl.pallas_call(
        project_kernel,
        grid=(rows // step,),
        in_specs=[pl.BlockSpec((step, model), lambda i: (i, 0)), fixed((1, model)), fixed((1, model)), fixed(weight.shape)],
        out_specs=[pl.BlockSpec((step, model), lambda i: (i, 0)), pl.BlockSpec((3, step, width), lambda i: (0, i, 0))],
        out_shape=[jax.ShapeDtypeStruct((rows, model), BF16), jax.ShapeDtypeStruct((3, rows, width), BF16)],
        cost_estimate=cost(6 * rows * model * width, 2 * (2 * rows * model + weight.size + 3 * rows * width)),
        name="project",
    )(x, gain, shift, weight)


def mix_kernel(own_blocks, x0_ref, x1_ref, m_ref, p_ref, w0_ref, w1_ref, gain_ref, shift_ref, mid_ref, low_ref):
    i = pl.program_id(0)
    attended = dot(m_ref[...], w0_ref[...], 1, 0) + dot(p_ref[...], w1_ref[...], 1, 0)

    def rows(x_ref):
        return x_ref[...].astype(F32) + attended

    def rest(middle):
        normed, _ = row_norm(middle)
        low_ref[...] = (normed * gain_ref[...] + shift_ref[...]).astype(BF16)

    @pl.when(i < own_blocks)
    def _():
        middle = rows(x0_ref)
        mid_ref[...] = middle
        rest(middle)

    @pl.when(i >= own_blocks)
    def _():
        rest(rows(x1_ref))


def mix(tokens, other, mixed, mixed_other, weight, weight_other, gain, shift):
    own, model = tokens.shape
    width = mixed.shape[1]
    step = 256
    n = own // step
    return pl.pallas_call(
        functools.partial(mix_kernel, n),
        grid=(2 * n,),
        in_specs=[
            pl.BlockSpec((step, model), lambda i: (jnp.minimum(i, n - 1), 0)),
            pl.BlockSpec((step, model), lambda i: (jnp.maximum(i - n, 0), 0)),
            pl.BlockSpec((step, width), lambda i: (i, 0)),
            pl.BlockSpec((step, width), lambda i: ((i + n) % (2 * n), 0)),
            fixed(weight.shape), fixed(weight.shape), fixed((1, model)), fixed((1, model)),
        ],
        out_specs=[
            pl.BlockSpec((step, model), lambda i: (jnp.minimum(i, n - 1), 0)),
            pl.BlockSpec((step, model), lambda i: (i, 0)),
        ],
        out_shape=[jax.ShapeDtypeStruct((own, model), F32), jax.ShapeDtypeStruct((2 * own, model), BF16)],
        cost_estimate=cost(8 * own * model * width, 2 * (4 * own * model + 4 * own * width + 2 * weight.size) + 4 * own * model),
        name="mix",
    )(tokens, other, mixed, mixed_other, weight, weight_other, gain, shift)


def expand_kernel(x_ref, g_ref, w_ref, b_ref, act_ref, ge_ref, gs_ref, bias_ref, acc_ref):
    i = pl.program_id(0)
    x = x_ref[...]
    width = w_ref.shape[1]
    sub = 256
    total = None
    for s in range(width // sub):
        cols = slice(s * sub, (s + 1) * sub)
        u = dot(x, w_ref[:, cols], 1, 0) + b_ref[:, cols].astype(F32)
        square = u * u
        t = jnp.tanh(HALF_TANH * u * (1.0 + 0.044715 * square))
        half = 0.5 + 0.5 * t
        act_ref[:, cols] = (u * half).astype(BF16)
        slope = half + 0.5 * u * (1.0 - t * t) * (HALF_TANH * (1.0 + 3 * 0.044715 * square))
        grad = g_ref[:, cols].astype(F32) * slope
        low = grad.astype(BF16)
        ge_ref[:, cols] = low
        bias_ref[:, cols] = jnp.sum(grad, axis=0, keepdims=True)
        part = dot(low, w_ref[:, cols], 1, 1)
        total = part if total is None else total + part

    @pl.when(i == 0)
    def _():
        acc_ref[...] = total

    @pl.when(i > 0)
    def _():
        acc_ref[...] += total

    @pl.when(i == pl.num_programs(0) - 1)
    def _():
        gs_ref[...] = acc_ref[...].astype(gs_ref.dtype)


def expand(x, block, rows, grad_active, weight, bias, dtype):
    model = x.shape[1]
    hidden = weight.shape[1]
    step = min(512, hidden)
    return pl.pallas_call(
        expand_kernel,
        grid=(hidden // step,),
        in_specs=[
            pl.BlockSpec((rows, model), lambda i: (block, 0)),
            pl.BlockSpec((rows, step), lambda i: (0, i)),
            pl.BlockSpec((model, step), lambda i: (0, i)),
            pl.BlockSpec((1, step), lambda i: (0, i)),
        ],
        out_specs=[
            pl.BlockSpec((rows, step), lambda i: (0, i)),
            pl.BlockSpec((rows, step), lambda i: (0, i)),
            fixed((rows, model)),
            pl.BlockSpec((1, step), lambda i: (0, i)),
        ],
        out_shape=[
            jax.ShapeDtypeStruct((rows, hidden), BF16),
            jax.ShapeDtypeStruct((rows, hidden), BF16),
            jax.ShapeDtypeStruct((rows, model), dtype),
            jax.ShapeDtypeStruct((1, hidden), F32),
        ],
        scratch_shapes=[pltpu.VMEM((rows, model), F32)],
        cost_estimate=cost(4 * rows * model * hidden, 2 * (2 * rows * model + 3 * rows * hidden + weight.size)),
        name="expand",
    )(x, grad_active, weight, bias)


STAGES = ((1, 2, 4, 8), (1, 4, 2, 8))


def place_of(index, stages):
    bit = [(index // s) % 2 for s in stages]
    return bit[0] * 4 + bit[1] * 2 + bit[2]


def trade(x, bit):
    size = lax.axis_size("dp")
    return lax.ppermute(x, "dp", [(i, i ^ bit) for i in range(size)])


def add_low(a, b):
    return (a.astype(F32) + b.astype(F32)).astype(BF16)


def part_of(give, s, slot):
    return (s[slot] // 4) ^ give


def pair_of(give, g, s, slot):
    return part_of(give, s, slot) * 2 + ((1 - g) ^ ((s[slot] // 2) % 2))


def put_pair(give, slot, s_ref, chunks, got_ref, outs):
    flip = s_ref[slot] % 2
    for j, value in enumerate(chunks):
        at = j ^ flip
        if give:
            outs[0][pl.ds(at, 1)] = value.astype(BF16)[None]
        else:
            value = (value + got_ref[pl.ds(at, 1)][0].astype(F32)).astype(BF16)[None]
            for step, out in enumerate(outs):
                @pl.when(pl.program_id(0) == step)
                def _(out=out):
                    out[pl.ds(at, 1)] = value


def pair_call(kernel, give, slot, s, arrays, specs, tail, got, flops, name):
    zeros = (0,) * len(tail)
    if give:
        out_specs = [pl.BlockSpec((2, *tail), lambda g, s: (1 - g, *zeros))]
        out_shape = [jax.ShapeDtypeStruct((4, *tail), BF16)]
    else:
        specs = specs + [pl.BlockSpec((2, *tail), lambda g, s: (1 - g, *zeros))]
        arrays = (*arrays, got)
        out_specs = [pl.BlockSpec((2, *tail), lambda g, s: (0, *zeros))] * 2
        out_shape = [jax.ShapeDtypeStruct((2, *tail), BF16)] * 2
    moved = sum(2 * x.size for x in arrays) + 8 * math.prod(tail)
    return pl.pallas_call(
        functools.partial(kernel, give, slot),
        grid_spec=pltpu.PrefetchScalarGridSpec(num_scalar_prefetch=1, grid=(2,), in_specs=specs, out_specs=out_specs),
        out_shape=out_shape,
        cost_estimate=cost(flops, moved),
        name=name,
    )(s, *arrays)


def split_refs(give, refs, count):
    return refs[:count], (None if give else refs[count]), refs[count + (0 if give else 1):]


def reduce_grad_kernel(give, slot, s_ref, *refs):
    (a0, a1, t0, t1), got, outs = split_refs(give, refs, 4)
    value = dot(a0[...], t0[...], 0, 0) + dot(a1[...], t1[...], 0, 0)
    width = value.shape[0] // 2
    put_pair(give, slot, s_ref, [value[:width], value[width:]], got, outs)


def reduce_grad_part(s, slot, act0, act1, t0, t1, got=None):
    give = got is None
    rows, hidden = act0.shape
    model = t0.shape[1]
    block = pl.BlockSpec((rows, hidden // 4), lambda g, s: (0, pair_of(int(give), g, s, slot)))
    return pair_call(
        reduce_grad_kernel, give, slot, s, (act0, act1, t0, t1), [block, block, fixed(t0.shape), fixed(t1.shape)],
        (hidden // 8, model), got, 2 * rows * model * hidden, "reduce_grad",
    )


def expand_grad_kernel(give, slot, s_ref, *refs):
    (x, g0, g1), got, outs = split_refs(give, refs, 3)
    rows = g0.shape[0]
    value = dot(x[:rows], g0[...], 0, 0) + dot(x[rows:], g1[...], 0, 0)
    width = value.shape[1] // 2
    put_pair(give, slot, s_ref, [value[:, :width], value[:, width:]], got, outs)


def expand_grad_part(s, slot, x, g0, g1, got=None):
    give = got is None
    rows, hidden = g0.shape
    model = x.shape[1]
    block = pl.BlockSpec((rows, hidden // 4), lambda g, s: (0, pair_of(int(give), g, s, slot)))
    return pair_call(
        expand_grad_kernel, give, slot, s, (x, g0, g1), [fixed(x.shape), block, block],
        (model, hidden // 8), got, 2 * rows * model * hidden, "expand_grad",
    )


def heads_grad_kernel(give, slot, s_ref, *refs):
    (l0, l1, g), got, outs = split_refs(give, refs, 3)
    rows = l0.shape[0]
    both = [dot(l0[...], g[c, :rows], 0, 0) + dot(l1[...], g[c, rows:], 0, 0) for c in range(2)]
    width = both[0].shape[0] // 2
    chunks = [jnp.stack([v[j * width:(j + 1) * width] for v in both]) for j in range(2)]
    put_pair(give, slot, s_ref, chunks, got, outs)


def heads_grad_part(s, slot, low0, low1, grad, got=None):
    give = got is None
    rows, model = low0.shape
    width = grad.shape[2]
    block = pl.BlockSpec((rows, model // 4), lambda g, s: (0, pair_of(int(give), g, s, slot)))
    return pair_call(
        heads_grad_kernel, give, slot, s, (low0, low1, grad),
        [block, block, pl.BlockSpec((2, 2 * rows, width), lambda g, s: (0, 0, 0))],
        (2, model // 8, width), got, 4 * rows * model * width, "heads_grad",
    )


def values_grad_kernel(give, slot, s_ref, *refs):
    (l0, l1, g, a0, a1, m), got, outs = split_refs(give, refs, 6)
    rows = l0.shape[0]
    both = [
        dot(l0[...], g[0, :rows], 0, 0) + dot(l1[...], g[0, rows:], 0, 0),
        dot(a0[...], m[:rows], 0, 0) + dot(a1[...], m[rows:], 0, 0),
    ]
    width = both[0].shape[0] // 2
    chunks = [jnp.stack([v[j * width:(j + 1) * width] for v in both]) for j in range(2)]
    put_pair(give, slot, s_ref, chunks, got, outs)


def values_grad_part(s, slot, low0, low1, grad, att0, att1, mixed, got=None):
    give = got is None
    rows, model = low0.shape
    width = grad.shape[2]
    block = pl.BlockSpec((rows, model // 4), lambda g, s: (0, pair_of(int(give), g, s, slot)))
    return pair_call(
        values_grad_kernel, give, slot, s, (low0, low1, grad, att0, att1, mixed),
        [block, block, pl.BlockSpec((1, 2 * rows, width), lambda g, s: (2, 0, 0)), block, block, fixed(mixed.shape)],
        (2, model // 8, width), got, 4 * rows * model * width, "values_grad",
    )


def spread_kernel(put, s_ref, *refs):
    g = pl.program_id(0)
    pieces, outs = refs[-4 - put.outs:-put.outs], refs[-put.outs:]
    for a in range(4):
        @pl.when(g // 2 == a)
        def _(a=a):
            put(pieces[a], outs)


def spread(places, slot, pieces, put, tail, out_specs, out_shape, given=None, name=None):
    zeros = (0,) * len(tail)
    at = lambda g, s: g ^ s[slot]
    in_specs = [
        pl.BlockSpec((1, *tail), lambda g, s, a=a: (jnp.clip(g - 2 * a, 0, 1), *zeros)) for a in range(4)
    ]
    args = list(pieces)
    aliases = {}
    if given is not None:
        in_specs.insert(0, pl.BlockSpec(memory_space=pl.ANY))
        args.insert(0, given)
        aliases = {1: 0}
    return pl.pallas_call(
        functools.partial(spread_kernel, put),
        grid_spec=pltpu.PrefetchScalarGridSpec(
            num_scalar_prefetch=1, grid=(8,), in_specs=in_specs, out_specs=[spec(at) for spec in out_specs],
        ),
        out_shape=out_shape,
        input_output_aliases=aliases,
        cost_estimate=cost(0, 6 * 8 * math.prod(tail)),
        name=name,
    )(places, *args)


def put_rows(piece, outs):
    outs[0][...] = piece[0].astype(F32)


put_rows.outs = 1


def put_values(piece, outs):
    outs[0][0] = piece[0, 0].astype(F32)
    outs[1][...] = piece[0, 1].astype(F32).T


put_values.outs = 2


def normalize(values):
    return row_norm(values)


def norm_back(grad_norm, normed, inverse):
    return inverse * (
        grad_norm
        - jnp.mean(grad_norm, axis=-1, keepdims=True)
        - normed * jnp.mean(grad_norm * normed, axis=-1, keepdims=True)
    )


def gelu_back(expanded, grad_active):
    pull = jax.vjp(lambda value: jax.nn.gelu(value, approximate=True), expanded)[1]
    return pull(grad_active)[0]


def swap(x):
    return lax.ppermute(x, "mp", [(0, 1), (1, 0)])


def keep_valid(x, places, length):
    return jnp.where((places < length)[:, None], x, jnp.zeros_like(x))


def tie(x, *others):
    return lax.optimization_barrier((x, *others))[0]


class Line:
    def __init__(self):
        self.last = None

    def __call__(self, step, *args):
        if self.last is not None:
            args, _ = lax.optimization_barrier((args, self.last))
        out = step(*args)
        self.last = min(jax.tree.leaves(out), key=lambda leaf: leaf.size)
        return out


def halve(stay, got):
    n = stay.shape[0] // 2
    return add_low(stay[n:], got[n:]), add_low(stay[:n], got[:n])


def join(a, b):
    return jnp.concatenate([a, b], axis=0)


def paired(
    tokens, lengths, first_gain, first_shift, heads_weight, relative_bias, mixer_weight, second_gain,
    second_shift, expand_weight, expand_bias, reduce_weight, reduce_bias, cotangent,
):
    member = lax.axis_index("mp")
    index = lax.axis_index("dp")
    length = lengths[0]
    own, model = tokens.shape
    buckets = relative_bias.shape[1]
    width = heads_weight.shape[2]
    hidden = expand_bias.shape[0]
    pairs = width // 128
    sp = jnp.stack([member.astype(jnp.int32), length.astype(jnp.int32)])
    at = jnp.stack([place_of(index, s).astype(jnp.int32) for s in STAGES])
    places = member * own + jnp.arange(own)
    places_other = (1 - member) * own + jnp.arange(own)
    row = lambda v: v.reshape(1, -1)
    line = Line()

    other = swap(tokens)
    core = index % 2
    n = width // 2
    mixer_half = swap(tie(lax.dynamic_slice_in_dim(mixer_weight, core * n, n, 0), other))
    mixer_rest = trade(mixer_half, 1)
    cotangent_other = swap(tie(cotangent, mixer_half))

    rows = bias_rows(relative_bias)
    target0 = keep_valid(cotangent, places, length)
    low0, projected0 = line(project, tokens, row(first_gain), row(first_shift), heads_weight)
    active_grad = lambda t, w: dot(t, w, 1, 1).astype(BF16)
    active_grad0 = line(active_grad, target0, reduce_weight)
    low1, projected1 = line(project, other, row(first_gain), row(first_shift), heads_weight)
    mixed, logsum = line(attend_forward, sp, projected0, projected1, rows)
    mixed_other = swap(mixed)
    mixer_other = jnp.where(core == 0, join(mixer_half, mixer_rest), join(mixer_rest, mixer_half))
    target1 = line(lambda x: keep_valid(x, places_other, length), cotangent_other)
    active_grad1 = line(active_grad, target1, reduce_weight)
    middle, second = line(mix, tokens, other, mixed, mixed_other, mixer_weight, mixer_other, row(second_gain), row(second_shift))

    act1, ge1, gs1, eb1 = line(
        lambda x, g, w, b: expand(x, 1, own, g, w, b, BF16), second, active_grad1, expand_weight, row(expand_bias)
    )
    gs_got = swap(gs1)
    act0, ge0, gs0, eb0 = line(
        lambda x, g, w, b: expand(x, 0, own, g, w, b, F32), second, active_grad0, expand_weight, row(expand_bias)
    )
    x_way, z_way = STAGES
    reduce_part = lambda *xs: reduce_grad_part(at, 0, *xs)
    expand_part = lambda *xs: expand_grad_part(at, 0, *xs)
    query_part = lambda *xs: heads_grad_part(at, 0, *xs)
    value_part = lambda *xs: values_grad_part(at, 1, *xs)

    (r_send,) = line(reduce_part, act0, act1, target0, target1)
    r_got = trade(r_send, x_way[0])
    (e_send,) = line(expand_part, second, ge0, ge1)
    e_got = trade(e_send, x_way[0])
    r_out, r_stay = line(reduce_part, act0, act1, target0, target1, r_got)
    r_got = trade(r_out, x_way[1])

    def middle_back(gs0, gs_got, middle, target):
        norm, inverse = normalize(middle)
        grad_second = gs0 + gs_got.astype(F32)
        target = target.astype(F32)
        grad = target + norm_back(grad_second * second_gain, norm, inverse)
        sums = (jnp.sum(grad_second * norm, axis=0), jnp.sum(grad_second, axis=0), jnp.sum(target, axis=0))
        return grad, grad.astype(BF16), sums

    grad_middle, attended0, second_sums = line(middle_back, gs0, gs_got, middle, target0)
    attended1 = swap(attended0)
    grad_mix = lambda a, w: dot(a, w, 1, 1).astype(BF16)
    grad_mixed0 = line(grad_mix, attended0, mixer_weight)
    reduced1 = line(lambda a, w: dot(a, w, 1, 0).astype(BF16), act1, reduce_weight)
    e_out, e_stay = line(expand_part, second, ge0, ge1, e_got)
    e_got = trade(tie(e_out, r_got), x_way[1])
    r_out, r_stay = line(halve, r_stay, r_got)
    r_got = trade(r_out, x_way[2])
    grad_mixed1 = line(grad_mix, attended1, mixer_weight)
    reduced_got = swap(tie(reduced1, attended1))

    half = pairs // 2
    grad_projected, sums0 = line(
        lambda *xs: attend_backward(*xs, 0, half), sp, projected0, projected1, grad_mixed0, grad_mixed1, mixed, logsum, rows
    )
    r_stay = line(add_low, r_stay, r_got)
    r_got = trade(r_stay, x_way[3])
    e_out, e_stay = line(halve, e_stay, e_got)
    e_got = trade(e_out, x_way[2])
    grad_projected, sums1 = line(
        lambda *xs: attend_backward(*xs[:8], half, pairs - half, xs[8]),
        sp, projected0, projected1, grad_mixed0, grad_mixed1, mixed, logsum, rows, grad_projected,
    )
    r_done = line(add_low, r_stay, r_got)
    r_next = trade(r_done, x_way[2])
    e_stay = line(add_low, e_stay, e_got)
    e_got = trade(e_stay, x_way[3])

    first_part = lambda g, w: sum(dot(g[c], w[c], 1, 1) for c in range(3))
    first_part1 = line(lambda g, w: first_part(g[:, own:], w).astype(BF16), grad_projected, heads_weight)
    first_got = swap(first_part1)
    (q_send,) = line(query_part, low0, low1, grad_projected)
    q_got = trade(q_send, x_way[0])
    (v_send,) = line(value_part, low0, low1, grad_projected, attended0, attended1, mixed)
    v_got = trade(v_send, z_way[0])
    r_first = line(join, r_done, r_next)
    r_second = trade(r_first, x_way[1])
    q_out, q_stay = line(query_part, low0, low1, grad_projected, q_got)
    q_got = trade(q_out, x_way[1])
    v_out, v_stay = line(value_part, low0, low1, grad_projected, attended0, attended1, mixed, v_got)
    v_got = trade(v_out, z_way[1])
    e_done = line(add_low, e_stay, e_got)
    e_next = trade(e_done, x_way[2])
    first_part0 = line(lambda g, w: first_part(g[:, :own], w), grad_projected, heads_weight)
    block_out = line(
        lambda m, a, w, r: (m + dot(a, w, 1, 0) + r.astype(F32) + reduce_bias).astype(BF16),
        middle, act0, reduce_weight, reduced_got,
    )
    v_out, v_stay = line(halve, v_stay, v_got)
    v_got = trade(v_out, z_way[2])

    def first_back(part, got, tokens, grad_middle):
        grad = part + got.astype(F32)
        norm, inverse = normalize(tokens.astype(F32))
        out = (grad_middle + norm_back(grad * first_gain, norm, inverse)).astype(BF16)
        return out, (jnp.sum(grad * norm, axis=0), jnp.sum(grad, axis=0))

    tokens_grad, first_sums = line(first_back, first_part0, first_got, tokens, grad_middle)
    both = jnp.stack([*first_sums, *second_sums])
    both_got = swap(both)
    e_first = line(join, e_done, e_next)
    e_second = trade(e_first, x_way[1])
    q_out, q_stay = line(halve, q_stay, q_got)
    q_got = trade(q_out, x_way[2])
    r_third, r_fourth = trade(r_first, x_way[0]), trade(r_second, x_way[0])
    v_stay = line(add_low, v_stay, v_got)
    v_got = trade(v_stay, z_way[3])

    bias_part = bias_grad(join(sums0, sums1), buckets)
    pack = line(
        lambda both, got, eb0, eb1, bias: jnp.concatenate(
            [(both + got).reshape(-1), (eb0 + eb1).reshape(-1), bias.reshape(-1)]
        ).reshape(-1, 128),
        both, both_got, eb0, eb1, bias_part,
    )
    pack_got = trade(pack, 1)
    q_stay = line(add_low, q_stay, q_got)
    q_got = trade(q_stay, x_way[3])
    pack = line(jnp.add, pack, pack_got)
    pack_got = trade(pack, 2)

    chunk = (hidden // 8, model)
    turned = (model, hidden // 8)
    piece = (2, model // 8, width)
    (reduce_grad,) = line(
        lambda *xs: spread(
            at, 0, xs, put_rows, chunk, [lambda to: pl.BlockSpec(chunk, lambda g, s: (to(g, s), 0))],
            [jax.ShapeDtypeStruct(reduce_weight.shape, F32)], name="spread_reduce",
        ),
        r_first, r_second, r_third, r_fourth,
    )
    v_done = line(add_low, v_stay, v_got)
    v_next = trade(v_done, z_way[2])
    pack = line(jnp.add, pack, pack_got)
    pack_got = trade(pack, 4)
    q_done = line(add_low, q_stay, q_got)
    q_next = trade(q_done, x_way[2])
    v_first = line(join, v_done, v_next)
    v_second = trade(v_first, z_way[1])
    pack = line(jnp.add, pack, pack_got)
    pack_got = trade(pack, 8)
    q_first = line(join, q_done, q_next)
    q_second = trade(q_first, x_way[1])
    e_third, e_fourth = trade(e_first, x_way[0]), trade(e_second, x_way[0])
    (expand_grad,) = line(
        lambda *xs: spread(
            at, 0, xs, put_rows, turned, [lambda to: pl.BlockSpec(turned, lambda g, s: (0, to(g, s)))],
            [jax.ShapeDtypeStruct(expand_weight.shape, F32)], name="spread_expand",
        ),
        e_first, e_second, e_third, e_fourth,
    )
    pack = line(jnp.add, pack, pack_got).reshape(-1)
    both = pack[: 5 * model].reshape(5, model)
    expand_bias_grad = pack[5 * model : 5 * model + hidden]
    bias_part = pack[5 * model + hidden :].reshape(relative_bias.shape)
    v_third, v_fourth = trade(v_first, z_way[0]), trade(v_second, z_way[0])
    q_third, q_fourth = trade(q_first, x_way[0]), trade(q_second, x_way[0])
    (heads_grad,) = line(
        lambda *xs: spread(
            at, 0, xs, put_rows, piece, [lambda to: pl.BlockSpec(piece, lambda g, s: (0, to(g, s), 0))],
            [jax.ShapeDtypeStruct(heads_weight.shape, F32)], name="spread_queries",
        ),
        q_first, q_second, q_third, q_fourth,
    )
    heads_grad, mixer_grad = line(
        lambda given, *xs: spread(
            at, 1, xs, put_values, piece,
            [
                lambda to: pl.BlockSpec((1, model // 8, width), lambda g, s: (2, to(g, s), 0)),
                lambda to: pl.BlockSpec((width, model // 8), lambda g, s: (0, to(g, s))),
            ],
            [jax.ShapeDtypeStruct(heads_weight.shape, F32), jax.ShapeDtypeStruct(mixer_weight.shape, F32)],
            given=given, name="spread_values",
        ),
        heads_grad, v_first, v_second, v_third, v_fourth,
    )
    return (
        block_out, tokens_grad, both[0], both[1], heads_grad, bias_part, mixer_grad, both[2], both[3],
        expand_grad, expand_bias_grad, reduce_grad, both[4],
    )


def gathered(
    tokens, lengths, first_gain, first_shift, heads_weight, relative_bias, mixer_weight, second_gain,
    second_shift, expand_weight, expand_bias, reduce_weight, reduce_bias, cotangent,
):
    def gather(x):
        return lax.all_gather(x, "mp", axis=0, tiled=True)

    def scatter(x):
        return lax.psum_scatter(x.astype(BF16), "mp", scatter_dimension=0, tiled=True).astype(F32)

    members = lax.axis_size("mp")
    length = lengths[0]
    own = tokens.shape[0]
    whole = own * members
    half = whole // 2
    buckets = relative_bias.shape[1]
    sp = jnp.stack([jnp.zeros((), jnp.int32), length.astype(jnp.int32)])
    places = lax.axis_index("mp") * own + jnp.arange(own)
    rows = bias_rows(relative_bias)
    source_all = gather(tokens)
    first_all, projected = project(source_all, first_gain.reshape(1, -1), first_shift.reshape(1, -1), heads_weight)
    projected0, projected1 = projected[:, :half], projected[:, half:]
    mixed, logsum = attend_forward(sp, projected0, projected1, rows)
    source = tokens.astype(F32)
    middle = source + scatter(dot(mixed, mixer_weight, 1, 0))
    second_norm, second_inverse = normalize(middle)
    second_all = gather((second_norm * second_gain + second_shift).astype(BF16))
    target = keep_valid(cotangent, places, length)
    target_wide = target.astype(F32)
    target_all = gather(target)
    expanded = dot(second_all, expand_weight, 1, 0) + expand_bias
    active_low = jax.nn.gelu(expanded, approximate=True).astype(BF16)
    grad_expanded = gelu_back(expanded, dot(target_all, reduce_weight, 1, 1)).astype(BF16)
    grad_second = scatter(dot(grad_expanded, expand_weight, 1, 1))
    reduced = scatter(dot(active_low, reduce_weight, 1, 0))
    reduce_grad = dot(active_low, target_all, 0, 0)
    expand_grad = dot(second_all, grad_expanded, 0, 0)
    expand_bias_grad = jnp.sum(grad_expanded.astype(F32), axis=0)
    block_out = (middle + reduced + reduce_bias).astype(BF16)
    grad_middle = target_wide + norm_back(grad_second * second_gain, second_norm, second_inverse)
    attended_all = gather(grad_middle.astype(BF16))
    mixer_grad = dot(mixed, attended_all, 0, 0)
    grad_mixed = dot(attended_all, mixer_weight, 1, 1).astype(BF16)
    grad_projected, sums = attend_backward(
        sp, projected0, projected1, grad_mixed[:half], grad_mixed[half:], mixed, logsum, rows
    )
    bias_part = bias_grad(sums, buckets)
    heads_grad = jnp.einsum("td,cte->cde", first_all, grad_projected, preferred_element_type=F32)
    grad_first = scatter(jnp.einsum("cte,cde->td", grad_projected, heads_weight, preferred_element_type=F32))
    first_norm, first_inverse = normalize(source)
    tokens_grad = (
        grad_middle + norm_back(grad_first * first_gain, first_norm, first_inverse)
    ).astype(BF16)
    first_gain_grad, first_shift_grad, second_gain_grad, second_shift_grad, reduce_bias_grad = (
        lax.psum(
            (
                jnp.sum(grad_first * first_norm, axis=0),
                jnp.sum(grad_first, axis=0),
                jnp.sum(grad_second * second_norm, axis=0),
                jnp.sum(grad_second, axis=0),
                jnp.sum(target_wide, axis=0),
            ),
            ("dp", "mp"),
        )
    )
    heads_grad, bias_part, mixer_grad, expand_grad, expand_bias_grad, reduce_grad = (
        lax.psum(x.astype(BF16), "dp").astype(F32)
        for x in (heads_grad, bias_part, mixer_grad, expand_grad, expand_bias_grad, reduce_grad)
    )
    return (
        block_out, tokens_grad, first_gain_grad, first_shift_grad, heads_grad, bias_part, mixer_grad,
        second_gain_grad, second_shift_grad, expand_grad, expand_bias_grad, reduce_grad, reduce_bias_grad,
    )


def per_device(*args):
    if lax.axis_size("mp") == 2 and lax.axis_size("dp") == 16:
        return paired(*args)
    return gathered(*args)


def solution(mesh):
    return jax.shard_map(
        per_device,
        mesh=mesh,
        in_specs=(
            P(("dp", "mp"), None),
            P("dp"),
            P(),
            P(),
            P(None, None, "mp"),
            P("mp", None),
            P("mp", None),
            P(),
            P(),
            P(None, "mp"),
            P("mp"),
            P("mp", None),
            P(),
            P(("dp", "mp"), None),
        ),
        out_specs=(
            P(("dp", "mp"), None),
            P(("dp", "mp"), None),
            P(),
            P(),
            P(None, None, "mp"),
            P("mp", None),
            P("mp", None),
            P(),
            P(),
            P(None, "mp"),
            P("mp"),
            P("mp", None),
            P(),
        ),
        check_vma=False,
    )
```

```python
import functools
import math

import jax
import jax.numpy as jnp
import numpy as np
from jax import lax
from jax.experimental import pallas as pl
from jax.experimental.pallas import tpu as pltpu
from jax.sharding import PartitionSpec as P

EPS = 1e-05
DH=64; MAXDIST=128; NEG=-1e30; BLK=256
F32=jnp.float32; BF16=jnp.bfloat16
HIGHEST=lax.Precision.HIGHEST

def bucket_table(count, buckets, reach):
    exact = buckets // 2
    entries = []
    for position in range(count):
        if position < exact:
            entries.append(position)
        else:
            level = exact + int(math.log(position / exact) / math.log(reach / exact) * (buckets - exact))
            entries.append(min(buckets - 1, level))
    return np.array(entries, dtype=np.int32)

def bias_tables(buckets):
    W=2*BLK
    tab=bucket_table(W,buckets,MAXDIST)
    oh=np.zeros((buckets,4,W),np.float32); neg=np.zeros((1,4,W),np.float32)
    for y in range(W):
        x = y if y < BLK else y-W
        if x<=0 and -x<BLK: oh[tab[-x],0,y]=1
        else: neg[0,0,y]=NEG
        d=BLK-x
        if 0<=d<W: oh[tab[d],1,y]=1
        if 0<=x: oh[tab[x],2,y]=1
        else: neg[0,2,y]=NEG
        d=BLK+x
        if 0<=d<W: oh[tab[d],3,y]=1
    return oh.reshape(buckets,4*W), neg.reshape(1,4*W)

def bias_rows(relative_bias):
    heads,buckets=relative_bias.shape
    oh,neg=bias_tables(buckets)
    rel=relative_bias-relative_bias[:,buckets-1:]
    rows=jnp.dot(rel,jnp.asarray(oh),precision=HIGHEST)+jnp.asarray(neg)
    return rows.reshape(heads//2,2,4*2*BLK)

def toeplitz(row):
    wide=jnp.broadcast_to(row,(BLK,2*BLK))
    return pltpu.roll(wide,0,1,stride=1,stride_axis=0)[:,:BLK]


def lane_masks():
    lane=lax.broadcasted_iota(jnp.int32,(1,128),1)
    head=[(lane//DH)==h for h in range(2)]
    mine=[jnp.where(m,1.0,0.0).astype(BF16) for m in head]
    spare=[jnp.where(lane==DH*(1-h),1.0,0.0) for h in range(2)]
    return head,mine,spare


def gone_rows(start,half,length,spare):
    pos=lax.broadcasted_iota(jnp.int32,(half,1),0)+start
    gone=jnp.where(pos<length,0.0,NEG)
    return [(gone*s).astype(BF16) for s in spare]


def fwd_kernel(sp, a_ref,c_ref,b_ref,o_ref,lse_ref,qs,ks,vs):
    half=a_ref.shape[1]; T=2*half; flip=sp[0]; length=sp[1]
    W=2*BLK
    head,mine,spare=lane_masks()
    for a,ref in enumerate((a_ref,c_ref)):
        start=pl.multiple_of((a^flip)*half,half)
        dst=pl.ds(start,half)
        gone=gone_rows(start,half,length,spare)
        for h in range(2):
            qs[h,dst,:]=ref[0]*(mine[h]*jnp.asarray(DH**-0.5,BF16))+spare[h].astype(BF16)
            ks[h,dst,:]=ref[1]*mine[h]+gone[h]
            vs[h,dst,:]=ref[2]*mine[h]+mine[1-h]
    tiles=[(toeplitz(b_ref[0,h:h+1,0:W]),toeplitz(b_ref[0,h:h+1,W:2*W])) for h in range(2)]
    outs={}

    def score(i,h):
        return dot(qs[h,i*BLK:(i+1)*BLK,:],ks[h,:(i+1)*BLK,:],1,1)

    def finish(i,h,s):
        kc=(i+1)*BLK; t0,t1=tiles[h]
        parts=[]
        if i>=2: parts.append(s[:,:kc-2*BLK])
        if i>=1: parts.append(s[:,kc-2*BLK:kc-BLK]+t1)
        parts.append(s[:,kc-BLK:]+t0)
        top=functools.reduce(jnp.maximum,[jnp.max(x,axis=1,keepdims=True) for x in parts])
        p=jnp.concatenate([jnp.exp(x-top).astype(BF16) for x in parts],axis=1)
        o=dot(p,vs[h,:kc,:],1,0)
        total=o[:,DH*(1-h):DH*(1-h)+1]
        outs[h]=(o*(1.0/total),top+jnp.log(total))
        if h==1:
            rows=pl.ds(pl.multiple_of((i*BLK+flip*half)%T,BLK),BLK)
            o_ref[rows,:]=jnp.where(head[0],outs[0][0],outs[1][0]).astype(BF16)
            lse_ref[0,i*BLK:kc,:]=jnp.where(head[0],outs[0][1],outs[1][1])

    run_ahead([(i,h) for i in range(T//BLK) for h in range(2)],score,finish,2)


def run_ahead(items,first,second,depth):
    waiting=[]
    for item in items:
        waiting.append((item,first(*item)))
        if len(waiting)>depth:
            done,value=waiting.pop(0)
            second(*done,value)
    for done,value in waiting:
        second(*done,value)


def attend_forward(sp,projected0,projected1,rows):
    _,half,HD=projected0.shape; pairs=HD//128; T=2*half
    part=pl.BlockSpec((3,half,128),lambda p,s:(0,0,p))
    return pl.pallas_call(
        fwd_kernel,
        grid_spec=pltpu.PrefetchScalarGridSpec(
            num_scalar_prefetch=1,grid=(pairs,),
            in_specs=[part,part,pl.BlockSpec((1,2,rows.shape[2]),lambda p,s:(p,0,0))],
            out_specs=[pl.BlockSpec((T,128),lambda p,s:(0,p)),pl.BlockSpec((1,T,128),lambda p,s:(p,0,0))],
            scratch_shapes=[pltpu.VMEM((2,T,128),BF16)]*3),
        out_shape=[jax.ShapeDtypeStruct((T,HD),BF16),jax.ShapeDtypeStruct((pairs,T,128),F32)],
        cost_estimate=cost(8*T*T*HD,8*T*HD+512*pairs*T),
        name="attend_forward",
    )(sp,projected0,projected1,rows)

def diagonal_sums(acc, offset):
    W=2*BLK
    wide=jnp.concatenate([acc,jnp.zeros_like(acc)],axis=1)
    n=BLK
    while n>1:
        n//=2
        top=wide[:n]; bottom=wide[n:2*n]
        wide=top+pltpu.roll(bottom,W-n,1)
    return pltpu.roll(wide,offset,1) if offset else wide

def bwd_kernel(sp, a_ref,c_ref,d0_ref,d1_ref,o_ref,lse_ref,b_ref,g_ref,d_ref,qs,ks,vs,dos,dq,acc0,acc1):
    half=a_ref.shape[1]; T=2*half; flip=sp[0]; length=sp[1]
    W=2*BLK
    n=T//BLK
    head,mine,spare=lane_masks()
    stats=[None,None]
    one=sum(spare).astype(BF16)
    for a,(ref,do_ref) in enumerate(((a_ref,d0_ref),(c_ref,d1_ref))):
        start=pl.multiple_of((a^flip)*half,half)
        dst=pl.ds(start,half)
        gone=gone_rows(start,half,length,spare)
        for h in range(2):
            qs[h,dst,:]=ref[0]*(mine[h]*jnp.asarray(DH**-0.5,BF16))+spare[h].astype(BF16)
            ks[h,dst,:]=ref[1]*mine[h]+gone[h]
            vs[h,dst,:]=ref[2]*mine[h]
        dos[dst,:]=do_ref[...]
        acc0[0,dst,:]=do_ref[...].astype(F32)*o_ref[a*half:(a+1)*half,:].astype(F32)
    turned=acc0[0].T
    deltas=[jnp.sum(turned[h*DH:(h+1)*DH],axis=0,keepdims=True) for h in range(2)]
    turned=lse_ref[0].T
    lses=[turned[h*DH:h*DH+1] for h in range(2)]
    near=acc1
    tiles=[(toeplitz(b_ref[0,h:h+1,2*W:3*W]),toeplitz(b_ref[0,h:h+1,3*W:])) for h in range(2)]

    def products(j,h):
        rj=slice(j*BLK,(j+1)*BLK)
        return dot(ks[h,rj,:],qs[h,j*BLK:,:],1,1),dot(vs[h,rj,:],dos[j*BLK:,:],1,1)

    keep={}

    def finish(j,h,value):
        s,dp=value
        rj=slice(j*BLK,(j+1)*BLK)
        ps=[];dss=[]
        for b in range(n-j):
            c=slice(b*BLK,(b+1)*BLK)
            cc=slice((j+b)*BLK,(j+b+1)*BLK)
            x=s[:,c]-lses[h][:,cc]
            if b<2: x=x+tiles[h][b]
            p=jnp.exp(x)
            ds=p*(dp[:,c]-deltas[h][:,cc])
            if b<2:
                if j==0: near[h,b]=ds
                else: near[h,b]+=ds
            ps.append(p.astype(BF16)); dss.append(ds.astype(BF16))
        p=jnp.concatenate(ps,axis=1); ds=jnp.concatenate(dss,axis=1)
        dv=dot(p,dos[j*BLK:,:],1,0)
        dk=dot(ds,qs[h,j*BLK:,:],1,0)
        kk=ks[h,rj,:]*mine[h]+mine[1-h]
        dqj=dot(ds,kk,0,0)
        if j==0: dq[h,:,:]=dqj
        else: dq[h,j*BLK:,:]+=dqj
        keep[h]=(dk,dv)
        if h==1:
            rows=pl.ds(pl.multiple_of((j*BLK+flip*half)%T,BLK),BLK)
            g_ref[1,rows,:]=jnp.where(head[0],keep[0][0],keep[1][0]).astype(BF16)
            g_ref[2,rows,:]=jnp.where(head[0],keep[0][1],keep[1][1]).astype(BF16)

    run_ahead([(j,h) for j in range(n) for h in range(2)],products,finish,1)
    for h in range(2):
        d_ref[0,h:h+1,:]=diagonal_sums(near[h,0],0)+diagonal_sums(near[h,1],BLK)
        total=jnp.sum(dq[h,:,:],axis=0,keepdims=True)[:,DH*(1-h):DH*(1-h)+1]
        d_ref[0,2+h:3+h,:]=jnp.broadcast_to(total,(1,W))
    for a in range(2):
        dst=pl.ds(pl.multiple_of((a^flip)*half,half),half)
        g_ref[0,a*half:(a+1)*half,:]=(jnp.where(head[0],dq[0,dst,:],dq[1,dst,:])*DH**-0.5).astype(BF16)

def attend_backward(sp,projected0,projected1,grad0,grad1,mixed,lse,rows):
    _,half,HD=projected0.shape; pairs=HD//128; T=2*half
    part=pl.BlockSpec((3,half,128),lambda p,s:(0,0,p))
    grad=pl.BlockSpec((half,128),lambda p,s:(0,p))
    return pl.pallas_call(
        bwd_kernel,
        grid_spec=pltpu.PrefetchScalarGridSpec(
            num_scalar_prefetch=1,grid=(pairs,),
            in_specs=[part,part,grad,grad,pl.BlockSpec((T,128),lambda p,s:(0,p)),
              pl.BlockSpec((1,T,128),lambda p,s:(p,0,0)),pl.BlockSpec((1,2,rows.shape[2]),lambda p,s:(p,0,0))],
            out_specs=[pl.BlockSpec((3,T,128),lambda p,s:(0,0,p)),pl.BlockSpec((1,4,2*BLK),lambda p,s:(p,0,0))],
            scratch_shapes=[pltpu.VMEM((2,T,128),BF16)]*3+[pltpu.VMEM((T,128),BF16),pltpu.VMEM((2,T,128),F32),pltpu.VMEM((1,T,128),F32),pltpu.VMEM((2,2,BLK,BLK),F32)]),
        out_shape=[jax.ShapeDtypeStruct((3,T,HD),BF16),jax.ShapeDtypeStruct((pairs,4,2*BLK),F32)],
        cost_estimate=cost(20*T*T*HD,16*T*HD+512*pairs*T),
        name="attend_backward",
    )(sp,projected0,projected1,grad0,grad1,mixed,lse,rows)

def bias_grad(sums, buckets):
    pairs=sums.shape[0]; W=2*BLK
    tab=bucket_table(W,buckets,MAXDIST)
    assert tab[BLK]==buckets-1
    m=np.zeros((W,buckets),np.float32)
    for d in range(W):
        if tab[d]<buckets-1:
            m[d,tab[d]]=1; m[d,buckets-1]=-1
    near=sums[:,0:2].reshape(pairs*2,W); total=sums[:,2:4,0].reshape(pairs*2,1)
    last=np.zeros((1,buckets),np.float32); last[0,-1]=1
    return jnp.dot(near,jnp.asarray(m),precision=HIGHEST)+total*jnp.asarray(last)


HALF_TANH = math.sqrt(2.0 / math.pi)


def dot(a, b, ca, cb):
    return lax.dot_general(a, b, (((ca,), (cb,)), ((), ())), preferred_element_type=F32)


def fixed(shape):
    return pl.BlockSpec(shape, lambda *_: (0,) * len(shape))


def cost(flops, moved):
    return pl.CostEstimate(flops=int(flops), transcendentals=0, bytes_accessed=int(moved))


def row_norm(values):
    center = jnp.mean(values, axis=-1, keepdims=True)
    centered = values - center
    inverse = lax.rsqrt(jnp.mean(centered * centered, axis=-1, keepdims=True) + EPS)
    return centered * inverse, inverse


def project_kernel(x_ref, gain_ref, shift_ref, w_ref, low_ref, out_ref):
    normed, _ = row_norm(x_ref[...].astype(F32))
    low = (normed * gain_ref[...] + shift_ref[...]).astype(BF16)
    low_ref[...] = low
    for c in range(3):
        out_ref[c] = dot(low, w_ref[c], 1, 0).astype(BF16)


def project(x, gain, shift, weight):
    rows, model = x.shape
    width = weight.shape[2]
    step = min(256, rows)
    return pl.pallas_call(
        project_kernel,
        grid=(rows // step,),
        in_specs=[pl.BlockSpec((step, model), lambda i: (i, 0)), fixed((1, model)), fixed((1, model)), fixed(weight.shape)],
        out_specs=[pl.BlockSpec((step, model), lambda i: (i, 0)), pl.BlockSpec((3, step, width), lambda i: (0, i, 0))],
        out_shape=[jax.ShapeDtypeStruct((rows, model), BF16), jax.ShapeDtypeStruct((3, rows, width), BF16)],
        cost_estimate=cost(6 * rows * model * width, 2 * (2 * rows * model + weight.size + 3 * rows * width)),
        name="project",
    )(x, gain, shift, weight)


def mix_kernel(own_blocks, x0_ref, x1_ref, m_ref, p_ref, w0_ref, w1_ref, gain_ref, shift_ref, mid_ref, low_ref):
    i = pl.program_id(0)
    attended = dot(m_ref[...], w0_ref[...], 1, 0) + dot(p_ref[...], w1_ref[...], 1, 0)

    def rows(x_ref):
        return x_ref[...].astype(F32) + attended

    def rest(middle):
        normed, _ = row_norm(middle)
        low_ref[...] = (normed * gain_ref[...] + shift_ref[...]).astype(BF16)

    @pl.when(i < own_blocks)
    def _():
        middle = rows(x0_ref)
        mid_ref[...] = middle
        rest(middle)

    @pl.when(i >= own_blocks)
    def _():
        rest(rows(x1_ref))


def mix(tokens, other, mixed, mixed_other, weight, weight_other, gain, shift):
    own, model = tokens.shape
    width = mixed.shape[1]
    step = 256
    n = own // step
    return pl.pallas_call(
        functools.partial(mix_kernel, n),
        grid=(2 * n,),
        in_specs=[
            pl.BlockSpec((step, model), lambda i: (jnp.minimum(i, n - 1), 0)),
            pl.BlockSpec((step, model), lambda i: (jnp.maximum(i - n, 0), 0)),
            pl.BlockSpec((step, width), lambda i: (i, 0)),
            pl.BlockSpec((step, width), lambda i: ((i + n) % (2 * n), 0)),
            fixed(weight.shape), fixed(weight.shape), fixed((1, model)), fixed((1, model)),
        ],
        out_specs=[
            pl.BlockSpec((step, model), lambda i: (jnp.minimum(i, n - 1), 0)),
            pl.BlockSpec((step, model), lambda i: (i, 0)),
        ],
        out_shape=[jax.ShapeDtypeStruct((own, model), F32), jax.ShapeDtypeStruct((2 * own, model), BF16)],
        cost_estimate=cost(8 * own * model * width, 2 * (4 * own * model + 4 * own * width + 2 * weight.size) + 4 * own * model),
        name="mix",
    )(tokens, other, mixed, mixed_other, weight, weight_other, gain, shift)


def expand_kernel(x_ref, g_ref, w_ref, b_ref, act_ref, ge_ref, gs_ref, bias_ref, acc_ref):
    i = pl.program_id(0)
    x = x_ref[...]
    width = w_ref.shape[1]
    sub = 256
    total = None
    for s in range(width // sub):
        cols = slice(s * sub, (s + 1) * sub)
        u = dot(x, w_ref[:, cols], 1, 0) + b_ref[:, cols].astype(F32)
        square = u * u
        t = jnp.tanh(HALF_TANH * u * (1.0 + 0.044715 * square))
        half = 0.5 + 0.5 * t
        act_ref[:, cols] = (u * half).astype(BF16)
        slope = half + 0.5 * u * (1.0 - t * t) * (HALF_TANH * (1.0 + 3 * 0.044715 * square))
        grad = g_ref[:, cols].astype(F32) * slope
        low = grad.astype(BF16)
        ge_ref[:, cols] = low
        bias_ref[:, cols] = jnp.sum(grad, axis=0, keepdims=True)
        part = dot(low, w_ref[:, cols], 1, 1)
        total = part if total is None else total + part

    @pl.when(i == 0)
    def _():
        acc_ref[...] = total

    @pl.when(i > 0)
    def _():
        acc_ref[...] += total

    @pl.when(i == pl.num_programs(0) - 1)
    def _():
        gs_ref[...] = acc_ref[...].astype(gs_ref.dtype)


def expand(x, block, rows, grad_active, weight, bias, dtype):
    model = x.shape[1]
    hidden = weight.shape[1]
    step = min(512, hidden)
    return pl.pallas_call(
        expand_kernel,
        grid=(hidden // step,),
        in_specs=[
            pl.BlockSpec((rows, model), lambda i: (block, 0)),
            pl.BlockSpec((rows, step), lambda i: (0, i)),
            pl.BlockSpec((model, step), lambda i: (0, i)),
            pl.BlockSpec((1, step), lambda i: (0, i)),
        ],
        out_specs=[
            pl.BlockSpec((rows, step), lambda i: (0, i)),
            pl.BlockSpec((rows, step), lambda i: (0, i)),
            fixed((rows, model)),
            pl.BlockSpec((1, step), lambda i: (0, i)),
        ],
        out_shape=[
            jax.ShapeDtypeStruct((rows, hidden), BF16),
            jax.ShapeDtypeStruct((rows, hidden), BF16),
            jax.ShapeDtypeStruct((rows, model), dtype),
            jax.ShapeDtypeStruct((1, hidden), F32),
        ],
        scratch_shapes=[pltpu.VMEM((rows, model), F32)],
        cost_estimate=cost(4 * rows * model * hidden, 2 * (2 * rows * model + 3 * rows * hidden + weight.size)),
        name="expand",
    )(x, grad_active, weight, bias)


STAGES = ((1, 2, 4, 8), (1, 4, 2, 8))


def place_of(index, stages):
    bit = [(index // s) % 2 for s in stages]
    return bit[0] * 4 + bit[1] * 2 + bit[2]


def trade(x, bit):
    size = lax.axis_size("dp")
    return lax.ppermute(x, "dp", [(i, i ^ bit) for i in range(size)])


def add_low(a, b):
    return (a.astype(F32) + b.astype(F32)).astype(BF16)


def part_of(give, s, slot):
    return (s[slot] // 4) ^ give


def pair_of(give, g, s, slot):
    return part_of(give, s, slot) * 2 + ((1 - g) ^ ((s[slot] // 2) % 2))


def put_pair(give, slot, s_ref, chunks, got_ref, outs):
    flip = s_ref[slot] % 2
    for j, value in enumerate(chunks):
        at = j ^ flip
        if give:
            outs[0][pl.ds(at, 1)] = value.astype(BF16)[None]
        else:
            value = (value + got_ref[pl.ds(at, 1)][0].astype(F32)).astype(BF16)[None]
            for step, out in enumerate(outs):
                @pl.when(pl.program_id(0) == step)
                def _(out=out):
                    out[pl.ds(at, 1)] = value


def pair_call(kernel, give, slot, s, arrays, specs, tail, got, flops, name):
    zeros = (0,) * len(tail)
    if give:
        out_specs = [pl.BlockSpec((2, *tail), lambda g, s: (1 - g, *zeros))]
        out_shape = [jax.ShapeDtypeStruct((4, *tail), BF16)]
    else:
        specs = specs + [pl.BlockSpec((2, *tail), lambda g, s: (1 - g, *zeros))]
        arrays = (*arrays, got)
        out_specs = [pl.BlockSpec((2, *tail), lambda g, s: (0, *zeros))] * 2
        out_shape = [jax.ShapeDtypeStruct((2, *tail), BF16)] * 2
    moved = sum(2 * x.size for x in arrays) + 8 * math.prod(tail)
    return pl.pallas_call(
        functools.partial(kernel, give, slot),
        grid_spec=pltpu.PrefetchScalarGridSpec(num_scalar_prefetch=1, grid=(2,), in_specs=specs, out_specs=out_specs),
        out_shape=out_shape,
        cost_estimate=cost(flops, moved),
        name=name,
    )(s, *arrays)


def split_refs(give, refs, count):
    return refs[:count], (None if give else refs[count]), refs[count + (0 if give else 1):]


def reduce_grad_kernel(give, slot, s_ref, *refs):
    (a0, a1, t0, t1), got, outs = split_refs(give, refs, 4)
    value = dot(a0[...], t0[...], 0, 0) + dot(a1[...], t1[...], 0, 0)
    width = value.shape[0] // 2
    put_pair(give, slot, s_ref, [value[:width], value[width:]], got, outs)


def reduce_grad_part(s, slot, act0, act1, t0, t1, got=None):
    give = got is None
    rows, hidden = act0.shape
    model = t0.shape[1]
    block = pl.BlockSpec((rows, hidden // 4), lambda g, s: (0, pair_of(int(give), g, s, slot)))
    return pair_call(
        reduce_grad_kernel, give, slot, s, (act0, act1, t0, t1), [block, block, fixed(t0.shape), fixed(t1.shape)],
        (hidden // 8, model), got, 2 * rows * model * hidden, "reduce_grad",
    )


def expand_grad_kernel(give, slot, s_ref, *refs):
    (x, g0, g1), got, outs = split_refs(give, refs, 3)
    rows = g0.shape[0]
    value = dot(x[:rows], g0[...], 0, 0) + dot(x[rows:], g1[...], 0, 0)
    width = value.shape[1] // 2
    put_pair(give, slot, s_ref, [value[:, :width], value[:, width:]], got, outs)


def expand_grad_part(s, slot, x, g0, g1, got=None):
    give = got is None
    rows, hidden = g0.shape
    model = x.shape[1]
    block = pl.BlockSpec((rows, hidden // 4), lambda g, s: (0, pair_of(int(give), g, s, slot)))
    return pair_call(
        expand_grad_kernel, give, slot, s, (x, g0, g1), [fixed(x.shape), block, block],
        (model, hidden // 8), got, 2 * rows * model * hidden, "expand_grad",
    )


def heads_grad_kernel(give, slot, s_ref, *refs):
    (l0, l1, g), got, outs = split_refs(give, refs, 3)
    rows = l0.shape[0]
    both = [dot(l0[...], g[c, :rows], 0, 0) + dot(l1[...], g[c, rows:], 0, 0) for c in range(2)]
    width = both[0].shape[0] // 2
    chunks = [jnp.stack([v[j * width:(j + 1) * width] for v in both]) for j in range(2)]
    put_pair(give, slot, s_ref, chunks, got, outs)


def heads_grad_part(s, slot, low0, low1, grad, got=None):
    give = got is None
    rows, model = low0.shape
    width = grad.shape[2]
    block = pl.BlockSpec((rows, model // 4), lambda g, s: (0, pair_of(int(give), g, s, slot)))
    return pair_call(
        heads_grad_kernel, give, slot, s, (low0, low1, grad),
        [block, block, pl.BlockSpec((2, 2 * rows, width), lambda g, s: (0, 0, 0))],
        (2, model // 8, width), got, 4 * rows * model * width, "heads_grad",
    )


def values_grad_kernel(give, slot, s_ref, *refs):
    (l0, l1, g, a0, a1, m), got, outs = split_refs(give, refs, 6)
    rows = l0.shape[0]
    both = [
        dot(l0[...], g[0, :rows], 0, 0) + dot(l1[...], g[0, rows:], 0, 0),
        dot(a0[...], m[:rows], 0, 0) + dot(a1[...], m[rows:], 0, 0),
    ]
    width = both[0].shape[0] // 2
    chunks = [jnp.stack([v[j * width:(j + 1) * width] for v in both]) for j in range(2)]
    put_pair(give, slot, s_ref, chunks, got, outs)


def values_grad_part(s, slot, low0, low1, grad, att0, att1, mixed, got=None):
    give = got is None
    rows, model = low0.shape
    width = grad.shape[2]
    block = pl.BlockSpec((rows, model // 4), lambda g, s: (0, pair_of(int(give), g, s, slot)))
    return pair_call(
        values_grad_kernel, give, slot, s, (low0, low1, grad, att0, att1, mixed),
        [block, block, pl.BlockSpec((1, 2 * rows, width), lambda g, s: (2, 0, 0)), block, block, fixed(mixed.shape)],
        (2, model // 8, width), got, 4 * rows * model * width, "values_grad",
    )


def spread_kernel(put, s_ref, *refs):
    g = pl.program_id(0)
    pieces, outs = refs[-4 - put.outs:-put.outs], refs[-put.outs:]
    for a in range(4):
        @pl.when(g // 2 == a)
        def _(a=a):
            put(pieces[a], outs)


def spread(places, slot, pieces, put, tail, out_specs, out_shape, given=None, name=None):
    zeros = (0,) * len(tail)
    at = lambda g, s: g ^ s[slot]
    in_specs = [
        pl.BlockSpec((1, *tail), lambda g, s, a=a: (jnp.clip(g - 2 * a, 0, 1), *zeros)) for a in range(4)
    ]
    args = list(pieces)
    aliases = {}
    if given is not None:
        in_specs.insert(0, pl.BlockSpec(memory_space=pl.ANY))
        args.insert(0, given)
        aliases = {1: 0}
    return pl.pallas_call(
        functools.partial(spread_kernel, put),
        grid_spec=pltpu.PrefetchScalarGridSpec(
            num_scalar_prefetch=1, grid=(8,), in_specs=in_specs, out_specs=[spec(at) for spec in out_specs],
        ),
        out_shape=out_shape,
        input_output_aliases=aliases,
        cost_estimate=cost(0, 6 * 8 * math.prod(tail)),
        name=name,
    )(places, *args)


def put_rows(piece, outs):
    outs[0][...] = piece[0].astype(F32)


put_rows.outs = 1


def rows_grad_kernel(a0, a1, t0, t1, out_ref):
    out_ref[...] = (dot(a0[...], t0[...], 0, 0) + dot(a1[...], t1[...], 0, 0)).astype(BF16)


def rows_grad(act0, act1, t0, t1):
    rows, hidden = act0.shape
    model = t0.shape[1]
    step = min(512, hidden)
    block = pl.BlockSpec((rows, step), lambda i: (0, i))
    return pl.pallas_call(
        rows_grad_kernel,
        grid=(hidden // step,),
        in_specs=[block, block, fixed(t0.shape), fixed(t1.shape)],
        out_specs=pl.BlockSpec((step, model), lambda i: (i, 0)),
        out_shape=jax.ShapeDtypeStruct((hidden, model), BF16),
        cost_estimate=cost(4 * rows * model * hidden, 4 * rows * (model + hidden) + 2 * model * hidden),
        name="rows_grad",
    )(act0, act1, t0, t1)


def spread_heads_kernel(s_ref, *refs):
    k = pl.program_id(0)
    heads_ref, mixer_ref = refs[8:]
    for slot in range(2):
        r = k ^ s_ref[slot]
        for a in range(4):
            piece = refs[4 * slot + a]

            @pl.when(r // 2 == a)
            def _(slot=slot, piece=piece):
                if slot == 0:
                    heads_ref[:2] = piece[0].astype(F32)
                else:
                    heads_ref[2] = piece[0, 0].astype(F32)
                    mixer_ref[...] = piece[0, 1].astype(F32).T


def spread_heads(places, queries, values, model, width):
    tail = (2, model // 8, width)

    def spec(slot, a):
        def at(k, s):
            r = k ^ s[slot]
            return (jnp.where(r // 2 == a, r % 2, 0), 0, 0, 0)

        return pl.BlockSpec((1, *tail), at)

    return pl.pallas_call(
        spread_heads_kernel,
        grid_spec=pltpu.PrefetchScalarGridSpec(
            num_scalar_prefetch=1, grid=(8,),
            in_specs=[spec(slot, a) for slot in range(2) for a in range(4)],
            out_specs=[
                pl.BlockSpec((3, model // 8, width), lambda k, s: (0, k, 0)),
                pl.BlockSpec((width, model // 8), lambda k, s: (0, k)),
            ],
        ),
        out_shape=[jax.ShapeDtypeStruct((3, model, width), F32), jax.ShapeDtypeStruct((width, model), F32)],
        cost_estimate=cost(0, 12 * 8 * math.prod(tail)),
        name="spread_heads",
    )(places, *queries, *values)


def normalize(values):
    return row_norm(values)


def norm_back(grad_norm, normed, inverse):
    return inverse * (
        grad_norm
        - jnp.mean(grad_norm, axis=-1, keepdims=True)
        - normed * jnp.mean(grad_norm * normed, axis=-1, keepdims=True)
    )


def gelu_back(expanded, grad_active):
    pull = jax.vjp(lambda value: jax.nn.gelu(value, approximate=True), expanded)[1]
    return pull(grad_active)[0]


def swap(x):
    return lax.ppermute(x, "mp", [(0, 1), (1, 0)])


def keep_valid(x, places, length):
    return jnp.where((places < length)[:, None], x, jnp.zeros_like(x))


def tie(x, *others):
    return lax.optimization_barrier((x, *others))[0]


class Line:
    def __init__(self):
        self.last = None

    def __call__(self, step, *args):
        if self.last is not None:
            args, _ = lax.optimization_barrier((args, self.last))
        out = step(*args)
        self.last = min(jax.tree.leaves(out), key=lambda leaf: leaf.size)
        return out


def halve(stay, got):
    n = stay.shape[0] // 2
    return add_low(stay[n:], got[n:]), add_low(stay[:n], got[:n])


def join(a, b):
    return jnp.concatenate([a, b], axis=0)


def paired(
    tokens, lengths, first_gain, first_shift, heads_weight, relative_bias, mixer_weight, second_gain,
    second_shift, expand_weight, expand_bias, reduce_weight, reduce_bias, cotangent,
):
    member = lax.axis_index("mp")
    index = lax.axis_index("dp")
    length = lengths[0]
    own, model = tokens.shape
    buckets = relative_bias.shape[1]
    width = heads_weight.shape[2]
    hidden = expand_bias.shape[0]
    sp = jnp.stack([member.astype(jnp.int32), length.astype(jnp.int32)])
    at = jnp.stack([place_of(index, s).astype(jnp.int32) for s in STAGES])
    places = member * own + jnp.arange(own)
    places_other = (1 - member) * own + jnp.arange(own)
    row = lambda v: v.reshape(1, -1)
    line = Line()

    rows = bias_rows(relative_bias)
    target0 = keep_valid(cotangent, places, length)
    other = swap(tokens)
    low0, projected0 = line(project, tokens, row(first_gain), row(first_shift), heads_weight)
    active_grad = lambda t, w: dot(t, w, 1, 1).astype(BF16)
    active_grad0 = line(active_grad, target0, reduce_weight)
    core = index % 2
    n = width // 2
    cotangent_other = swap(tie(cotangent, other, active_grad0))
    mixer_half = swap(tie(lax.dynamic_slice_in_dim(mixer_weight, core * n, n, 0), other, active_grad0))
    low1, projected1 = line(project, other, row(first_gain), row(first_shift), heads_weight)
    mixed, logsum = line(attend_forward, sp, projected0, projected1, rows)
    mixed_other = swap(mixed)
    mixer_rest = trade(tie(mixer_half, mixed), 1)
    mixer_other = jnp.where(core == 0, join(mixer_half, mixer_rest), join(mixer_rest, mixer_half))
    target1 = line(lambda x: keep_valid(x, places_other, length), cotangent_other)
    active_grad1 = line(active_grad, target1, reduce_weight)
    middle, second = line(mix, tokens, other, mixed, mixed_other, mixer_weight, mixer_other, row(second_gain), row(second_shift))

    act1, ge1, gs1, eb1 = line(
        lambda x, g, w, b: expand(x, 1, own, g, w, b, BF16), second, active_grad1, expand_weight, row(expand_bias)
    )
    gs_got = swap(gs1)
    act0, ge0, gs0, eb0 = line(
        lambda x, g, w, b: expand(x, 0, own, g, w, b, F32), second, active_grad0, expand_weight, row(expand_bias)
    )
    x_way, z_way = STAGES
    expand_part = lambda *xs: expand_grad_part(at, 0, *xs)
    query_part = lambda *xs: heads_grad_part(at, 0, *xs)
    value_part = lambda *xs: values_grad_part(at, 1, *xs)

    reduce_sum = lax.psum(line(rows_grad, act0, act1, target0, target1), "dp")

    def middle_back(gs0, gs_got, middle, target):
        norm, inverse = normalize(middle)
        grad_second = gs0 + gs_got.astype(F32)
        target = target.astype(F32)
        grad = target + norm_back(grad_second * second_gain, norm, inverse)
        sums = (jnp.sum(grad_second * norm, axis=0), jnp.sum(grad_second, axis=0), jnp.sum(target, axis=0))
        return grad, grad.astype(BF16), sums

    grad_middle, attended0, second_sums = line(middle_back, gs0, gs_got, middle, target0)
    attended1 = swap(attended0)
    grad_mix = lambda a, w: dot(a, w, 1, 1).astype(BF16)
    (e_send,) = line(expand_part, second, ge0, ge1)
    e_got = trade(e_send, x_way[0])
    grad_mixed0 = line(grad_mix, attended0, mixer_weight)
    reduced1 = line(lambda a, w: dot(a, w, 1, 0).astype(BF16), act1, reduce_weight)
    e_out, e_stay = line(expand_part, second, ge0, ge1, e_got)
    e_got = trade(e_out, x_way[1])
    grad_mixed1 = line(grad_mix, attended1, mixer_weight)
    reduced_got = swap(tie(reduced1, attended1))
    grad_projected, sums = line(
        attend_backward, sp, projected0, projected1, grad_mixed0, grad_mixed1, mixed, logsum, rows
    )
    e_out, e_stay = line(halve, e_stay, e_got)
    e_got = trade(e_out, x_way[2])

    first_part = lambda g, w: sum(dot(g[c], w[c], 1, 1) for c in range(3))
    first_part1 = line(lambda g, w: first_part(g[:, own:], w).astype(BF16), grad_projected, heads_weight)
    first_got = swap(first_part1)
    (q_send,) = line(query_part, low0, low1, grad_projected)
    q_got = trade(q_send, x_way[0])
    (v_send,) = line(value_part, low0, low1, grad_projected, attended0, attended1, mixed)
    v_got = trade(v_send, z_way[0])
    e_stay = line(add_low, e_stay, e_got)
    e_got = trade(e_stay, x_way[3])
    q_out, q_stay = line(query_part, low0, low1, grad_projected, q_got)
    q_got = trade(q_out, x_way[1])
    v_out, v_stay = line(value_part, low0, low1, grad_projected, attended0, attended1, mixed, v_got)
    v_got = trade(v_out, z_way[1])
    e_done = line(add_low, e_stay, e_got)
    e_next = trade(e_done, x_way[2])
    first_part0 = line(lambda g, w: first_part(g[:, :own], w), grad_projected, heads_weight)
    block_out = line(
        lambda m, a, w, r: (m + dot(a, w, 1, 0) + r.astype(F32) + reduce_bias).astype(BF16),
        middle, act0, reduce_weight, reduced_got,
    )
    v_out, v_stay = line(halve, v_stay, v_got)
    v_got = trade(v_out, z_way[2])

    def first_back(part, got, tokens, grad_middle):
        grad = part + got.astype(F32)
        norm, inverse = normalize(tokens.astype(F32))
        out = (grad_middle + norm_back(grad * first_gain, norm, inverse)).astype(BF16)
        return out, (jnp.sum(grad * norm, axis=0), jnp.sum(grad, axis=0))

    tokens_grad, first_sums = line(first_back, first_part0, first_got, tokens, grad_middle)
    both = jnp.stack([*first_sums, *second_sums])
    both_got = swap(both)
    e_first = line(join, e_done, e_next)
    e_second = trade(e_first, x_way[1])
    q_out, q_stay = line(halve, q_stay, q_got)
    q_got = trade(q_out, x_way[2])
    v_stay = line(add_low, v_stay, v_got)
    v_got = trade(v_stay, z_way[3])

    bias_part = bias_grad(sums, buckets)
    pack = line(
        lambda both, got, eb0, eb1, bias: jnp.concatenate(
            [(both + got).reshape(-1), (eb0 + eb1).reshape(-1), bias.reshape(-1)]
        ).reshape(-1, 128),
        both, both_got, eb0, eb1, bias_part,
    )
    pack_got = trade(pack, 1)
    q_stay = line(add_low, q_stay, q_got)
    q_got = trade(q_stay, x_way[3])
    pack = line(jnp.add, pack, pack_got)
    pack_got = trade(pack, 2)

    turned = (model, hidden // 8)
    v_done = line(add_low, v_stay, v_got)
    v_next = trade(v_done, z_way[2])
    pack = line(jnp.add, pack, pack_got)
    pack_got = trade(pack, 4)
    q_done = line(add_low, q_stay, q_got)
    q_next = trade(q_done, x_way[2])
    v_first = line(join, v_done, v_next)
    v_second = trade(v_first, z_way[1])
    pack = line(jnp.add, pack, pack_got)
    pack_got = trade(pack, 8)
    q_first = line(join, q_done, q_next)
    q_second = trade(q_first, x_way[1])
    e_third, e_fourth = trade(e_first, x_way[0]), trade(e_second, x_way[0])
    (expand_grad,) = line(
        lambda *xs: spread(
            at, 0, xs, put_rows, turned, [lambda to: pl.BlockSpec(turned, lambda g, s: (0, to(g, s)))],
            [jax.ShapeDtypeStruct(expand_weight.shape, F32)], name="spread_expand",
        ),
        e_first, e_second, e_third, e_fourth,
    )
    pack = line(jnp.add, pack, pack_got).reshape(-1)
    both = pack[: 5 * model].reshape(5, model)
    expand_bias_grad = pack[5 * model : 5 * model + hidden]
    bias_part = pack[5 * model + hidden :].reshape(relative_bias.shape)
    v_third, v_fourth = trade(v_first, z_way[0]), trade(v_second, z_way[0])
    q_third, q_fourth = trade(q_first, x_way[0]), trade(q_second, x_way[0])
    reduce_grad = line(lambda x: x.astype(F32), reduce_sum)
    heads_grad, mixer_grad = line(
        lambda *xs: spread_heads(at, xs[:4], xs[4:], model, width),
        q_first, q_second, q_third, q_fourth, v_first, v_second, v_third, v_fourth,
    )
    return (
        block_out, tokens_grad, both[0], both[1], heads_grad, bias_part, mixer_grad, both[2], both[3],
        expand_grad, expand_bias_grad, reduce_grad, both[4],
    )


def gathered(
    tokens, lengths, first_gain, first_shift, heads_weight, relative_bias, mixer_weight, second_gain,
    second_shift, expand_weight, expand_bias, reduce_weight, reduce_bias, cotangent,
):
    def gather(x):
        return lax.all_gather(x, "mp", axis=0, tiled=True)

    def scatter(x):
        return lax.psum_scatter(x.astype(BF16), "mp", scatter_dimension=0, tiled=True).astype(F32)

    members = lax.axis_size("mp")
    length = lengths[0]
    own = tokens.shape[0]
    whole = own * members
    half = whole // 2
    buckets = relative_bias.shape[1]
    sp = jnp.stack([jnp.zeros((), jnp.int32), length.astype(jnp.int32)])
    places = lax.axis_index("mp") * own + jnp.arange(own)
    rows = bias_rows(relative_bias)
    source_all = gather(tokens)
    first_all, projected = project(source_all, first_gain.reshape(1, -1), first_shift.reshape(1, -1), heads_weight)
    projected0, projected1 = projected[:, :half], projected[:, half:]
    mixed, logsum = attend_forward(sp, projected0, projected1, rows)
    source = tokens.astype(F32)
    middle = source + scatter(dot(mixed, mixer_weight, 1, 0))
    second_norm, second_inverse = normalize(middle)
    second_all = gather((second_norm * second_gain + second_shift).astype(BF16))
    target = keep_valid(cotangent, places, length)
    target_wide = target.astype(F32)
    target_all = gather(target)
    expanded = dot(second_all, expand_weight, 1, 0) + expand_bias
    active_low = jax.nn.gelu(expanded, approximate=True).astype(BF16)
    grad_expanded = gelu_back(expanded, dot(target_all, reduce_weight, 1, 1)).astype(BF16)
    grad_second = scatter(dot(grad_expanded, expand_weight, 1, 1))
    reduced = scatter(dot(active_low, reduce_weight, 1, 0))
    reduce_grad = dot(active_low, target_all, 0, 0)
    expand_grad = dot(second_all, grad_expanded, 0, 0)
    expand_bias_grad = jnp.sum(grad_expanded.astype(F32), axis=0)
    block_out = (middle + reduced + reduce_bias).astype(BF16)
    grad_middle = target_wide + norm_back(grad_second * second_gain, second_norm, second_inverse)
    attended_all = gather(grad_middle.astype(BF16))
    mixer_grad = dot(mixed, attended_all, 0, 0)
    grad_mixed = dot(attended_all, mixer_weight, 1, 1).astype(BF16)
    grad_projected, sums = attend_backward(
        sp, projected0, projected1, grad_mixed[:half], grad_mixed[half:], mixed, logsum, rows
    )
    bias_part = bias_grad(sums, buckets)
    heads_grad = jnp.einsum("td,cte->cde", first_all, grad_projected, preferred_element_type=F32)
    grad_first = scatter(jnp.einsum("cte,cde->td", grad_projected, heads_weight, preferred_element_type=F32))
    first_norm, first_inverse = normalize(source)
    tokens_grad = (
        grad_middle + norm_back(grad_first * first_gain, first_norm, first_inverse)
    ).astype(BF16)
    first_gain_grad, first_shift_grad, second_gain_grad, second_shift_grad, reduce_bias_grad = (
        lax.psum(
            (
                jnp.sum(grad_first * first_norm, axis=0),
                jnp.sum(grad_first, axis=0),
                jnp.sum(grad_second * second_norm, axis=0),
                jnp.sum(grad_second, axis=0),
                jnp.sum(target_wide, axis=0),
            ),
            ("dp", "mp"),
        )
    )
    heads_grad, bias_part, mixer_grad, expand_grad, expand_bias_grad, reduce_grad = (
        lax.psum(x.astype(BF16), "dp").astype(F32)
        for x in (heads_grad, bias_part, mixer_grad, expand_grad, expand_bias_grad, reduce_grad)
    )
    return (
        block_out, tokens_grad, first_gain_grad, first_shift_grad, heads_grad, bias_part, mixer_grad,
        second_gain_grad, second_shift_grad, expand_grad, expand_bias_grad, reduce_grad, reduce_bias_grad,
    )


def per_device(*args):
    if lax.axis_size("mp") == 2 and lax.axis_size("dp") == 16:
        return paired(*args)
    return gathered(*args)


def solution(mesh):
    return jax.shard_map(
        per_device,
        mesh=mesh,
        in_specs=(
            P(("dp", "mp"), None),
            P("dp"),
            P(),
            P(),
            P(None, None, "mp"),
            P("mp", None),
            P("mp", None),
            P(),
            P(),
            P(None, "mp"),
            P("mp"),
            P("mp", None),
            P(),
            P(("dp", "mp"), None),
        ),
        out_specs=(
            P(("dp", "mp"), None),
            P(("dp", "mp"), None),
            P(),
            P(),
            P(None, None, "mp"),
            P("mp", None),
            P("mp", None),
            P(),
            P(),
            P(None, "mp"),
            P("mp"),
            P("mp", None),
            P(),
        ),
        check_vma=False,
    )
```

```python
import functools
import math

import jax
import jax.numpy as jnp
import numpy as np
from jax import lax
from jax.experimental import pallas as pl
from jax.experimental.pallas import tpu as pltpu
from jax.sharding import PartitionSpec as P

EPS = 1e-05
DH=64; MAXDIST=128; NEG=-1e30; BLK=256
F32=jnp.float32; BF16=jnp.bfloat16
HIGHEST=lax.Precision.HIGHEST

def bucket_table(count, buckets, reach):
    exact = buckets // 2
    entries = []
    for position in range(count):
        if position < exact:
            entries.append(position)
        else:
            level = exact + int(math.log(position / exact) / math.log(reach / exact) * (buckets - exact))
            entries.append(min(buckets - 1, level))
    return np.array(entries, dtype=np.int32)

def bias_tables(buckets):
    W=2*BLK
    tab=bucket_table(W,buckets,MAXDIST)
    oh=np.zeros((buckets,4,W),np.float32); neg=np.zeros((1,4,W),np.float32)
    for y in range(W):
        x = y if y < BLK else y-W
        if x<=0 and -x<BLK: oh[tab[-x],0,y]=1
        else: neg[0,0,y]=NEG
        d=BLK-x
        if 0<=d<W: oh[tab[d],1,y]=1
        if 0<=x: oh[tab[x],2,y]=1
        else: neg[0,2,y]=NEG
        d=BLK+x
        if 0<=d<W: oh[tab[d],3,y]=1
    return oh.reshape(buckets,4*W), neg.reshape(1,4*W)

def bias_rows(relative_bias):
    heads,buckets=relative_bias.shape
    oh,neg=bias_tables(buckets)
    rel=relative_bias-relative_bias[:,buckets-1:]
    rows=jnp.dot(rel,jnp.asarray(oh),precision=HIGHEST)+jnp.asarray(neg)
    return rows.reshape(heads//2,2,4*2*BLK)

def toeplitz(row):
    wide=jnp.broadcast_to(row,(BLK,2*BLK))
    return pltpu.roll(wide,0,1,stride=1,stride_axis=0)[:,:BLK]


def lane_masks():
    lane=lax.broadcasted_iota(jnp.int32,(1,128),1)
    head=[(lane//DH)==h for h in range(2)]
    mine=[jnp.where(m,1.0,0.0).astype(BF16) for m in head]
    spare=[jnp.where(lane==DH*(1-h),1.0,0.0) for h in range(2)]
    return head,mine,spare


def gone_rows(start,half,length,spare):
    pos=lax.broadcasted_iota(jnp.int32,(half,1),0)+start
    gone=jnp.where(pos<length,0.0,NEG)
    return [(gone*s).astype(BF16) for s in spare]


def fwd_kernel(sp, a_ref,c_ref,b_ref,o_ref,lse_ref,qs,ks,vs):
    half=a_ref.shape[1]; T=2*half; flip=sp[0]; length=sp[1]
    W=2*BLK
    head,mine,spare=lane_masks()
    for a,ref in enumerate((a_ref,c_ref)):
        start=pl.multiple_of((a^flip)*half,half)
        dst=pl.ds(start,half)
        gone=gone_rows(start,half,length,spare)
        for h in range(2):
            qs[h,dst,:]=ref[0]*(mine[h]*jnp.asarray(DH**-0.5,BF16))+spare[h].astype(BF16)
            ks[h,dst,:]=ref[1]*mine[h]+gone[h]
            vs[h,dst,:]=ref[2]*mine[h]+mine[1-h]
    tiles=[(toeplitz(b_ref[0,h:h+1,0:W]),toeplitz(b_ref[0,h:h+1,W:2*W])) for h in range(2)]
    outs={}

    def score(i,h):
        return dot(qs[h,i*BLK:(i+1)*BLK,:],ks[h,:(i+1)*BLK,:],1,1)

    def finish(i,h,s):
        kc=(i+1)*BLK; t0,t1=tiles[h]
        parts=[]
        if i>=2: parts.append(s[:,:kc-2*BLK])
        if i>=1: parts.append(s[:,kc-2*BLK:kc-BLK]+t1)
        parts.append(s[:,kc-BLK:]+t0)
        top=functools.reduce(jnp.maximum,[jnp.max(x,axis=1,keepdims=True) for x in parts])
        p=jnp.concatenate([jnp.exp(x-top).astype(BF16) for x in parts],axis=1)
        o=dot(p,vs[h,:kc,:],1,0)
        total=o[:,DH*(1-h):DH*(1-h)+1]
        outs[h]=(o*(1.0/total),top+jnp.log(total))
        if h==1:
            rows=pl.ds(pl.multiple_of((i*BLK+flip*half)%T,BLK),BLK)
            o_ref[rows,:]=jnp.where(head[0],outs[0][0],outs[1][0]).astype(BF16)
            lse_ref[0,i*BLK:kc,:]=jnp.where(head[0],outs[0][1],outs[1][1])

    run_ahead([(i,h) for i in range(T//BLK) for h in range(2)],score,finish,2)


def run_ahead(items,first,second,depth):
    waiting=[]
    for item in items:
        waiting.append((item,first(*item)))
        if len(waiting)>depth:
            done,value=waiting.pop(0)
            second(*done,value)
    for done,value in waiting:
        second(*done,value)


def attend_forward(sp,projected0,projected1,rows):
    _,half,HD=projected0.shape; pairs=HD//128; T=2*half
    part=pl.BlockSpec((3,half,128),lambda p,s:(0,0,p))
    return pl.pallas_call(
        fwd_kernel,
        grid_spec=pltpu.PrefetchScalarGridSpec(
            num_scalar_prefetch=1,grid=(pairs,),
            in_specs=[part,part,pl.BlockSpec((1,2,rows.shape[2]),lambda p,s:(p,0,0))],
            out_specs=[pl.BlockSpec((T,128),lambda p,s:(0,p)),pl.BlockSpec((1,T,128),lambda p,s:(p,0,0))],
            scratch_shapes=[pltpu.VMEM((2,T,128),BF16)]*3),
        out_shape=[jax.ShapeDtypeStruct((T,HD),BF16),jax.ShapeDtypeStruct((pairs,T,128),F32)],
        cost_estimate=cost(8*T*T*HD,8*T*HD+512*pairs*T),
        name="attend_forward",
    )(sp,projected0,projected1,rows)

def diagonal_sums(acc, offset):
    W=2*BLK
    wide=jnp.concatenate([acc,jnp.zeros_like(acc)],axis=1)
    n=BLK
    while n>1:
        n//=2
        top=wide[:n]; bottom=wide[n:2*n]
        wide=top+pltpu.roll(bottom,W-n,1)
    return pltpu.roll(wide,offset,1) if offset else wide

def bwd_kernel(sp, a_ref,c_ref,d0_ref,d1_ref,o_ref,lse_ref,b_ref,g_ref,d_ref,qs,ks,vs,dos,dq,acc0,acc1):
    half=a_ref.shape[1]; T=2*half; flip=sp[0]; length=sp[1]
    W=2*BLK
    n=T//BLK
    head,mine,spare=lane_masks()
    stats=[None,None]
    one=sum(spare).astype(BF16)
    for a,(ref,do_ref) in enumerate(((a_ref,d0_ref),(c_ref,d1_ref))):
        start=pl.multiple_of((a^flip)*half,half)
        dst=pl.ds(start,half)
        gone=gone_rows(start,half,length,spare)
        for h in range(2):
            qs[h,dst,:]=ref[0]*(mine[h]*jnp.asarray(DH**-0.5,BF16))+spare[h].astype(BF16)
            ks[h,dst,:]=ref[1]*mine[h]+gone[h]
            vs[h,dst,:]=ref[2]*mine[h]
        dos[dst,:]=do_ref[...]
        acc0[0,dst,:]=do_ref[...].astype(F32)*o_ref[a*half:(a+1)*half,:].astype(F32)
    turned=acc0[0].T
    deltas=[jnp.sum(turned[h*DH:(h+1)*DH],axis=0,keepdims=True) for h in range(2)]
    turned=lse_ref[0].T
    lses=[turned[h*DH:h*DH+1] for h in range(2)]
    near=acc1
    tiles=[(toeplitz(b_ref[0,h:h+1,2*W:3*W]),toeplitz(b_ref[0,h:h+1,3*W:])) for h in range(2)]

    def products(j,h):
        rj=slice(j*BLK,(j+1)*BLK)
        return dot(ks[h,rj,:],qs[h,j*BLK:,:],1,1),dot(vs[h,rj,:],dos[j*BLK:,:],1,1)

    keep={}

    def finish(j,h,value):
        s,dp=value
        rj=slice(j*BLK,(j+1)*BLK)
        ps=[];dss=[]
        for b in range(n-j):
            c=slice(b*BLK,(b+1)*BLK)
            cc=slice((j+b)*BLK,(j+b+1)*BLK)
            x=s[:,c]-lses[h][:,cc]
            if b<2: x=x+tiles[h][b]
            p=jnp.exp(x)
            ds=p*(dp[:,c]-deltas[h][:,cc])
            if b<2:
                if j==0: near[h,b]=ds
                else: near[h,b]+=ds
            ps.append(p.astype(BF16)); dss.append(ds.astype(BF16))
        p=jnp.concatenate(ps,axis=1); ds=jnp.concatenate(dss,axis=1)
        dv=dot(p,dos[j*BLK:,:],1,0)
        dk=dot(ds,qs[h,j*BLK:,:],1,0)
        kk=ks[h,rj,:]*mine[h]+mine[1-h]
        dqj=dot(ds,kk,0,0)
        if j==0: dq[h,:,:]=dqj
        else: dq[h,j*BLK:,:]+=dqj
        keep[h]=(dk,dv)
        if h==1:
            rows=pl.ds(pl.multiple_of((j*BLK+flip*half)%T,BLK),BLK)
            g_ref[1,rows,:]=jnp.where(head[0],keep[0][0],keep[1][0]).astype(BF16)
            g_ref[2,rows,:]=jnp.where(head[0],keep[0][1],keep[1][1]).astype(BF16)

    run_ahead([(j,h) for j in range(n) for h in range(2)],products,finish,1)
    for h in range(2):
        d_ref[0,h:h+1,:]=diagonal_sums(near[h,0],0)+diagonal_sums(near[h,1],BLK)
        total=jnp.sum(dq[h,:,:],axis=0,keepdims=True)[:,DH*(1-h):DH*(1-h)+1]
        d_ref[0,2+h:3+h,:]=jnp.broadcast_to(total,(1,W))
    for a in range(2):
        dst=pl.ds(pl.multiple_of((a^flip)*half,half),half)
        g_ref[0,a*half:(a+1)*half,:]=(jnp.where(head[0],dq[0,dst,:],dq[1,dst,:])*DH**-0.5).astype(BF16)

def attend_backward(sp,projected0,projected1,grad0,grad1,mixed,lse,rows,start=0,count=None,given=None):
    _,half,HD=projected0.shape; pairs=HD//128; T=2*half
    count=pairs if count is None else count
    part=pl.BlockSpec((3,half,128),lambda p,s:(0,0,p+start))
    grad=pl.BlockSpec((half,128),lambda p,s:(0,p+start))
    in_specs=[part,part,grad,grad,pl.BlockSpec((T,128),lambda p,s:(0,p+start)),
              pl.BlockSpec((1,T,128),lambda p,s:(p+start,0,0)),pl.BlockSpec((1,2,rows.shape[2]),lambda p,s:(p+start,0,0))]
    args=[sp,projected0,projected1,grad0,grad1,mixed,lse,rows]
    kernel=bwd_kernel
    if given is not None:
        in_specs.append(pl.BlockSpec(memory_space=pl.ANY)); args.append(given)
        kernel=lambda *refs: bwd_kernel(*refs[:8],*refs[9:])
    return pl.pallas_call(
        kernel,
        grid_spec=pltpu.PrefetchScalarGridSpec(
            num_scalar_prefetch=1,grid=(count,),
            in_specs=in_specs,
            out_specs=[pl.BlockSpec((3,T,128),lambda p,s:(0,0,p+start)),pl.BlockSpec((1,4,2*BLK),lambda p,s:(p,0,0))],
            scratch_shapes=[pltpu.VMEM((2,T,128),BF16)]*3+[pltpu.VMEM((T,128),BF16),pltpu.VMEM((2,T,128),F32),pltpu.VMEM((1,T,128),F32),pltpu.VMEM((2,2,BLK,BLK),F32)]),
        out_shape=[jax.ShapeDtypeStruct((3,T,HD),BF16),jax.ShapeDtypeStruct((count,4,2*BLK),F32)],
        input_output_aliases={} if given is None else {8:0},
        cost_estimate=cost(20*T*T*128*count,(16*T*128+512*T)*count),
        name="attend_backward",
    )(*args)

def bias_grad(sums, buckets):
    pairs=sums.shape[0]; W=2*BLK
    tab=bucket_table(W,buckets,MAXDIST)
    assert tab[BLK]==buckets-1
    m=np.zeros((W,buckets),np.float32)
    for d in range(W):
        if tab[d]<buckets-1:
            m[d,tab[d]]=1; m[d,buckets-1]=-1
    near=sums[:,0:2].reshape(pairs*2,W); total=sums[:,2:4,0].reshape(pairs*2,1)
    last=np.zeros((1,buckets),np.float32); last[0,-1]=1
    return jnp.dot(near,jnp.asarray(m),precision=HIGHEST)+total*jnp.asarray(last)


HALF_TANH = math.sqrt(2.0 / math.pi)


def dot(a, b, ca, cb):
    return lax.dot_general(a, b, (((ca,), (cb,)), ((), ())), preferred_element_type=F32)


def fixed(shape):
    return pl.BlockSpec(shape, lambda *_: (0,) * len(shape))


def cost(flops, moved):
    return pl.CostEstimate(flops=int(flops), transcendentals=0, bytes_accessed=int(moved))


def row_norm(values):
    center = jnp.mean(values, axis=-1, keepdims=True)
    centered = values - center
    inverse = lax.rsqrt(jnp.mean(centered * centered, axis=-1, keepdims=True) + EPS)
    return centered * inverse, inverse


def project_kernel(x_ref, gain_ref, shift_ref, w_ref, low_ref, out_ref):
    normed, _ = row_norm(x_ref[...].astype(F32))
    low = (normed * gain_ref[...] + shift_ref[...]).astype(BF16)
    low_ref[...] = low
    for c in range(3):
        out_ref[c] = dot(low, w_ref[c], 1, 0).astype(BF16)


def project(x, gain, shift, weight):
    rows, model = x.shape
    width = weight.shape[2]
    step = min(256, rows)
    return pl.pallas_call(
        project_kernel,
        grid=(rows // step,),
        in_specs=[pl.BlockSpec((step, model), lambda i: (i, 0)), fixed((1, model)), fixed((1, model)), fixed(weight.shape)],
        out_specs=[pl.BlockSpec((step, model), lambda i: (i, 0)), pl.BlockSpec((3, step, width), lambda i: (0, i, 0))],
        out_shape=[jax.ShapeDtypeStruct((rows, model), BF16), jax.ShapeDtypeStruct((3, rows, width), BF16)],
        cost_estimate=cost(6 * rows * model * width, 2 * (2 * rows * model + weight.size + 3 * rows * width)),
        name="project",
    )(x, gain, shift, weight)


def mix_kernel(own_blocks, x0_ref, x1_ref, m_ref, p_ref, w0_ref, w1_ref, gain_ref, shift_ref, mid_ref, low_ref):
    i = pl.program_id(0)
    attended = dot(m_ref[...], w0_ref[...], 1, 0) + dot(p_ref[...], w1_ref[...], 1, 0)

    def rows(x_ref):
        return x_ref[...].astype(F32) + attended

    def rest(middle):
        normed, _ = row_norm(middle)
        low_ref[...] = (normed * gain_ref[...] + shift_ref[...]).astype(BF16)

    @pl.when(i < own_blocks)
    def _():
        middle = rows(x0_ref)
        mid_ref[...] = middle
        rest(middle)

    @pl.when(i >= own_blocks)
    def _():
        rest(rows(x1_ref))


def mix(tokens, other, mixed, mixed_other, weight, weight_other, gain, shift):
    own, model = tokens.shape
    width = mixed.shape[1]
    step = 256
    n = own // step
    return pl.pallas_call(
        functools.partial(mix_kernel, n),
        grid=(2 * n,),
        in_specs=[
            pl.BlockSpec((step, model), lambda i: (jnp.minimum(i, n - 1), 0)),
            pl.BlockSpec((step, model), lambda i: (jnp.maximum(i - n, 0), 0)),
            pl.BlockSpec((step, width), lambda i: (i, 0)),
            pl.BlockSpec((step, width), lambda i: ((i + n) % (2 * n), 0)),
            fixed(weight.shape), fixed(weight.shape), fixed((1, model)), fixed((1, model)),
        ],
        out_specs=[
            pl.BlockSpec((step, model), lambda i: (jnp.minimum(i, n - 1), 0)),
            pl.BlockSpec((step, model), lambda i: (i, 0)),
        ],
        out_shape=[jax.ShapeDtypeStruct((own, model), F32), jax.ShapeDtypeStruct((2 * own, model), BF16)],
        cost_estimate=cost(8 * own * model * width, 2 * (4 * own * model + 4 * own * width + 2 * weight.size) + 4 * own * model),
        name="mix",
    )(tokens, other, mixed, mixed_other, weight, weight_other, gain, shift)


def expand_kernel(x_ref, g_ref, w_ref, b_ref, act_ref, ge_ref, gs_ref, bias_ref, acc_ref):
    i = pl.program_id(0)
    x = x_ref[...]
    width = w_ref.shape[1]
    sub = 256
    total = None
    for s in range(width // sub):
        cols = slice(s * sub, (s + 1) * sub)
        u = dot(x, w_ref[:, cols], 1, 0) + b_ref[:, cols].astype(F32)
        square = u * u
        t = jnp.tanh(HALF_TANH * u * (1.0 + 0.044715 * square))
        half = 0.5 + 0.5 * t
        act_ref[:, cols] = (u * half).astype(BF16)
        slope = half + 0.5 * u * (1.0 - t * t) * (HALF_TANH * (1.0 + 3 * 0.044715 * square))
        grad = g_ref[:, cols].astype(F32) * slope
        low = grad.astype(BF16)
        ge_ref[:, cols] = low
        bias_ref[:, cols] = jnp.sum(grad, axis=0, keepdims=True)
        part = dot(low, w_ref[:, cols], 1, 1)
        total = part if total is None else total + part

    @pl.when(i == 0)
    def _():
        acc_ref[...] = total

    @pl.when(i > 0)
    def _():
        acc_ref[...] += total

    @pl.when(i == pl.num_programs(0) - 1)
    def _():
        gs_ref[...] = acc_ref[...].astype(gs_ref.dtype)


def expand(x, block, rows, grad_active, weight, bias, dtype):
    model = x.shape[1]
    hidden = weight.shape[1]
    step = min(512, hidden)
    return pl.pallas_call(
        expand_kernel,
        grid=(hidden // step,),
        in_specs=[
            pl.BlockSpec((rows, model), lambda i: (block, 0)),
            pl.BlockSpec((rows, step), lambda i: (0, i)),
            pl.BlockSpec((model, step), lambda i: (0, i)),
            pl.BlockSpec((1, step), lambda i: (0, i)),
        ],
        out_specs=[
            pl.BlockSpec((rows, step), lambda i: (0, i)),
            pl.BlockSpec((rows, step), lambda i: (0, i)),
            fixed((rows, model)),
            pl.BlockSpec((1, step), lambda i: (0, i)),
        ],
        out_shape=[
            jax.ShapeDtypeStruct((rows, hidden), BF16),
            jax.ShapeDtypeStruct((rows, hidden), BF16),
            jax.ShapeDtypeStruct((rows, model), dtype),
            jax.ShapeDtypeStruct((1, hidden), F32),
        ],
        scratch_shapes=[pltpu.VMEM((rows, model), F32)],
        cost_estimate=cost(4 * rows * model * hidden, 2 * (2 * rows * model + 3 * rows * hidden + weight.size)),
        name="expand",
    )(x, grad_active, weight, bias)


STAGES = ((1, 2, 4, 8), (1, 4, 2, 8))


def place_of(index, stages):
    bit = [(index // s) % 2 for s in stages]
    return bit[0] * 4 + bit[1] * 2 + bit[2]


def trade(x, bit):
    size = lax.axis_size("dp")
    return lax.ppermute(x, "dp", [(i, i ^ bit) for i in range(size)])


def add_low(a, b):
    return (a.astype(F32) + b.astype(F32)).astype(BF16)


def pair_of(g, s, slot):
    return (3 - g) ^ (s[slot] // 2)


def put_pair(slot, s_ref, chunks, outs):
    flip = s_ref[slot] % 2
    sent = pl.program_id(0) < 2
    for j, value in enumerate(chunks):
        value = value.astype(BF16)[None]
        for out, here in zip(outs, (sent, jnp.logical_not(sent))):
            @pl.when(here)
            def _(out=out):
                out[pl.ds(j ^ flip, 1)] = value


def pair_call(kernel, slot, s, arrays, specs, tail, flops, name):
    zeros = (0,) * len(tail)
    moved = sum(2 * x.size for x in arrays) + 16 * math.prod(tail)
    return pl.pallas_call(
        functools.partial(kernel, slot),
        grid_spec=pltpu.PrefetchScalarGridSpec(
            num_scalar_prefetch=1, grid=(4,), in_specs=specs,
            out_specs=[
                pl.BlockSpec((2, *tail), lambda g, s: (jnp.maximum(1 - g, 0), *zeros)),
                pl.BlockSpec((2, *tail), lambda g, s: (jnp.minimum(3 - g, 1), *zeros)),
            ],
        ),
        out_shape=[jax.ShapeDtypeStruct((4, *tail), BF16)] * 2,
        cost_estimate=cost(flops, moved),
        name=name,
    )(s, *arrays)


def reduce_grad_kernel(slot, s_ref, *refs):
    (a0, a1, t0, t1), outs = refs[:4], refs[4:]
    value = dot(a0[...], t0[...], 0, 0) + dot(a1[...], t1[...], 0, 0)
    width = value.shape[0] // 2
    put_pair(slot, s_ref, [value[:width], value[width:]], outs)


def reduce_grad_part(s, slot, act0, act1, t0, t1):
    rows, hidden = act0.shape
    model = t0.shape[1]
    block = pl.BlockSpec((rows, hidden // 4), lambda g, s: (0, pair_of(g, s, slot)))
    return pair_call(
        reduce_grad_kernel, slot, s, (act0, act1, t0, t1), [block, block, fixed(t0.shape), fixed(t1.shape)],
        (hidden // 8, model), 4 * rows * model * hidden, "reduce_grad",
    )


def expand_grad_kernel(slot, s_ref, *refs):
    (x, g0, g1), outs = refs[:3], refs[3:]
    rows = g0.shape[0]
    value = dot(x[:rows], g0[...], 0, 0) + dot(x[rows:], g1[...], 0, 0)
    width = value.shape[1] // 2
    put_pair(slot, s_ref, [value[:, :width], value[:, width:]], outs)


def expand_grad_part(s, slot, x, g0, g1):
    rows, hidden = g0.shape
    model = x.shape[1]
    block = pl.BlockSpec((rows, hidden // 4), lambda g, s: (0, pair_of(g, s, slot)))
    return pair_call(
        expand_grad_kernel, slot, s, (x, g0, g1), [fixed(x.shape), block, block],
        (model, hidden // 8), 4 * rows * model * hidden, "expand_grad",
    )


def heads_grad_kernel(slot, s_ref, *refs):
    (l0, l1, g), outs = refs[:3], refs[3:]
    rows = l0.shape[0]
    both = [dot(l0[...], g[c, :rows], 0, 0) + dot(l1[...], g[c, rows:], 0, 0) for c in range(2)]
    width = both[0].shape[0] // 2
    chunks = [jnp.stack([v[j * width:(j + 1) * width] for v in both]) for j in range(2)]
    put_pair(slot, s_ref, chunks, outs)


def heads_grad_part(s, slot, low0, low1, grad):
    rows, model = low0.shape
    width = grad.shape[2]
    block = pl.BlockSpec((rows, model // 4), lambda g, s: (0, pair_of(g, s, slot)))
    return pair_call(
        heads_grad_kernel, slot, s, (low0, low1, grad),
        [block, block, pl.BlockSpec((2, 2 * rows, width), lambda g, s: (0, 0, 0))],
        (2, model // 8, width), 8 * rows * model * width, "heads_grad",
    )


def values_grad_kernel(slot, s_ref, *refs):
    (l0, l1, g, a0, a1, m), outs = refs[:6], refs[6:]
    rows = l0.shape[0]
    both = [
        dot(l0[...], g[0, :rows], 0, 0) + dot(l1[...], g[0, rows:], 0, 0),
        dot(a0[...], m[:rows], 0, 0) + dot(a1[...], m[rows:], 0, 0),
    ]
    width = both[0].shape[0] // 2
    chunks = [jnp.stack([v[j * width:(j + 1) * width] for v in both]) for j in range(2)]
    put_pair(slot, s_ref, chunks, outs)


def values_grad_part(s, slot, low0, low1, grad, att0, att1, mixed):
    rows, model = low0.shape
    width = grad.shape[2]
    block = pl.BlockSpec((rows, model // 4), lambda g, s: (0, pair_of(g, s, slot)))
    return pair_call(
        values_grad_kernel, slot, s, (low0, low1, grad, att0, att1, mixed),
        [block, block, pl.BlockSpec((1, 2 * rows, width), lambda g, s: (2, 0, 0)), block, block, fixed(mixed.shape)],
        (2, model // 8, width), 8 * rows * model * width, "values_grad",
    )


def spread_kernel(put, s_ref, *refs):
    g = pl.program_id(0)
    pieces, outs = refs[-4 - put.outs:-put.outs], refs[-put.outs:]
    for a in range(4):
        @pl.when(g // 2 == a)
        def _(a=a):
            put(pieces[a], outs)


def spread(places, slot, pieces, put, tail, out_specs, out_shape, given=None, name=None):
    zeros = (0,) * len(tail)
    at = lambda g, s: g ^ s[slot]
    in_specs = [
        pl.BlockSpec((1, *tail), lambda g, s, a=a: (jnp.clip(g - 2 * a, 0, 1), *zeros)) for a in range(4)
    ]
    args = list(pieces)
    aliases = {}
    if given is not None:
        in_specs.insert(0, pl.BlockSpec(memory_space=pl.ANY))
        args.insert(0, given)
        aliases = {1: 0}
    return pl.pallas_call(
        functools.partial(spread_kernel, put),
        grid_spec=pltpu.PrefetchScalarGridSpec(
            num_scalar_prefetch=1, grid=(8,), in_specs=in_specs, out_specs=[spec(at) for spec in out_specs],
        ),
        out_shape=out_shape,
        input_output_aliases=aliases,
        cost_estimate=cost(0, 6 * 8 * math.prod(tail)),
        name=name,
    )(places, *args)


def put_rows(piece, outs):
    outs[0][...] = piece[0].astype(F32)


put_rows.outs = 1


def rows_grad_kernel(a0, a1, t0, t1, out_ref):
    out_ref[...] = (dot(a0[...], t0[...], 0, 0) + dot(a1[...], t1[...], 0, 0)).astype(BF16)


def rows_grad(act0, act1, t0, t1):
    rows, hidden = act0.shape
    model = t0.shape[1]
    step = min(512, hidden)
    block = pl.BlockSpec((rows, step), lambda i: (0, i))
    return pl.pallas_call(
        rows_grad_kernel,
        grid=(hidden // step,),
        in_specs=[block, block, fixed(t0.shape), fixed(t1.shape)],
        out_specs=pl.BlockSpec((step, model), lambda i: (i, 0)),
        out_shape=jax.ShapeDtypeStruct((hidden, model), BF16),
        cost_estimate=cost(4 * rows * model * hidden, 4 * rows * (model + hidden) + 2 * model * hidden),
        name="rows_grad",
    )(act0, act1, t0, t1)


def spread_heads_kernel(s_ref, *refs):
    k = pl.program_id(0)
    heads_ref, mixer_ref = refs[8:]
    for slot in range(2):
        r = k ^ s_ref[slot]
        for a in range(4):
            piece = refs[4 * slot + a]

            @pl.when(r // 2 == a)
            def _(slot=slot, piece=piece):
                if slot == 0:
                    heads_ref[:2] = piece[0].astype(F32)
                else:
                    heads_ref[2] = piece[0, 0].astype(F32)
                    mixer_ref[...] = piece[0, 1].astype(F32).T


def spread_heads(places, queries, values, model, width):
    tail = (2, model // 8, width)

    def spec(slot, a):
        def at(k, s):
            r = k ^ s[slot]
            return (jnp.where(r // 2 == a, r % 2, 0), 0, 0, 0)

        return pl.BlockSpec((1, *tail), at)

    return pl.pallas_call(
        spread_heads_kernel,
        grid_spec=pltpu.PrefetchScalarGridSpec(
            num_scalar_prefetch=1, grid=(8,),
            in_specs=[spec(slot, a) for slot in range(2) for a in range(4)],
            out_specs=[
                pl.BlockSpec((3, model // 8, width), lambda k, s: (0, k, 0)),
                pl.BlockSpec((width, model // 8), lambda k, s: (0, k)),
            ],
        ),
        out_shape=[jax.ShapeDtypeStruct((3, model, width), F32), jax.ShapeDtypeStruct((width, model), F32)],
        cost_estimate=cost(0, 12 * 8 * math.prod(tail)),
        name="spread_heads",
    )(places, *queries, *values)


def normalize(values):
    return row_norm(values)


def norm_back(grad_norm, normed, inverse):
    return inverse * (
        grad_norm
        - jnp.mean(grad_norm, axis=-1, keepdims=True)
        - normed * jnp.mean(grad_norm * normed, axis=-1, keepdims=True)
    )


def gelu_back(expanded, grad_active):
    pull = jax.vjp(lambda value: jax.nn.gelu(value, approximate=True), expanded)[1]
    return pull(grad_active)[0]


def swap(x):
    return lax.ppermute(x, "mp", [(0, 1), (1, 0)])


def keep_valid(x, places, length):
    return jnp.where((places < length)[:, None], x, jnp.zeros_like(x))


def tie(x, *others):
    return lax.optimization_barrier((x, *others))[0]


class Line:
    def __init__(self):
        self.last = None

    def __call__(self, step, *args):
        if self.last is not None:
            args, _ = lax.optimization_barrier((args, self.last))
        out = step(*args)
        self.last = jax.tree.leaves(out)
        return out


def halve(stay, got):
    n = stay.shape[0] // 2
    return add_low(stay[n:], got[n:]), add_low(stay[:n], got[:n])


def join(a, b):
    return jnp.concatenate([a, b], axis=0)


def paired(
    tokens, lengths, first_gain, first_shift, heads_weight, relative_bias, mixer_weight, second_gain,
    second_shift, expand_weight, expand_bias, reduce_weight, reduce_bias, cotangent,
):
    member = lax.axis_index("mp")
    index = lax.axis_index("dp")
    length = lengths[0]
    own, model = tokens.shape
    buckets = relative_bias.shape[1]
    width = heads_weight.shape[2]
    hidden = expand_bias.shape[0]
    sp = jnp.stack([member.astype(jnp.int32), length.astype(jnp.int32)])
    at = jnp.stack([place_of(index, s).astype(jnp.int32) for s in STAGES])
    places = member * own + jnp.arange(own)
    places_other = (1 - member) * own + jnp.arange(own)
    row = lambda v: v.reshape(1, -1)
    line = Line()

    rows = bias_rows(relative_bias)
    target0 = keep_valid(cotangent, places, length)
    other = swap(tokens)
    low0, projected0 = line(project, tokens, row(first_gain), row(first_shift), heads_weight)
    active_grad = lambda t, w: dot(t, w, 1, 1).astype(BF16)
    active_grad0 = line(active_grad, target0, reduce_weight)
    core = index % 2
    n = width // 2
    cotangent_other = swap(tie(cotangent, other, active_grad0))
    mixer_half = swap(tie(lax.dynamic_slice_in_dim(mixer_weight, core * n, n, 0), other, active_grad0))
    low1, projected1 = line(project, other, row(first_gain), row(first_shift), heads_weight)
    mixed, logsum = line(attend_forward, sp, projected0, projected1, rows)
    mixed_other = swap(mixed)
    target1 = line(lambda x: keep_valid(x, places_other, length), cotangent_other)
    mixer_rest = trade(tie(mixer_half, target1), 1)
    active_grad1 = line(active_grad, target1, reduce_weight)
    mixer_other = jnp.where(core == 0, join(mixer_half, mixer_rest), join(mixer_rest, mixer_half))
    middle, second = line(mix, tokens, other, mixed, mixed_other, mixer_weight, mixer_other, row(second_gain), row(second_shift))

    act1, ge1, gs1, eb1 = line(
        lambda x, g, w, b: expand(x, 1, own, g, w, b, BF16), second, active_grad1, expand_weight, row(expand_bias)
    )
    gs_got = swap(gs1)
    act0, ge0, gs0, eb0 = line(
        lambda x, g, w, b: expand(x, 0, own, g, w, b, F32), second, active_grad0, expand_weight, row(expand_bias)
    )
    x_way, z_way = STAGES
    reduce_part = lambda *xs: reduce_grad_part(at, 0, *xs)
    expand_part = lambda *xs: expand_grad_part(at, 0, *xs)
    query_part = lambda *xs: heads_grad_part(at, 0, *xs)
    value_part = lambda *xs: values_grad_part(at, 1, *xs)

    r_send, r_stay = line(reduce_part, act0, act1, target0, target1)
    r_got = trade(r_send, x_way[0])

    def middle_back(gs0, gs_got, middle, target):
        norm, inverse = normalize(middle)
        grad_second = gs0 + gs_got.astype(F32)
        target = target.astype(F32)
        grad = target + norm_back(grad_second * second_gain, norm, inverse)
        sums = (jnp.sum(grad_second * norm, axis=0), jnp.sum(grad_second, axis=0), jnp.sum(target, axis=0))
        return grad, grad.astype(BF16), sums

    grad_middle, attended0, second_sums = line(middle_back, gs0, gs_got, middle, target0)
    attended1 = swap(attended0)
    grad_mix = lambda a, w: dot(a, w, 1, 1).astype(BF16)
    e_send, e_stay = line(expand_part, second, ge0, ge1)
    e_got = trade(e_send, x_way[0])
    grad_mixed0 = line(grad_mix, attended0, mixer_weight)
    r_out, r_stay = line(halve, r_stay, r_got)
    r_got = trade(r_out, x_way[1])
    grad_mixed1 = line(grad_mix, attended1, mixer_weight)

    half = width // 256
    inputs = (sp, projected0, projected1, grad_mixed0, grad_mixed1, mixed, logsum, rows)
    grad_projected, sums0 = line(lambda *xs: attend_backward(*xs, 0, half), *inputs)
    r_out, r_stay = line(halve, r_stay, r_got)
    e_out, e_stay = line(halve, e_stay, e_got)
    e_got = trade(tie(e_out, r_out), x_way[1])
    r_got = trade(r_out, x_way[2])
    grad_projected, sums1 = line(lambda *xs: attend_backward(*xs[:8], half, half, xs[8]), *inputs, grad_projected)
    r_stay = line(add_low, r_stay, r_got)
    r_got = trade(r_stay, x_way[3])
    e_out, e_stay = line(halve, e_stay, e_got)
    e_got = trade(e_out, x_way[2])
    q_send, q_stay = line(query_part, low0, low1, grad_projected)
    q_got = trade(q_send, x_way[0])
    v_send, v_stay = line(value_part, low0, low1, grad_projected, attended0, attended1, mixed)
    v_got = trade(v_send, z_way[0])
    first_part = lambda g, w: sum(dot(g[c], w[c], 1, 1) for c in range(3))
    first_part1 = line(lambda g, w: first_part(g[:, own:], w).astype(BF16), grad_projected, heads_weight)
    first_got = swap(first_part1)
    q_out, q_stay = line(halve, q_stay, q_got)
    q_got = trade(q_out, x_way[1])
    v_out, v_stay = line(halve, v_stay, v_got)
    v_got = trade(v_out, z_way[1])
    e_stay = line(add_low, e_stay, e_got)
    e_got = trade(e_stay, x_way[3])
    r_done = line(add_low, r_stay, r_got)
    r_next = trade(r_done, x_way[2])

    q_out, q_stay = line(halve, q_stay, q_got)
    q_got = trade(q_out, x_way[2])
    v_out, v_stay = line(halve, v_stay, v_got)
    v_got = trade(v_out, z_way[2])
    r_first = line(join, r_done, r_next)
    r_second = trade(r_first, x_way[1])
    reduced1 = line(lambda a, w: dot(a, w, 1, 0).astype(BF16), act1, reduce_weight)
    reduced_got = swap(reduced1)
    e_done = line(add_low, e_stay, e_got)
    e_next = trade(e_done, x_way[2])
    first_part0 = line(lambda g, w: first_part(g[:, :own], w), grad_projected, heads_weight)
    q_stay = line(add_low, q_stay, q_got)
    q_got = trade(q_stay, x_way[3])
    v_stay = line(add_low, v_stay, v_got)
    v_got = trade(v_stay, z_way[3])

    def first_back(part, got, tokens, grad_middle):
        grad = part + got.astype(F32)
        norm, inverse = normalize(tokens.astype(F32))
        out = (grad_middle + norm_back(grad * first_gain, norm, inverse)).astype(BF16)
        return out, (jnp.sum(grad * norm, axis=0), jnp.sum(grad, axis=0))

    tokens_grad, first_sums = line(first_back, first_part0, first_got, tokens, grad_middle)
    both = jnp.stack([*first_sums, *second_sums])
    both_got = swap(both)
    e_first = line(join, e_done, e_next)
    e_second = trade(e_first, x_way[1])
    r_third, r_fourth = trade(r_first, x_way[0]), trade(r_second, x_way[0])
    block_out = line(
        lambda m, a, w, r: (m + dot(a, w, 1, 0) + r.astype(F32) + reduce_bias).astype(BF16),
        middle, act0, reduce_weight, reduced_got,
    )
    bias_part = bias_grad(join(sums0, sums1), buckets)
    pack = line(
        lambda both, got, eb0, eb1, bias: jnp.concatenate(
            [(both + got).reshape(-1), (eb0 + eb1).reshape(-1), bias.reshape(-1)]
        ).reshape(-1, 128),
        both, both_got, eb0, eb1, bias_part,
    )
    pack_got = trade(pack, 1)
    q_done = line(add_low, q_stay, q_got)
    q_next = trade(q_done, x_way[2])
    v_done = line(add_low, v_stay, v_got)
    v_next = trade(v_done, z_way[2])
    pack = line(jnp.add, pack, pack_got)
    pack_got = trade(pack, 2)

    chunk = (hidden // 8, model)
    turned = (model, hidden // 8)
    (reduce_grad,) = line(
        lambda *xs: spread(
            at, 0, xs, put_rows, chunk, [lambda to: pl.BlockSpec(chunk, lambda g, s: (to(g, s), 0))],
            [jax.ShapeDtypeStruct(reduce_weight.shape, F32)], name="spread_reduce",
        ),
        r_first, r_second, r_third, r_fourth,
    )
    q_first = line(join, q_done, q_next)
    q_second = trade(q_first, x_way[1])
    v_first = line(join, v_done, v_next)
    v_second = trade(v_first, z_way[1])
    pack = line(jnp.add, pack, pack_got)
    pack_got = trade(pack, 4)
    e_third, e_fourth = trade(e_first, x_way[0]), trade(e_second, x_way[0])
    pack = line(jnp.add, pack, pack_got)
    pack_got = trade(pack, 8)
    (expand_grad,) = line(
        lambda *xs: spread(
            at, 0, xs, put_rows, turned, [lambda to: pl.BlockSpec(turned, lambda g, s: (0, to(g, s)))],
            [jax.ShapeDtypeStruct(expand_weight.shape, F32)], name="spread_expand",
        ),
        e_first, e_second, e_third, e_fourth,
    )
    pack = line(jnp.add, pack, pack_got).reshape(-1)
    both = pack[: 5 * model].reshape(5, model)
    expand_bias_grad = pack[5 * model : 5 * model + hidden]
    bias_part = pack[5 * model + hidden :].reshape(relative_bias.shape)
    q_third, q_fourth = trade(q_first, x_way[0]), trade(q_second, x_way[0])
    v_third, v_fourth = trade(v_first, z_way[0]), trade(v_second, z_way[0])
    heads_grad, mixer_grad = line(
        lambda *xs: spread_heads(at, xs[:4], xs[4:], model, width),
        q_first, q_second, q_third, q_fourth, v_first, v_second, v_third, v_fourth,
    )
    return (
        block_out, tokens_grad, both[0], both[1], heads_grad, bias_part, mixer_grad, both[2], both[3],
        expand_grad, expand_bias_grad, reduce_grad, both[4],
    )


def gathered(
    tokens, lengths, first_gain, first_shift, heads_weight, relative_bias, mixer_weight, second_gain,
    second_shift, expand_weight, expand_bias, reduce_weight, reduce_bias, cotangent,
):
    def gather(x):
        return lax.all_gather(x, "mp", axis=0, tiled=True)

    def scatter(x):
        return lax.psum_scatter(x.astype(BF16), "mp", scatter_dimension=0, tiled=True).astype(F32)

    members = lax.axis_size("mp")
    length = lengths[0]
    own = tokens.shape[0]
    whole = own * members
    half = whole // 2
    buckets = relative_bias.shape[1]
    sp = jnp.stack([jnp.zeros((), jnp.int32), length.astype(jnp.int32)])
    places = lax.axis_index("mp") * own + jnp.arange(own)
    rows = bias_rows(relative_bias)
    source_all = gather(tokens)
    first_all, projected = project(source_all, first_gain.reshape(1, -1), first_shift.reshape(1, -1), heads_weight)
    projected0, projected1 = projected[:, :half], projected[:, half:]
    mixed, logsum = attend_forward(sp, projected0, projected1, rows)
    source = tokens.astype(F32)
    middle = source + scatter(dot(mixed, mixer_weight, 1, 0))
    second_norm, second_inverse = normalize(middle)
    second_all = gather((second_norm * second_gain + second_shift).astype(BF16))
    target = keep_valid(cotangent, places, length)
    target_wide = target.astype(F32)
    target_all = gather(target)
    expanded = dot(second_all, expand_weight, 1, 0) + expand_bias
    active_low = jax.nn.gelu(expanded, approximate=True).astype(BF16)
    grad_expanded = gelu_back(expanded, dot(target_all, reduce_weight, 1, 1)).astype(BF16)
    grad_second = scatter(dot(grad_expanded, expand_weight, 1, 1))
    reduced = scatter(dot(active_low, reduce_weight, 1, 0))
    reduce_grad = dot(active_low, target_all, 0, 0)
    expand_grad = dot(second_all, grad_expanded, 0, 0)
    expand_bias_grad = jnp.sum(grad_expanded.astype(F32), axis=0)
    block_out = (middle + reduced + reduce_bias).astype(BF16)
    grad_middle = target_wide + norm_back(grad_second * second_gain, second_norm, second_inverse)
    attended_all = gather(grad_middle.astype(BF16))
    mixer_grad = dot(mixed, attended_all, 0, 0)
    grad_mixed = dot(attended_all, mixer_weight, 1, 1).astype(BF16)
    grad_projected, sums = attend_backward(
        sp, projected0, projected1, grad_mixed[:half], grad_mixed[half:], mixed, logsum, rows
    )
    bias_part = bias_grad(sums, buckets)
    heads_grad = jnp.einsum("td,cte->cde", first_all, grad_projected, preferred_element_type=F32)
    grad_first = scatter(jnp.einsum("cte,cde->td", grad_projected, heads_weight, preferred_element_type=F32))
    first_norm, first_inverse = normalize(source)
    tokens_grad = (
        grad_middle + norm_back(grad_first * first_gain, first_norm, first_inverse)
    ).astype(BF16)
    first_gain_grad, first_shift_grad, second_gain_grad, second_shift_grad, reduce_bias_grad = (
        lax.psum(
            (
                jnp.sum(grad_first * first_norm, axis=0),
                jnp.sum(grad_first, axis=0),
                jnp.sum(grad_second * second_norm, axis=0),
                jnp.sum(grad_second, axis=0),
                jnp.sum(target_wide, axis=0),
            ),
            ("dp", "mp"),
        )
    )
    heads_grad, bias_part, mixer_grad, expand_grad, expand_bias_grad, reduce_grad = (
        lax.psum(x.astype(BF16), "dp").astype(F32)
        for x in (heads_grad, bias_part, mixer_grad, expand_grad, expand_bias_grad, reduce_grad)
    )
    return (
        block_out, tokens_grad, first_gain_grad, first_shift_grad, heads_grad, bias_part, mixer_grad,
        second_gain_grad, second_shift_grad, expand_grad, expand_bias_grad, reduce_grad, reduce_bias_grad,
    )


def per_device(*args):
    if lax.axis_size("mp") == 2 and lax.axis_size("dp") == 16:
        return paired(*args)
    return gathered(*args)


def solution(mesh):
    return jax.shard_map(
        per_device,
        mesh=mesh,
        in_specs=(
            P(("dp", "mp"), None),
            P("dp"),
            P(),
            P(),
            P(None, None, "mp"),
            P("mp", None),
            P("mp", None),
            P(),
            P(),
            P(None, "mp"),
            P("mp"),
            P("mp", None),
            P(),
            P(("dp", "mp"), None),
        ),
        out_specs=(
            P(("dp", "mp"), None),
            P(("dp", "mp"), None),
            P(),
            P(),
            P(None, None, "mp"),
            P("mp", None),
            P("mp", None),
            P(),
            P(),
            P(None, "mp"),
            P("mp"),
            P("mp", None),
            P(),
        ),
        check_vma=False,
    )
```

```python
import functools
import math

import jax
import jax.numpy as jnp
import numpy as np
from jax import lax
from jax.experimental import pallas as pl
from jax.experimental.pallas import tpu as pltpu
from jax.sharding import PartitionSpec as P

EPS = 1e-05
DH=64; MAXDIST=128; NEG=-1e30; BLK=256
F32=jnp.float32; BF16=jnp.bfloat16
HIGHEST=lax.Precision.HIGHEST

def bucket_table(count, buckets, reach):
    exact = buckets // 2
    entries = []
    for position in range(count):
        if position < exact:
            entries.append(position)
        else:
            level = exact + int(math.log(position / exact) / math.log(reach / exact) * (buckets - exact))
            entries.append(min(buckets - 1, level))
    return np.array(entries, dtype=np.int32)

def bias_tables(buckets):
    W=2*BLK
    tab=bucket_table(W,buckets,MAXDIST)
    oh=np.zeros((buckets,4,W),np.float32); neg=np.zeros((1,4,W),np.float32)
    for y in range(W):
        x = y if y < BLK else y-W
        if x<=0 and -x<BLK: oh[tab[-x],0,y]=1
        else: neg[0,0,y]=NEG
        d=BLK-x
        if 0<=d<W: oh[tab[d],1,y]=1
        if 0<=x: oh[tab[x],2,y]=1
        else: neg[0,2,y]=NEG
        d=BLK+x
        if 0<=d<W: oh[tab[d],3,y]=1
    return oh.reshape(buckets,4*W), neg.reshape(1,4*W)

def bias_rows(relative_bias):
    heads,buckets=relative_bias.shape
    oh,neg=bias_tables(buckets)
    rel=relative_bias-relative_bias[:,buckets-1:]
    rows=jnp.dot(rel,jnp.asarray(oh),precision=HIGHEST)+jnp.asarray(neg)
    return rows.reshape(heads//2,2,4*2*BLK)

def toeplitz(row):
    wide=jnp.broadcast_to(row,(BLK,2*BLK))
    return pltpu.roll(wide,0,1,stride=1,stride_axis=0)[:,:BLK]


def lane_masks():
    lane=lax.broadcasted_iota(jnp.int32,(1,128),1)
    head=[(lane//DH)==h for h in range(2)]
    mine=[jnp.where(m,1.0,0.0).astype(BF16) for m in head]
    spare=[jnp.where(lane==DH*(1-h),1.0,0.0) for h in range(2)]
    return head,mine,spare


def gone_rows(start,half,length,spare):
    pos=lax.broadcasted_iota(jnp.int32,(half,1),0)+start
    gone=jnp.where(pos<length,0.0,NEG)
    return [(gone*s).astype(BF16) for s in spare]


def fwd_kernel(sp, a_ref,c_ref,b_ref,o_ref,lse_ref,qs,ks,vs):
    half=a_ref.shape[1]; T=2*half; flip=sp[0]; length=sp[1]
    W=2*BLK
    head,mine,spare=lane_masks()
    for a,ref in enumerate((a_ref,c_ref)):
        start=pl.multiple_of((a^flip)*half,half)
        dst=pl.ds(start,half)
        gone=gone_rows(start,half,length,spare)
        for h in range(2):
            qs[h,dst,:]=ref[0]*(mine[h]*jnp.asarray(DH**-0.5,BF16))+spare[h].astype(BF16)
            ks[h,dst,:]=ref[1]*mine[h]+gone[h]
            vs[h,dst,:]=ref[2]*mine[h]+mine[1-h]
    tiles=[(toeplitz(b_ref[0,h:h+1,0:W]),toeplitz(b_ref[0,h:h+1,W:2*W])) for h in range(2)]
    outs={}

    def score(i,h):
        return dot(qs[h,i*BLK:(i+1)*BLK,:],ks[h,:(i+1)*BLK,:],1,1)

    def finish(i,h,s):
        kc=(i+1)*BLK; t0,t1=tiles[h]
        parts=[]
        if i>=2: parts.append(s[:,:kc-2*BLK])
        if i>=1: parts.append(s[:,kc-2*BLK:kc-BLK]+t1)
        parts.append(s[:,kc-BLK:]+t0)
        top=functools.reduce(jnp.maximum,[jnp.max(x,axis=1,keepdims=True) for x in parts])
        p=jnp.concatenate([jnp.exp(x-top).astype(BF16) for x in parts],axis=1)
        o=dot(p,vs[h,:kc,:],1,0)
        total=o[:,DH*(1-h):DH*(1-h)+1]
        outs[h]=(o*(1.0/total),top+jnp.log(total))
        if h==1:
            rows=pl.ds(pl.multiple_of((i*BLK+flip*half)%T,BLK),BLK)
            o_ref[rows,:]=jnp.where(head[0],outs[0][0],outs[1][0]).astype(BF16)
            lse_ref[0,i*BLK:kc,:]=jnp.where(head[0],outs[0][1],outs[1][1])

    run_ahead([(i,h) for i in range(T//BLK) for h in range(2)],score,finish,2)


def run_ahead(items,first,second,depth):
    waiting=[]
    for item in items:
        waiting.append((item,first(*item)))
        if len(waiting)>depth:
            done,value=waiting.pop(0)
            second(*done,value)
    for done,value in waiting:
        second(*done,value)


def attend_forward(sp,projected0,projected1,rows):
    _,half,HD=projected0.shape; pairs=HD//128; T=2*half
    part=pl.BlockSpec((3,half,128),lambda p,s:(0,0,p))
    return pl.pallas_call(
        fwd_kernel,
        grid_spec=pltpu.PrefetchScalarGridSpec(
            num_scalar_prefetch=1,grid=(pairs,),
            in_specs=[part,part,pl.BlockSpec((1,2,rows.shape[2]),lambda p,s:(p,0,0))],
            out_specs=[pl.BlockSpec((T,128),lambda p,s:(0,p)),pl.BlockSpec((1,T,128),lambda p,s:(p,0,0))],
            scratch_shapes=[pltpu.VMEM((2,T,128),BF16)]*3),
        out_shape=[jax.ShapeDtypeStruct((T,HD),BF16),jax.ShapeDtypeStruct((pairs,T,128),F32)],
        cost_estimate=cost(8*T*T*HD,8*T*HD+512*pairs*T),
        name="attend_forward",
    )(sp,projected0,projected1,rows)

def diagonal_sums(acc, offset):
    W=2*BLK
    wide=jnp.concatenate([acc,jnp.zeros_like(acc)],axis=1)
    n=BLK
    while n>1:
        n//=2
        top=wide[:n]; bottom=wide[n:2*n]
        wide=top+pltpu.roll(bottom,W-n,1)
    return pltpu.roll(wide,offset,1) if offset else wide

def bwd_kernel(sp, a_ref,c_ref,d0_ref,d1_ref,o_ref,lse_ref,b_ref,g_ref,d_ref,qs,ks,vs,dos,dq,acc0,acc1):
    half=a_ref.shape[1]; T=2*half; flip=sp[0]; length=sp[1]
    W=2*BLK
    n=T//BLK
    head,mine,spare=lane_masks()
    stats=[None,None]
    one=sum(spare).astype(BF16)
    for a,(ref,do_ref) in enumerate(((a_ref,d0_ref),(c_ref,d1_ref))):
        start=pl.multiple_of((a^flip)*half,half)
        dst=pl.ds(start,half)
        gone=gone_rows(start,half,length,spare)
        for h in range(2):
            qs[h,dst,:]=ref[0]*(mine[h]*jnp.asarray(DH**-0.5,BF16))+spare[h].astype(BF16)
            ks[h,dst,:]=ref[1]*mine[h]+gone[h]
            vs[h,dst,:]=ref[2]*mine[h]
        dos[dst,:]=do_ref[...]
        acc0[0,dst,:]=do_ref[...].astype(F32)*o_ref[a*half:(a+1)*half,:].astype(F32)
    turned=acc0[0].T
    deltas=[jnp.sum(turned[h*DH:(h+1)*DH],axis=0,keepdims=True) for h in range(2)]
    turned=lse_ref[0].T
    lses=[turned[h*DH:h*DH+1] for h in range(2)]
    near=acc1
    tiles=[(toeplitz(b_ref[0,h:h+1,2*W:3*W]),toeplitz(b_ref[0,h:h+1,3*W:])) for h in range(2)]

    def products(j,h):
        rj=slice(j*BLK,(j+1)*BLK)
        return dot(ks[h,rj,:],qs[h,j*BLK:,:],1,1),dot(vs[h,rj,:],dos[j*BLK:,:],1,1)

    keep={}

    def finish(j,h,value):
        s,dp=value
        rj=slice(j*BLK,(j+1)*BLK)
        ps=[];dss=[]
        for b in range(n-j):
            c=slice(b*BLK,(b+1)*BLK)
            cc=slice((j+b)*BLK,(j+b+1)*BLK)
            x=s[:,c]-lses[h][:,cc]
            if b<2: x=x+tiles[h][b]
            p=jnp.exp(x)
            ds=p*(dp[:,c]-deltas[h][:,cc])
            if b<2:
                if j==0: near[h,b]=ds
                else: near[h,b]+=ds
            ps.append(p.astype(BF16)); dss.append(ds.astype(BF16))
        p=jnp.concatenate(ps,axis=1); ds=jnp.concatenate(dss,axis=1)
        dv=dot(p,dos[j*BLK:,:],1,0)
        dk=dot(ds,qs[h,j*BLK:,:],1,0)
        kk=ks[h,rj,:]*mine[h]+mine[1-h]
        dqj=dot(ds,kk,0,0)
        if j==0: dq[h,:,:]=dqj
        else: dq[h,j*BLK:,:]+=dqj
        keep[h]=(dk,dv)
        if h==1:
            rows=pl.ds(pl.multiple_of((j*BLK+flip*half)%T,BLK),BLK)
            g_ref[1,rows,:]=jnp.where(head[0],keep[0][0],keep[1][0]).astype(BF16)
            g_ref[2,rows,:]=jnp.where(head[0],keep[0][1],keep[1][1]).astype(BF16)

    run_ahead([(j,h) for j in range(n) for h in range(2)],products,finish,1)
    for h in range(2):
        d_ref[0,h:h+1,:]=diagonal_sums(near[h,0],0)+diagonal_sums(near[h,1],BLK)
        total=jnp.sum(dq[h,:,:],axis=0,keepdims=True)[:,DH*(1-h):DH*(1-h)+1]
        d_ref[0,2+h:3+h,:]=jnp.broadcast_to(total,(1,W))
    for a in range(2):
        dst=pl.ds(pl.multiple_of((a^flip)*half,half),half)
        g_ref[0,a*half:(a+1)*half,:]=(jnp.where(head[0],dq[0,dst,:],dq[1,dst,:])*DH**-0.5).astype(BF16)

def attend_backward(sp,projected0,projected1,grad0,grad1,mixed,lse,rows,start=0,count=None,given=None):
    _,half,HD=projected0.shape; pairs=HD//128; T=2*half
    count=pairs if count is None else count
    part=pl.BlockSpec((3,half,128),lambda p,s:(0,0,p+start))
    grad=pl.BlockSpec((half,128),lambda p,s:(0,p+start))
    in_specs=[part,part,grad,grad,pl.BlockSpec((T,128),lambda p,s:(0,p+start)),
              pl.BlockSpec((1,T,128),lambda p,s:(p+start,0,0)),pl.BlockSpec((1,2,rows.shape[2]),lambda p,s:(p+start,0,0))]
    args=[sp,projected0,projected1,grad0,grad1,mixed,lse,rows]
    kernel=bwd_kernel
    if given is not None:
        in_specs.append(pl.BlockSpec(memory_space=pl.ANY)); args.append(given)
        kernel=lambda *refs: bwd_kernel(*refs[:8],*refs[9:])
    return pl.pallas_call(
        kernel,
        grid_spec=pltpu.PrefetchScalarGridSpec(
            num_scalar_prefetch=1,grid=(count,),
            in_specs=in_specs,
            out_specs=[pl.BlockSpec((3,T,128),lambda p,s:(0,0,p+start)),pl.BlockSpec((1,4,2*BLK),lambda p,s:(p,0,0))],
            scratch_shapes=[pltpu.VMEM((2,T,128),BF16)]*3+[pltpu.VMEM((T,128),BF16),pltpu.VMEM((2,T,128),F32),pltpu.VMEM((1,T,128),F32),pltpu.VMEM((2,2,BLK,BLK),F32)]),
        out_shape=[jax.ShapeDtypeStruct((3,T,HD),BF16),jax.ShapeDtypeStruct((count,4,2*BLK),F32)],
        input_output_aliases={} if given is None else {8:0},
        cost_estimate=cost(20*T*T*128*count,(16*T*128+512*T)*count),
        name="attend_backward",
    )(*args)

def bias_grad(sums, buckets):
    pairs=sums.shape[0]; W=2*BLK
    tab=bucket_table(W,buckets,MAXDIST)
    assert tab[BLK]==buckets-1
    m=np.zeros((W,buckets),np.float32)
    for d in range(W):
        if tab[d]<buckets-1:
            m[d,tab[d]]=1; m[d,buckets-1]=-1
    near=sums[:,0:2].reshape(pairs*2,W); total=sums[:,2:4,0].reshape(pairs*2,1)
    last=np.zeros((1,buckets),np.float32); last[0,-1]=1
    return jnp.dot(near,jnp.asarray(m),precision=HIGHEST)+total*jnp.asarray(last)


HALF_TANH = math.sqrt(2.0 / math.pi)


def dot(a, b, ca, cb):
    return lax.dot_general(a, b, (((ca,), (cb,)), ((), ())), preferred_element_type=F32)


def fixed(shape):
    return pl.BlockSpec(shape, lambda *_: (0,) * len(shape))


def cost(flops, moved):
    return pl.CostEstimate(flops=int(flops), transcendentals=0, bytes_accessed=int(moved))


def row_norm(values):
    center = jnp.mean(values, axis=-1, keepdims=True)
    centered = values - center
    inverse = lax.rsqrt(jnp.mean(centered * centered, axis=-1, keepdims=True) + EPS)
    return centered * inverse, inverse


def project_kernel(x_ref, gain_ref, shift_ref, w_ref, low_ref, out_ref):
    normed, _ = row_norm(x_ref[...].astype(F32))
    low = (normed * gain_ref[...] + shift_ref[...]).astype(BF16)
    low_ref[...] = low
    for c in range(3):
        out_ref[c] = dot(low, w_ref[c], 1, 0).astype(BF16)


def project(x, gain, shift, weight):
    rows, model = x.shape
    width = weight.shape[2]
    step = min(256, rows)
    return pl.pallas_call(
        project_kernel,
        grid=(rows // step,),
        in_specs=[pl.BlockSpec((step, model), lambda i: (i, 0)), fixed((1, model)), fixed((1, model)), fixed(weight.shape)],
        out_specs=[pl.BlockSpec((step, model), lambda i: (i, 0)), pl.BlockSpec((3, step, width), lambda i: (0, i, 0))],
        out_shape=[jax.ShapeDtypeStruct((rows, model), BF16), jax.ShapeDtypeStruct((3, rows, width), BF16)],
        cost_estimate=cost(6 * rows * model * width, 2 * (2 * rows * model + weight.size + 3 * rows * width)),
        name="project",
    )(x, gain, shift, weight)


def mix_kernel(own_blocks, x0_ref, x1_ref, m_ref, p_ref, w0_ref, w1_ref, gain_ref, shift_ref, mid_ref, low_ref):
    i = pl.program_id(0)
    attended = dot(m_ref[...], w0_ref[...], 1, 0) + dot(p_ref[...], w1_ref[...], 1, 0)

    def rows(x_ref):
        return x_ref[...].astype(F32) + attended

    def rest(middle):
        normed, _ = row_norm(middle)
        low_ref[...] = (normed * gain_ref[...] + shift_ref[...]).astype(BF16)

    @pl.when(i < own_blocks)
    def _():
        middle = rows(x0_ref)
        mid_ref[...] = middle
        rest(middle)

    @pl.when(i >= own_blocks)
    def _():
        rest(rows(x1_ref))


def mix(tokens, other, mixed, mixed_other, weight, weight_other, gain, shift):
    own, model = tokens.shape
    width = mixed.shape[1]
    step = 256
    n = own // step
    return pl.pallas_call(
        functools.partial(mix_kernel, n),
        grid=(2 * n,),
        in_specs=[
            pl.BlockSpec((step, model), lambda i: (jnp.minimum(i, n - 1), 0)),
            pl.BlockSpec((step, model), lambda i: (jnp.maximum(i - n, 0), 0)),
            pl.BlockSpec((step, width), lambda i: (i, 0)),
            pl.BlockSpec((step, width), lambda i: ((i + n) % (2 * n), 0)),
            fixed(weight.shape), fixed(weight.shape), fixed((1, model)), fixed((1, model)),
        ],
        out_specs=[
            pl.BlockSpec((step, model), lambda i: (jnp.minimum(i, n - 1), 0)),
            pl.BlockSpec((step, model), lambda i: (i, 0)),
        ],
        out_shape=[jax.ShapeDtypeStruct((own, model), F32), jax.ShapeDtypeStruct((2 * own, model), BF16)],
        cost_estimate=cost(8 * own * model * width, 2 * (4 * own * model + 4 * own * width + 2 * weight.size) + 4 * own * model),
        name="mix",
    )(tokens, other, mixed, mixed_other, weight, weight_other, gain, shift)


def expand_kernel(x_ref, g_ref, w_ref, b_ref, act_ref, ge_ref, gs_ref, bias_ref, acc_ref):
    i = pl.program_id(0)
    x = x_ref[...]
    width = w_ref.shape[1]
    sub = 256
    total = None
    for s in range(width // sub):
        cols = slice(s * sub, (s + 1) * sub)
        u = dot(x, w_ref[:, cols], 1, 0) + b_ref[:, cols].astype(F32)
        square = u * u
        t = jnp.tanh(HALF_TANH * u * (1.0 + 0.044715 * square))
        half = 0.5 + 0.5 * t
        act_ref[:, cols] = (u * half).astype(BF16)
        slope = half + 0.5 * u * (1.0 - t * t) * (HALF_TANH * (1.0 + 3 * 0.044715 * square))
        grad = g_ref[:, cols].astype(F32) * slope
        low = grad.astype(BF16)
        ge_ref[:, cols] = low
        bias_ref[:, cols] = jnp.sum(grad, axis=0, keepdims=True)
        part = dot(low, w_ref[:, cols], 1, 1)
        total = part if total is None else total + part

    @pl.when(i == 0)
    def _():
        acc_ref[...] = total

    @pl.when(i > 0)
    def _():
        acc_ref[...] += total

    @pl.when(i == pl.num_programs(0) - 1)
    def _():
        gs_ref[...] = acc_ref[...].astype(gs_ref.dtype)


def expand(x, block, rows, grad_active, weight, bias, dtype):
    model = x.shape[1]
    hidden = weight.shape[1]
    step = min(512, hidden)
    return pl.pallas_call(
        expand_kernel,
        grid=(hidden // step,),
        in_specs=[
            pl.BlockSpec((rows, model), lambda i: (block, 0)),
            pl.BlockSpec((rows, step), lambda i: (0, i)),
            pl.BlockSpec((model, step), lambda i: (0, i)),
            pl.BlockSpec((1, step), lambda i: (0, i)),
        ],
        out_specs=[
            pl.BlockSpec((rows, step), lambda i: (0, i)),
            pl.BlockSpec((rows, step), lambda i: (0, i)),
            fixed((rows, model)),
            pl.BlockSpec((1, step), lambda i: (0, i)),
        ],
        out_shape=[
            jax.ShapeDtypeStruct((rows, hidden), BF16),
            jax.ShapeDtypeStruct((rows, hidden), BF16),
            jax.ShapeDtypeStruct((rows, model), dtype),
            jax.ShapeDtypeStruct((1, hidden), F32),
        ],
        scratch_shapes=[pltpu.VMEM((rows, model), F32)],
        cost_estimate=cost(4 * rows * model * hidden, 2 * (2 * rows * model + 3 * rows * hidden + weight.size)),
        name="expand",
    )(x, grad_active, weight, bias)


STAGES = ((1, 2, 4, 8), (1, 4, 2, 8))


def place_of(index, stages):
    bit = [(index // s) % 2 for s in stages]
    return bit[0] * 4 + bit[1] * 2 + bit[2]


def trade(x, bit):
    size = lax.axis_size("dp")
    return lax.ppermute(x, "dp", [(i, i ^ bit) for i in range(size)])


def add_low(a, b):
    return (a.astype(F32) + b.astype(F32)).astype(BF16)


def pair_of(g, s, slot):
    return (3 - g) ^ (s[slot] // 2)


def put_pair(slot, s_ref, chunks, outs):
    flip = s_ref[slot] % 2
    sent = pl.program_id(0) < 2
    for j, value in enumerate(chunks):
        value = value.astype(BF16)[None]
        for out, here in zip(outs, (sent, jnp.logical_not(sent))):
            @pl.when(here)
            def _(out=out):
                out[pl.ds(j ^ flip, 1)] = value


def pair_call(kernel, slot, s, arrays, specs, tail, flops, name):
    zeros = (0,) * len(tail)
    moved = sum(2 * x.size for x in arrays) + 16 * math.prod(tail)
    return pl.pallas_call(
        functools.partial(kernel, slot),
        grid_spec=pltpu.PrefetchScalarGridSpec(
            num_scalar_prefetch=1, grid=(4,), in_specs=specs,
            out_specs=[
                pl.BlockSpec((2, *tail), lambda g, s: (jnp.maximum(1 - g, 0), *zeros)),
                pl.BlockSpec((2, *tail), lambda g, s: (jnp.minimum(3 - g, 1), *zeros)),
            ],
        ),
        out_shape=[jax.ShapeDtypeStruct((4, *tail), BF16)] * 2,
        cost_estimate=cost(flops, moved),
        name=name,
    )(s, *arrays)


def reduce_grad_kernel(slot, s_ref, *refs):
    (a0, a1, t0, t1), outs = refs[:4], refs[4:]
    value = dot(a0[...], t0[...], 0, 0) + dot(a1[...], t1[...], 0, 0)
    width = value.shape[0] // 2
    put_pair(slot, s_ref, [value[:width], value[width:]], outs)


def reduce_grad_part(s, slot, act0, act1, t0, t1):
    rows, hidden = act0.shape
    model = t0.shape[1]
    block = pl.BlockSpec((rows, hidden // 4), lambda g, s: (0, pair_of(g, s, slot)))
    return pair_call(
        reduce_grad_kernel, slot, s, (act0, act1, t0, t1), [block, block, fixed(t0.shape), fixed(t1.shape)],
        (hidden // 8, model), 4 * rows * model * hidden, "reduce_grad",
    )


def expand_grad_kernel(slot, s_ref, *refs):
    (x, g0, g1), outs = refs[:3], refs[3:]
    rows = g0.shape[0]
    value = dot(x[:rows], g0[...], 0, 0) + dot(x[rows:], g1[...], 0, 0)
    width = value.shape[1] // 2
    put_pair(slot, s_ref, [value[:, :width], value[:, width:]], outs)


def expand_grad_part(s, slot, x, g0, g1):
    rows, hidden = g0.shape
    model = x.shape[1]
    block = pl.BlockSpec((rows, hidden // 4), lambda g, s: (0, pair_of(g, s, slot)))
    return pair_call(
        expand_grad_kernel, slot, s, (x, g0, g1), [fixed(x.shape), block, block],
        (model, hidden // 8), 4 * rows * model * hidden, "expand_grad",
    )


def heads_grad_kernel(slot, s_ref, *refs):
    (l0, l1, g), outs = refs[:3], refs[3:]
    rows = l0.shape[0]
    both = [dot(l0[...], g[c, :rows], 0, 0) + dot(l1[...], g[c, rows:], 0, 0) for c in range(2)]
    width = both[0].shape[0] // 2
    chunks = [jnp.stack([v[j * width:(j + 1) * width] for v in both]) for j in range(2)]
    put_pair(slot, s_ref, chunks, outs)


def heads_grad_part(s, slot, low0, low1, grad):
    rows, model = low0.shape
    width = grad.shape[2]
    block = pl.BlockSpec((rows, model // 4), lambda g, s: (0, pair_of(g, s, slot)))
    return pair_call(
        heads_grad_kernel, slot, s, (low0, low1, grad),
        [block, block, pl.BlockSpec((2, 2 * rows, width), lambda g, s: (0, 0, 0))],
        (2, model // 8, width), 8 * rows * model * width, "heads_grad",
    )


def values_grad_kernel(slot, s_ref, *refs):
    (l0, l1, g, a0, a1, m), outs = refs[:6], refs[6:]
    rows = l0.shape[0]
    both = [
        dot(l0[...], g[0, :rows], 0, 0) + dot(l1[...], g[0, rows:], 0, 0),
        dot(a0[...], m[:rows], 0, 0) + dot(a1[...], m[rows:], 0, 0),
    ]
    width = both[0].shape[0] // 2
    chunks = [jnp.stack([v[j * width:(j + 1) * width] for v in both]) for j in range(2)]
    put_pair(slot, s_ref, chunks, outs)


def values_grad_part(s, slot, low0, low1, grad, att0, att1, mixed):
    rows, model = low0.shape
    width = grad.shape[2]
    block = pl.BlockSpec((rows, model // 4), lambda g, s: (0, pair_of(g, s, slot)))
    return pair_call(
        values_grad_kernel, slot, s, (low0, low1, grad, att0, att1, mixed),
        [block, block, pl.BlockSpec((1, 2 * rows, width), lambda g, s: (2, 0, 0)), block, block, fixed(mixed.shape)],
        (2, model // 8, width), 8 * rows * model * width, "values_grad",
    )


def spread_kernel(put, s_ref, *refs):
    g = pl.program_id(0)
    pieces, outs = refs[-4 - put.outs:-put.outs], refs[-put.outs:]
    for a in range(4):
        @pl.when(g // 2 == a)
        def _(a=a):
            put(pieces[a], outs)


def spread(places, slot, pieces, put, tail, out_specs, out_shape, given=None, name=None):
    zeros = (0,) * len(tail)
    at = lambda g, s: g ^ s[slot]
    in_specs = [
        pl.BlockSpec((1, *tail), lambda g, s, a=a: (jnp.clip(g - 2 * a, 0, 1), *zeros)) for a in range(4)
    ]
    args = list(pieces)
    aliases = {}
    if given is not None:
        in_specs.insert(0, pl.BlockSpec(memory_space=pl.ANY))
        args.insert(0, given)
        aliases = {1: 0}
    return pl.pallas_call(
        functools.partial(spread_kernel, put),
        grid_spec=pltpu.PrefetchScalarGridSpec(
            num_scalar_prefetch=1, grid=(8,), in_specs=in_specs, out_specs=[spec(at) for spec in out_specs],
        ),
        out_shape=out_shape,
        input_output_aliases=aliases,
        cost_estimate=cost(0, 6 * 8 * math.prod(tail)),
        name=name,
    )(places, *args)


def put_rows(piece, outs):
    outs[0][...] = piece[0].astype(F32)


put_rows.outs = 1


def spread_heads_kernel(value_slot, s_ref, *refs):
    k = pl.program_id(0)
    heads_ref, mixer_ref = refs[8:]
    for slot in range(2):
        r = k ^ s_ref[slot * value_slot]
        for a in range(4):
            piece = refs[4 * slot + a]

            @pl.when(r // 2 == a)
            def _(slot=slot, piece=piece):
                if slot == 0:
                    heads_ref[:2] = piece[0].astype(F32)
                else:
                    heads_ref[2] = piece[0, 0].astype(F32)
                    mixer_ref[...] = piece[0, 1].astype(F32).T


def spread_heads(places, value_slot, queries, values, model, width):
    tail = (2, model // 8, width)

    def spec(slot, a):
        def at(k, s):
            r = k ^ s[slot]
            return (jnp.where(r // 2 == a, r % 2, 0), 0, 0, 0)

        return pl.BlockSpec((1, *tail), at)

    return pl.pallas_call(
        functools.partial(spread_heads_kernel, value_slot),
        grid_spec=pltpu.PrefetchScalarGridSpec(
            num_scalar_prefetch=1, grid=(8,),
            in_specs=[spec(slot * value_slot, a) for slot in range(2) for a in range(4)],
            out_specs=[
                pl.BlockSpec((3, model // 8, width), lambda k, s: (0, k, 0)),
                pl.BlockSpec((width, model // 8), lambda k, s: (0, k)),
            ],
        ),
        out_shape=[jax.ShapeDtypeStruct((3, model, width), F32), jax.ShapeDtypeStruct((width, model), F32)],
        cost_estimate=cost(0, 12 * 8 * math.prod(tail)),
        name="spread_heads",
    )(places, *queries, *values)


def normalize(values):
    return row_norm(values)


def norm_back(grad_norm, normed, inverse):
    return inverse * (
        grad_norm
        - jnp.mean(grad_norm, axis=-1, keepdims=True)
        - normed * jnp.mean(grad_norm * normed, axis=-1, keepdims=True)
    )


def gelu_back(expanded, grad_active):
    pull = jax.vjp(lambda value: jax.nn.gelu(value, approximate=True), expanded)[1]
    return pull(grad_active)[0]


def swap(x):
    return lax.ppermute(x, "mp", [(0, 1), (1, 0)])


def keep_valid(x, places, length):
    return jnp.where((places < length)[:, None], x, jnp.zeros_like(x))


def tie(x, *others):
    return lax.optimization_barrier((x, *others))[0]


class Line:
    def __init__(self):
        self.last = None

    def __call__(self, step, *args):
        if self.last is not None:
            args, _ = lax.optimization_barrier((args, self.last))
        out = step(*args)
        self.last = jax.tree.leaves(out)
        return out


def halve(stay, got):
    n = stay.shape[0] // 2
    return add_low(stay[n:], got[n:]), add_low(stay[:n], got[:n])


def join(a, b):
    return jnp.concatenate([a, b], axis=0)


class Sum:
    def __init__(self, line, stages):
        self.line, self.stages = line, stages

    def begin(self, send, stay):
        self.stay, self.got = stay, trade(send, self.stages[0])

    def first(self, *after):
        out, self.stay = self.line(halve, self.stay, self.got)
        self.got = trade(tie(out, *after) if after else out, self.stages[1])

    def second(self):
        out, self.stay = self.line(halve, self.stay, self.got)
        self.got = trade(out, self.stages[2])

    def third(self):
        self.stay = self.line(add_low, self.stay, self.got)
        self.got = trade(self.stay, self.stages[3])

    def fourth(self):
        self.done = self.line(add_low, self.stay, self.got)
        self.got = trade(self.done, self.stages[2])

    def fifth(self):
        self.near = self.line(join, self.done, self.got)
        self.far = trade(self.near, self.stages[1])
        self.near_other = trade(self.near, self.stages[0])

    def sixth(self):
        self.far_other = trade(tie(self.far, self.line.last), self.stages[0])

    def pieces(self):
        return self.near, self.far, self.near_other, self.far_other


class Held:
    pass


def paired(
    tokens, lengths, first_gain, first_shift, heads_weight, relative_bias, mixer_weight, second_gain,
    second_shift, expand_weight, expand_bias, reduce_weight, reduce_bias, cotangent,
):
    member = lax.axis_index("mp")
    index = lax.axis_index("dp")
    core = index % 2
    length = lengths[0]
    own, model = tokens.shape
    buckets = relative_bias.shape[1]
    width = heads_weight.shape[2]
    hidden = expand_bias.shape[0]
    sp = jnp.stack([member.astype(jnp.int32), length.astype(jnp.int32)])
    at = jnp.stack([place_of(index, s).astype(jnp.int32) for s in STAGES])
    places = member * own + jnp.arange(own)
    places_other = (1 - member) * own + jnp.arange(own)
    row = lambda v: v.reshape(1, -1)
    line = Line()
    v = Held()
    reduce_sum, expand_sum = Sum(line, STAGES[0]), Sum(line, STAGES[0])
    query_sum, value_sum = Sum(line, STAGES[0]), Sum(line, STAGES[0])

    rows = bias_rows(relative_bias)
    target0 = keep_valid(cotangent, places, length)
    other = swap(tokens)

    def project_own():
        v.low0, v.projected0 = line(project, tokens, row(first_gain), row(first_shift), heads_weight)

    def project_other():
        v.low1, v.projected1 = line(project, other, row(first_gain), row(first_shift), heads_weight)

    active_grad = lambda t, w: dot(t, w, 1, 1).astype(BF16)

    def active_own():
        v.active_grad0 = line(active_grad, target0, reduce_weight)

    def send_more():
        n = width // 2
        half = lax.dynamic_slice_in_dim(mixer_weight, core * n, n, 0)
        ready = line.last
        v.cotangent_other = swap(tie(cotangent, other, *ready))
        v.mixer_half = swap(tie(half, other, *ready))

    def attend():
        v.mixed, v.logsum = line(attend_forward, sp, v.projected0, v.projected1, rows)
        v.mixed_other = swap(v.mixed)

    def active_other():
        v.target1 = line(lambda x: keep_valid(x, places_other, length), v.cotangent_other)
        v.active_grad1 = line(active_grad, v.target1, reduce_weight)

    def mixer_rest():
        v.mixer_rest = trade(tie(v.mixer_half, *line.last), 1)

    def mixer_both():
        a, b = v.mixer_half, v.mixer_rest
        v.mixer_other = line(lambda a, b: jnp.where(core == 0, join(a, b), join(b, a)), a, b)

    def mix_rows():
        v.middle, v.second = line(
            mix, tokens, other, v.mixed, v.mixed_other, mixer_weight, v.mixer_other,
            row(second_gain), row(second_shift),
        )

    def expand_other():
        v.act1, v.ge1, gs1, v.eb1 = line(
            lambda x, g, w, b: expand(x, 1, own, g, w, b, BF16),
            v.second, v.active_grad1, expand_weight, row(expand_bias),
        )
        v.gs_got = swap(gs1)

    def expand_own():
        v.act0, v.ge0, v.gs0, v.eb0 = line(
            lambda x, g, w, b: expand(x, 0, own, g, w, b, F32),
            v.second, v.active_grad0, expand_weight, row(expand_bias),
        )

    def reduce_chunks():
        reduce_sum.begin(*line(
            lambda *xs: reduce_grad_part(at, 0, *xs), v.act0, v.act1, target0, v.target1
        ))

    def expand_chunks():
        expand_sum.begin(*line(lambda *xs: expand_grad_part(at, 0, *xs), v.second, v.ge0, v.ge1))

    def back(gs0, gs_got, middle, target):
        norm, inverse = normalize(middle)
        grad_second = gs0 + gs_got.astype(F32)
        target = target.astype(F32)
        grad = target + norm_back(grad_second * second_gain, norm, inverse)
        sums = (jnp.sum(grad_second * norm, axis=0), jnp.sum(grad_second, axis=0), jnp.sum(target, axis=0))
        return grad, grad.astype(BF16), sums

    def middle_back():
        v.grad_middle, v.attended0, v.second_sums = line(back, v.gs0, v.gs_got, v.middle, target0)
        v.attended1 = swap(v.attended0)

    grad_mix = lambda a, w: dot(a, w, 1, 1).astype(BF16)

    def mixed_own():
        v.grad_mixed0 = line(grad_mix, v.attended0, mixer_weight)

    def mixed_other():
        v.grad_mixed1 = line(grad_mix, v.attended1, mixer_weight)

    def reduced_other():
        out = line(lambda a, w: dot(a, w, 1, 0).astype(BF16), v.act1, reduce_weight)
        v.reduced_got = swap(out)

    def attend_back():
        v.grad_projected, v.sums = line(
            attend_backward, sp, v.projected0, v.projected1, v.grad_mixed0, v.grad_mixed1,
            v.mixed, v.logsum, rows,
        )

    def query_chunks():
        query_sum.begin(*line(lambda *xs: heads_grad_part(at, 0, *xs), v.low0, v.low1, v.grad_projected))

    def value_chunks():
        value_sum.begin(*line(
            lambda *xs: values_grad_part(at, 0, *xs), v.low0, v.low1, v.grad_projected,
            v.attended0, v.attended1, v.mixed,
        ))

    first_part = lambda g, w: sum(dot(g[c], w[c], 1, 1) for c in range(3))

    def first_other():
        out = line(lambda g, w: first_part(g[:, own:], w).astype(BF16), v.grad_projected, heads_weight)
        v.first_got = swap(out)

    def first_own():
        v.first_part = line(lambda g, w: first_part(g[:, :own], w), v.grad_projected, heads_weight)

    def tokens_back(part, got, tokens, grad_middle):
        grad = part + got.astype(F32)
        norm, inverse = normalize(tokens.astype(F32))
        out = (grad_middle + norm_back(grad * first_gain, norm, inverse)).astype(BF16)
        return out, (jnp.sum(grad * norm, axis=0), jnp.sum(grad, axis=0))

    def first_back():
        v.tokens_grad, first_sums = line(tokens_back, v.first_part, v.first_got, tokens, v.grad_middle)
        v.both = jnp.stack([*first_sums, *v.second_sums])
        v.both_got = swap(v.both)

    def output():
        v.block_out = line(
            lambda m, a, w, r: (m + dot(a, w, 1, 0) + r.astype(F32) + reduce_bias).astype(BF16),
            v.middle, v.act0, reduce_weight, v.reduced_got,
        )

    def pack_first():
        v.pack = line(
            lambda both, got, eb0, eb1, bias: jnp.concatenate(
                [(both + got).reshape(-1), (eb0 + eb1).reshape(-1), bias.reshape(-1)]
            ).reshape(-1, 128),
            v.both, v.both_got, v.eb0, v.eb1, bias_grad(v.sums, buckets),
        )
        v.pack_got = trade(v.pack, 1)

    def pack_next(bit):
        def step():
            v.pack = line(jnp.add, v.pack, v.pack_got)
            if bit:
                v.pack_got = trade(v.pack, bit)

        return step

    chunk = (hidden // 8, model)
    turned = (model, hidden // 8)

    def reduce_spread():
        (v.reduce_grad,) = line(
            lambda *xs: spread(
                at, 0, xs, put_rows, chunk, [lambda to: pl.BlockSpec(chunk, lambda g, s: (to(g, s), 0))],
                [jax.ShapeDtypeStruct(reduce_weight.shape, F32)], name="spread_reduce",
            ),
            *reduce_sum.pieces(),
        )

    def expand_spread():
        (v.expand_grad,) = line(
            lambda *xs: spread(
                at, 0, xs, put_rows, turned, [lambda to: pl.BlockSpec(turned, lambda g, s: (0, to(g, s)))],
                [jax.ShapeDtypeStruct(expand_weight.shape, F32)], name="spread_expand",
            ),
            *expand_sum.pieces(),
        )

    def heads_spread():
        v.heads_grad, v.mixer_grad = line(
            lambda *xs: spread_heads(at, 0, xs[:4], xs[4:], model, width), *query_sum.pieces(), *value_sum.pieces()
        )

    order = (
        project_own, active_own, send_more, project_other, attend, mixer_rest, mixer_both, active_other,
        mix_rows, expand_other, expand_own, reduce_chunks, middle_back, reduce_sum.first, mixed_own,
        expand_chunks, mixed_other, reduce_sum.second, attend_back, expand_sum.first, reduce_sum.third,
        query_chunks, value_chunks, reduced_other, expand_sum.second, query_sum.first, reduce_sum.fourth,
        first_other, expand_sum.third, value_sum.first, reduce_sum.fifth, query_sum.second, first_own,
        value_sum.second, first_back, expand_sum.fourth, reduce_sum.sixth, value_sum.third, pack_first,
        expand_sum.fifth, pack_next(2), query_sum.third, reduce_spread, value_sum.fourth, expand_sum.sixth,
        pack_next(4), query_sum.fourth, pack_next(8), value_sum.fifth, output, query_sum.fifth, value_sum.sixth,
        expand_spread, query_sum.sixth, heads_spread, pack_next(0),
    )
    for step in order:
        step()
    pack = v.pack.reshape(-1)
    both = pack[: 5 * model].reshape(5, model)
    expand_bias_grad = pack[5 * model : 5 * model + hidden]
    bias_part = pack[5 * model + hidden :].reshape(relative_bias.shape)
    return (
        v.block_out, v.tokens_grad, both[0], both[1], v.heads_grad, bias_part, v.mixer_grad, both[2], both[3],
        v.expand_grad, expand_bias_grad, v.reduce_grad, both[4],
    )


def gathered(
    tokens, lengths, first_gain, first_shift, heads_weight, relative_bias, mixer_weight, second_gain,
    second_shift, expand_weight, expand_bias, reduce_weight, reduce_bias, cotangent,
):
    def gather(x):
        return lax.all_gather(x, "mp", axis=0, tiled=True)

    def scatter(x):
        return lax.psum_scatter(x.astype(BF16), "mp", scatter_dimension=0, tiled=True).astype(F32)

    members = lax.axis_size("mp")
    length = lengths[0]
    own = tokens.shape[0]
    whole = own * members
    half = whole // 2
    buckets = relative_bias.shape[1]
    sp = jnp.stack([jnp.zeros((), jnp.int32), length.astype(jnp.int32)])
    places = lax.axis_index("mp") * own + jnp.arange(own)
    rows = bias_rows(relative_bias)
    source_all = gather(tokens)
    first_all, projected = project(source_all, first_gain.reshape(1, -1), first_shift.reshape(1, -1), heads_weight)
    projected0, projected1 = projected[:, :half], projected[:, half:]
    mixed, logsum = attend_forward(sp, projected0, projected1, rows)
    source = tokens.astype(F32)
    middle = source + scatter(dot(mixed, mixer_weight, 1, 0))
    second_norm, second_inverse = normalize(middle)
    second_all = gather((second_norm * second_gain + second_shift).astype(BF16))
    target = keep_valid(cotangent, places, length)
    target_wide = target.astype(F32)
    target_all = gather(target)
    expanded = dot(second_all, expand_weight, 1, 0) + expand_bias
    active_low = jax.nn.gelu(expanded, approximate=True).astype(BF16)
    grad_expanded = gelu_back(expanded, dot(target_all, reduce_weight, 1, 1)).astype(BF16)
    grad_second = scatter(dot(grad_expanded, expand_weight, 1, 1))
    reduced = scatter(dot(active_low, reduce_weight, 1, 0))
    reduce_grad = dot(active_low, target_all, 0, 0)
    expand_grad = dot(second_all, grad_expanded, 0, 0)
    expand_bias_grad = jnp.sum(grad_expanded.astype(F32), axis=0)
    block_out = (middle + reduced + reduce_bias).astype(BF16)
    grad_middle = target_wide + norm_back(grad_second * second_gain, second_norm, second_inverse)
    attended_all = gather(grad_middle.astype(BF16))
    mixer_grad = dot(mixed, attended_all, 0, 0)
    grad_mixed = dot(attended_all, mixer_weight, 1, 1).astype(BF16)
    grad_projected, sums = attend_backward(
        sp, projected0, projected1, grad_mixed[:half], grad_mixed[half:], mixed, logsum, rows
    )
    bias_part = bias_grad(sums, buckets)
    heads_grad = jnp.einsum("td,cte->cde", first_all, grad_projected, preferred_element_type=F32)
    grad_first = scatter(jnp.einsum("cte,cde->td", grad_projected, heads_weight, preferred_element_type=F32))
    first_norm, first_inverse = normalize(source)
    tokens_grad = (
        grad_middle + norm_back(grad_first * first_gain, first_norm, first_inverse)
    ).astype(BF16)
    first_gain_grad, first_shift_grad, second_gain_grad, second_shift_grad, reduce_bias_grad = (
        lax.psum(
            (
                jnp.sum(grad_first * first_norm, axis=0),
                jnp.sum(grad_first, axis=0),
                jnp.sum(grad_second * second_norm, axis=0),
                jnp.sum(grad_second, axis=0),
                jnp.sum(target_wide, axis=0),
            ),
            ("dp", "mp"),
        )
    )
    heads_grad, bias_part, mixer_grad, expand_grad, expand_bias_grad, reduce_grad = (
        lax.psum(x.astype(BF16), "dp").astype(F32)
        for x in (heads_grad, bias_part, mixer_grad, expand_grad, expand_bias_grad, reduce_grad)
    )
    return (
        block_out, tokens_grad, first_gain_grad, first_shift_grad, heads_grad, bias_part, mixer_grad,
        second_gain_grad, second_shift_grad, expand_grad, expand_bias_grad, reduce_grad, reduce_bias_grad,
    )


def per_device(*args):
    if lax.axis_size("mp") == 2 and lax.axis_size("dp") == 16:
        return paired(*args)
    return gathered(*args)


def solution(mesh):
    return jax.shard_map(
        per_device,
        mesh=mesh,
        in_specs=(
            P(("dp", "mp"), None),
            P("dp"),
            P(),
            P(),
            P(None, None, "mp"),
            P("mp", None),
            P("mp", None),
            P(),
            P(),
            P(None, "mp"),
            P("mp"),
            P("mp", None),
            P(),
            P(("dp", "mp"), None),
        ),
        out_specs=(
            P(("dp", "mp"), None),
            P(("dp", "mp"), None),
            P(),
            P(),
            P(None, None, "mp"),
            P("mp", None),
            P("mp", None),
            P(),
            P(),
            P(None, "mp"),
            P("mp"),
            P("mp", None),
            P(),
        ),
        check_vma=False,
    )
```

```python
import functools
import math

import jax
import jax.numpy as jnp
import numpy as np
from jax import lax
from jax.experimental import pallas as pl
from jax.experimental.pallas import tpu as pltpu
from jax.sharding import PartitionSpec as P

EPS = 1e-05
DH=64; MAXDIST=128; NEG=-1e30; BLK=256
F32=jnp.float32; BF16=jnp.bfloat16
HIGHEST=lax.Precision.HIGHEST

def bucket_table(count, buckets, reach):
    exact = buckets // 2
    entries = []
    for position in range(count):
        if position < exact:
            entries.append(position)
        else:
            level = exact + int(math.log(position / exact) / math.log(reach / exact) * (buckets - exact))
            entries.append(min(buckets - 1, level))
    return np.array(entries, dtype=np.int32)

def bucket_starts(buckets):
    table=bucket_table(4*MAXDIST+2*buckets,buckets,MAXDIST)
    return [int(np.argmax(table>=level)) for level in range(1,buckets)]

def bias_rows_kernel(r_ref,o_ref):
    heads,buckets=r_ref.shape
    W=2*BLK
    rel=r_ref[...]-r_ref[:,buckets-1:]
    place=lax.broadcasted_iota(jnp.int32,(heads,W),1)
    signed=jnp.where(place<BLK,place,place-W)
    for part,distance in enumerate((-signed,BLK-signed,signed,BLK+signed)):
        value=jnp.broadcast_to(rel[:,:1],(heads,W))
        for level,start in enumerate(bucket_starts(buckets)):
            value=jnp.where(distance>=start,rel[:,level+1:level+2],value)
        value=jnp.where(distance>=0,value,NEG)
        for pair in range(heads//2):
            o_ref[pair,:,part*W:(part+1)*W]=value[2*pair:2*pair+2]

def bias_rows(relative_bias):
    heads=relative_bias.shape[0]
    return pl.pallas_call(
        bias_rows_kernel,
        out_shape=jax.ShapeDtypeStruct((heads//2,2,8*BLK),F32),
        name="bias_rows",
    )(relative_bias)

def toeplitz(row):
    wide=jnp.broadcast_to(row,(BLK,2*BLK))
    return pltpu.roll(wide,0,1,stride=1,stride_axis=0)[:,:BLK]


def lane_masks():
    lane=lax.broadcasted_iota(jnp.int32,(1,128),1)
    head=[(lane//DH)==h for h in range(2)]
    mine=[jnp.where(m,1.0,0.0).astype(BF16) for m in head]
    spare=[jnp.where(lane==DH*(1-h),1.0,0.0) for h in range(2)]
    return head,mine,spare


def gone_rows(start,half,length,spare):
    pos=lax.broadcasted_iota(jnp.int32,(half,1),0)+start
    gone=jnp.where(pos<length,0.0,NEG)
    return [(gone*s).astype(BF16) for s in spare]


def fwd_kernel(sp, a_ref,c_ref,b_ref,o_ref,lse_ref,qs,ks,vs):
    half=a_ref.shape[1]; T=2*half; flip=sp[0]; length=sp[1]
    W=2*BLK
    head,mine,spare=lane_masks()
    for a,ref in enumerate((a_ref,c_ref)):
        start=pl.multiple_of((a^flip)*half,half)
        dst=pl.ds(start,half)
        gone=gone_rows(start,half,length,spare)
        for h in range(2):
            qs[h,dst,:]=ref[0]*(mine[h]*jnp.asarray(DH**-0.5,BF16))+spare[h].astype(BF16)
            ks[h,dst,:]=ref[1]*mine[h]+gone[h]
            vs[h,dst,:]=ref[2]*mine[h]+mine[1-h]
    tiles=[(toeplitz(b_ref[0,h:h+1,0:W]),toeplitz(b_ref[0,h:h+1,W:2*W])) for h in range(2)]
    outs={}

    def score(i,h):
        return dot(qs[h,i*BLK:(i+1)*BLK,:],ks[h,:(i+1)*BLK,:],1,1)

    def finish(i,h,s):
        kc=(i+1)*BLK; t0,t1=tiles[h]
        parts=[]
        if i>=2: parts.append(s[:,:kc-2*BLK])
        if i>=1: parts.append(s[:,kc-2*BLK:kc-BLK]+t1)
        parts.append(s[:,kc-BLK:]+t0)
        top=functools.reduce(jnp.maximum,[jnp.max(x,axis=1,keepdims=True) for x in parts])
        p=jnp.concatenate([jnp.exp(x-top).astype(BF16) for x in parts],axis=1)
        o=dot(p,vs[h,:kc,:],1,0)
        total=o[:,DH*(1-h):DH*(1-h)+1]
        outs[h]=(o*(1.0/total),top+jnp.log(total))
        if h==1:
            rows=pl.ds(pl.multiple_of((i*BLK+flip*half)%T,BLK),BLK)
            o_ref[rows,:]=jnp.where(head[0],outs[0][0],outs[1][0]).astype(BF16)
            lse_ref[0,i*BLK:kc,:]=jnp.where(head[0],outs[0][1],outs[1][1])

    run_ahead([(i,h) for i in range(T//BLK) for h in range(2)],score,finish,2)


def run_ahead(items,first,second,depth):
    waiting=[]
    for item in items:
        waiting.append((item,first(*item)))
        if len(waiting)>depth:
            done,value=waiting.pop(0)
            second(*done,value)
    for done,value in waiting:
        second(*done,value)


def attend_forward(sp,projected0,projected1,rows):
    _,half,HD=projected0.shape; pairs=HD//128; T=2*half
    part=pl.BlockSpec((3,half,128),lambda p,s:(0,0,p))
    return pl.pallas_call(
        fwd_kernel,
        grid_spec=pltpu.PrefetchScalarGridSpec(
            num_scalar_prefetch=1,grid=(pairs,),
            in_specs=[part,part,pl.BlockSpec((1,2,rows.shape[2]),lambda p,s:(p,0,0))],
            out_specs=[pl.BlockSpec((T,128),lambda p,s:(0,p)),pl.BlockSpec((1,T,128),lambda p,s:(p,0,0))],
            scratch_shapes=[pltpu.VMEM((2,T,128),BF16)]*3),
        out_shape=[jax.ShapeDtypeStruct((T,HD),BF16),jax.ShapeDtypeStruct((pairs,T,128),F32)],
        cost_estimate=cost(8*T*T*HD,8*T*HD+512*pairs*T),
        name="attend_forward",
    )(sp,projected0,projected1,rows)

def diagonal_sums(acc, offset):
    W=2*BLK
    wide=jnp.concatenate([acc,jnp.zeros_like(acc)],axis=1)
    n=BLK
    while n>1:
        n//=2
        top=wide[:n]; bottom=wide[n:2*n]
        wide=top+pltpu.roll(bottom,W-n,1)
    return pltpu.roll(wide,offset,1) if offset else wide

def bwd_kernel(sp, a_ref,c_ref,d0_ref,d1_ref,o_ref,lse_ref,b_ref,g_ref,d_ref,qs,ks,vs,dos,dq,acc0,acc1):
    half=a_ref.shape[1]; T=2*half; flip=sp[0]; length=sp[1]
    W=2*BLK
    n=T//BLK
    head,mine,spare=lane_masks()
    stats=[None,None]
    one=sum(spare).astype(BF16)
    for a,(ref,do_ref) in enumerate(((a_ref,d0_ref),(c_ref,d1_ref))):
        start=pl.multiple_of((a^flip)*half,half)
        dst=pl.ds(start,half)
        gone=gone_rows(start,half,length,spare)
        for h in range(2):
            qs[h,dst,:]=ref[0]*(mine[h]*jnp.asarray(DH**-0.5,BF16))+spare[h].astype(BF16)
            ks[h,dst,:]=ref[1]*mine[h]+gone[h]
            vs[h,dst,:]=ref[2]*mine[h]
        dos[dst,:]=do_ref[...]
        acc0[0,dst,:]=do_ref[...].astype(F32)*o_ref[a*half:(a+1)*half,:].astype(F32)
    turned=acc0[0].T
    deltas=[jnp.sum(turned[h*DH:(h+1)*DH],axis=0,keepdims=True) for h in range(2)]
    turned=lse_ref[0].T
    lses=[turned[h*DH:h*DH+1] for h in range(2)]
    near=acc1
    tiles=[(toeplitz(b_ref[0,h:h+1,2*W:3*W]),toeplitz(b_ref[0,h:h+1,3*W:])) for h in range(2)]

    def products(j,h):
        rj=slice(j*BLK,(j+1)*BLK)
        return dot(ks[h,rj,:],qs[h,j*BLK:,:],1,1),dot(vs[h,rj,:],dos[j*BLK:,:],1,1)

    keep={}

    def finish(j,h,value):
        s,dp=value
        rj=slice(j*BLK,(j+1)*BLK)
        ps=[];dss=[]
        for b in range(n-j):
            c=slice(b*BLK,(b+1)*BLK)
            cc=slice((j+b)*BLK,(j+b+1)*BLK)
            x=s[:,c]-lses[h][:,cc]
            if b<2: x=x+tiles[h][b]
            p=jnp.exp(x)
            ds=p*(dp[:,c]-deltas[h][:,cc])
            if b<2:
                if j==0: near[h,b]=ds
                else: near[h,b]+=ds
            ps.append(p.astype(BF16)); dss.append(ds.astype(BF16))
        p=jnp.concatenate(ps,axis=1); ds=jnp.concatenate(dss,axis=1)
        dv=dot(p,dos[j*BLK:,:],1,0)
        dk=dot(ds,qs[h,j*BLK:,:],1,0)
        kk=ks[h,rj,:]*mine[h]+mine[1-h]
        dqj=dot(ds,kk,0,0)
        if j==0: dq[h,:,:]=dqj
        else: dq[h,j*BLK:,:]+=dqj
        keep[h]=(dk,dv)
        if h==1:
            rows=pl.ds(pl.multiple_of((j*BLK+flip*half)%T,BLK),BLK)
            g_ref[1,rows,:]=jnp.where(head[0],keep[0][0],keep[1][0]).astype(BF16)
            g_ref[2,rows,:]=jnp.where(head[0],keep[0][1],keep[1][1]).astype(BF16)

    run_ahead([(j,h) for j in range(n) for h in range(2)],products,finish,1)
    for h in range(2):
        d_ref[0,h:h+1,:]=diagonal_sums(near[h,0],0)+diagonal_sums(near[h,1],BLK)
        total=jnp.sum(dq[h,:,:],axis=0,keepdims=True)[:,DH*(1-h):DH*(1-h)+1]
        d_ref[0,2+h:3+h,:]=jnp.broadcast_to(total,(1,W))
    for a in range(2):
        dst=pl.ds(pl.multiple_of((a^flip)*half,half),half)
        g_ref[0,a*half:(a+1)*half,:]=(jnp.where(head[0],dq[0,dst,:],dq[1,dst,:])*DH**-0.5).astype(BF16)

def attend_backward(sp,projected0,projected1,grad0,grad1,mixed,lse,rows,start=0,count=None,given=None):
    _,half,HD=projected0.shape; pairs=HD//128; T=2*half
    count=pairs if count is None else count
    part=pl.BlockSpec((3,half,128),lambda p,s:(0,0,p+start))
    grad=pl.BlockSpec((half,128),lambda p,s:(0,p+start))
    in_specs=[part,part,grad,grad,pl.BlockSpec((T,128),lambda p,s:(0,p+start)),
              pl.BlockSpec((1,T,128),lambda p,s:(p+start,0,0)),pl.BlockSpec((1,2,rows.shape[2]),lambda p,s:(p+start,0,0))]
    args=[sp,projected0,projected1,grad0,grad1,mixed,lse,rows]
    kernel=bwd_kernel
    if given is not None:
        in_specs.append(pl.BlockSpec(memory_space=pl.ANY)); args.append(given)
        kernel=lambda *refs: bwd_kernel(*refs[:8],*refs[9:])
    return pl.pallas_call(
        kernel,
        grid_spec=pltpu.PrefetchScalarGridSpec(
            num_scalar_prefetch=1,grid=(count,),
            in_specs=in_specs,
            out_specs=[pl.BlockSpec((3,T,128),lambda p,s:(0,0,p+start)),pl.BlockSpec((1,4,2*BLK),lambda p,s:(p,0,0))],
            scratch_shapes=[pltpu.VMEM((2,T,128),BF16)]*3+[pltpu.VMEM((T,128),BF16),pltpu.VMEM((2,T,128),F32),pltpu.VMEM((1,T,128),F32),pltpu.VMEM((2,2,BLK,BLK),F32)]),
        out_shape=[jax.ShapeDtypeStruct((3,T,HD),BF16),jax.ShapeDtypeStruct((count,4,2*BLK),F32)],
        input_output_aliases={} if given is None else {8:0},
        cost_estimate=cost(20*T*T*128*count,(16*T*128+512*T)*count),
        name="attend_backward",
    )(*args)

def bias_grad(sums, buckets):
    pairs=sums.shape[0]; W=2*BLK
    near=sums[:,0:2].reshape(pairs*2,W); total=sums[:,2:4,0].reshape(pairs*2,1)
    edges=[0]+bucket_starts(buckets)
    distance=jnp.arange(W)[None,None]
    low=jnp.asarray(np.array(edges[:-1],np.int32))[None,:,None]
    high=jnp.asarray(np.array(edges[1:],np.int32))[None,:,None]
    parts=jnp.sum(jnp.where((distance>=low)&(distance<high),near[:,None,:],0.0),axis=2)
    return jnp.concatenate([parts,total-jnp.sum(parts,axis=1,keepdims=True)],axis=1)


HALF_TANH = math.sqrt(2.0 / math.pi)


def dot(a, b, ca, cb):
    return lax.dot_general(a, b, (((ca,), (cb,)), ((), ())), preferred_element_type=F32)


def fixed(shape):
    return pl.BlockSpec(shape, lambda *_: (0,) * len(shape))


def cost(flops, moved):
    return pl.CostEstimate(flops=int(flops), transcendentals=0, bytes_accessed=int(moved))


def cost4(flops, moved):
    return cost(4 * flops, 4 * moved)


def cost16(flops, moved):
    return cost(16 * flops, 16 * moved)


def row_norm(values):
    center = jnp.mean(values, axis=-1, keepdims=True)
    centered = values - center
    inverse = lax.rsqrt(jnp.mean(centered * centered, axis=-1, keepdims=True) + EPS)
    return centered * inverse, inverse


def project_kernel(x_ref, gain_ref, shift_ref, w_ref, low_ref, out_ref):
    @pl.when(pl.program_id(0) == 0)
    def _():
        def some(i, _):
            rows = pl.ds(pl.multiple_of(i * 128, 128), 128)
            normed, _ = row_norm(x_ref[rows, :].astype(F32))
            low_ref[rows, :] = (normed * gain_ref[...] + shift_ref[...]).astype(BF16)
            return 0

        lax.fori_loop(0, x_ref.shape[0] // 128, some, 0)

    out_ref[0] = dot(low_ref[...], w_ref[0], 1, 0).astype(BF16)


def project(x, gain, shift, weight):
    rows, model = x.shape
    width = weight.shape[2]
    return pl.pallas_call(
        project_kernel,
        grid=(3,),
        in_specs=[fixed((rows, model)), fixed((1, model)), fixed((1, model)), pl.BlockSpec((1, model, width), lambda c: (c, 0, 0))],
        out_specs=[fixed((rows, model)), pl.BlockSpec((1, rows, width), lambda c: (c, 0, 0))],
        out_shape=[jax.ShapeDtypeStruct((rows, model), BF16), jax.ShapeDtypeStruct((3, rows, width), BF16)],
        cost_estimate=cost(6 * rows * model * width, 2 * (2 * rows * model + weight.size + 3 * rows * width)),
        name="project",
    )(x, gain, shift, weight)


def mix_kernel(own_blocks, x0_ref, x1_ref, m_ref, p_ref, w0_ref, w1_ref, gain_ref, shift_ref, mid_ref, low_ref):
    i = pl.program_id(0)
    attended = dot(m_ref[...], w0_ref[...], 1, 0) + dot(p_ref[...], w1_ref[...], 1, 0)

    def rows(x_ref):
        return x_ref[...].astype(F32) + attended

    def rest(middle):
        normed, _ = row_norm(middle)
        low_ref[...] = (normed * gain_ref[...] + shift_ref[...]).astype(BF16)

    @pl.when(i < own_blocks)
    def _():
        middle = rows(x0_ref)
        mid_ref[...] = middle
        rest(middle)

    @pl.when(i >= own_blocks)
    def _():
        rest(rows(x1_ref))


def mix(tokens, other, mixed, mixed_other, weight, weight_other, gain, shift):
    own, model = tokens.shape
    width = mixed.shape[1]
    step = 256
    n = own // step
    return pl.pallas_call(
        functools.partial(mix_kernel, n),
        grid=(2 * n,),
        in_specs=[
            pl.BlockSpec((step, model), lambda i: (jnp.minimum(i, n - 1), 0)),
            pl.BlockSpec((step, model), lambda i: (jnp.maximum(i - n, 0), 0)),
            pl.BlockSpec((step, width), lambda i: (i, 0)),
            pl.BlockSpec((step, width), lambda i: ((i + n) % (2 * n), 0)),
            fixed(weight.shape), fixed(weight.shape), fixed((1, model)), fixed((1, model)),
        ],
        out_specs=[
            pl.BlockSpec((step, model), lambda i: (jnp.minimum(i, n - 1), 0)),
            pl.BlockSpec((step, model), lambda i: (i, 0)),
        ],
        out_shape=[jax.ShapeDtypeStruct((own, model), F32), jax.ShapeDtypeStruct((2 * own, model), BF16)],
        cost_estimate=cost(8 * own * model * width, 2 * (4 * own * model + 4 * own * width + 2 * weight.size) + 4 * own * model),
        name="mix",
    )(tokens, other, mixed, mixed_other, weight, weight_other, gain, shift)


def expand_kernel(x_ref, g_ref, w_ref, b_ref, act_ref, ge_ref, gs_ref, bias_ref, acc_ref):
    i = pl.program_id(0)
    x = x_ref[...]
    width = w_ref.shape[1]
    sub = min(512, width)
    total = None
    for s in range(width // sub):
        cols = slice(s * sub, (s + 1) * sub)
        u = dot(x, w_ref[:, cols], 1, 0) + b_ref[:, cols].astype(F32)
        square = u * u
        t = jnp.tanh(HALF_TANH * u * (1.0 + 0.044715 * square))
        half = 0.5 + 0.5 * t
        act_ref[:, cols] = (u * half).astype(BF16)
        slope = half + 0.5 * u * (1.0 - t * t) * (HALF_TANH * (1.0 + 3 * 0.044715 * square))
        grad = g_ref[:, cols].astype(F32) * slope
        low = grad.astype(BF16)
        ge_ref[:, cols] = low
        bias_ref[:, cols] = jnp.sum(grad, axis=0, keepdims=True)
        part = dot(low, w_ref[:, cols], 1, 1)
        total = part if total is None else total + part

    @pl.when(i == 0)
    def _():
        acc_ref[...] = total

    @pl.when(i > 0)
    def _():
        acc_ref[...] += total

    @pl.when(i == pl.num_programs(0) - 1)
    def _():
        gs_ref[...] = acc_ref[...].astype(gs_ref.dtype)


def expand(x, block, rows, grad_active, weight, bias, dtype):
    model = x.shape[1]
    hidden = weight.shape[1]
    step = min(512, hidden)
    return pl.pallas_call(
        expand_kernel,
        grid=(hidden // step,),
        in_specs=[
            pl.BlockSpec((rows, model), lambda i: (block, 0)),
            pl.BlockSpec((rows, step), lambda i: (0, i)),
            pl.BlockSpec((model, step), lambda i: (0, i)),
            pl.BlockSpec((1, step), lambda i: (0, i)),
        ],
        out_specs=[
            pl.BlockSpec((rows, step), lambda i: (0, i)),
            pl.BlockSpec((rows, step), lambda i: (0, i)),
            fixed((rows, model)),
            pl.BlockSpec((1, step), lambda i: (0, i)),
        ],
        out_shape=[
            jax.ShapeDtypeStruct((rows, hidden), BF16),
            jax.ShapeDtypeStruct((rows, hidden), BF16),
            jax.ShapeDtypeStruct((rows, model), dtype),
            jax.ShapeDtypeStruct((1, hidden), F32),
        ],
        scratch_shapes=[pltpu.VMEM((rows, model), F32)],
        cost_estimate=cost(4 * rows * model * hidden, 2 * (2 * rows * model + 3 * rows * hidden + weight.size)),
        name="expand",
    )(x, grad_active, weight, bias)


STAGES = ((1, 2, 4, 8), (1, 4, 2, 8))


def place_of(index, stages):
    bit = [(index // s) % 2 for s in stages]
    return bit[0] * 4 + bit[1] * 2 + bit[2]


def trade(x, bit):
    size = lax.axis_size("dp")
    return lax.ppermute(x, "dp", [(i, i ^ bit) for i in range(size)])


def add_low(a, b):
    return (a.astype(F32) + b.astype(F32)).astype(BF16)


def pair_of(g, s, slot):
    return (3 - g) ^ (s[slot] // 2)


def put_pair(slot, s_ref, chunks, outs):
    flip = s_ref[slot] % 2
    sent = pl.program_id(0) < 2
    for j, value in enumerate(chunks):
        value = value.astype(BF16)[None]
        for out, here in zip(outs, (sent, jnp.logical_not(sent))):
            @pl.when(here)
            def _(out=out):
                out[pl.ds(j ^ flip, 1)] = value


def pair_call(kernel, slot, s, arrays, specs, tail, flops, name):
    zeros = (0,) * len(tail)
    moved = sum(2 * x.size for x in arrays) + 16 * math.prod(tail)
    return pl.pallas_call(
        functools.partial(kernel, slot),
        grid_spec=pltpu.PrefetchScalarGridSpec(
            num_scalar_prefetch=1, grid=(4,), in_specs=specs,
            out_specs=[
                pl.BlockSpec((2, *tail), lambda g, s: (jnp.maximum(1 - g, 0), *zeros)),
                pl.BlockSpec((2, *tail), lambda g, s: (jnp.minimum(3 - g, 1), *zeros)),
            ],
        ),
        out_shape=[jax.ShapeDtypeStruct((4, *tail), BF16)] * 2,
        cost_estimate=cost(flops, moved),
        name=name,
    )(s, *arrays)


def reduce_grad_kernel(slot, s_ref, *refs):
    (a0, a1, t0, t1), outs = refs[:4], refs[4:]
    value = dot(a0[...], t0[...], 0, 0) + dot(a1[...], t1[...], 0, 0)
    width = value.shape[0] // 2
    put_pair(slot, s_ref, [value[:width], value[width:]], outs)


def reduce_grad_part(s, slot, act0, act1, t0, t1):
    rows, hidden = act0.shape
    model = t0.shape[1]
    block = pl.BlockSpec((rows, hidden // 4), lambda g, s: (0, pair_of(g, s, slot)))
    return pair_call(
        reduce_grad_kernel, slot, s, (act0, act1, t0, t1), [block, block, fixed(t0.shape), fixed(t1.shape)],
        (hidden // 8, model), 4 * rows * model * hidden, "reduce_grad",
    )


def expand_grad_kernel(slot, s_ref, *refs):
    (x, g0, g1), outs = refs[:3], refs[3:]
    rows = g0.shape[0]
    value = dot(x[:rows], g0[...], 0, 0) + dot(x[rows:], g1[...], 0, 0)
    width = value.shape[1] // 2
    put_pair(slot, s_ref, [value[:, :width], value[:, width:]], outs)


def expand_grad_part(s, slot, x, g0, g1):
    rows, hidden = g0.shape
    model = x.shape[1]
    block = pl.BlockSpec((rows, hidden // 4), lambda g, s: (0, pair_of(g, s, slot)))
    return pair_call(
        expand_grad_kernel, slot, s, (x, g0, g1), [fixed(x.shape), block, block],
        (model, hidden // 8), 4 * rows * model * hidden, "expand_grad",
    )


def heads_grad_kernel(slot, s_ref, *refs):
    (l0, l1, g), outs = refs[:3], refs[3:]
    rows = l0.shape[0]
    both = [dot(l0[...], g[c, :rows], 0, 0) + dot(l1[...], g[c, rows:], 0, 0) for c in range(2)]
    width = both[0].shape[0] // 2
    chunks = [jnp.stack([v[j * width:(j + 1) * width] for v in both]) for j in range(2)]
    put_pair(slot, s_ref, chunks, outs)


def heads_grad_part(s, slot, low0, low1, grad):
    rows, model = low0.shape
    width = grad.shape[2]
    block = pl.BlockSpec((rows, model // 4), lambda g, s: (0, pair_of(g, s, slot)))
    return pair_call(
        heads_grad_kernel, slot, s, (low0, low1, grad),
        [block, block, pl.BlockSpec((2, 2 * rows, width), lambda g, s: (0, 0, 0))],
        (2, model // 8, width), 8 * rows * model * width, "heads_grad",
    )


def values_grad_kernel(slot, s_ref, *refs):
    (l0, l1, g, a0, a1, m), outs = refs[:6], refs[6:]
    rows = l0.shape[0]
    both = [
        dot(l0[...], g[0, :rows], 0, 0) + dot(l1[...], g[0, rows:], 0, 0),
        dot(a0[...], m[:rows], 0, 0) + dot(a1[...], m[rows:], 0, 0),
    ]
    width = both[0].shape[0] // 2
    chunks = [jnp.stack([v[j * width:(j + 1) * width] for v in both]) for j in range(2)]
    put_pair(slot, s_ref, chunks, outs)


def values_grad_part(s, slot, low0, low1, grad, att0, att1, mixed):
    rows, model = low0.shape
    width = grad.shape[2]
    block = pl.BlockSpec((rows, model // 4), lambda g, s: (0, pair_of(g, s, slot)))
    return pair_call(
        values_grad_kernel, slot, s, (low0, low1, grad, att0, att1, mixed),
        [block, block, pl.BlockSpec((1, 2 * rows, width), lambda g, s: (2, 0, 0)), block, block, fixed(mixed.shape)],
        (2, model // 8, width), 8 * rows * model * width, "values_grad",
    )


def columns_kernel(turn, a_ref, b_ref, out_ref):
    out_ref[...] = dot(a_ref[...], b_ref[...], 1, turn).astype(out_ref.dtype)


def columns_dot(a, b, turn, name):
    rows, depth = a.shape
    columns = b.shape[1 - turn]
    step = min(512, columns)
    block = ((step, depth), lambda i: (i, 0)) if turn else ((depth, step), lambda i: (0, i))
    return pl.pallas_call(
        functools.partial(columns_kernel, turn),
        grid=(columns // step,),
        in_specs=[fixed(a.shape), pl.BlockSpec(*block)],
        out_specs=pl.BlockSpec((rows, step), lambda i: (0, i)),
        out_shape=jax.ShapeDtypeStruct((rows, columns), BF16),
        cost_estimate=cost(2 * rows * depth * columns, 2 * (a.size + b.size + rows * columns)),
        name=name,
    )(a, b)


def output_kernel(m_ref, a_ref, w_ref, r_ref, bias_ref, out_ref):
    out_ref[...] = (
        m_ref[...] + dot(a_ref[...], w_ref[...], 1, 0) + r_ref[...].astype(F32) + bias_ref[...]
    ).astype(BF16)


def output_rows(middle, act, weight, reduced, bias):
    rows, hidden = act.shape
    model = weight.shape[1]
    step = 256
    block = pl.BlockSpec((rows, step), lambda i: (0, i))
    return pl.pallas_call(
        output_kernel,
        grid=(model // step,),
        in_specs=[
            block, fixed(act.shape), pl.BlockSpec((hidden, step), lambda i: (0, i)), block,
            pl.BlockSpec((1, step), lambda i: (0, i)),
        ],
        out_specs=block,
        out_shape=jax.ShapeDtypeStruct((rows, model), BF16),
        cost_estimate=cost16(2 * rows * hidden * model, 2 * (act.size + weight.size) + 8 * rows * model),
        name="output",
    )(middle, act, weight, reduced, bias)


def first_kernel(g_ref, w_ref, out_ref, acc_ref):
    c = pl.program_id(0)
    value = dot(g_ref[0], w_ref[0], 1, 1)

    @pl.when(c == 0)
    def _():
        acc_ref[...] = value

    @pl.when(c > 0)
    def _():
        acc_ref[...] += value

    @pl.when(c == pl.num_programs(0) - 1)
    def _():
        out_ref[...] = acc_ref[...].astype(out_ref.dtype)


def first_rows(grad, weight, part, rows, dtype):
    kinds, model, width = weight.shape
    return pl.pallas_call(
        first_kernel,
        grid=(kinds,),
        in_specs=[
            pl.BlockSpec((1, rows, width), lambda c: (c, part, 0)),
            pl.BlockSpec((1, model, width), lambda c: (c, 0, 0)),
        ],
        out_specs=fixed((rows, model)),
        out_shape=jax.ShapeDtypeStruct((rows, model), dtype),
        scratch_shapes=[pltpu.VMEM((rows, model), F32)],
        cost_estimate=cost(2 * kinds * rows * width * model, 2 * (grad.size + weight.size) + 4 * rows * model),
        name="first_rows",
    )(grad, weight)


def back_kernel(keep, a_ref, b_ref, source_ref, add_ref, gain_ref, *outs):
    @pl.when(pl.program_id(0) == 0)
    def _():
        outs[-1][...] = jnp.zeros_like(outs[-1])

    def some(i, _):
        rows = pl.ds(pl.multiple_of(i * 64, 64), 64)
        normed, inverse = row_norm(source_ref[rows, :].astype(F32))
        grad = a_ref[rows, :] + b_ref[rows, :].astype(F32)
        add = add_ref[rows, :].astype(F32)
        scaled = grad * gain_ref[...]
        weighted = grad * normed
        mean = jnp.mean(scaled, axis=-1, keepdims=True)
        along = jnp.mean(scaled * normed, axis=-1, keepdims=True)
        out = add + inverse * (scaled - mean - normed * along)
        if keep:
            outs[0][rows, :] = out
        outs[-2][rows, :] = out.astype(BF16)
        for k, value in enumerate((weighted, grad, add)):
            outs[-1][k:k + 1] += jnp.sum(value, axis=0, keepdims=True)
        return 0

    lax.fori_loop(0, source_ref.shape[0] // 64, some, 0)


def back_rows(a, b, source, add, gain, keep):
    rows, model = a.shape
    step = 256
    block = pl.BlockSpec((step, model), lambda i: (i, 0))
    kinds = ([F32] if keep else []) + [BF16]
    return pl.pallas_call(
        functools.partial(back_kernel, keep),
        grid=(rows // step,),
        in_specs=[block] * 4 + [fixed((1, model))],
        out_specs=[block] * len(kinds) + [fixed((8, model))],
        out_shape=[jax.ShapeDtypeStruct((rows, model), kind) for kind in kinds] + [jax.ShapeDtypeStruct((8, model), F32)],
        cost_estimate=cost(30 * rows * model, 16 * rows * model),
        name="back_rows",
    )(a, b, source, add, gain)


def order_kernel(s_ref, a_ref, b_ref, out_ref):
    @pl.when(pl.program_id(0) == 0)
    def _():
        out_ref[...] = a_ref[...]

    @pl.when(pl.program_id(0) == 1)
    def _():
        out_ref[...] = b_ref[...]


def order_rows(core, a, b):
    rows, model = a.shape
    return pl.pallas_call(
        order_kernel,
        grid_spec=pltpu.PrefetchScalarGridSpec(
            num_scalar_prefetch=1, grid=(2,),
            in_specs=[pl.BlockSpec((rows, model), lambda g, s: (0, 0))] * 2,
            out_specs=pl.BlockSpec((rows, model), lambda g, s: (g ^ s[0], 0)),
        ),
        out_shape=jax.ShapeDtypeStruct((2 * rows, model), a.dtype),
        cost_estimate=cost(0, 8 * rows * model),
        name="order_rows",
    )(core, a, b)


def spread_kernel(put, s_ref, *refs):
    g = pl.program_id(0)
    pieces, outs = refs[-4 - put.outs:-put.outs], refs[-put.outs:]
    for a in range(4):
        @pl.when(g // 2 == a)
        def _(a=a):
            put(pieces[a], outs)


def spread(places, slot, pieces, put, tail, out_specs, out_shape, given=None, name=None):
    zeros = (0,) * len(tail)
    at = lambda g, s: g ^ s[slot]
    in_specs = [
        pl.BlockSpec((1, *tail), lambda g, s, a=a: (jnp.clip(g - 2 * a, 0, 1), *zeros)) for a in range(4)
    ]
    args = list(pieces)
    aliases = {}
    if given is not None:
        in_specs.insert(0, pl.BlockSpec(memory_space=pl.ANY))
        args.insert(0, given)
        aliases = {1: 0}
    return pl.pallas_call(
        functools.partial(spread_kernel, put),
        grid_spec=pltpu.PrefetchScalarGridSpec(
            num_scalar_prefetch=1, grid=(8,), in_specs=in_specs, out_specs=[spec(at) for spec in out_specs],
        ),
        out_shape=out_shape,
        input_output_aliases=aliases,
        cost_estimate=cost(0, 6 * 8 * math.prod(tail)),
        name=name,
    )(places, *args)


def put_rows(piece, outs):
    outs[0][...] = piece[0].astype(F32)


put_rows.outs = 1


def spread_heads_kernel(value_slot, s_ref, *refs):
    k = pl.program_id(0)
    heads_ref, mixer_ref = refs[8:]
    for slot in range(2):
        r = k ^ s_ref[slot * value_slot]
        for a in range(4):
            piece = refs[4 * slot + a]

            @pl.when(r // 2 == a)
            def _(slot=slot, piece=piece):
                if slot == 0:
                    heads_ref[:2] = piece[0].astype(F32)
                else:
                    heads_ref[2] = piece[0, 0].astype(F32)
                    mixer_ref[...] = piece[0, 1].astype(F32).T


def spread_heads(places, value_slot, queries, values, model, width):
    tail = (2, model // 8, width)

    def spec(slot, a):
        def at(k, s):
            r = k ^ s[slot]
            return (jnp.where(r // 2 == a, r % 2, 0), 0, 0, 0)

        return pl.BlockSpec((1, *tail), at)

    return pl.pallas_call(
        functools.partial(spread_heads_kernel, value_slot),
        grid_spec=pltpu.PrefetchScalarGridSpec(
            num_scalar_prefetch=1, grid=(8,),
            in_specs=[spec(slot * value_slot, a) for slot in range(2) for a in range(4)],
            out_specs=[
                pl.BlockSpec((3, model // 8, width), lambda k, s: (0, k, 0)),
                pl.BlockSpec((width, model // 8), lambda k, s: (0, k)),
            ],
        ),
        out_shape=[jax.ShapeDtypeStruct((3, model, width), F32), jax.ShapeDtypeStruct((width, model), F32)],
        cost_estimate=cost(0, 12 * 8 * math.prod(tail)),
        name="spread_heads",
    )(places, *queries, *values)


def normalize(values):
    return row_norm(values)


def norm_back(grad_norm, normed, inverse):
    return inverse * (
        grad_norm
        - jnp.mean(grad_norm, axis=-1, keepdims=True)
        - normed * jnp.mean(grad_norm * normed, axis=-1, keepdims=True)
    )


def gelu_back(expanded, grad_active):
    pull = jax.vjp(lambda value: jax.nn.gelu(value, approximate=True), expanded)[1]
    return pull(grad_active)[0]


def swap(x):
    return lax.ppermute(x, "mp", [(0, 1), (1, 0)])


def keep_valid(x, places, length):
    return jnp.where((places < length)[:, None], x, jnp.zeros_like(x))


def tie(x, *others):
    return lax.optimization_barrier((x, *others))[0]


class Line:
    def __init__(self):
        self.last = None

    def __call__(self, step, *args):
        if self.last is not None:
            args, _ = lax.optimization_barrier((args, self.last))
        out = step(*args)
        self.last = jax.tree.leaves(out)
        return out


def halve(stay, got):
    n = stay.shape[0] // 2
    return add_low(stay[n:], got[n:]), add_low(stay[:n], got[:n])


def join(a, b):
    return jnp.concatenate([a, b], axis=0)


class Sum:
    def __init__(self, line, stages):
        self.line, self.stages = line, stages

    def begin(self, send, stay):
        self.stay, self.got = stay, trade(send, self.stages[0])

    def first(self, *after):
        out, self.stay = self.line(halve, self.stay, self.got)
        self.got = trade(tie(out, *after) if after else out, self.stages[1])

    def second(self):
        out, self.stay = self.line(halve, self.stay, self.got)
        self.got = trade(out, self.stages[2])

    def third(self):
        self.stay = self.line(add_low, self.stay, self.got)
        self.got = trade(self.stay, self.stages[3])

    def fourth(self):
        self.done = self.line(add_low, self.stay, self.got)
        self.got = trade(self.done, self.stages[2])

    def fifth(self):
        self.near = self.line(join, self.done, self.got)
        self.far = trade(self.near, self.stages[1])
        self.near_other = trade(self.near, self.stages[0])

    def sixth(self):
        self.far_other = trade(tie(self.far, self.line.last), self.stages[0])

    def pieces(self):
        return self.near, self.far, self.near_other, self.far_other


class Held:
    pass


def paired(
    tokens, lengths, first_gain, first_shift, heads_weight, relative_bias, mixer_weight, second_gain,
    second_shift, expand_weight, expand_bias, reduce_weight, reduce_bias, cotangent,
):
    member = lax.axis_index("mp")
    index = lax.axis_index("dp")
    core = index % 2
    length = lengths[0]
    own, model = tokens.shape
    buckets = relative_bias.shape[1]
    width = heads_weight.shape[2]
    hidden = expand_bias.shape[0]
    sp = jnp.stack([member.astype(jnp.int32), length.astype(jnp.int32)])
    at = jnp.stack([place_of(index, s).astype(jnp.int32) for s in STAGES])
    places = member * own + jnp.arange(own)
    places_other = (1 - member) * own + jnp.arange(own)
    row = lambda v: v.reshape(1, -1)
    line = Line()
    v = Held()
    reduce_sum, expand_sum = Sum(line, STAGES[0]), Sum(line, STAGES[0])
    query_sum, value_sum = Sum(line, STAGES[0]), Sum(line, STAGES[0])

    rows = bias_rows(relative_bias)
    target0 = keep_valid(cotangent, places, length)
    other = swap(tokens)

    def project_own():
        v.low0, v.projected0 = line(project, tokens, row(first_gain), row(first_shift), heads_weight)

    def project_other():
        v.low1, v.projected1 = line(project, other, row(first_gain), row(first_shift), heads_weight)

    active_grad = lambda t, w: columns_dot(t, w, 1, name="active_grad")

    def active_own():
        v.active_grad0 = line(active_grad, target0, reduce_weight)

    def send_more():
        n = width // 2
        half = lax.dynamic_slice_in_dim(mixer_weight, core * n, n, 0)
        ready = line.last
        v.cotangent_other = swap(tie(cotangent, other, *ready))
        v.mixer_half = swap(tie(half, other, *ready))

    def attend():
        v.mixed, v.logsum = line(attend_forward, sp, v.projected0, v.projected1, rows)
        v.mixed_other = swap(v.mixed)

    def active_other():
        v.target1 = line(lambda x: keep_valid(x, places_other, length), v.cotangent_other)
        v.active_grad1 = line(active_grad, v.target1, reduce_weight)

    def mixer_rest():
        v.mixer_rest = trade(tie(v.mixer_half, *line.last), 1)

    def mixer_both():
        a, b = v.mixer_half, v.mixer_rest
        v.mixer_other = line(order_rows, core.astype(jnp.int32).reshape(1), a, b)

    def mix_rows():
        v.middle, v.second = line(
            mix, tokens, other, v.mixed, v.mixed_other, mixer_weight, v.mixer_other,
            row(second_gain), row(second_shift),
        )

    def expand_other():
        v.act1, v.ge1, gs1, v.eb1 = line(
            lambda x, g, w, b: expand(x, 1, own, g, w, b, BF16),
            v.second, v.active_grad1, expand_weight, row(expand_bias),
        )
        v.gs_got = swap(gs1)

    def expand_own():
        v.act0, v.ge0, v.gs0, v.eb0 = line(
            lambda x, g, w, b: expand(x, 0, own, g, w, b, F32),
            v.second, v.active_grad0, expand_weight, row(expand_bias),
        )

    def reduce_chunks():
        reduce_sum.begin(*line(
            lambda *xs: reduce_grad_part(at, 0, *xs), v.act0, v.act1, target0, v.target1
        ))

    def expand_chunks():
        expand_sum.begin(*line(lambda *xs: expand_grad_part(at, 0, *xs), v.second, v.ge0, v.ge1))

    def middle_back():
        v.grad_middle, v.attended0, v.second_sums = line(
            lambda *xs: back_rows(*xs, True), v.gs0, v.gs_got, v.middle, target0, row(second_gain)
        )

    grad_mix = lambda a, w: dot(a, w, 1, 1).astype(BF16)

    def mixed_send():
        out = line(grad_mix, v.attended0, v.mixer_other)
        v.grad_mixed1 = swap(out)

    def mixed_own():
        v.grad_mixed0 = line(grad_mix, v.attended0, mixer_weight)

    def attended_send():
        v.attended1 = swap(tie(v.attended0, *line.last))

    def reduced_other():
        out = line(lambda a, w: columns_dot(a, w, 0, name="reduced"), v.act1, reduce_weight)
        v.reduced_got = swap(out)

    def attend_back():
        v.grad_projected, v.sums = line(
            attend_backward, sp, v.projected0, v.projected1, v.grad_mixed0, v.grad_mixed1,
            v.mixed, v.logsum, rows,
        )

    def query_chunks():
        query_sum.begin(*line(lambda *xs: heads_grad_part(at, 0, *xs), v.low0, v.low1, v.grad_projected))

    def value_chunks():
        value_sum.begin(*line(
            lambda *xs: values_grad_part(at, 0, *xs), v.low0, v.low1, v.grad_projected,
            v.attended0, v.attended1, v.mixed,
        ))

    def first_other():
        out = line(lambda g, w: first_rows(g, w, 1, own, BF16), v.grad_projected, heads_weight)
        v.first_got = swap(out)

    def first_own():
        v.first_part = line(lambda g, w: first_rows(g, w, 0, own, F32), v.grad_projected, heads_weight)

    def first_back():
        v.tokens_grad, first_sums = line(
            lambda *xs: back_rows(*xs, False), v.first_part, v.first_got, tokens, v.grad_middle, row(first_gain)
        )
        v.both = join(first_sums[:2], v.second_sums[:3])
        v.both_got = swap(v.both)

    def output():
        v.block_out = line(
            output_rows, v.middle, v.act0, reduce_weight, v.reduced_got, row(reduce_bias)
        )

    def pack_first():
        v.pack = line(
            lambda both, got, eb0, eb1, bias: jnp.concatenate(
                [(both + got).reshape(-1), (eb0 + eb1).reshape(-1), bias.reshape(-1)]
            ).reshape(-1, 128),
            v.both, v.both_got, v.eb0, v.eb1, bias_grad(v.sums, buckets),
        )
        v.pack_got = trade(v.pack, 1)

    def pack_next(bit):
        def step():
            v.pack = line(jnp.add, v.pack, v.pack_got)
            if bit:
                v.pack_got = trade(v.pack, bit)

        return step

    chunk = (hidden // 8, model)
    turned = (model, hidden // 8)

    def reduce_spread():
        (v.reduce_grad,) = line(
            lambda *xs: spread(
                at, 0, xs, put_rows, chunk, [lambda to: pl.BlockSpec(chunk, lambda g, s: (to(g, s), 0))],
                [jax.ShapeDtypeStruct(reduce_weight.shape, F32)], name="spread_reduce",
            ),
            *reduce_sum.pieces(),
        )

    def expand_spread():
        (v.expand_grad,) = line(
            lambda *xs: spread(
                at, 0, xs, put_rows, turned, [lambda to: pl.BlockSpec(turned, lambda g, s: (0, to(g, s)))],
                [jax.ShapeDtypeStruct(expand_weight.shape, F32)], name="spread_expand",
            ),
            *expand_sum.pieces(),
        )

    def heads_spread():
        v.heads_grad, v.mixer_grad = line(
            lambda *xs: spread_heads(at, 0, xs[:4], xs[4:], model, width), *query_sum.pieces(), *value_sum.pieces()
        )

    order = (
        project_own, active_own, send_more, project_other, attend, mixer_rest, mixer_both, active_other,
        mix_rows, expand_other, expand_own, reduce_chunks, middle_back, mixed_send, expand_chunks,
        attended_send, mixed_own, reduce_sum.first, expand_sum.first, attend_back, reduce_sum.second,
        query_chunks, reduce_sum.third, value_chunks, first_other, expand_sum.second, reduce_sum.fourth,
        query_sum.first, value_sum.first, expand_sum.third, reduce_sum.fifth, query_sum.second,
        value_sum.second, first_own, first_back, expand_sum.fourth, pack_first, reduce_sum.sixth, pack_next(2),
        value_sum.third, expand_sum.fifth, query_sum.third, reduced_other, value_sum.fourth, reduce_spread,
        query_sum.fourth, expand_sum.sixth, pack_next(4), value_sum.fifth, query_sum.fifth, output,
        value_sum.sixth, expand_spread, pack_next(8), query_sum.sixth, pack_next(0), heads_spread,
    )
    for step in order:
        step()
    pack = v.pack.reshape(-1)
    both = pack[: 5 * model].reshape(5, model)
    expand_bias_grad = pack[5 * model : 5 * model + hidden]
    bias_part = pack[5 * model + hidden :].reshape(relative_bias.shape)
    return (
        v.block_out, v.tokens_grad, both[0], both[1], v.heads_grad, bias_part, v.mixer_grad, both[2], both[3],
        v.expand_grad, expand_bias_grad, v.reduce_grad, both[4],
    )


def gathered(
    tokens, lengths, first_gain, first_shift, heads_weight, relative_bias, mixer_weight, second_gain,
    second_shift, expand_weight, expand_bias, reduce_weight, reduce_bias, cotangent,
):
    def gather(x):
        return lax.all_gather(x, "mp", axis=0, tiled=True)

    def scatter(x):
        return lax.psum_scatter(x.astype(BF16), "mp", scatter_dimension=0, tiled=True).astype(F32)

    members = lax.axis_size("mp")
    length = lengths[0]
    own = tokens.shape[0]
    whole = own * members
    half = whole // 2
    buckets = relative_bias.shape[1]
    sp = jnp.stack([jnp.zeros((), jnp.int32), length.astype(jnp.int32)])
    places = lax.axis_index("mp") * own + jnp.arange(own)
    rows = bias_rows(relative_bias)
    source_all = gather(tokens)
    first_all, projected = project(source_all, first_gain.reshape(1, -1), first_shift.reshape(1, -1), heads_weight)
    projected0, projected1 = projected[:, :half], projected[:, half:]
    mixed, logsum = attend_forward(sp, projected0, projected1, rows)
    source = tokens.astype(F32)
    middle = source + scatter(dot(mixed, mixer_weight, 1, 0))
    second_norm, second_inverse = normalize(middle)
    second_all = gather((second_norm * second_gain + second_shift).astype(BF16))
    target = keep_valid(cotangent, places, length)
    target_wide = target.astype(F32)
    target_all = gather(target)
    expanded = dot(second_all, expand_weight, 1, 0) + expand_bias
    active_low = jax.nn.gelu(expanded, approximate=True).astype(BF16)
    grad_expanded = gelu_back(expanded, dot(target_all, reduce_weight, 1, 1)).astype(BF16)
    grad_second = scatter(dot(grad_expanded, expand_weight, 1, 1))
    reduced = scatter(dot(active_low, reduce_weight, 1, 0))
    reduce_grad = dot(active_low, target_all, 0, 0)
    expand_grad = dot(second_all, grad_expanded, 0, 0)
    expand_bias_grad = jnp.sum(grad_expanded.astype(F32), axis=0)
    block_out = (middle + reduced + reduce_bias).astype(BF16)
    grad_middle = target_wide + norm_back(grad_second * second_gain, second_norm, second_inverse)
    attended_all = gather(grad_middle.astype(BF16))
    mixer_grad = dot(mixed, attended_all, 0, 0)
    grad_mixed = dot(attended_all, mixer_weight, 1, 1).astype(BF16)
    grad_projected, sums = attend_backward(
        sp, projected0, projected1, grad_mixed[:half], grad_mixed[half:], mixed, logsum, rows
    )
    bias_part = bias_grad(sums, buckets)
    heads_grad = jnp.einsum("td,cte->cde", first_all, grad_projected, preferred_element_type=F32)
    grad_first = scatter(jnp.einsum("cte,cde->td", grad_projected, heads_weight, preferred_element_type=F32))
    first_norm, first_inverse = normalize(source)
    tokens_grad = (
        grad_middle + norm_back(grad_first * first_gain, first_norm, first_inverse)
    ).astype(BF16)
    first_gain_grad, first_shift_grad, second_gain_grad, second_shift_grad, reduce_bias_grad = (
        lax.psum(
            (
                jnp.sum(grad_first * first_norm, axis=0),
                jnp.sum(grad_first, axis=0),
                jnp.sum(grad_second * second_norm, axis=0),
                jnp.sum(grad_second, axis=0),
                jnp.sum(target_wide, axis=0),
            ),
            ("dp", "mp"),
        )
    )
    heads_grad, bias_part, mixer_grad, expand_grad, expand_bias_grad, reduce_grad = (
        lax.psum(x.astype(BF16), "dp").astype(F32)
        for x in (heads_grad, bias_part, mixer_grad, expand_grad, expand_bias_grad, reduce_grad)
    )
    return (
        block_out, tokens_grad, first_gain_grad, first_shift_grad, heads_grad, bias_part, mixer_grad,
        second_gain_grad, second_shift_grad, expand_grad, expand_bias_grad, reduce_grad, reduce_bias_grad,
    )


def per_device(*args):
    if lax.axis_size("mp") == 2 and lax.axis_size("dp") == 16:
        return paired(*args)
    return gathered(*args)


def solution(mesh):
    return jax.shard_map(
        per_device,
        mesh=mesh,
        in_specs=(
            P(("dp", "mp"), None),
            P("dp"),
            P(),
            P(),
            P(None, None, "mp"),
            P("mp", None),
            P("mp", None),
            P(),
            P(),
            P(None, "mp"),
            P("mp"),
            P("mp", None),
            P(),
            P(("dp", "mp"), None),
        ),
        out_specs=(
            P(("dp", "mp"), None),
            P(("dp", "mp"), None),
            P(),
            P(),
            P(None, None, "mp"),
            P("mp", None),
            P("mp", None),
            P(),
            P(),
            P(None, "mp"),
            P("mp"),
            P("mp", None),
            P(),
        ),
        check_vma=False,
    )
```

```python
import functools
import math

import jax
import jax.numpy as jnp
import numpy as np
from jax import lax
from jax.experimental import pallas as pl
from jax.experimental.pallas import tpu as pltpu
from jax.sharding import PartitionSpec as P

EPS = 1e-05
DH=64; MAXDIST=128; NEG=-1e30; BLK=256
F32=jnp.float32; BF16=jnp.bfloat16
HIGHEST=lax.Precision.HIGHEST

def bucket_table(count, buckets, reach):
    exact = buckets // 2
    entries = []
    for position in range(count):
        if position < exact:
            entries.append(position)
        else:
            level = exact + int(math.log(position / exact) / math.log(reach / exact) * (buckets - exact))
            entries.append(min(buckets - 1, level))
    return np.array(entries, dtype=np.int32)

def bucket_starts(buckets):
    table=bucket_table(4*MAXDIST+2*buckets,buckets,MAXDIST)
    return [int(np.argmax(table>=level)) for level in range(1,buckets)]

def bias_rows_kernel(r_ref,o_ref):
    heads,buckets=r_ref.shape
    W=2*BLK
    rel=r_ref[...]-r_ref[:,buckets-1:]
    place=lax.broadcasted_iota(jnp.int32,(heads,W),1)
    signed=jnp.where(place<BLK,place,place-W)
    for part,distance in enumerate((-signed,BLK-signed,signed,BLK+signed)):
        value=jnp.broadcast_to(rel[:,:1],(heads,W))
        for level,start in enumerate(bucket_starts(buckets)):
            value=jnp.where(distance>=start,rel[:,level+1:level+2],value)
        value=jnp.where(distance>=0,value,NEG)
        for pair in range(heads//2):
            o_ref[pair,:,part*W:(part+1)*W]=value[2*pair:2*pair+2]

def bias_rows(relative_bias):
    heads=relative_bias.shape[0]
    return pl.pallas_call(
        bias_rows_kernel,
        out_shape=jax.ShapeDtypeStruct((heads//2,2,8*BLK),F32),
        name="bias_rows",
    )(relative_bias)

def toeplitz(row):
    wide=jnp.broadcast_to(row,(BLK,2*BLK))
    return pltpu.roll(wide,0,1,stride=1,stride_axis=0)[:,:BLK]


def lane_masks():
    lane=lax.broadcasted_iota(jnp.int32,(1,128),1)
    head=[(lane//DH)==h for h in range(2)]
    mine=[jnp.where(m,1.0,0.0).astype(BF16) for m in head]
    spare=[jnp.where(lane==DH*(1-h),1.0,0.0) for h in range(2)]
    return head,mine,spare


def gone_rows(start,half,length,spare):
    pos=lax.broadcasted_iota(jnp.int32,(half,1),0)+start
    gone=jnp.where(pos<length,0.0,NEG)
    return [(gone*s).astype(BF16) for s in spare]


def fwd_kernel(sp, a_ref,c_ref,b_ref,o_ref,lse_ref,qs,ks,vs):
    half=a_ref.shape[1]; T=2*half; flip=sp[0]; length=sp[1]
    W=2*BLK
    head,mine,spare=lane_masks()
    for a,ref in enumerate((a_ref,c_ref)):
        start=pl.multiple_of((a^flip)*half,half)
        dst=pl.ds(start,half)
        gone=gone_rows(start,half,length,spare)
        for h in range(2):
            qs[h,dst,:]=ref[0]*(mine[h]*jnp.asarray(DH**-0.5,BF16))+spare[h].astype(BF16)
            ks[h,dst,:]=ref[1]*mine[h]+gone[h]
            vs[h,dst,:]=ref[2]*mine[h]+mine[1-h]
    tiles=[(toeplitz(b_ref[0,h:h+1,0:W]),toeplitz(b_ref[0,h:h+1,W:2*W])) for h in range(2)]
    outs={}

    def score(i,h):
        return dot(qs[h,i*BLK:(i+1)*BLK,:],ks[h,:(i+1)*BLK,:],1,1)

    def finish(i,h,s):
        kc=(i+1)*BLK; t0,t1=tiles[h]
        parts=[]
        if i>=2: parts.append(s[:,:kc-2*BLK])
        if i>=1: parts.append(s[:,kc-2*BLK:kc-BLK]+t1)
        parts.append(s[:,kc-BLK:]+t0)
        top=functools.reduce(jnp.maximum,[jnp.max(x,axis=1,keepdims=True) for x in parts])
        p=jnp.concatenate([jnp.exp(x-top).astype(BF16) for x in parts],axis=1)
        o=dot(p,vs[h,:kc,:],1,0)
        total=o[:,DH*(1-h):DH*(1-h)+1]
        outs[h]=(o*(1.0/total),top+jnp.log(total))
        if h==1:
            rows=pl.ds(pl.multiple_of((i*BLK+flip*half)%T,BLK),BLK)
            o_ref[rows,:]=jnp.where(head[0],outs[0][0],outs[1][0]).astype(BF16)
            lse_ref[0,i*BLK:kc,:]=jnp.where(head[0],outs[0][1],outs[1][1])

    run_ahead([(i,h) for i in range(T//BLK) for h in range(2)],score,finish,2)


def run_ahead(items,first,second,depth):
    waiting=[]
    for item in items:
        waiting.append((item,first(*item)))
        if len(waiting)>depth:
            done,value=waiting.pop(0)
            second(*done,value)
    for done,value in waiting:
        second(*done,value)


def attend_forward(sp,projected0,projected1,rows):
    _,half,HD=projected0.shape; pairs=HD//128; T=2*half
    part=pl.BlockSpec((3,half,128),lambda p,s:(0,0,p))
    return pl.pallas_call(
        fwd_kernel,
        grid_spec=pltpu.PrefetchScalarGridSpec(
            num_scalar_prefetch=1,grid=(pairs,),
            in_specs=[part,part,pl.BlockSpec((1,2,rows.shape[2]),lambda p,s:(p,0,0))],
            out_specs=[pl.BlockSpec((T,128),lambda p,s:(0,p)),pl.BlockSpec((1,T,128),lambda p,s:(p,0,0))],
            scratch_shapes=[pltpu.VMEM((2,T,128),BF16)]*3),
        out_shape=[jax.ShapeDtypeStruct((T,HD),BF16),jax.ShapeDtypeStruct((pairs,T,128),F32)],
        cost_estimate=cost(8*T*T*HD,8*T*HD+512*pairs*T),
        name="attend_forward",
    )(sp,projected0,projected1,rows)

def diagonal_sums(acc, offset):
    W=2*BLK
    wide=jnp.concatenate([acc,jnp.zeros_like(acc)],axis=1)
    n=BLK
    while n>1:
        n//=2
        top=wide[:n]; bottom=wide[n:2*n]
        wide=top+pltpu.roll(bottom,W-n,1)
    return pltpu.roll(wide,offset,1) if offset else wide

def bwd_kernel(sp, a_ref,c_ref,d0_ref,d1_ref,o_ref,lse_ref,b_ref,g_ref,d_ref,qs,ks,vs,dos,dq,acc0,acc1):
    half=a_ref.shape[1]; T=2*half; flip=sp[0]; length=sp[1]
    W=2*BLK
    n=T//BLK
    head,mine,spare=lane_masks()
    stats=[None,None]
    one=sum(spare).astype(BF16)
    for a,(ref,do_ref) in enumerate(((a_ref,d0_ref),(c_ref,d1_ref))):
        start=pl.multiple_of((a^flip)*half,half)
        dst=pl.ds(start,half)
        gone=gone_rows(start,half,length,spare)
        for h in range(2):
            qs[h,dst,:]=ref[0]*(mine[h]*jnp.asarray(DH**-0.5,BF16))+spare[h].astype(BF16)
            ks[h,dst,:]=ref[1]*mine[h]+gone[h]
            vs[h,dst,:]=ref[2]*mine[h]
        dos[dst,:]=do_ref[...]
        acc0[0,dst,:]=do_ref[...].astype(F32)*o_ref[a*half:(a+1)*half,:].astype(F32)
    turned=acc0[0].T
    deltas=[jnp.sum(turned[h*DH:(h+1)*DH],axis=0,keepdims=True) for h in range(2)]
    turned=lse_ref[0].T
    lses=[turned[h*DH:h*DH+1] for h in range(2)]
    near=acc1
    tiles=[(toeplitz(b_ref[0,h:h+1,2*W:3*W]),toeplitz(b_ref[0,h:h+1,3*W:])) for h in range(2)]

    def products(j,h):
        rj=slice(j*BLK,(j+1)*BLK)
        return dot(ks[h,rj,:],qs[h,j*BLK:,:],1,1),dot(vs[h,rj,:],dos[j*BLK:,:],1,1)

    keep={}

    def finish(j,h,value):
        s,dp=value
        rj=slice(j*BLK,(j+1)*BLK)
        ps=[];dss=[]
        for b in range(n-j):
            c=slice(b*BLK,(b+1)*BLK)
            cc=slice((j+b)*BLK,(j+b+1)*BLK)
            x=s[:,c]-lses[h][:,cc]
            if b<2: x=x+tiles[h][b]
            p=jnp.exp(x)
            ds=p*(dp[:,c]-deltas[h][:,cc])
            if b<2:
                if j==0: near[h,b]=ds
                else: near[h,b]+=ds
            ps.append(p.astype(BF16)); dss.append(ds.astype(BF16))
        p=jnp.concatenate(ps,axis=1); ds=jnp.concatenate(dss,axis=1)
        dv=dot(p,dos[j*BLK:,:],1,0)
        dk=dot(ds,qs[h,j*BLK:,:],1,0)
        kk=ks[h,rj,:]*mine[h]+mine[1-h]
        dqj=dot(ds,kk,0,0)
        if j==0: dq[h,:,:]=dqj
        else: dq[h,j*BLK:,:]+=dqj
        keep[h]=(dk,dv)
        if h==1:
            rows=pl.ds(pl.multiple_of((j*BLK+flip*half)%T,BLK),BLK)
            g_ref[1,rows,:]=jnp.where(head[0],keep[0][0],keep[1][0]).astype(BF16)
            g_ref[2,rows,:]=jnp.where(head[0],keep[0][1],keep[1][1]).astype(BF16)

    run_ahead([(j,h) for j in range(n) for h in range(2)],products,finish,1)
    for h in range(2):
        d_ref[0,h:h+1,:]=diagonal_sums(near[h,0],0)+diagonal_sums(near[h,1],BLK)
        total=jnp.sum(dq[h,:,:],axis=0,keepdims=True)[:,DH*(1-h):DH*(1-h)+1]
        d_ref[0,2+h:3+h,:]=jnp.broadcast_to(total,(1,W))
    for a in range(2):
        dst=pl.ds(pl.multiple_of((a^flip)*half,half),half)
        g_ref[0,a*half:(a+1)*half,:]=(jnp.where(head[0],dq[0,dst,:],dq[1,dst,:])*DH**-0.5).astype(BF16)

def attend_backward(sp,projected0,projected1,grad0,grad1,mixed,lse,rows,start=0,count=None,given=None):
    _,half,HD=projected0.shape; pairs=HD//128; T=2*half
    count=pairs if count is None else count
    part=pl.BlockSpec((3,half,128),lambda p,s:(0,0,p+start))
    grad=pl.BlockSpec((half,128),lambda p,s:(0,p+start))
    in_specs=[part,part,grad,grad,pl.BlockSpec((T,128),lambda p,s:(0,p+start)),
              pl.BlockSpec((1,T,128),lambda p,s:(p+start,0,0)),pl.BlockSpec((1,2,rows.shape[2]),lambda p,s:(p+start,0,0))]
    args=[sp,projected0,projected1,grad0,grad1,mixed,lse,rows]
    kernel=bwd_kernel
    if given is not None:
        in_specs.append(pl.BlockSpec(memory_space=pl.ANY)); args.append(given)
        kernel=lambda *refs: bwd_kernel(*refs[:8],*refs[9:])
    return pl.pallas_call(
        kernel,
        grid_spec=pltpu.PrefetchScalarGridSpec(
            num_scalar_prefetch=1,grid=(count,),
            in_specs=in_specs,
            out_specs=[pl.BlockSpec((3,T,128),lambda p,s:(0,0,p+start)),pl.BlockSpec((1,4,2*BLK),lambda p,s:(p,0,0))],
            scratch_shapes=[pltpu.VMEM((2,T,128),BF16)]*3+[pltpu.VMEM((T,128),BF16),pltpu.VMEM((2,T,128),F32),pltpu.VMEM((1,T,128),F32),pltpu.VMEM((2,2,BLK,BLK),F32)]),
        out_shape=[jax.ShapeDtypeStruct((3,T,HD),BF16),jax.ShapeDtypeStruct((count,4,2*BLK),F32)],
        input_output_aliases={} if given is None else {8:0},
        cost_estimate=cost(20*T*T*128*count,(16*T*128+512*T)*count),
        name="attend_backward",
    )(*args)

def bias_grad(sums, buckets):
    pairs=sums.shape[0]; W=2*BLK
    near=sums[:,0:2].reshape(pairs*2,W); total=sums[:,2:4,0].reshape(pairs*2,1)
    edges=[0]+bucket_starts(buckets)
    distance=jnp.arange(W)[None,None]
    low=jnp.asarray(np.array(edges[:-1],np.int32))[None,:,None]
    high=jnp.asarray(np.array(edges[1:],np.int32))[None,:,None]
    parts=jnp.sum(jnp.where((distance>=low)&(distance<high),near[:,None,:],0.0),axis=2)
    return jnp.concatenate([parts,total-jnp.sum(parts,axis=1,keepdims=True)],axis=1)


HALF_TANH = math.sqrt(2.0 / math.pi)


def dot(a, b, ca, cb):
    return lax.dot_general(a, b, (((ca,), (cb,)), ((), ())), preferred_element_type=F32)


def fixed(shape):
    return pl.BlockSpec(shape, lambda *_: (0,) * len(shape))


def cost(flops, moved):
    return pl.CostEstimate(flops=int(flops), transcendentals=0, bytes_accessed=int(moved))


def cost4(flops, moved):
    return cost(4 * flops, 4 * moved)


def cost16(flops, moved):
    return cost(16 * flops, 16 * moved)


def row_norm(values):
    center = jnp.mean(values, axis=-1, keepdims=True)
    centered = values - center
    inverse = lax.rsqrt(jnp.mean(centered * centered, axis=-1, keepdims=True) + EPS)
    return centered * inverse, inverse


def project_kernel(x_ref, gain_ref, shift_ref, w_ref, low_ref, out_ref):
    normed, _ = row_norm(x_ref[...].astype(F32))
    low = (normed * gain_ref[...] + shift_ref[...]).astype(BF16)
    low_ref[...] = low
    for c in range(3):
        out_ref[c] = dot(low, w_ref[c], 1, 0).astype(BF16)


def project(x, gain, shift, weight):
    rows, model = x.shape
    width = weight.shape[2]
    step = min(256, rows)
    return pl.pallas_call(
        project_kernel,
        grid=(rows // step,),
        in_specs=[pl.BlockSpec((step, model), lambda i: (i, 0)), fixed((1, model)), fixed((1, model)), fixed(weight.shape)],
        out_specs=[pl.BlockSpec((step, model), lambda i: (i, 0)), pl.BlockSpec((3, step, width), lambda i: (0, i, 0))],
        out_shape=[jax.ShapeDtypeStruct((rows, model), BF16), jax.ShapeDtypeStruct((3, rows, width), BF16)],
        cost_estimate=cost(6 * rows * model * width, 2 * (2 * rows * model + weight.size + 3 * rows * width)),
        name="project",
    )(x, gain, shift, weight)


def mix_kernel(own_blocks, x0_ref, x1_ref, m_ref, p_ref, w0_ref, w1_ref, gain_ref, shift_ref, mid_ref, low_ref):
    i = pl.program_id(0)
    attended = dot(m_ref[...], w0_ref[...], 1, 0) + dot(p_ref[...], w1_ref[...], 1, 0)

    def rows(x_ref):
        return x_ref[...].astype(F32) + attended

    def rest(middle):
        normed, _ = row_norm(middle)
        low_ref[...] = (normed * gain_ref[...] + shift_ref[...]).astype(BF16)

    @pl.when(i < own_blocks)
    def _():
        middle = rows(x0_ref)
        mid_ref[...] = middle.astype(BF16)
        rest(middle)

    @pl.when(i >= own_blocks)
    def _():
        rest(rows(x1_ref))


def mix(tokens, other, mixed, mixed_other, weight, weight_other, gain, shift):
    own, model = tokens.shape
    width = mixed.shape[1]
    step = 256
    n = own // step
    return pl.pallas_call(
        functools.partial(mix_kernel, n),
        grid=(2 * n,),
        in_specs=[
            pl.BlockSpec((step, model), lambda i: (jnp.minimum(i, n - 1), 0)),
            pl.BlockSpec((step, model), lambda i: (jnp.maximum(i - n, 0), 0)),
            pl.BlockSpec((step, width), lambda i: (i, 0)),
            pl.BlockSpec((step, width), lambda i: ((i + n) % (2 * n), 0)),
            fixed(weight.shape), fixed(weight.shape), fixed((1, model)), fixed((1, model)),
        ],
        out_specs=[
            pl.BlockSpec((step, model), lambda i: (jnp.minimum(i, n - 1), 0)),
            pl.BlockSpec((step, model), lambda i: (i, 0)),
        ],
        out_shape=[jax.ShapeDtypeStruct((own, model), BF16), jax.ShapeDtypeStruct((2 * own, model), BF16)],
        cost_estimate=cost(8 * own * model * width, 2 * (4 * own * model + 4 * own * width + 2 * weight.size) + 4 * own * model),
        name="mix",
    )(tokens, other, mixed, mixed_other, weight, weight_other, gain, shift)


def expand_kernel(x_ref, g_ref, w_ref, b_ref, act_ref, ge_ref, gs_ref, bias_ref, acc_ref):
    i = pl.program_id(0)
    x = x_ref[...]
    width = w_ref.shape[1]
    sub = min(512, width)
    total = None
    for s in range(width // sub):
        cols = slice(s * sub, (s + 1) * sub)
        u = dot(x, w_ref[:, cols], 1, 0) + b_ref[:, cols].astype(F32)
        square = u * u
        t = jnp.tanh(HALF_TANH * u * (1.0 + 0.044715 * square))
        half = 0.5 + 0.5 * t
        act_ref[:, cols] = (u * half).astype(BF16)
        slope = half + 0.5 * u * (1.0 - t * t) * (HALF_TANH * (1.0 + 3 * 0.044715 * square))
        grad = g_ref[:, cols].astype(F32) * slope
        low = grad.astype(BF16)
        ge_ref[:, cols] = low
        bias_ref[:, cols] = jnp.sum(grad, axis=0, keepdims=True)
        part = dot(low, w_ref[:, cols], 1, 1)
        total = part if total is None else total + part

    @pl.when(i == 0)
    def _():
        acc_ref[...] = total

    @pl.when(i > 0)
    def _():
        acc_ref[...] += total

    @pl.when(i == pl.num_programs(0) - 1)
    def _():
        gs_ref[...] = acc_ref[...].astype(gs_ref.dtype)


def expand(x, block, rows, grad_active, weight, bias, dtype):
    model = x.shape[1]
    hidden = weight.shape[1]
    step = min(512, hidden)
    return pl.pallas_call(
        expand_kernel,
        grid=(hidden // step,),
        in_specs=[
            pl.BlockSpec((rows, model), lambda i: (block, 0)),
            pl.BlockSpec((rows, step), lambda i: (0, i)),
            pl.BlockSpec((model, step), lambda i: (0, i)),
            pl.BlockSpec((1, step), lambda i: (0, i)),
        ],
        out_specs=[
            pl.BlockSpec((rows, step), lambda i: (0, i)),
            pl.BlockSpec((rows, step), lambda i: (0, i)),
            fixed((rows, model)),
            pl.BlockSpec((1, step), lambda i: (0, i)),
        ],
        out_shape=[
            jax.ShapeDtypeStruct((rows, hidden), BF16),
            jax.ShapeDtypeStruct((rows, hidden), BF16),
            jax.ShapeDtypeStruct((rows, model), dtype),
            jax.ShapeDtypeStruct((1, hidden), F32),
        ],
        scratch_shapes=[pltpu.VMEM((rows, model), F32)],
        cost_estimate=cost(4 * rows * model * hidden, 2 * (2 * rows * model + 3 * rows * hidden + weight.size)),
        name="expand",
    )(x, grad_active, weight, bias)


STAGES = ((1, 2, 4, 8), (1, 4, 2, 8))


def place_of(index, stages):
    bit = [(index // s) % 2 for s in stages]
    return bit[0] * 4 + bit[1] * 2 + bit[2]


def trade(x, bit):
    size = lax.axis_size("dp")
    return lax.ppermute(x, "dp", [(i, i ^ bit) for i in range(size)])


def add_low(a, b):
    return (a.astype(F32) + b.astype(F32)).astype(BF16)


def pair_of(g, s, slot):
    return (3 - g) ^ (s[slot] // 2)


def put_pair(slot, s_ref, chunks, outs):
    flip = s_ref[slot] % 2
    sent = pl.program_id(0) < 2
    for j, value in enumerate(chunks):
        value = value.astype(BF16)[None]
        for out, here in zip(outs, (sent, jnp.logical_not(sent))):
            @pl.when(here)
            def _(out=out):
                out[pl.ds(j ^ flip, 1)] = value


def pair_call(kernel, slot, s, arrays, specs, tail, flops, name):
    zeros = (0,) * len(tail)
    moved = sum(2 * x.size for x in arrays) + 16 * math.prod(tail)
    return pl.pallas_call(
        functools.partial(kernel, slot),
        grid_spec=pltpu.PrefetchScalarGridSpec(
            num_scalar_prefetch=1, grid=(4,), in_specs=specs,
            out_specs=[
                pl.BlockSpec((2, *tail), lambda g, s: (jnp.maximum(1 - g, 0), *zeros)),
                pl.BlockSpec((2, *tail), lambda g, s: (jnp.minimum(3 - g, 1), *zeros)),
            ],
        ),
        out_shape=[jax.ShapeDtypeStruct((4, *tail), BF16)] * 2,
        cost_estimate=cost(flops, moved),
        name=name,
    )(s, *arrays)


def reduce_grad_kernel(slot, s_ref, *refs):
    (a0, a1, t0, t1), outs = refs[:4], refs[4:]
    value = dot(a0[...], t0[...], 0, 0) + dot(a1[...], t1[...], 0, 0)
    width = value.shape[0] // 2
    put_pair(slot, s_ref, [value[:width], value[width:]], outs)


def reduce_grad_part(s, slot, act0, act1, t0, t1):
    rows, hidden = act0.shape
    model = t0.shape[1]
    block = pl.BlockSpec((rows, hidden // 4), lambda g, s: (0, pair_of(g, s, slot)))
    return pair_call(
        reduce_grad_kernel, slot, s, (act0, act1, t0, t1), [block, block, fixed(t0.shape), fixed(t1.shape)],
        (hidden // 8, model), 4 * rows * model * hidden, "reduce_grad",
    )


def expand_grad_kernel(slot, s_ref, *refs):
    (x, g0, g1), outs = refs[:3], refs[3:]
    rows = g0.shape[0]
    value = dot(x[:rows], g0[...], 0, 0) + dot(x[rows:], g1[...], 0, 0)
    width = value.shape[1] // 2
    put_pair(slot, s_ref, [value[:, :width], value[:, width:]], outs)


def expand_grad_part(s, slot, x, g0, g1):
    rows, hidden = g0.shape
    model = x.shape[1]
    block = pl.BlockSpec((rows, hidden // 4), lambda g, s: (0, pair_of(g, s, slot)))
    return pair_call(
        expand_grad_kernel, slot, s, (x, g0, g1), [fixed(x.shape), block, block],
        (model, hidden // 8), 4 * rows * model * hidden, "expand_grad",
    )


def heads_grad_kernel(slot, s_ref, *refs):
    (l0, l1, g), outs = refs[:3], refs[3:]
    rows = l0.shape[0]
    both = [dot(l0[...], g[c, :rows], 0, 0) + dot(l1[...], g[c, rows:], 0, 0) for c in range(2)]
    width = both[0].shape[0] // 2
    chunks = [jnp.stack([v[j * width:(j + 1) * width] for v in both]) for j in range(2)]
    put_pair(slot, s_ref, chunks, outs)


def heads_grad_part(s, slot, low0, low1, grad):
    rows, model = low0.shape
    width = grad.shape[2]
    block = pl.BlockSpec((rows, model // 4), lambda g, s: (0, pair_of(g, s, slot)))
    return pair_call(
        heads_grad_kernel, slot, s, (low0, low1, grad),
        [block, block, pl.BlockSpec((2, 2 * rows, width), lambda g, s: (0, 0, 0))],
        (2, model // 8, width), 8 * rows * model * width, "heads_grad",
    )


def values_grad_kernel(slot, s_ref, *refs):
    (l0, l1, g, a0, a1, m), outs = refs[:6], refs[6:]
    rows = l0.shape[0]
    both = [
        dot(l0[...], g[0, :rows], 0, 0) + dot(l1[...], g[0, rows:], 0, 0),
        dot(a0[...], m[:rows], 0, 0) + dot(a1[...], m[rows:], 0, 0),
    ]
    width = both[0].shape[0] // 2
    chunks = [jnp.stack([v[j * width:(j + 1) * width] for v in both]) for j in range(2)]
    put_pair(slot, s_ref, chunks, outs)


def values_grad_part(s, slot, low0, low1, grad, att0, att1, mixed):
    rows, model = low0.shape
    width = grad.shape[2]
    block = pl.BlockSpec((rows, model // 4), lambda g, s: (0, pair_of(g, s, slot)))
    return pair_call(
        values_grad_kernel, slot, s, (low0, low1, grad, att0, att1, mixed),
        [block, block, pl.BlockSpec((1, 2 * rows, width), lambda g, s: (2, 0, 0)), block, block, fixed(mixed.shape)],
        (2, model // 8, width), 8 * rows * model * width, "values_grad",
    )


def columns_kernel(turn, a_ref, b_ref, out_ref):
    out_ref[...] = dot(a_ref[...], b_ref[...], 1, turn).astype(out_ref.dtype)


def columns_dot(a, b, turn, name):
    rows, depth = a.shape
    columns = b.shape[1 - turn]
    step = min(512, columns)
    block = ((step, depth), lambda i: (i, 0)) if turn else ((depth, step), lambda i: (0, i))
    return pl.pallas_call(
        functools.partial(columns_kernel, turn),
        grid=(columns // step,),
        in_specs=[fixed(a.shape), pl.BlockSpec(*block)],
        out_specs=pl.BlockSpec((rows, step), lambda i: (0, i)),
        out_shape=jax.ShapeDtypeStruct((rows, columns), BF16),
        cost_estimate=cost16(2 * rows * depth * columns, 2 * (a.size + b.size + rows * columns)),
        name=name,
    )(a, b)


def output_kernel(m_ref, a_ref, w_ref, r_ref, bias_ref, out_ref):
    out_ref[...] = (
        m_ref[...].astype(F32) + dot(a_ref[...], w_ref[...], 1, 0) + r_ref[...].astype(F32) + bias_ref[...]
    ).astype(BF16)


def output_rows(middle, act, weight, reduced, bias):
    rows, hidden = act.shape
    model = weight.shape[1]
    step = 256
    block = pl.BlockSpec((rows, step), lambda i: (0, i))
    return pl.pallas_call(
        output_kernel,
        grid=(model // step,),
        in_specs=[
            block, fixed(act.shape), pl.BlockSpec((hidden, step), lambda i: (0, i)), block,
            pl.BlockSpec((1, step), lambda i: (0, i)),
        ],
        out_specs=block,
        out_shape=jax.ShapeDtypeStruct((rows, model), BF16),
        cost_estimate=cost16(2 * rows * hidden * model, 2 * (act.size + weight.size) + 8 * rows * model),
        name="output",
    )(middle, act, weight, reduced, bias)


def first_kernel(g_ref, w_ref, out_ref, acc_ref):
    c = pl.program_id(0)
    value = dot(g_ref[0], w_ref[0], 1, 1)

    @pl.when(c == 0)
    def _():
        acc_ref[...] = value

    @pl.when(c > 0)
    def _():
        acc_ref[...] += value

    @pl.when(c == pl.num_programs(0) - 1)
    def _():
        out_ref[...] = acc_ref[...].astype(out_ref.dtype)


def first_rows(grad, weight, part, rows, dtype):
    kinds, model, width = weight.shape
    return pl.pallas_call(
        first_kernel,
        grid=(kinds,),
        in_specs=[
            pl.BlockSpec((1, rows, width), lambda c: (c, part, 0)),
            pl.BlockSpec((1, model, width), lambda c: (c, 0, 0)),
        ],
        out_specs=fixed((rows, model)),
        out_shape=jax.ShapeDtypeStruct((rows, model), dtype),
        scratch_shapes=[pltpu.VMEM((rows, model), F32)],
        cost_estimate=cost(2 * kinds * rows * width * model, 2 * (grad.size + weight.size) + 4 * rows * model),
        name="first_rows",
    )(grad, weight)


def back_kernel(a_ref, b_ref, source_ref, add_ref, gain_ref, out_ref, sums_ref):
    @pl.when(pl.program_id(0) == 0)
    def _():
        sums_ref[...] = jnp.zeros_like(sums_ref)

    def some(i, _):
        rows = pl.ds(pl.multiple_of(i * 64, 64), 64)
        normed, inverse = row_norm(source_ref[rows, :].astype(F32))
        grad = a_ref[rows, :].astype(F32) + b_ref[rows, :].astype(F32)
        add = add_ref[rows, :].astype(F32)
        scaled = grad * gain_ref[...]
        weighted = grad * normed
        mean = jnp.mean(scaled, axis=-1, keepdims=True)
        along = jnp.mean(scaled * normed, axis=-1, keepdims=True)
        out_ref[rows, :] = (add + inverse * (scaled - mean - normed * along)).astype(BF16)
        for k, value in enumerate((weighted, grad, add)):
            sums_ref[k:k + 1] += jnp.sum(value, axis=0, keepdims=True)
        return 0

    lax.fori_loop(0, source_ref.shape[0] // 64, some, 0)


def back_rows(a, b, source, add, gain):
    rows, model = a.shape
    step = 256
    block = pl.BlockSpec((step, model), lambda i: (i, 0))
    return pl.pallas_call(
        back_kernel,
        grid=(rows // step,),
        in_specs=[block] * 4 + [fixed((1, model))],
        out_specs=[block, fixed((8, model))],
        out_shape=[jax.ShapeDtypeStruct((rows, model), BF16), jax.ShapeDtypeStruct((8, model), F32)],
        cost_estimate=cost(30 * rows * model, 10 * rows * model),
        name="back_rows",
    )(a, b, source, add, gain)


def order_kernel(s_ref, a_ref, b_ref, out_ref):
    @pl.when(pl.program_id(0) == 0)
    def _():
        out_ref[...] = a_ref[...]

    @pl.when(pl.program_id(0) == 1)
    def _():
        out_ref[...] = b_ref[...]


def order_rows(core, a, b):
    rows, model = a.shape
    return pl.pallas_call(
        order_kernel,
        grid_spec=pltpu.PrefetchScalarGridSpec(
            num_scalar_prefetch=1, grid=(2,),
            in_specs=[pl.BlockSpec((rows, model), lambda g, s: (0, 0))] * 2,
            out_specs=pl.BlockSpec((rows, model), lambda g, s: (g ^ s[0], 0)),
        ),
        out_shape=jax.ShapeDtypeStruct((2 * rows, model), a.dtype),
        cost_estimate=cost(0, 8 * rows * model),
        name="order_rows",
    )(core, a, b)


def spread_kernel(put, s_ref, *refs):
    g = pl.program_id(0)
    count = put.pieces
    pieces, outs = refs[-2 * count - put.outs:-put.outs], refs[-put.outs:]
    for a in range(2):
        @pl.when(g // 2 == a)
        def _(a=a):
            put(pieces[a::2], outs)


def spread(places, part, pieces, put, tail, out_specs, out_shape, given=None, name=None):
    zeros = (0,) * len(tail)

    def at(g, s):
        return (g % 2 + 4 * (g // 2) + 2 * part) ^ s[0]

    in_specs = [
        pl.BlockSpec((1, *tail), lambda g, s, a=k % 2: (jnp.clip(g - 2 * a, 0, 1), *zeros)) for k in range(len(pieces))
    ]
    args = list(pieces)
    aliases = {}
    if given is not None:
        in_specs = [pl.BlockSpec(memory_space=pl.ANY)] * len(given) + in_specs
        args = [*given, *args]
        aliases = {1 + k: k for k in range(len(given))}
    return pl.pallas_call(
        functools.partial(spread_kernel, put),
        grid_spec=pltpu.PrefetchScalarGridSpec(
            num_scalar_prefetch=1, grid=(4,), in_specs=in_specs, out_specs=[spec(at) for spec in out_specs],
        ),
        out_shape=out_shape,
        input_output_aliases=aliases,
        cost_estimate=cost(0, 24 * len(pieces) // 2 * math.prod(tail)),
        name=name,
    )(places, *args)


def by_rows(count, step):
    def some(i, _):
        step(pl.ds(pl.multiple_of(i * 64, 64), 64))
        return 0

    lax.fori_loop(0, count // 64, some, 0)


def put_rows(pieces, outs):
    def some(rows):
        outs[0][rows, :] = pieces[0][0, rows, :].astype(F32)

    by_rows(outs[0].shape[0], some)


put_rows.outs = 1
put_rows.pieces = 1


def put_heads(pieces, outs):
    queries, values = pieces

    def some(rows):
        for c in range(2):
            outs[0][c, rows, :] = queries[0, c, rows, :].astype(F32)
        outs[0][2, rows, :] = values[0, 0, rows, :].astype(F32)

    by_rows(outs[0].shape[1], some)
    outs[1][...] = values[0, 1].astype(F32).T


put_heads.outs = 2
put_heads.pieces = 2


def normalize(values):
    return row_norm(values)


def norm_back(grad_norm, normed, inverse):
    return inverse * (
        grad_norm
        - jnp.mean(grad_norm, axis=-1, keepdims=True)
        - normed * jnp.mean(grad_norm * normed, axis=-1, keepdims=True)
    )


def gelu_back(expanded, grad_active):
    pull = jax.vjp(lambda value: jax.nn.gelu(value, approximate=True), expanded)[1]
    return pull(grad_active)[0]


def swap(x):
    return lax.ppermute(x, "mp", [(0, 1), (1, 0)])


def keep_valid(x, places, length):
    return jnp.where((places < length)[:, None], x, jnp.zeros_like(x))


def tie(x, *others):
    return lax.optimization_barrier((x, *others))[0]


class Line:
    def __init__(self):
        self.last = None

    def __call__(self, step, *args):
        if self.last is not None:
            args, _ = lax.optimization_barrier((args, self.last))
        out = step(*args)
        self.last = jax.tree.leaves(out)
        return out


def halve(stay, got):
    n = stay.shape[0] // 2
    return add_low(stay[n:], got[n:]), add_low(stay[:n], got[:n])


def join(a, b):
    return jnp.concatenate([a, b], axis=0)


class Sum:
    def __init__(self, line, stages):
        self.line, self.stages = line, stages

    def begin(self, send, stay):
        self.stay, self.got = stay, trade(send, self.stages[0])

    def first(self, *after):
        out, self.stay = self.line(halve, self.stay, self.got)
        self.got = trade(tie(out, *after) if after else out, self.stages[1])

    def second(self):
        out, self.stay = self.line(halve, self.stay, self.got)
        self.got = trade(out, self.stages[2])

    def third(self):
        self.stay = self.line(add_low, self.stay, self.got)
        self.got = trade(self.stay, self.stages[3])

    def fourth(self):
        self.done = self.line(add_low, self.stay, self.got)
        self.got = trade(self.done, self.stages[2])

    def fifth(self):
        self.near = self.line(join, self.done, self.got)
        self.far = trade(self.near, self.stages[1])
        self.near_other = trade(self.near, self.stages[0])

    def sixth(self):
        self.far_other = trade(tie(self.far, self.line.last), self.stages[0])

    def nears(self):
        return self.near, self.near_other

    def fars(self):
        return self.far, self.far_other


class Held:
    pass


def paired(
    tokens, lengths, first_gain, first_shift, heads_weight, relative_bias, mixer_weight, second_gain,
    second_shift, expand_weight, expand_bias, reduce_weight, reduce_bias, cotangent,
):
    member = lax.axis_index("mp")
    index = lax.axis_index("dp")
    core = index % 2
    length = lengths[0]
    own, model = tokens.shape
    buckets = relative_bias.shape[1]
    width = heads_weight.shape[2]
    hidden = expand_bias.shape[0]
    sp = jnp.stack([member.astype(jnp.int32), length.astype(jnp.int32)])
    at = jnp.stack([place_of(index, s).astype(jnp.int32) for s in STAGES])
    places = member * own + jnp.arange(own)
    places_other = (1 - member) * own + jnp.arange(own)
    row = lambda v: v.reshape(1, -1)
    line = Line()
    v = Held()
    reduce_sum, expand_sum = Sum(line, STAGES[0]), Sum(line, STAGES[0])
    query_sum, value_sum = Sum(line, STAGES[0]), Sum(line, STAGES[0])

    rows = bias_rows(relative_bias)
    target0 = keep_valid(cotangent, places, length)
    other = swap(tokens)

    def project_own():
        v.low0, v.projected0 = line(project, tokens, row(first_gain), row(first_shift), heads_weight)

    def project_other():
        v.low1, v.projected1 = line(project, other, row(first_gain), row(first_shift), heads_weight)

    active_grad = lambda t, w: columns_dot(t, w, 1, name="active_grad")

    def active_own():
        v.active_grad0 = line(active_grad, target0, reduce_weight)

    def send_more():
        n = width // 2
        half = lax.dynamic_slice_in_dim(mixer_weight, core * n, n, 0)
        ready = line.last
        v.cotangent_other = swap(tie(cotangent, other, *ready))
        v.mixer_half = swap(tie(half, other, *ready))

    def attend():
        v.mixed, v.logsum = line(attend_forward, sp, v.projected0, v.projected1, rows)
        v.mixed_other = swap(v.mixed)

    def active_other():
        v.target1 = line(lambda x: keep_valid(x, places_other, length), v.cotangent_other)
        v.active_grad1 = line(active_grad, v.target1, reduce_weight)

    def mixer_rest():
        v.mixer_rest = trade(tie(v.mixer_half, *line.last), 1)

    def mixer_both():
        a, b = v.mixer_half, v.mixer_rest
        v.mixer_other = line(order_rows, core.astype(jnp.int32).reshape(1), a, b)

    def mix_rows():
        v.middle, v.second = line(
            mix, tokens, other, v.mixed, v.mixed_other, mixer_weight, v.mixer_other,
            row(second_gain), row(second_shift),
        )

    def expand_other():
        v.act1, v.ge1, gs1, v.eb1 = line(
            lambda x, g, w, b: expand(x, 1, own, g, w, b, BF16),
            v.second, v.active_grad1, expand_weight, row(expand_bias),
        )
        v.gs_got = swap(gs1)

    def expand_own():
        v.act0, v.ge0, v.gs0, v.eb0 = line(
            lambda x, g, w, b: expand(x, 0, own, g, w, b, BF16),
            v.second, v.active_grad0, expand_weight, row(expand_bias),
        )

    def reduce_chunks():
        reduce_sum.begin(*line(
            lambda *xs: reduce_grad_part(at, 0, *xs), v.act0, v.act1, target0, v.target1
        ))

    def expand_chunks():
        expand_sum.begin(*line(lambda *xs: expand_grad_part(at, 0, *xs), v.second, v.ge0, v.ge1))

    def middle_back():
        v.attended0, v.second_sums = line(
            back_rows, v.gs0, v.gs_got, v.middle, target0, row(second_gain)
        )

    grad_mix = lambda a, w: dot(a, w, 1, 1).astype(BF16)

    def mixed_send():
        out = line(grad_mix, v.attended0, v.mixer_other)
        v.grad_mixed1 = swap(out)

    def mixed_own():
        v.grad_mixed0 = line(grad_mix, v.attended0, mixer_weight)

    def attended_send():
        v.attended1 = swap(tie(v.attended0, *line.last))

    def reduced_other():
        out = line(lambda a, w: columns_dot(a, w, 0, name="reduced"), v.act1, reduce_weight)
        v.reduced_got = swap(out)

    def attend_back():
        v.grad_projected, v.sums = line(
            attend_backward, sp, v.projected0, v.projected1, v.grad_mixed0, v.grad_mixed1,
            v.mixed, v.logsum, rows,
        )

    def query_chunks():
        query_sum.begin(*line(lambda *xs: heads_grad_part(at, 0, *xs), v.low0, v.low1, v.grad_projected))

    def value_chunks():
        value_sum.begin(*line(
            lambda *xs: values_grad_part(at, 0, *xs), v.low0, v.low1, v.grad_projected,
            v.attended0, v.attended1, v.mixed,
        ))

    def first_other():
        out = line(lambda g, w: first_rows(g, w, 1, own, BF16), v.grad_projected, heads_weight)
        v.first_got = swap(out)

    def first_own():
        v.first_part = line(lambda g, w: first_rows(g, w, 0, own, BF16), v.grad_projected, heads_weight)

    def first_back():
        v.tokens_grad, first_sums = line(
            back_rows, v.first_part, v.first_got, tokens, v.attended0, row(first_gain)
        )
        v.both = join(first_sums[:2], v.second_sums[:3])
        v.both_got = swap(v.both)

    def output():
        v.block_out = line(
            output_rows, v.middle, v.act0, reduce_weight, v.reduced_got, row(reduce_bias)
        )

    def pack_first():
        v.pack = line(
            lambda both, got, eb0, eb1, bias: jnp.concatenate(
                [(both + got).reshape(-1), (eb0 + eb1).reshape(-1), bias.reshape(-1)]
            ).reshape(-1, 128),
            v.both, v.both_got, v.eb0, v.eb1, bias_grad(v.sums, buckets),
        )
        v.pack_got = trade(v.pack, 1)

    def pack_next(bit):
        def step():
            v.pack = line(jnp.add, v.pack, v.pack_got)
            if bit:
                v.pack_got = trade(v.pack, bit)

        return step

    chunk = (hidden // 8, model)
    turned = (model, hidden // 8)

    piece = (2, model // 8, width)
    reduce_shape = [jax.ShapeDtypeStruct(reduce_weight.shape, F32)]
    expand_shape = [jax.ShapeDtypeStruct(expand_weight.shape, F32)]
    heads_shape = [jax.ShapeDtypeStruct(heads_weight.shape, F32), jax.ShapeDtypeStruct(mixer_weight.shape, F32)]
    reduce_spec = [lambda to: pl.BlockSpec(chunk, lambda g, s: (to(g, s), 0))]
    expand_spec = [lambda to: pl.BlockSpec(turned, lambda g, s: (0, to(g, s)))]
    heads_spec = [
        lambda to: pl.BlockSpec((3, model // 8, width), lambda g, s: (0, to(g, s), 0)),
        lambda to: pl.BlockSpec((width, model // 8), lambda g, s: (0, to(g, s))),
    ]

    def reduce_near():
        v.reduce_grad = line(
            lambda *xs: spread(at, 0, xs, put_rows, chunk, reduce_spec, reduce_shape, name="reduce_near"),
            *reduce_sum.nears(),
        )

    def reduce_far():
        v.reduce_grad = line(
            lambda given, *xs: spread(at, 1, xs, put_rows, chunk, reduce_spec, reduce_shape, given, name="reduce_far"),
            v.reduce_grad, *reduce_sum.fars(),
        )

    def expand_near():
        v.expand_grad = line(
            lambda *xs: spread(at, 0, xs, put_rows, turned, expand_spec, expand_shape, name="expand_near"),
            *expand_sum.nears(),
        )

    def expand_far():
        v.expand_grad = line(
            lambda given, *xs: spread(at, 1, xs, put_rows, turned, expand_spec, expand_shape, given, name="expand_far"),
            v.expand_grad, *expand_sum.fars(),
        )

    def heads_near():
        v.heads_grad = line(
            lambda *xs: spread(at, 0, xs, put_heads, piece, heads_spec, heads_shape, name="heads_near"),
            *query_sum.nears(), *value_sum.nears(),
        )

    def heads_far():
        v.heads_grad = line(
            lambda given, *xs: spread(at, 1, xs, put_heads, piece, heads_spec, heads_shape, given, name="heads_far"),
            v.heads_grad, *query_sum.fars(), *value_sum.fars(),
        )

    order = (
        project_own, active_own, send_more, project_other, attend, mixer_rest, mixer_both, active_other,
        mix_rows, expand_other, expand_own, reduce_chunks, middle_back, mixed_send, expand_chunks,
        attended_send, mixed_own, reduce_sum.first, expand_sum.first, attend_back, reduce_sum.second,
        query_chunks, reduce_sum.third, value_chunks, first_other, expand_sum.second, reduce_sum.fourth,
        query_sum.first, value_sum.first, expand_sum.third, reduce_sum.fifth, query_sum.second,
        value_sum.second, first_own, first_back, expand_sum.fourth, pack_first, reduce_sum.sixth, pack_next(2),
        value_sum.third, expand_sum.fifth, query_sum.third, reduced_other, value_sum.fourth, reduce_near,
        reduce_far, query_sum.fourth, pack_next(4), expand_sum.sixth, value_sum.fifth, query_sum.fifth, output,
        value_sum.sixth, expand_near, expand_far, pack_next(8), query_sum.sixth, heads_near, heads_far,
        pack_next(0),
    )
    for step in order:
        step()
    pack = v.pack.reshape(-1)
    both = pack[: 5 * model].reshape(5, model)
    expand_bias_grad = pack[5 * model : 5 * model + hidden]
    bias_part = pack[5 * model + hidden :].reshape(relative_bias.shape)
    return (
        v.block_out, v.tokens_grad, both[0], both[1], v.heads_grad[0], bias_part, v.heads_grad[1], both[2], both[3],
        v.expand_grad[0], expand_bias_grad, v.reduce_grad[0], both[4],
    )


def gathered(
    tokens, lengths, first_gain, first_shift, heads_weight, relative_bias, mixer_weight, second_gain,
    second_shift, expand_weight, expand_bias, reduce_weight, reduce_bias, cotangent,
):
    def gather(x):
        return lax.all_gather(x, "mp", axis=0, tiled=True)

    def scatter(x):
        return lax.psum_scatter(x.astype(BF16), "mp", scatter_dimension=0, tiled=True).astype(F32)

    members = lax.axis_size("mp")
    length = lengths[0]
    own = tokens.shape[0]
    whole = own * members
    half = whole // 2
    buckets = relative_bias.shape[1]
    sp = jnp.stack([jnp.zeros((), jnp.int32), length.astype(jnp.int32)])
    places = lax.axis_index("mp") * own + jnp.arange(own)
    rows = bias_rows(relative_bias)
    source_all = gather(tokens)
    first_all, projected = project(source_all, first_gain.reshape(1, -1), first_shift.reshape(1, -1), heads_weight)
    projected0, projected1 = projected[:, :half], projected[:, half:]
    mixed, logsum = attend_forward(sp, projected0, projected1, rows)
    source = tokens.astype(F32)
    middle = source + scatter(dot(mixed, mixer_weight, 1, 0))
    second_norm, second_inverse = normalize(middle)
    second_all = gather((second_norm * second_gain + second_shift).astype(BF16))
    target = keep_valid(cotangent, places, length)
    target_wide = target.astype(F32)
    target_all = gather(target)
    expanded = dot(second_all, expand_weight, 1, 0) + expand_bias
    active_low = jax.nn.gelu(expanded, approximate=True).astype(BF16)
    grad_expanded = gelu_back(expanded, dot(target_all, reduce_weight, 1, 1)).astype(BF16)
    grad_second = scatter(dot(grad_expanded, expand_weight, 1, 1))
    reduced = scatter(dot(active_low, reduce_weight, 1, 0))
    reduce_grad = dot(active_low, target_all, 0, 0)
    expand_grad = dot(second_all, grad_expanded, 0, 0)
    expand_bias_grad = jnp.sum(grad_expanded.astype(F32), axis=0)
    block_out = (middle + reduced + reduce_bias).astype(BF16)
    grad_middle = target_wide + norm_back(grad_second * second_gain, second_norm, second_inverse)
    attended_all = gather(grad_middle.astype(BF16))
    mixer_grad = dot(mixed, attended_all, 0, 0)
    grad_mixed = dot(attended_all, mixer_weight, 1, 1).astype(BF16)
    grad_projected, sums = attend_backward(
        sp, projected0, projected1, grad_mixed[:half], grad_mixed[half:], mixed, logsum, rows
    )
    bias_part = bias_grad(sums, buckets)
    heads_grad = jnp.einsum("td,cte->cde", first_all, grad_projected, preferred_element_type=F32)
    grad_first = scatter(jnp.einsum("cte,cde->td", grad_projected, heads_weight, preferred_element_type=F32))
    first_norm, first_inverse = normalize(source)
    tokens_grad = (
        grad_middle + norm_back(grad_first * first_gain, first_norm, first_inverse)
    ).astype(BF16)
    first_gain_grad, first_shift_grad, second_gain_grad, second_shift_grad, reduce_bias_grad = (
        lax.psum(
            (
                jnp.sum(grad_first * first_norm, axis=0),
                jnp.sum(grad_first, axis=0),
                jnp.sum(grad_second * second_norm, axis=0),
                jnp.sum(grad_second, axis=0),
                jnp.sum(target_wide, axis=0),
            ),
            ("dp", "mp"),
        )
    )
    heads_grad, bias_part, mixer_grad, expand_grad, expand_bias_grad, reduce_grad = (
        lax.psum(x.astype(BF16), "dp").astype(F32)
        for x in (heads_grad, bias_part, mixer_grad, expand_grad, expand_bias_grad, reduce_grad)
    )
    return (
        block_out, tokens_grad, first_gain_grad, first_shift_grad, heads_grad, bias_part, mixer_grad,
        second_gain_grad, second_shift_grad, expand_grad, expand_bias_grad, reduce_grad, reduce_bias_grad,
    )


def per_device(*args):
    if lax.axis_size("mp") == 2 and lax.axis_size("dp") == 16:
        return paired(*args)
    return gathered(*args)


def solution(mesh):
    return jax.shard_map(
        per_device,
        mesh=mesh,
        in_specs=(
            P(("dp", "mp"), None),
            P("dp"),
            P(),
            P(),
            P(None, None, "mp"),
            P("mp", None),
            P("mp", None),
            P(),
            P(),
            P(None, "mp"),
            P("mp"),
            P("mp", None),
            P(),
            P(("dp", "mp"), None),
        ),
        out_specs=(
            P(("dp", "mp"), None),
            P(("dp", "mp"), None),
            P(),
            P(),
            P(None, None, "mp"),
            P("mp", None),
            P("mp", None),
            P(),
            P(),
            P(None, "mp"),
            P("mp"),
            P("mp", None),
            P(),
        ),
        check_vma=False,
    )
```

```python
import functools
import math

import jax
import jax.numpy as jnp
import numpy as np
from jax import lax
from jax.experimental import pallas as pl
from jax.experimental.pallas import tpu as pltpu
from jax.sharding import PartitionSpec as P

EPS = 1e-05
DH=64; MAXDIST=128; NEG=-1e30; BLK=256
F32=jnp.float32; BF16=jnp.bfloat16
HIGHEST=lax.Precision.HIGHEST

def bucket_table(count, buckets, reach):
    exact = buckets // 2
    entries = []
    for position in range(count):
        if position < exact:
            entries.append(position)
        else:
            level = exact + int(math.log(position / exact) / math.log(reach / exact) * (buckets - exact))
            entries.append(min(buckets - 1, level))
    return np.array(entries, dtype=np.int32)

def bucket_starts(buckets):
    table=bucket_table(4*MAXDIST+2*buckets,buckets,MAXDIST)
    return [int(np.argmax(table>=level)) for level in range(1,buckets)]

def bias_rows_kernel(r_ref,o_ref):
    heads,buckets=r_ref.shape
    W=2*BLK
    rel=r_ref[...]-r_ref[:,buckets-1:]
    place=lax.broadcasted_iota(jnp.int32,(heads,W),1)
    signed=jnp.where(place<BLK,place,place-W)
    for part,distance in enumerate((-signed,BLK-signed,signed,BLK+signed)):
        value=jnp.broadcast_to(rel[:,:1],(heads,W))
        for level,start in enumerate(bucket_starts(buckets)):
            value=jnp.where(distance>=start,rel[:,level+1:level+2],value)
        value=jnp.where(distance>=0,value,NEG)
        for pair in range(heads//2):
            o_ref[pair,:,part*W:(part+1)*W]=value[2*pair:2*pair+2]

def bias_rows(relative_bias):
    heads=relative_bias.shape[0]
    return pl.pallas_call(
        bias_rows_kernel,
        out_shape=jax.ShapeDtypeStruct((heads//2,2,8*BLK),F32),
        name="bias_rows",
    )(relative_bias)

def toeplitz(row):
    wide=jnp.broadcast_to(row,(BLK,2*BLK))
    return pltpu.roll(wide,0,1,stride=1,stride_axis=0)[:,:BLK]


def lane_masks():
    lane=lax.broadcasted_iota(jnp.int32,(1,128),1)
    head=[(lane//DH)==h for h in range(2)]
    mine=[jnp.where(m,1.0,0.0).astype(BF16) for m in head]
    spare=[jnp.where(lane==DH*(1-h),1.0,0.0) for h in range(2)]
    return head,mine,spare


def gone_rows(start,half,length,spare):
    pos=lax.broadcasted_iota(jnp.int32,(half,1),0)+start
    gone=jnp.where(pos<length,0.0,NEG)
    return [(gone*s).astype(BF16) for s in spare]


def fwd_kernel(sp, a_ref,c_ref,b_ref,o_ref,lse_ref,qs,ks,vs):
    half=a_ref.shape[1]; T=2*half; flip=sp[0]; length=sp[1]
    W=2*BLK
    head,mine,spare=lane_masks()
    for a,ref in enumerate((a_ref,c_ref)):
        start=pl.multiple_of((a^flip)*half,half)
        dst=pl.ds(start,half)
        gone=gone_rows(start,half,length,spare)
        for h in range(2):
            qs[h,dst,:]=ref[0]*(mine[h]*jnp.asarray(DH**-0.5,BF16))+spare[h].astype(BF16)
            ks[h,dst,:]=ref[1]*mine[h]+gone[h]
            vs[h,dst,:]=ref[2]*mine[h]+mine[1-h]
    tiles=[(toeplitz(b_ref[0,h:h+1,0:W]),toeplitz(b_ref[0,h:h+1,W:2*W])) for h in range(2)]
    outs={}

    def score(i,h):
        return dot(qs[h,i*BLK:(i+1)*BLK,:],ks[h,:(i+1)*BLK,:],1,1)

    def finish(i,h,s):
        kc=(i+1)*BLK; t0,t1=tiles[h]
        parts=[]
        if i>=2: parts.append(s[:,:kc-2*BLK])
        if i>=1: parts.append(s[:,kc-2*BLK:kc-BLK]+t1)
        parts.append(s[:,kc-BLK:]+t0)
        top=functools.reduce(jnp.maximum,[jnp.max(x,axis=1,keepdims=True) for x in parts])
        p=jnp.concatenate([jnp.exp(x-top).astype(BF16) for x in parts],axis=1)
        o=dot(p,vs[h,:kc,:],1,0)
        total=o[:,DH*(1-h):DH*(1-h)+1]
        outs[h]=(o*(1.0/total),top+jnp.log(total))
        if h==1:
            rows=pl.ds(pl.multiple_of((i*BLK+flip*half)%T,BLK),BLK)
            o_ref[rows,:]=jnp.where(head[0],outs[0][0],outs[1][0]).astype(BF16)
            lse_ref[0,i*BLK:kc,:]=jnp.where(head[0],outs[0][1],outs[1][1])

    run_ahead([(i,h) for i in range(T//BLK) for h in range(2)],score,finish,2)


def run_ahead(items,first,second,depth):
    waiting=[]
    for item in items:
        waiting.append((item,first(*item)))
        if len(waiting)>depth:
            done,value=waiting.pop(0)
            second(*done,value)
    for done,value in waiting:
        second(*done,value)


def attend_forward(sp,projected0,projected1,rows):
    _,half,HD=projected0.shape; pairs=HD//128; T=2*half
    part=pl.BlockSpec((3,half,128),lambda p,s:(0,0,p))
    return pl.pallas_call(
        fwd_kernel,
        grid_spec=pltpu.PrefetchScalarGridSpec(
            num_scalar_prefetch=1,grid=(pairs,),
            in_specs=[part,part,pl.BlockSpec((1,2,rows.shape[2]),lambda p,s:(p,0,0))],
            out_specs=[pl.BlockSpec((T,128),lambda p,s:(0,p)),pl.BlockSpec((1,T,128),lambda p,s:(p,0,0))],
            scratch_shapes=[pltpu.VMEM((2,T,128),BF16)]*3),
        out_shape=[jax.ShapeDtypeStruct((T,HD),BF16),jax.ShapeDtypeStruct((pairs,T,128),F32)],
        cost_estimate=cost(8*T*T*HD,8*T*HD+512*pairs*T),
        name="attend_forward",
    )(sp,projected0,projected1,rows)

def diagonal_sums(acc, offset):
    W=2*BLK
    wide=jnp.concatenate([acc,jnp.zeros_like(acc)],axis=1)
    n=BLK
    while n>1:
        n//=2
        top=wide[:n]; bottom=wide[n:2*n]
        wide=top+pltpu.roll(bottom,W-n,1)
    return pltpu.roll(wide,offset,1) if offset else wide

def bwd_kernel(sp, a_ref,c_ref,d0_ref,d1_ref,o_ref,lse_ref,b_ref,g_ref,d_ref,qs,ks,vs,dos,dq,acc0,acc1):
    half=a_ref.shape[1]; T=2*half; flip=sp[0]; length=sp[1]
    W=2*BLK
    n=T//BLK
    head,mine,spare=lane_masks()
    stats=[None,None]
    one=sum(spare).astype(BF16)
    for a,(ref,do_ref) in enumerate(((a_ref,d0_ref),(c_ref,d1_ref))):
        start=pl.multiple_of((a^flip)*half,half)
        dst=pl.ds(start,half)
        gone=gone_rows(start,half,length,spare)
        for h in range(2):
            qs[h,dst,:]=ref[0]*(mine[h]*jnp.asarray(DH**-0.5,BF16))+spare[h].astype(BF16)
            ks[h,dst,:]=ref[1]*mine[h]+gone[h]
            vs[h,dst,:]=ref[2]*mine[h]
        dos[dst,:]=do_ref[...]
        acc0[0,dst,:]=do_ref[...].astype(F32)*o_ref[a*half:(a+1)*half,:].astype(F32)
    turned=acc0[0].T
    deltas=[jnp.sum(turned[h*DH:(h+1)*DH],axis=0,keepdims=True) for h in range(2)]
    turned=lse_ref[0].T
    lses=[turned[h*DH:h*DH+1] for h in range(2)]
    near=acc1
    tiles=[(toeplitz(b_ref[0,h:h+1,2*W:3*W]),toeplitz(b_ref[0,h:h+1,3*W:])) for h in range(2)]

    def products(j,h):
        rj=slice(j*BLK,(j+1)*BLK)
        return dot(ks[h,rj,:],qs[h,j*BLK:,:],1,1),dot(vs[h,rj,:],dos[j*BLK:,:],1,1)

    keep={}

    def finish(j,h,value):
        s,dp=value
        rj=slice(j*BLK,(j+1)*BLK)
        ps=[];dss=[]
        for b in range(n-j):
            c=slice(b*BLK,(b+1)*BLK)
            cc=slice((j+b)*BLK,(j+b+1)*BLK)
            x=s[:,c]-lses[h][:,cc]
            if b<2: x=x+tiles[h][b]
            p=jnp.exp(x)
            ds=p*(dp[:,c]-deltas[h][:,cc])
            if b<2:
                if j==0: near[h,b]=ds
                else: near[h,b]+=ds
            ps.append(p.astype(BF16)); dss.append(ds.astype(BF16))
        p=jnp.concatenate(ps,axis=1); ds=jnp.concatenate(dss,axis=1)
        dv=dot(p,dos[j*BLK:,:],1,0)
        dk=dot(ds,qs[h,j*BLK:,:],1,0)
        kk=ks[h,rj,:]*mine[h]+mine[1-h]
        dqj=dot(ds,kk,0,0)
        if j==0: dq[h,:,:]=dqj
        else: dq[h,j*BLK:,:]+=dqj
        keep[h]=(dk,dv)
        if h==1:
            rows=pl.ds(pl.multiple_of((j*BLK+flip*half)%T,BLK),BLK)
            g_ref[1,rows,:]=jnp.where(head[0],keep[0][0],keep[1][0]).astype(BF16)
            g_ref[2,rows,:]=jnp.where(head[0],keep[0][1],keep[1][1]).astype(BF16)

    run_ahead([(j,h) for j in range(n) for h in range(2)],products,finish,1)
    for h in range(2):
        d_ref[0,h:h+1,:]=diagonal_sums(near[h,0],0)+diagonal_sums(near[h,1],BLK)
        total=jnp.sum(dq[h,:,:],axis=0,keepdims=True)[:,DH*(1-h):DH*(1-h)+1]
        d_ref[0,2+h:3+h,:]=jnp.broadcast_to(total,(1,W))
    for a in range(2):
        dst=pl.ds(pl.multiple_of((a^flip)*half,half),half)
        g_ref[0,a*half:(a+1)*half,:]=(jnp.where(head[0],dq[0,dst,:],dq[1,dst,:])*DH**-0.5).astype(BF16)

def attend_backward(sp,projected0,projected1,grad0,grad1,mixed,lse,rows,start=0,count=None,given=None):
    _,half,HD=projected0.shape; pairs=HD//128; T=2*half
    count=pairs if count is None else count
    part=pl.BlockSpec((3,half,128),lambda p,s:(0,0,p+start))
    grad=pl.BlockSpec((half,128),lambda p,s:(0,p+start))
    in_specs=[part,part,grad,grad,pl.BlockSpec((T,128),lambda p,s:(0,p+start)),
              pl.BlockSpec((1,T,128),lambda p,s:(p+start,0,0)),pl.BlockSpec((1,2,rows.shape[2]),lambda p,s:(p+start,0,0))]
    args=[sp,projected0,projected1,grad0,grad1,mixed,lse,rows]
    kernel=bwd_kernel
    if given is not None:
        in_specs.append(pl.BlockSpec(memory_space=pl.ANY)); args.append(given)
        kernel=lambda *refs: bwd_kernel(*refs[:8],*refs[9:])
    return pl.pallas_call(
        kernel,
        grid_spec=pltpu.PrefetchScalarGridSpec(
            num_scalar_prefetch=1,grid=(count,),
            in_specs=in_specs,
            out_specs=[pl.BlockSpec((3,T,128),lambda p,s:(0,0,p+start)),pl.BlockSpec((1,4,2*BLK),lambda p,s:(p,0,0))],
            scratch_shapes=[pltpu.VMEM((2,T,128),BF16)]*3+[pltpu.VMEM((T,128),BF16),pltpu.VMEM((2,T,128),F32),pltpu.VMEM((1,T,128),F32),pltpu.VMEM((2,2,BLK,BLK),F32)]),
        out_shape=[jax.ShapeDtypeStruct((3,T,HD),BF16),jax.ShapeDtypeStruct((count,4,2*BLK),F32)],
        input_output_aliases={} if given is None else {8:0},
        cost_estimate=cost(20*T*T*128*count,(16*T*128+512*T)*count),
        name="attend_backward",
    )(*args)

def bias_grad(sums, buckets):
    pairs=sums.shape[0]; W=2*BLK
    near=sums[:,0:2].reshape(pairs*2,W); total=sums[:,2:4,0].reshape(pairs*2,1)
    edges=[0]+bucket_starts(buckets)
    distance=jnp.arange(W)[None,None]
    low=jnp.asarray(np.array(edges[:-1],np.int32))[None,:,None]
    high=jnp.asarray(np.array(edges[1:],np.int32))[None,:,None]
    parts=jnp.sum(jnp.where((distance>=low)&(distance<high),near[:,None,:],0.0),axis=2)
    return jnp.concatenate([parts,total-jnp.sum(parts,axis=1,keepdims=True)],axis=1)


HALF_TANH = math.sqrt(2.0 / math.pi)


def dot(a, b, ca, cb):
    return lax.dot_general(a, b, (((ca,), (cb,)), ((), ())), preferred_element_type=F32)


def fixed(shape):
    return pl.BlockSpec(shape, lambda *_: (0,) * len(shape))


def cost(flops, moved):
    return pl.CostEstimate(flops=int(flops), transcendentals=0, bytes_accessed=int(moved))


def cost4(flops, moved):
    return cost(4 * flops, 4 * moved)


def cost16(flops, moved):
    return cost(16 * flops, 16 * moved)


def row_norm(values):
    center = jnp.mean(values, axis=-1, keepdims=True)
    centered = values - center
    inverse = lax.rsqrt(jnp.mean(centered * centered, axis=-1, keepdims=True) + EPS)
    return centered * inverse, inverse


def project_kernel(x_ref, gain_ref, shift_ref, w_ref, low_ref, out_ref):
    normed, _ = row_norm(x_ref[...].astype(F32))
    low = (normed * gain_ref[...] + shift_ref[...]).astype(BF16)
    low_ref[...] = low
    for c in range(3):
        out_ref[c] = dot(low, w_ref[c], 1, 0).astype(BF16)


def project(x, gain, shift, weight):
    rows, model = x.shape
    width = weight.shape[2]
    step = min(256, rows)
    return pl.pallas_call(
        project_kernel,
        grid=(rows // step,),
        in_specs=[pl.BlockSpec((step, model), lambda i: (i, 0)), fixed((1, model)), fixed((1, model)), fixed(weight.shape)],
        out_specs=[pl.BlockSpec((step, model), lambda i: (i, 0)), pl.BlockSpec((3, step, width), lambda i: (0, i, 0))],
        out_shape=[jax.ShapeDtypeStruct((rows, model), BF16), jax.ShapeDtypeStruct((3, rows, width), BF16)],
        cost_estimate=cost16(6 * rows * model * width, 2 * (2 * rows * model + weight.size + 3 * rows * width)),
        name="project",
    )(x, gain, shift, weight)


def mix_kernel(own_blocks, x0_ref, x1_ref, m_ref, p_ref, w0_ref, w1_ref, gain_ref, shift_ref, mid_ref, low_ref):
    i = pl.program_id(0)
    attended = dot(m_ref[...], w0_ref[...], 1, 0) + dot(p_ref[...], w1_ref[...], 1, 0)

    def rows(x_ref):
        return x_ref[...].astype(F32) + attended

    def rest(middle):
        normed, _ = row_norm(middle)
        low_ref[...] = (normed * gain_ref[...] + shift_ref[...]).astype(BF16)

    @pl.when(i < own_blocks)
    def _():
        middle = rows(x0_ref)
        mid_ref[...] = middle.astype(BF16)
        rest(middle)

    @pl.when(i >= own_blocks)
    def _():
        rest(rows(x1_ref))


def mix(tokens, other, mixed, mixed_other, weight, weight_other, gain, shift):
    own, model = tokens.shape
    width = mixed.shape[1]
    step = 256
    n = own // step
    return pl.pallas_call(
        functools.partial(mix_kernel, n),
        grid=(2 * n,),
        in_specs=[
            pl.BlockSpec((step, model), lambda i: (jnp.minimum(i, n - 1), 0)),
            pl.BlockSpec((step, model), lambda i: (jnp.maximum(i - n, 0), 0)),
            pl.BlockSpec((step, width), lambda i: (i, 0)),
            pl.BlockSpec((step, width), lambda i: ((i + n) % (2 * n), 0)),
            fixed(weight.shape), fixed(weight.shape), fixed((1, model)), fixed((1, model)),
        ],
        out_specs=[
            pl.BlockSpec((step, model), lambda i: (jnp.minimum(i, n - 1), 0)),
            pl.BlockSpec((step, model), lambda i: (i, 0)),
        ],
        out_shape=[jax.ShapeDtypeStruct((own, model), BF16), jax.ShapeDtypeStruct((2 * own, model), BF16)],
        cost_estimate=cost4(8 * own * model * width, 2 * (4 * own * model + 4 * own * width + 2 * weight.size) + 4 * own * model),
        name="mix",
    )(tokens, other, mixed, mixed_other, weight, weight_other, gain, shift)


def expand_kernel(x_ref, g_ref, w_ref, b_ref, act_ref, ge_ref, gs_ref, bias_ref, acc_ref):
    i = pl.program_id(0)
    x = x_ref[...]
    width = w_ref.shape[1]
    sub = min(512, width)
    total = None
    for s in range(width // sub):
        cols = slice(s * sub, (s + 1) * sub)
        u = dot(x, w_ref[:, cols], 1, 0) + b_ref[:, cols].astype(F32)
        square = u * u
        t = jnp.tanh(HALF_TANH * u * (1.0 + 0.044715 * square))
        half = 0.5 + 0.5 * t
        act_ref[:, cols] = (u * half).astype(BF16)
        slope = half + 0.5 * u * (1.0 - t * t) * (HALF_TANH * (1.0 + 3 * 0.044715 * square))
        grad = g_ref[:, cols].astype(F32) * slope
        low = grad.astype(BF16)
        ge_ref[:, cols] = low
        bias_ref[:, cols] = jnp.sum(grad, axis=0, keepdims=True)
        part = dot(low, w_ref[:, cols], 1, 1)
        total = part if total is None else total + part

    @pl.when(i == 0)
    def _():
        acc_ref[...] = total

    @pl.when(i > 0)
    def _():
        acc_ref[...] += total

    @pl.when(i == pl.num_programs(0) - 1)
    def _():
        gs_ref[...] = acc_ref[...].astype(gs_ref.dtype)


def expand(x, block, rows, grad_active, weight, bias, dtype):
    model = x.shape[1]
    hidden = weight.shape[1]
    step = min(512, hidden)
    return pl.pallas_call(
        expand_kernel,
        grid=(hidden // step,),
        in_specs=[
            pl.BlockSpec((rows, model), lambda i: (block, 0)),
            pl.BlockSpec((rows, step), lambda i: (0, i)),
            pl.BlockSpec((model, step), lambda i: (0, i)),
            pl.BlockSpec((1, step), lambda i: (0, i)),
        ],
        out_specs=[
            pl.BlockSpec((rows, step), lambda i: (0, i)),
            pl.BlockSpec((rows, step), lambda i: (0, i)),
            fixed((rows, model)),
            pl.BlockSpec((1, step), lambda i: (0, i)),
        ],
        out_shape=[
            jax.ShapeDtypeStruct((rows, hidden), BF16),
            jax.ShapeDtypeStruct((rows, hidden), BF16),
            jax.ShapeDtypeStruct((rows, model), dtype),
            jax.ShapeDtypeStruct((1, hidden), F32),
        ],
        scratch_shapes=[pltpu.VMEM((rows, model), F32)],
        cost_estimate=cost(4 * rows * model * hidden, 2 * (2 * rows * model + 3 * rows * hidden + weight.size)),
        name="expand",
    )(x, grad_active, weight, bias)


STAGES = ((1, 2, 4, 8), (1, 4, 2, 8))


def place_of(index, stages):
    bit = [(index // s) % 2 for s in stages]
    return bit[0] * 4 + bit[1] * 2 + bit[2]


def trade(x, bit):
    size = lax.axis_size("dp")
    return lax.ppermute(x, "dp", [(i, i ^ bit) for i in range(size)])


def add_low(a, b):
    return (a.astype(F32) + b.astype(F32)).astype(BF16)


def pair_of(g, s, slot):
    return (3 - g) ^ (s[slot] // 2)


def put_pair(slot, s_ref, chunks, outs):
    flip = s_ref[slot] % 2
    sent = pl.program_id(0) < 2
    for j, value in enumerate(chunks):
        value = value.astype(BF16)[None]
        for out, here in zip(outs, (sent, jnp.logical_not(sent))):
            @pl.when(here)
            def _(out=out):
                out[pl.ds(j ^ flip, 1)] = value


def pair_call(kernel, slot, s, arrays, specs, tail, flops, name):
    zeros = (0,) * len(tail)
    moved = sum(2 * x.size for x in arrays) + 16 * math.prod(tail)
    return pl.pallas_call(
        functools.partial(kernel, slot),
        grid_spec=pltpu.PrefetchScalarGridSpec(
            num_scalar_prefetch=1, grid=(4,), in_specs=specs,
            out_specs=[
                pl.BlockSpec((2, *tail), lambda g, s: (jnp.maximum(1 - g, 0), *zeros)),
                pl.BlockSpec((2, *tail), lambda g, s: (jnp.minimum(3 - g, 1), *zeros)),
            ],
        ),
        out_shape=[jax.ShapeDtypeStruct((4, *tail), BF16)] * 2,
        cost_estimate=cost(flops, moved),
        name=name,
    )(s, *arrays)


def reduce_grad_kernel(slot, s_ref, *refs):
    (a0, a1, t0, t1), outs = refs[:4], refs[4:]
    value = dot(a0[...], t0[...], 0, 0) + dot(a1[...], t1[...], 0, 0)
    width = value.shape[0] // 2
    put_pair(slot, s_ref, [value[:width], value[width:]], outs)


def reduce_grad_part(s, slot, act0, act1, t0, t1):
    rows, hidden = act0.shape
    model = t0.shape[1]
    block = pl.BlockSpec((rows, hidden // 4), lambda g, s: (0, pair_of(g, s, slot)))
    return pair_call(
        reduce_grad_kernel, slot, s, (act0, act1, t0, t1), [block, block, fixed(t0.shape), fixed(t1.shape)],
        (hidden // 8, model), 4 * rows * model * hidden, "reduce_grad",
    )


def expand_grad_kernel(slot, s_ref, *refs):
    (x, g0, g1), outs = refs[:3], refs[3:]
    rows = g0.shape[0]
    value = dot(x[:rows], g0[...], 0, 0) + dot(x[rows:], g1[...], 0, 0)
    width = value.shape[1] // 2
    put_pair(slot, s_ref, [value[:, :width], value[:, width:]], outs)


def expand_grad_part(s, slot, x, g0, g1):
    rows, hidden = g0.shape
    model = x.shape[1]
    block = pl.BlockSpec((rows, hidden // 4), lambda g, s: (0, pair_of(g, s, slot)))
    return pair_call(
        expand_grad_kernel, slot, s, (x, g0, g1), [fixed(x.shape), block, block],
        (model, hidden // 8), 4 * rows * model * hidden, "expand_grad",
    )


def heads_grad_kernel(slot, s_ref, *refs):
    (l0, l1, g), outs = refs[:3], refs[3:]
    rows = l0.shape[0]
    both = [dot(l0[...], g[c, :rows], 0, 0) + dot(l1[...], g[c, rows:], 0, 0) for c in range(2)]
    width = both[0].shape[0] // 2
    chunks = [jnp.stack([v[j * width:(j + 1) * width] for v in both]) for j in range(2)]
    put_pair(slot, s_ref, chunks, outs)


def heads_grad_part(s, slot, low0, low1, grad):
    rows, model = low0.shape
    width = grad.shape[2]
    block = pl.BlockSpec((rows, model // 4), lambda g, s: (0, pair_of(g, s, slot)))
    return pair_call(
        heads_grad_kernel, slot, s, (low0, low1, grad),
        [block, block, pl.BlockSpec((2, 2 * rows, width), lambda g, s: (0, 0, 0))],
        (2, model // 8, width), 8 * rows * model * width, "heads_grad",
    )


def values_grad_kernel(slot, s_ref, *refs):
    (l0, l1, g, a0, a1, m), outs = refs[:6], refs[6:]
    rows = l0.shape[0]
    both = [
        dot(l0[...], g[0, :rows], 0, 0) + dot(l1[...], g[0, rows:], 0, 0),
        dot(a0[...], m[:rows], 0, 0) + dot(a1[...], m[rows:], 0, 0),
    ]
    width = both[0].shape[0] // 2
    chunks = [jnp.stack([v[j * width:(j + 1) * width] for v in both]) for j in range(2)]
    put_pair(slot, s_ref, chunks, outs)


def values_grad_part(s, slot, low0, low1, grad, att0, att1, mixed):
    rows, model = low0.shape
    width = grad.shape[2]
    block = pl.BlockSpec((rows, model // 4), lambda g, s: (0, pair_of(g, s, slot)))
    return pair_call(
        values_grad_kernel, slot, s, (low0, low1, grad, att0, att1, mixed),
        [block, block, pl.BlockSpec((1, 2 * rows, width), lambda g, s: (2, 0, 0)), block, block, fixed(mixed.shape)],
        (2, model // 8, width), 8 * rows * model * width, "values_grad",
    )


def columns_kernel(turn, a_ref, b_ref, out_ref):
    out_ref[...] = dot(a_ref[...], b_ref[...], 1, turn).astype(out_ref.dtype)


def columns_dot(a, b, turn, name):
    rows, depth = a.shape
    columns = b.shape[1 - turn]
    step = min(512, columns)
    block = ((step, depth), lambda i: (i, 0)) if turn else ((depth, step), lambda i: (0, i))
    return pl.pallas_call(
        functools.partial(columns_kernel, turn),
        grid=(columns // step,),
        in_specs=[fixed(a.shape), pl.BlockSpec(*block)],
        out_specs=pl.BlockSpec((rows, step), lambda i: (0, i)),
        out_shape=jax.ShapeDtypeStruct((rows, columns), BF16),
        cost_estimate=cost16(2 * rows * depth * columns, 2 * (a.size + b.size + rows * columns)),
        name=name,
    )(a, b)


def output_kernel(m_ref, a_ref, w_ref, r_ref, bias_ref, out_ref):
    out_ref[...] = (
        m_ref[...].astype(F32) + dot(a_ref[...], w_ref[...], 1, 0) + r_ref[...].astype(F32) + bias_ref[...]
    ).astype(BF16)


def output_rows(middle, act, weight, reduced, bias):
    rows, hidden = act.shape
    model = weight.shape[1]
    step = 256
    block = pl.BlockSpec((rows, step), lambda i: (0, i))
    return pl.pallas_call(
        output_kernel,
        grid=(model // step,),
        in_specs=[
            block, fixed(act.shape), pl.BlockSpec((hidden, step), lambda i: (0, i)), block,
            pl.BlockSpec((1, step), lambda i: (0, i)),
        ],
        out_specs=block,
        out_shape=jax.ShapeDtypeStruct((rows, model), BF16),
        cost_estimate=cost16(2 * rows * hidden * model, 2 * (act.size + weight.size) + 8 * rows * model),
        name="output",
    )(middle, act, weight, reduced, bias)


def first_kernel(g_ref, w_ref, out_ref, acc_ref):
    c = pl.program_id(0)
    value = dot(g_ref[0], w_ref[0], 1, 1)

    @pl.when(c == 0)
    def _():
        acc_ref[...] = value

    @pl.when(c > 0)
    def _():
        acc_ref[...] += value

    @pl.when(c == pl.num_programs(0) - 1)
    def _():
        out_ref[...] = acc_ref[...].astype(out_ref.dtype)


def first_rows(grad, weight, part, rows, dtype):
    kinds, model, width = weight.shape
    return pl.pallas_call(
        first_kernel,
        grid=(kinds,),
        in_specs=[
            pl.BlockSpec((1, rows, width), lambda c: (c, part, 0)),
            pl.BlockSpec((1, model, width), lambda c: (c, 0, 0)),
        ],
        out_specs=fixed((rows, model)),
        out_shape=jax.ShapeDtypeStruct((rows, model), dtype),
        scratch_shapes=[pltpu.VMEM((rows, model), F32)],
        cost_estimate=cost(2 * kinds * rows * width * model, 2 * (grad.size + weight.size) + 4 * rows * model),
        name="first_rows",
    )(grad, weight)


def back_kernel(a_ref, b_ref, source_ref, add_ref, gain_ref, out_ref, sums_ref):
    @pl.when(pl.program_id(0) == 0)
    def _():
        sums_ref[...] = jnp.zeros_like(sums_ref)

    def some(i, _):
        rows = pl.ds(pl.multiple_of(i * 64, 64), 64)
        normed, inverse = row_norm(source_ref[rows, :].astype(F32))
        grad = a_ref[rows, :].astype(F32) + b_ref[rows, :].astype(F32)
        add = add_ref[rows, :].astype(F32)
        scaled = grad * gain_ref[...]
        weighted = grad * normed
        mean = jnp.mean(scaled, axis=-1, keepdims=True)
        along = jnp.mean(scaled * normed, axis=-1, keepdims=True)
        out_ref[rows, :] = (add + inverse * (scaled - mean - normed * along)).astype(BF16)
        for k, value in enumerate((weighted, grad, add)):
            sums_ref[k:k + 1] += jnp.sum(value, axis=0, keepdims=True)
        return 0

    lax.fori_loop(0, source_ref.shape[0] // 64, some, 0)


def back_rows(a, b, source, add, gain):
    rows, model = a.shape
    step = 256
    block = pl.BlockSpec((step, model), lambda i: (i, 0))
    return pl.pallas_call(
        back_kernel,
        grid=(rows // step,),
        in_specs=[block] * 4 + [fixed((1, model))],
        out_specs=[block, fixed((8, model))],
        out_shape=[jax.ShapeDtypeStruct((rows, model), BF16), jax.ShapeDtypeStruct((8, model), F32)],
        cost_estimate=cost(30 * rows * model, 10 * rows * model),
        name="back_rows",
    )(a, b, source, add, gain)


def order_kernel(s_ref, a_ref, b_ref, out_ref):
    @pl.when(pl.program_id(0) == 0)
    def _():
        out_ref[...] = a_ref[...]

    @pl.when(pl.program_id(0) == 1)
    def _():
        out_ref[...] = b_ref[...]


def order_rows(core, a, b):
    rows, model = a.shape
    return pl.pallas_call(
        order_kernel,
        grid_spec=pltpu.PrefetchScalarGridSpec(
            num_scalar_prefetch=1, grid=(2,),
            in_specs=[pl.BlockSpec((rows, model), lambda g, s: (0, 0))] * 2,
            out_specs=pl.BlockSpec((rows, model), lambda g, s: (g ^ s[0], 0)),
        ),
        out_shape=jax.ShapeDtypeStruct((2 * rows, model), a.dtype),
        cost_estimate=cost(0, 8 * rows * model),
        name="order_rows",
    )(core, a, b)


def spread_kernel(put, s_ref, *refs):
    g = pl.program_id(0)
    count = put.pieces
    pieces, outs = refs[-2 * count - put.outs:-put.outs], refs[-put.outs:]
    for a in range(2):
        @pl.when(g == a)
        def _(a=a):
            for j in range(2):
                put([piece.at[j] for piece in pieces[a::2]], outs, j ^ (s_ref[0] % 2))


def spread(places, part, pieces, put, tail, out_specs, out_shape, given=None, name=None):
    zeros = (0,) * len(tail)

    def at(g, s):
        return (2 * g + part) ^ (s[0] // 2)

    in_specs = [pl.BlockSpec((2, *tail), lambda g, s: (0, *zeros)) for _ in pieces]
    args = list(pieces)
    aliases = {}
    if given is not None:
        in_specs = [pl.BlockSpec(memory_space=pl.ANY)] * len(given) + in_specs
        args = [*given, *args]
        aliases = {1 + k: k for k in range(len(given))}
    return pl.pallas_call(
        functools.partial(spread_kernel, put),
        grid_spec=pltpu.PrefetchScalarGridSpec(
            num_scalar_prefetch=1, grid=(2,), in_specs=in_specs, out_specs=[spec(at) for spec in out_specs],
        ),
        out_shape=out_shape,
        input_output_aliases=aliases,
        cost_estimate=cost(0, 24 * len(pieces) // 2 * math.prod(tail)),
        name=name,
    )(places, *args)


def by_rows(count, step):
    def some(i, _):
        step(pl.multiple_of(i * 64, 64))
        return 0

    lax.fori_loop(0, count // 64, some, 0)


def put_rows(pieces, outs, where):
    rows = pieces[0].shape[0]
    base = pl.multiple_of(where * rows, rows)

    def some(start):
        outs[0][pl.ds(base + start, 64), :] = pieces[0][pl.ds(start, 64), :].astype(F32)

    by_rows(rows, some)


put_rows.outs = 1
put_rows.pieces = 1


def put_columns(pieces, outs, where):
    rows, columns = pieces[0].shape
    base = pl.multiple_of(where * columns, columns)

    def some(start):
        outs[0][pl.ds(start, 64), pl.ds(base, columns)] = pieces[0][pl.ds(start, 64), :].astype(F32)

    by_rows(rows, some)


put_columns.outs = 1
put_columns.pieces = 1


def put_heads(pieces, outs, where):
    queries, values = pieces
    rows = queries.shape[1]
    base = pl.multiple_of(where * rows, rows)

    def some(start):
        here, there = pl.ds(start, 64), pl.ds(base + start, 64)
        for c in range(2):
            outs[0][c, there, :] = queries[c, here, :].astype(F32)
        outs[0][2, there, :] = values[0, here, :].astype(F32)

    by_rows(rows, some)
    outs[1][:, pl.ds(base, rows)] = values[1].astype(F32).T


put_heads.outs = 2
put_heads.pieces = 2


def normalize(values):
    return row_norm(values)


def norm_back(grad_norm, normed, inverse):
    return inverse * (
        grad_norm
        - jnp.mean(grad_norm, axis=-1, keepdims=True)
        - normed * jnp.mean(grad_norm * normed, axis=-1, keepdims=True)
    )


def gelu_back(expanded, grad_active):
    pull = jax.vjp(lambda value: jax.nn.gelu(value, approximate=True), expanded)[1]
    return pull(grad_active)[0]


def swap(x):
    return lax.ppermute(x, "mp", [(0, 1), (1, 0)])


def keep_valid(x, places, length):
    return jnp.where((places < length)[:, None], x, jnp.zeros_like(x))


def tie(x, *others):
    return lax.optimization_barrier((x, *others))[0]


class Line:
    def __init__(self):
        self.last = None

    def __call__(self, step, *args):
        if self.last is not None:
            args, _ = lax.optimization_barrier((args, self.last))
        out = step(*args)
        self.last = jax.tree.leaves(out)
        return out


def halve(stay, got):
    n = stay.shape[0] // 2
    return add_low(stay[n:], got[n:]), add_low(stay[:n], got[:n])


def join(a, b):
    return jnp.concatenate([a, b], axis=0)


class Sum:
    def __init__(self, line, stages):
        self.line, self.stages = line, stages

    def begin(self, send, stay):
        self.stay, self.got = stay, trade(send, self.stages[0])

    def first(self, *after):
        out, self.stay = self.line(halve, self.stay, self.got)
        self.got = trade(tie(out, *after) if after else out, self.stages[1])

    def second(self):
        out, self.stay = self.line(halve, self.stay, self.got)
        self.got = trade(out, self.stages[2])

    def third(self):
        self.stay = self.line(add_low, self.stay, self.got)
        self.got = trade(self.stay, self.stages[3])

    def fourth(self):
        self.done = self.line(add_low, self.stay, self.got)
        self.got = trade(self.done, self.stages[2])

    def fifth(self):
        self.near = self.line(join, self.done, self.got)
        self.far = trade(self.near, self.stages[1])
        self.near_other = trade(self.near, self.stages[0])

    def sixth(self):
        self.far_other = trade(tie(self.far, self.line.last), self.stages[0])

    def nears(self):
        return self.near, self.near_other

    def fars(self):
        return self.far, self.far_other


class Held:
    pass


def paired(
    tokens, lengths, first_gain, first_shift, heads_weight, relative_bias, mixer_weight, second_gain,
    second_shift, expand_weight, expand_bias, reduce_weight, reduce_bias, cotangent,
):
    member = lax.axis_index("mp")
    index = lax.axis_index("dp")
    core = index % 2
    length = lengths[0]
    own, model = tokens.shape
    buckets = relative_bias.shape[1]
    width = heads_weight.shape[2]
    hidden = expand_bias.shape[0]
    sp = jnp.stack([member.astype(jnp.int32), length.astype(jnp.int32)])
    at = jnp.stack([place_of(index, s).astype(jnp.int32) for s in STAGES])
    places = member * own + jnp.arange(own)
    places_other = (1 - member) * own + jnp.arange(own)
    row = lambda v: v.reshape(1, -1)
    line = Line()
    v = Held()
    reduce_sum, expand_sum = Sum(line, STAGES[0]), Sum(line, STAGES[0])
    query_sum, value_sum = Sum(line, STAGES[0]), Sum(line, STAGES[0])

    rows = bias_rows(relative_bias)
    target0 = keep_valid(cotangent, places, length)
    other = swap(tokens)

    def project_own():
        v.low0, v.projected0 = line(project, tokens, row(first_gain), row(first_shift), heads_weight)

    def project_other():
        v.low1, v.projected1 = line(project, other, row(first_gain), row(first_shift), heads_weight)

    active_grad = lambda t, w: columns_dot(t, w, 1, name="active_grad")

    def active_own():
        v.active_grad0 = line(active_grad, target0, reduce_weight)

    def send_more():
        n = width // 2
        half = lax.dynamic_slice_in_dim(mixer_weight, core * n, n, 0)
        ready = line.last
        v.cotangent_other = swap(tie(cotangent, other, *ready))
        v.mixer_half = swap(tie(half, other, *ready))

    def attend():
        v.mixed, v.logsum = line(attend_forward, sp, v.projected0, v.projected1, rows)
        v.mixed_other = swap(v.mixed)

    def active_other():
        v.target1 = line(lambda x: keep_valid(x, places_other, length), v.cotangent_other)
        v.active_grad1 = line(active_grad, v.target1, reduce_weight)

    def mixer_rest():
        v.mixer_rest = trade(tie(v.mixer_half, *line.last), 1)

    def mixer_both():
        a, b = v.mixer_half, v.mixer_rest
        v.mixer_other = line(order_rows, core.astype(jnp.int32).reshape(1), a, b)

    def mix_rows():
        v.middle, v.second = line(
            mix, tokens, other, v.mixed, v.mixed_other, mixer_weight, v.mixer_other,
            row(second_gain), row(second_shift),
        )

    def expand_other():
        v.act1, v.ge1, gs1, v.eb1 = line(
            lambda x, g, w, b: expand(x, 1, own, g, w, b, BF16),
            v.second, v.active_grad1, expand_weight, row(expand_bias),
        )
        v.gs_got = swap(gs1)

    def expand_own():
        v.act0, v.ge0, v.gs0, v.eb0 = line(
            lambda x, g, w, b: expand(x, 0, own, g, w, b, BF16),
            v.second, v.active_grad0, expand_weight, row(expand_bias),
        )

    def reduce_chunks():
        reduce_sum.begin(*line(
            lambda *xs: reduce_grad_part(at, 0, *xs), v.act0, v.act1, target0, v.target1
        ))

    def expand_chunks():
        expand_sum.begin(*line(lambda *xs: expand_grad_part(at, 0, *xs), v.second, v.ge0, v.ge1))

    def middle_back():
        v.attended0, v.second_sums = line(
            back_rows, v.gs0, v.gs_got, v.middle, target0, row(second_gain)
        )

    grad_mix = lambda a, w: dot(a, w, 1, 1).astype(BF16)

    def mixed_send():
        out = line(grad_mix, v.attended0, v.mixer_other)
        v.grad_mixed1 = swap(out)

    def mixed_own():
        v.grad_mixed0 = line(grad_mix, v.attended0, mixer_weight)

    def attended_send():
        v.attended1 = swap(tie(v.attended0, *line.last))

    def reduced_other():
        out = line(lambda a, w: columns_dot(a, w, 0, name="reduced"), v.act1, reduce_weight)
        v.reduced_got = swap(out)

    def attend_back():
        v.grad_projected, v.sums = line(
            attend_backward, sp, v.projected0, v.projected1, v.grad_mixed0, v.grad_mixed1,
            v.mixed, v.logsum, rows,
        )

    def query_chunks():
        query_sum.begin(*line(lambda *xs: heads_grad_part(at, 0, *xs), v.low0, v.low1, v.grad_projected))

    def value_chunks():
        value_sum.begin(*line(
            lambda *xs: values_grad_part(at, 0, *xs), v.low0, v.low1, v.grad_projected,
            v.attended0, v.attended1, v.mixed,
        ))

    def first_other():
        out = line(lambda g, w: first_rows(g, w, 1, own, BF16), v.grad_projected, heads_weight)
        v.first_got = swap(out)

    def first_own():
        v.first_part = line(lambda g, w: first_rows(g, w, 0, own, BF16), v.grad_projected, heads_weight)

    def first_back():
        v.tokens_grad, first_sums = line(
            back_rows, v.first_part, v.first_got, tokens, v.attended0, row(first_gain)
        )
        v.both = join(first_sums[:2], v.second_sums[:3])
        v.both_got = swap(v.both)

    def output():
        v.block_out = line(
            output_rows, v.middle, v.act0, reduce_weight, v.reduced_got, row(reduce_bias)
        )

    def pack_first():
        v.pack = line(
            lambda both, got, eb0, eb1, bias: jnp.concatenate(
                [(both + got).reshape(-1), (eb0 + eb1).reshape(-1), bias.reshape(-1)]
            ).reshape(-1, 128),
            v.both, v.both_got, v.eb0, v.eb1, bias_grad(v.sums, buckets),
        )
        v.pack_got = trade(v.pack, 1)

    def pack_next(bit):
        def step():
            v.pack = line(jnp.add, v.pack, v.pack_got)
            if bit:
                v.pack_got = trade(v.pack, bit)

        return step

    chunk = (hidden // 8, model)
    turned = (model, hidden // 8)

    piece = (2, model // 8, width)
    reduce_shape = [jax.ShapeDtypeStruct(reduce_weight.shape, F32)]
    expand_shape = [jax.ShapeDtypeStruct(expand_weight.shape, F32)]
    heads_shape = [jax.ShapeDtypeStruct(heads_weight.shape, F32), jax.ShapeDtypeStruct(mixer_weight.shape, F32)]
    reduce_spec = [lambda to: pl.BlockSpec((hidden // 4, model), lambda g, s: (to(g, s), 0))]
    expand_spec = [lambda to: pl.BlockSpec((model, hidden // 4), lambda g, s: (0, to(g, s)))]
    heads_spec = [
        lambda to: pl.BlockSpec((3, model // 4, width), lambda g, s: (0, to(g, s), 0)),
        lambda to: pl.BlockSpec((width, model // 4), lambda g, s: (0, to(g, s))),
    ]

    def reduce_near():
        v.reduce_grad = line(
            lambda *xs: spread(at, 0, xs, put_rows, chunk, reduce_spec, reduce_shape, name="reduce_near"),
            *reduce_sum.nears(),
        )

    def reduce_far():
        v.reduce_grad = line(
            lambda given, *xs: spread(at, 1, xs, put_rows, chunk, reduce_spec, reduce_shape, given, name="reduce_far"),
            v.reduce_grad, *reduce_sum.fars(),
        )

    def expand_near():
        v.expand_grad = line(
            lambda *xs: spread(at, 0, xs, put_columns, turned, expand_spec, expand_shape, name="expand_near"),
            *expand_sum.nears(),
        )

    def expand_far():
        v.expand_grad = line(
            lambda given, *xs: spread(at, 1, xs, put_columns, turned, expand_spec, expand_shape, given, name="expand_far"),
            v.expand_grad, *expand_sum.fars(),
        )

    def heads_near():
        v.heads_grad = line(
            lambda *xs: spread(at, 0, xs, put_heads, piece, heads_spec, heads_shape, name="heads_near"),
            *query_sum.nears(), *value_sum.nears(),
        )

    def heads_far():
        v.heads_grad = line(
            lambda given, *xs: spread(at, 1, xs, put_heads, piece, heads_spec, heads_shape, given, name="heads_far"),
            v.heads_grad, *query_sum.fars(), *value_sum.fars(),
        )

    order = (
        project_own, active_own, send_more, project_other, attend, mixer_rest, mixer_both, active_other,
        mix_rows, expand_other, expand_own, reduce_chunks, middle_back, mixed_send, expand_chunks,
        attended_send, mixed_own, reduce_sum.first, expand_sum.first, attend_back, reduce_sum.second,
        query_chunks, reduce_sum.third, value_chunks, first_other, expand_sum.second, reduce_sum.fourth,
        query_sum.first, value_sum.first, expand_sum.third, reduce_sum.fifth, query_sum.second,
        value_sum.second, first_own, first_back, expand_sum.fourth, pack_first, reduce_sum.sixth, pack_next(2),
        value_sum.third, expand_sum.fifth, reduced_other, query_sum.third, reduce_near, value_sum.fourth,
        reduce_far, query_sum.fourth, pack_next(4), expand_sum.sixth, value_sum.fifth, query_sum.fifth, output,
        value_sum.sixth, expand_near, expand_far, pack_next(8), query_sum.sixth, heads_near, heads_far,
        pack_next(0),
    )
    for step in order:
        step()
    pack = v.pack.reshape(-1)
    both = pack[: 5 * model].reshape(5, model)
    expand_bias_grad = pack[5 * model : 5 * model + hidden]
    bias_part = pack[5 * model + hidden :].reshape(relative_bias.shape)
    return (
        v.block_out, v.tokens_grad, both[0], both[1], v.heads_grad[0], bias_part, v.heads_grad[1], both[2], both[3],
        v.expand_grad[0], expand_bias_grad, v.reduce_grad[0], both[4],
    )


def gathered(
    tokens, lengths, first_gain, first_shift, heads_weight, relative_bias, mixer_weight, second_gain,
    second_shift, expand_weight, expand_bias, reduce_weight, reduce_bias, cotangent,
):
    def gather(x):
        return lax.all_gather(x, "mp", axis=0, tiled=True)

    def scatter(x):
        return lax.psum_scatter(x.astype(BF16), "mp", scatter_dimension=0, tiled=True).astype(F32)

    members = lax.axis_size("mp")
    length = lengths[0]
    own = tokens.shape[0]
    whole = own * members
    half = whole // 2
    buckets = relative_bias.shape[1]
    sp = jnp.stack([jnp.zeros((), jnp.int32), length.astype(jnp.int32)])
    places = lax.axis_index("mp") * own + jnp.arange(own)
    rows = bias_rows(relative_bias)
    source_all = gather(tokens)
    first_all, projected = project(source_all, first_gain.reshape(1, -1), first_shift.reshape(1, -1), heads_weight)
    projected0, projected1 = projected[:, :half], projected[:, half:]
    mixed, logsum = attend_forward(sp, projected0, projected1, rows)
    source = tokens.astype(F32)
    middle = source + scatter(dot(mixed, mixer_weight, 1, 0))
    second_norm, second_inverse = normalize(middle)
    second_all = gather((second_norm * second_gain + second_shift).astype(BF16))
    target = keep_valid(cotangent, places, length)
    target_wide = target.astype(F32)
    target_all = gather(target)
    expanded = dot(second_all, expand_weight, 1, 0) + expand_bias
    active_low = jax.nn.gelu(expanded, approximate=True).astype(BF16)
    grad_expanded = gelu_back(expanded, dot(target_all, reduce_weight, 1, 1)).astype(BF16)
    grad_second = scatter(dot(grad_expanded, expand_weight, 1, 1))
    reduced = scatter(dot(active_low, reduce_weight, 1, 0))
    reduce_grad = dot(active_low, target_all, 0, 0)
    expand_grad = dot(second_all, grad_expanded, 0, 0)
    expand_bias_grad = jnp.sum(grad_expanded.astype(F32), axis=0)
    block_out = (middle + reduced + reduce_bias).astype(BF16)
    grad_middle = target_wide + norm_back(grad_second * second_gain, second_norm, second_inverse)
    attended_all = gather(grad_middle.astype(BF16))
    mixer_grad = dot(mixed, attended_all, 0, 0)
    grad_mixed = dot(attended_all, mixer_weight, 1, 1).astype(BF16)
    grad_projected, sums = attend_backward(
        sp, projected0, projected1, grad_mixed[:half], grad_mixed[half:], mixed, logsum, rows
    )
    bias_part = bias_grad(sums, buckets)
    heads_grad = jnp.einsum("td,cte->cde", first_all, grad_projected, preferred_element_type=F32)
    grad_first = scatter(jnp.einsum("cte,cde->td", grad_projected, heads_weight, preferred_element_type=F32))
    first_norm, first_inverse = normalize(source)
    tokens_grad = (
        grad_middle + norm_back(grad_first * first_gain, first_norm, first_inverse)
    ).astype(BF16)
    first_gain_grad, first_shift_grad, second_gain_grad, second_shift_grad, reduce_bias_grad = (
        lax.psum(
            (
                jnp.sum(grad_first * first_norm, axis=0),
                jnp.sum(grad_first, axis=0),
                jnp.sum(grad_second * second_norm, axis=0),
                jnp.sum(grad_second, axis=0),
                jnp.sum(target_wide, axis=0),
            ),
            ("dp", "mp"),
        )
    )
    heads_grad, bias_part, mixer_grad, expand_grad, expand_bias_grad, reduce_grad = (
        lax.psum(x.astype(BF16), "dp").astype(F32)
        for x in (heads_grad, bias_part, mixer_grad, expand_grad, expand_bias_grad, reduce_grad)
    )
    return (
        block_out, tokens_grad, first_gain_grad, first_shift_grad, heads_grad, bias_part, mixer_grad,
        second_gain_grad, second_shift_grad, expand_grad, expand_bias_grad, reduce_grad, reduce_bias_grad,
    )


def per_device(*args):
    if lax.axis_size("mp") == 2 and lax.axis_size("dp") == 16:
        return paired(*args)
    return gathered(*args)


def solution(mesh):
    return jax.shard_map(
        per_device,
        mesh=mesh,
        in_specs=(
            P(("dp", "mp"), None),
            P("dp"),
            P(),
            P(),
            P(None, None, "mp"),
            P("mp", None),
            P("mp", None),
            P(),
            P(),
            P(None, "mp"),
            P("mp"),
            P("mp", None),
            P(),
            P(("dp", "mp"), None),
        ),
        out_specs=(
            P(("dp", "mp"), None),
            P(("dp", "mp"), None),
            P(),
            P(),
            P(None, None, "mp"),
            P("mp", None),
            P("mp", None),
            P(),
            P(),
            P(None, "mp"),
            P("mp"),
            P("mp", None),
            P(),
        ),
        check_vma=False,
    )
```

```python
import functools
import math

import jax
import jax.numpy as jnp
import numpy as np
from jax import lax
from jax.experimental import pallas as pl
from jax.experimental.pallas import tpu as pltpu
from jax.sharding import PartitionSpec as P

EPS = 1e-05
DH=64; MAXDIST=128; NEG=-1e30; BLK=256
F32=jnp.float32; BF16=jnp.bfloat16
HIGHEST=lax.Precision.HIGHEST

def bucket_table(count, buckets, reach):
    exact = buckets // 2
    entries = []
    for position in range(count):
        if position < exact:
            entries.append(position)
        else:
            level = exact + int(math.log(position / exact) / math.log(reach / exact) * (buckets - exact))
            entries.append(min(buckets - 1, level))
    return np.array(entries, dtype=np.int32)

def bucket_starts(buckets):
    table=bucket_table(4*MAXDIST+2*buckets,buckets,MAXDIST)
    return [int(np.argmax(table>=level)) for level in range(1,buckets)]

def bias_rows_kernel(r_ref,o_ref):
    heads,buckets=r_ref.shape
    W=2*BLK
    rel=r_ref[...]-r_ref[:,buckets-1:]
    place=lax.broadcasted_iota(jnp.int32,(heads,W),1)
    signed=jnp.where(place<BLK,place,place-W)
    for part,distance in enumerate((-signed,BLK-signed,signed,BLK+signed)):
        value=jnp.broadcast_to(rel[:,:1],(heads,W))
        for level,start in enumerate(bucket_starts(buckets)):
            value=jnp.where(distance>=start,rel[:,level+1:level+2],value)
        value=jnp.where(distance>=0,value,NEG)
        for pair in range(heads//2):
            o_ref[pair,:,part*W:(part+1)*W]=value[2*pair:2*pair+2]

def bias_rows(relative_bias):
    heads=relative_bias.shape[0]
    return pl.pallas_call(
        bias_rows_kernel,
        out_shape=jax.ShapeDtypeStruct((heads//2,2,8*BLK),F32),
        name="bias_rows",
    )(relative_bias)

def toeplitz(row):
    wide=jnp.broadcast_to(row,(BLK,2*BLK))
    return pltpu.roll(wide,0,1,stride=1,stride_axis=0)[:,:BLK]


def lane_masks():
    lane=lax.broadcasted_iota(jnp.int32,(1,128),1)
    head=[(lane//DH)==h for h in range(2)]
    mine=[jnp.where(m,1.0,0.0).astype(BF16) for m in head]
    spare=[jnp.where(lane==DH*(1-h),1.0,0.0) for h in range(2)]
    return head,mine,spare


def gone_rows(start,half,length,spare):
    pos=lax.broadcasted_iota(jnp.int32,(half,1),0)+start
    gone=jnp.where(pos<length,0.0,NEG)
    return [(gone*s).astype(BF16) for s in spare]


def fwd_kernel(sp, a_ref,c_ref,b_ref,o_ref,lse_ref,qs,ks,vs):
    half=a_ref.shape[1]; T=2*half; flip=sp[0]; length=sp[1]
    W=2*BLK
    head,mine,spare=lane_masks()
    for a,ref in enumerate((a_ref,c_ref)):
        start=pl.multiple_of((a^flip)*half,half)
        dst=pl.ds(start,half)
        gone=gone_rows(start,half,length,spare)
        for h in range(2):
            qs[h,dst,:]=ref[0]*(mine[h]*jnp.asarray(DH**-0.5,BF16))+spare[h].astype(BF16)
            ks[h,dst,:]=ref[1]*mine[h]+gone[h]
            vs[h,dst,:]=ref[2]*mine[h]+mine[1-h]
    tiles=[(toeplitz(b_ref[0,h:h+1,0:W]),toeplitz(b_ref[0,h:h+1,W:2*W])) for h in range(2)]
    outs={}

    def score(i,h):
        return dot(qs[h,i*BLK:(i+1)*BLK,:],ks[h,:(i+1)*BLK,:],1,1)

    def finish(i,h,s):
        kc=(i+1)*BLK; t0,t1=tiles[h]
        parts=[]
        if i>=2: parts.append(s[:,:kc-2*BLK])
        if i>=1: parts.append(s[:,kc-2*BLK:kc-BLK]+t1)
        parts.append(s[:,kc-BLK:]+t0)
        top=functools.reduce(jnp.maximum,[jnp.max(x,axis=1,keepdims=True) for x in parts])
        p=jnp.concatenate([jnp.exp(x-top).astype(BF16) for x in parts],axis=1)
        o=dot(p,vs[h,:kc,:],1,0)
        total=o[:,DH*(1-h):DH*(1-h)+1]
        outs[h]=(o*(1.0/total),top+jnp.log(total))
        if h==1:
            rows=pl.ds(pl.multiple_of((i*BLK+flip*half)%T,BLK),BLK)
            o_ref[rows,:]=jnp.where(head[0],outs[0][0],outs[1][0]).astype(BF16)
            lse_ref[0,i*BLK:kc,:]=jnp.where(head[0],outs[0][1],outs[1][1])

    run_ahead([(i,h) for i in range(T//BLK) for h in range(2)],score,finish,2)


def run_ahead(items,first,second,depth):
    waiting=[]
    for item in items:
        waiting.append((item,first(*item)))
        if len(waiting)>depth:
            done,value=waiting.pop(0)
            second(*done,value)
    for done,value in waiting:
        second(*done,value)


def attend_forward(sp,projected0,projected1,rows):
    _,half,HD=projected0.shape; pairs=HD//128; T=2*half
    part=pl.BlockSpec((3,half,128),lambda p,s:(0,0,p))
    return pl.pallas_call(
        fwd_kernel,
        grid_spec=pltpu.PrefetchScalarGridSpec(
            num_scalar_prefetch=1,grid=(pairs,),
            in_specs=[part,part,pl.BlockSpec((1,2,rows.shape[2]),lambda p,s:(p,0,0))],
            out_specs=[pl.BlockSpec((T,128),lambda p,s:(0,p)),pl.BlockSpec((1,T,128),lambda p,s:(p,0,0))],
            scratch_shapes=[pltpu.VMEM((2,T,128),BF16)]*3),
        out_shape=[jax.ShapeDtypeStruct((T,HD),BF16),jax.ShapeDtypeStruct((pairs,T,128),F32)],
        cost_estimate=cost(8*T*T*HD,8*T*HD+512*pairs*T),
        name="attend_forward",
    )(sp,projected0,projected1,rows)

def diagonal_sums(acc, offset):
    W=2*BLK
    wide=jnp.concatenate([acc,jnp.zeros_like(acc)],axis=1)
    n=BLK
    while n>1:
        n//=2
        top=wide[:n]; bottom=wide[n:2*n]
        wide=top+pltpu.roll(bottom,W-n,1)
    return pltpu.roll(wide,offset,1) if offset else wide

def bwd_kernel(sp, a_ref,c_ref,d0_ref,d1_ref,o_ref,lse_ref,b_ref,g_ref,d_ref,qs,ks,vs,dos,dq,acc0,acc1):
    half=a_ref.shape[1]; T=2*half; flip=sp[0]; length=sp[1]
    W=2*BLK
    n=T//BLK
    head,mine,spare=lane_masks()
    stats=[None,None]
    one=sum(spare).astype(BF16)
    for a,(ref,do_ref) in enumerate(((a_ref,d0_ref),(c_ref,d1_ref))):
        start=pl.multiple_of((a^flip)*half,half)
        dst=pl.ds(start,half)
        gone=gone_rows(start,half,length,spare)
        for h in range(2):
            qs[h,dst,:]=ref[0]*(mine[h]*jnp.asarray(DH**-0.5,BF16))+spare[h].astype(BF16)
            ks[h,dst,:]=ref[1]*mine[h]+gone[h]
            vs[h,dst,:]=ref[2]*mine[h]
        dos[dst,:]=do_ref[...]
        acc0[0,dst,:]=do_ref[...].astype(F32)*o_ref[a*half:(a+1)*half,:].astype(F32)
    turned=acc0[0].T
    deltas=[jnp.sum(turned[h*DH:(h+1)*DH],axis=0,keepdims=True) for h in range(2)]
    turned=lse_ref[0].T
    lses=[turned[h*DH:h*DH+1] for h in range(2)]
    near=acc1
    tiles=[(toeplitz(b_ref[0,h:h+1,2*W:3*W]),toeplitz(b_ref[0,h:h+1,3*W:])) for h in range(2)]

    def products(j,h):
        rj=slice(j*BLK,(j+1)*BLK)
        return dot(ks[h,rj,:],qs[h,j*BLK:,:],1,1),dot(vs[h,rj,:],dos[j*BLK:,:],1,1)

    keep={}

    def finish(j,h,value):
        s,dp=value
        rj=slice(j*BLK,(j+1)*BLK)
        ps=[];dss=[]
        for b in range(n-j):
            c=slice(b*BLK,(b+1)*BLK)
            cc=slice((j+b)*BLK,(j+b+1)*BLK)
            x=s[:,c]-lses[h][:,cc]
            if b<2: x=x+tiles[h][b]
            p=jnp.exp(x)
            ds=p*(dp[:,c]-deltas[h][:,cc])
            if b<2:
                if j==0: near[h,b]=ds
                else: near[h,b]+=ds
            ps.append(p.astype(BF16)); dss.append(ds.astype(BF16))
        p=jnp.concatenate(ps,axis=1); ds=jnp.concatenate(dss,axis=1)
        dv=dot(p,dos[j*BLK:,:],1,0)
        dk=dot(ds,qs[h,j*BLK:,:],1,0)
        kk=ks[h,rj,:]*mine[h]+mine[1-h]
        dqj=dot(ds,kk,0,0)
        if j==0: dq[h,:,:]=dqj
        else: dq[h,j*BLK:,:]+=dqj
        keep[h]=(dk,dv)
        if h==1:
            rows=pl.ds(pl.multiple_of((j*BLK+flip*half)%T,BLK),BLK)
            g_ref[1,rows,:]=jnp.where(head[0],keep[0][0],keep[1][0]).astype(BF16)
            g_ref[2,rows,:]=jnp.where(head[0],keep[0][1],keep[1][1]).astype(BF16)

    run_ahead([(j,h) for j in range(n) for h in range(2)],products,finish,1)
    for h in range(2):
        d_ref[0,h:h+1,:]=diagonal_sums(near[h,0],0)+diagonal_sums(near[h,1],BLK)
        total=jnp.sum(dq[h,:,:],axis=0,keepdims=True)[:,DH*(1-h):DH*(1-h)+1]
        d_ref[0,2+h:3+h,:]=jnp.broadcast_to(total,(1,W))
    for a in range(2):
        dst=pl.ds(pl.multiple_of((a^flip)*half,half),half)
        g_ref[0,a*half:(a+1)*half,:]=(jnp.where(head[0],dq[0,dst,:],dq[1,dst,:])*DH**-0.5).astype(BF16)

def attend_backward(sp,projected0,projected1,grad0,grad1,mixed,lse,rows,start=0,count=None,given=None):
    _,half,HD=projected0.shape; pairs=HD//128; T=2*half
    count=pairs if count is None else count
    part=pl.BlockSpec((3,half,128),lambda p,s:(0,0,p+start))
    grad=pl.BlockSpec((half,128),lambda p,s:(0,p+start))
    in_specs=[part,part,grad,grad,pl.BlockSpec((T,128),lambda p,s:(0,p+start)),
              pl.BlockSpec((1,T,128),lambda p,s:(p+start,0,0)),pl.BlockSpec((1,2,rows.shape[2]),lambda p,s:(p+start,0,0))]
    args=[sp,projected0,projected1,grad0,grad1,mixed,lse,rows]
    kernel=bwd_kernel
    if given is not None:
        in_specs.append(pl.BlockSpec(memory_space=pl.ANY)); args.append(given)
        kernel=lambda *refs: bwd_kernel(*refs[:8],*refs[9:])
    return pl.pallas_call(
        kernel,
        grid_spec=pltpu.PrefetchScalarGridSpec(
            num_scalar_prefetch=1,grid=(count,),
            in_specs=in_specs,
            out_specs=[pl.BlockSpec((3,T,128),lambda p,s:(0,0,p+start)),pl.BlockSpec((1,4,2*BLK),lambda p,s:(p,0,0))],
            scratch_shapes=[pltpu.VMEM((2,T,128),BF16)]*3+[pltpu.VMEM((T,128),BF16),pltpu.VMEM((2,T,128),F32),pltpu.VMEM((1,T,128),F32),pltpu.VMEM((2,2,BLK,BLK),F32)]),
        out_shape=[jax.ShapeDtypeStruct((3,T,HD),BF16),jax.ShapeDtypeStruct((count,4,2*BLK),F32)],
        input_output_aliases={} if given is None else {8:0},
        cost_estimate=cost(20*T*T*128*count,(16*T*128+512*T)*count),
        name="attend_backward",
    )(*args)

def bias_grad(sums, buckets):
    pairs=sums.shape[0]; W=2*BLK
    near=sums[:,0:2].reshape(pairs*2,W); total=sums[:,2:4,0].reshape(pairs*2,1)
    edges=[0]+bucket_starts(buckets)
    distance=jnp.arange(W)[None,None]
    low=jnp.asarray(np.array(edges[:-1],np.int32))[None,:,None]
    high=jnp.asarray(np.array(edges[1:],np.int32))[None,:,None]
    parts=jnp.sum(jnp.where((distance>=low)&(distance<high),near[:,None,:],0.0),axis=2)
    return jnp.concatenate([parts,total-jnp.sum(parts,axis=1,keepdims=True)],axis=1)


HALF_TANH = math.sqrt(2.0 / math.pi)


def dot(a, b, ca, cb):
    return lax.dot_general(a, b, (((ca,), (cb,)), ((), ())), preferred_element_type=F32)


def fixed(shape):
    return pl.BlockSpec(shape, lambda *_: (0,) * len(shape))


def cost(flops, moved):
    return pl.CostEstimate(flops=int(flops), transcendentals=0, bytes_accessed=int(moved))


def cost4(flops, moved):
    return cost(4 * flops, 4 * moved)


def cost16(flops, moved):
    return cost(16 * flops, 16 * moved)


def row_norm(values):
    center = jnp.mean(values, axis=-1, keepdims=True)
    centered = values - center
    inverse = lax.rsqrt(jnp.mean(centered * centered, axis=-1, keepdims=True) + EPS)
    return centered * inverse, inverse


def project_kernel(x_ref, gain_ref, shift_ref, w_ref, low_ref, out_ref):
    normed, _ = row_norm(x_ref[...].astype(F32))
    low = (normed * gain_ref[...] + shift_ref[...]).astype(BF16)
    low_ref[...] = low
    for c in range(3):
        out_ref[c] = dot(low, w_ref[c], 1, 0).astype(BF16)


def project(x, gain, shift, weight):
    rows, model = x.shape
    width = weight.shape[2]
    step = min(256, rows)
    return pl.pallas_call(
        project_kernel,
        grid=(rows // step,),
        in_specs=[pl.BlockSpec((step, model), lambda i: (i, 0)), fixed((1, model)), fixed((1, model)), fixed(weight.shape)],
        out_specs=[pl.BlockSpec((step, model), lambda i: (i, 0)), pl.BlockSpec((3, step, width), lambda i: (0, i, 0))],
        out_shape=[jax.ShapeDtypeStruct((rows, model), BF16), jax.ShapeDtypeStruct((3, rows, width), BF16)],
        cost_estimate=cost16(6 * rows * model * width, 2 * (2 * rows * model + weight.size + 3 * rows * width)),
        name="project",
    )(x, gain, shift, weight)


def mix_kernel(own_blocks, x0_ref, x1_ref, m_ref, p_ref, w0_ref, w1_ref, gain_ref, shift_ref, mid_ref, low_ref):
    i = pl.program_id(0)
    attended = dot(m_ref[...], w0_ref[...], 1, 0) + dot(p_ref[...], w1_ref[...], 1, 0)

    def rows(x_ref):
        return x_ref[...].astype(F32) + attended

    def rest(middle):
        normed, _ = row_norm(middle)
        low_ref[...] = (normed * gain_ref[...] + shift_ref[...]).astype(BF16)

    @pl.when(i < own_blocks)
    def _():
        middle = rows(x0_ref)
        mid_ref[...] = middle.astype(BF16)
        rest(middle)

    @pl.when(i >= own_blocks)
    def _():
        rest(rows(x1_ref))


def mix(tokens, other, mixed, mixed_other, weight, weight_other, gain, shift):
    own, model = tokens.shape
    width = mixed.shape[1]
    step = 256
    n = own // step
    return pl.pallas_call(
        functools.partial(mix_kernel, n),
        grid=(2 * n,),
        in_specs=[
            pl.BlockSpec((step, model), lambda i: (jnp.minimum(i, n - 1), 0)),
            pl.BlockSpec((step, model), lambda i: (jnp.maximum(i - n, 0), 0)),
            pl.BlockSpec((step, width), lambda i: (i, 0)),
            pl.BlockSpec((step, width), lambda i: ((i + n) % (2 * n), 0)),
            fixed(weight.shape), fixed(weight.shape), fixed((1, model)), fixed((1, model)),
        ],
        out_specs=[
            pl.BlockSpec((step, model), lambda i: (jnp.minimum(i, n - 1), 0)),
            pl.BlockSpec((step, model), lambda i: (i, 0)),
        ],
        out_shape=[jax.ShapeDtypeStruct((own, model), BF16), jax.ShapeDtypeStruct((2 * own, model), BF16)],
        cost_estimate=cost4(8 * own * model * width, 2 * (4 * own * model + 4 * own * width + 2 * weight.size) + 4 * own * model),
        name="mix",
    )(tokens, other, mixed, mixed_other, weight, weight_other, gain, shift)


def expand_kernel(x_ref, g_ref, w_ref, b_ref, act_ref, ge_ref, gs_ref, bias_ref, acc_ref):
    i = pl.program_id(0)
    x = x_ref[...]
    width = w_ref.shape[1]
    sub = min(512, width)
    total = None
    for s in range(width // sub):
        cols = slice(s * sub, (s + 1) * sub)
        u = dot(x, w_ref[:, cols], 1, 0) + b_ref[:, cols].astype(F32)
        square = u * u
        t = jnp.tanh(HALF_TANH * u * (1.0 + 0.044715 * square))
        half = 0.5 + 0.5 * t
        act_ref[:, cols] = (u * half).astype(BF16)
        slope = half + 0.5 * u * (1.0 - t * t) * (HALF_TANH * (1.0 + 3 * 0.044715 * square))
        grad = g_ref[:, cols].astype(F32) * slope
        low = grad.astype(BF16)
        ge_ref[:, cols] = low
        bias_ref[:, cols] = jnp.sum(grad, axis=0, keepdims=True)
        part = dot(low, w_ref[:, cols], 1, 1)
        total = part if total is None else total + part

    @pl.when(i == 0)
    def _():
        acc_ref[...] = total

    @pl.when(i > 0)
    def _():
        acc_ref[...] += total

    @pl.when(i == pl.num_programs(0) - 1)
    def _():
        gs_ref[...] = acc_ref[...].astype(gs_ref.dtype)


def expand(x, block, rows, grad_active, weight, bias, dtype):
    model = x.shape[1]
    hidden = weight.shape[1]
    step = min(512, hidden)
    return pl.pallas_call(
        expand_kernel,
        grid=(hidden // step,),
        in_specs=[
            pl.BlockSpec((rows, model), lambda i: (block, 0)),
            pl.BlockSpec((rows, step), lambda i: (0, i)),
            pl.BlockSpec((model, step), lambda i: (0, i)),
            pl.BlockSpec((1, step), lambda i: (0, i)),
        ],
        out_specs=[
            pl.BlockSpec((rows, step), lambda i: (0, i)),
            pl.BlockSpec((rows, step), lambda i: (0, i)),
            fixed((rows, model)),
            pl.BlockSpec((1, step), lambda i: (0, i)),
        ],
        out_shape=[
            jax.ShapeDtypeStruct((rows, hidden), BF16),
            jax.ShapeDtypeStruct((rows, hidden), BF16),
            jax.ShapeDtypeStruct((rows, model), dtype),
            jax.ShapeDtypeStruct((1, hidden), F32),
        ],
        scratch_shapes=[pltpu.VMEM((rows, model), F32)],
        cost_estimate=cost(4 * rows * model * hidden, 2 * (2 * rows * model + 3 * rows * hidden + weight.size)),
        name="expand",
    )(x, grad_active, weight, bias)


STAGES = ((1, 2, 4, 8), (1, 4, 2, 8))


def place_of(index, stages):
    bit = [(index // s) % 2 for s in stages]
    return bit[0] * 4 + bit[1] * 2 + bit[2]


def trade(x, bit):
    size = lax.axis_size("dp")
    return lax.ppermute(x, "dp", [(i, i ^ bit) for i in range(size)])


def add_low(a, b):
    return (a.astype(F32) + b.astype(F32)).astype(BF16)


def pair_of(g, s, slot):
    return (3 - g) ^ (s[slot] // 2)


def put_pair(slot, s_ref, chunks, outs):
    flip = s_ref[slot] % 2
    sent = pl.program_id(0) < 2
    for j, value in enumerate(chunks):
        value = value.astype(BF16)[None]
        for out, here in zip(outs, (sent, jnp.logical_not(sent))):
            @pl.when(here)
            def _(out=out):
                out[pl.ds(j ^ flip, 1)] = value


def pair_call(kernel, slot, s, arrays, specs, tail, flops, name):
    zeros = (0,) * len(tail)
    moved = sum(2 * x.size for x in arrays) + 16 * math.prod(tail)
    return pl.pallas_call(
        functools.partial(kernel, slot),
        grid_spec=pltpu.PrefetchScalarGridSpec(
            num_scalar_prefetch=1, grid=(4,), in_specs=specs,
            out_specs=[
                pl.BlockSpec((2, *tail), lambda g, s: (jnp.maximum(1 - g, 0), *zeros)),
                pl.BlockSpec((2, *tail), lambda g, s: (jnp.minimum(3 - g, 1), *zeros)),
            ],
        ),
        out_shape=[jax.ShapeDtypeStruct((4, *tail), BF16)] * 2,
        cost_estimate=cost(flops, moved),
        name=name,
    )(s, *arrays)


def reduce_grad_kernel(slot, s_ref, *refs):
    (a0, a1, t0, t1), outs = refs[:4], refs[4:]
    value = dot(a0[...], t0[...], 0, 0) + dot(a1[...], t1[...], 0, 0)
    width = value.shape[0] // 2
    put_pair(slot, s_ref, [value[:width], value[width:]], outs)


def reduce_grad_part(s, slot, act0, act1, t0, t1):
    rows, hidden = act0.shape
    model = t0.shape[1]
    block = pl.BlockSpec((rows, hidden // 4), lambda g, s: (0, pair_of(g, s, slot)))
    return pair_call(
        reduce_grad_kernel, slot, s, (act0, act1, t0, t1), [block, block, fixed(t0.shape), fixed(t1.shape)],
        (hidden // 8, model), 4 * rows * model * hidden, "reduce_grad",
    )


def expand_grad_kernel(slot, s_ref, *refs):
    (x, g0, g1), outs = refs[:3], refs[3:]
    rows = g0.shape[0]
    value = dot(x[:rows], g0[...], 0, 0) + dot(x[rows:], g1[...], 0, 0)
    width = value.shape[1] // 2
    put_pair(slot, s_ref, [value[:, :width], value[:, width:]], outs)


def expand_grad_part(s, slot, x, g0, g1):
    rows, hidden = g0.shape
    model = x.shape[1]
    block = pl.BlockSpec((rows, hidden // 4), lambda g, s: (0, pair_of(g, s, slot)))
    return pair_call(
        expand_grad_kernel, slot, s, (x, g0, g1), [fixed(x.shape), block, block],
        (model, hidden // 8), 4 * rows * model * hidden, "expand_grad",
    )


def heads_grad_kernel(slot, s_ref, *refs):
    (l0, l1, g), outs = refs[:3], refs[3:]
    rows = l0.shape[0]
    both = [dot(l0[...], g[c, :rows], 0, 0) + dot(l1[...], g[c, rows:], 0, 0) for c in range(2)]
    width = both[0].shape[0] // 2
    chunks = [jnp.stack([v[j * width:(j + 1) * width] for v in both]) for j in range(2)]
    put_pair(slot, s_ref, chunks, outs)


def heads_grad_part(s, slot, low0, low1, grad):
    rows, model = low0.shape
    width = grad.shape[2]
    block = pl.BlockSpec((rows, model // 4), lambda g, s: (0, pair_of(g, s, slot)))
    return pair_call(
        heads_grad_kernel, slot, s, (low0, low1, grad),
        [block, block, pl.BlockSpec((2, 2 * rows, width), lambda g, s: (0, 0, 0))],
        (2, model // 8, width), 8 * rows * model * width, "heads_grad",
    )


def values_grad_kernel(slot, s_ref, *refs):
    (l0, l1, g, a0, a1, m), outs = refs[:6], refs[6:]
    rows = l0.shape[0]
    both = [
        dot(l0[...], g[0, :rows], 0, 0) + dot(l1[...], g[0, rows:], 0, 0),
        dot(a0[...], m[:rows], 0, 0) + dot(a1[...], m[rows:], 0, 0),
    ]
    width = both[0].shape[0] // 2
    chunks = [jnp.stack([v[j * width:(j + 1) * width] for v in both]) for j in range(2)]
    put_pair(slot, s_ref, chunks, outs)


def values_grad_part(s, slot, low0, low1, grad, att0, att1, mixed):
    rows, model = low0.shape
    width = grad.shape[2]
    block = pl.BlockSpec((rows, model // 4), lambda g, s: (0, pair_of(g, s, slot)))
    return pair_call(
        values_grad_kernel, slot, s, (low0, low1, grad, att0, att1, mixed),
        [block, block, pl.BlockSpec((1, 2 * rows, width), lambda g, s: (2, 0, 0)), block, block, fixed(mixed.shape)],
        (2, model // 8, width), 8 * rows * model * width, "values_grad",
    )


def columns_kernel(turn, a_ref, b_ref, out_ref):
    out_ref[...] = dot(a_ref[...], b_ref[...], 1, turn).astype(out_ref.dtype)


def columns_dot(a, b, turn, name):
    rows, depth = a.shape
    columns = b.shape[1 - turn]
    step = min(512, columns)
    block = ((step, depth), lambda i: (i, 0)) if turn else ((depth, step), lambda i: (0, i))
    return pl.pallas_call(
        functools.partial(columns_kernel, turn),
        grid=(columns // step,),
        in_specs=[fixed(a.shape), pl.BlockSpec(*block)],
        out_specs=pl.BlockSpec((rows, step), lambda i: (0, i)),
        out_shape=jax.ShapeDtypeStruct((rows, columns), BF16),
        cost_estimate=cost16(2 * rows * depth * columns, 2 * (a.size + b.size + rows * columns)),
        name=name,
    )(a, b)


def output_kernel(m_ref, a_ref, w_ref, r_ref, bias_ref, out_ref):
    out_ref[...] = (
        m_ref[...].astype(F32) + dot(a_ref[...], w_ref[...], 1, 0) + r_ref[...].astype(F32) + bias_ref[...]
    ).astype(BF16)


def output_rows(middle, act, weight, reduced, bias):
    rows, hidden = act.shape
    model = weight.shape[1]
    step = 256
    block = pl.BlockSpec((rows, step), lambda i: (0, i))
    return pl.pallas_call(
        output_kernel,
        grid=(model // step,),
        in_specs=[
            block, fixed(act.shape), pl.BlockSpec((hidden, step), lambda i: (0, i)), block,
            pl.BlockSpec((1, step), lambda i: (0, i)),
        ],
        out_specs=block,
        out_shape=jax.ShapeDtypeStruct((rows, model), BF16),
        cost_estimate=cost16(2 * rows * hidden * model, 2 * (act.size + weight.size) + 8 * rows * model),
        name="output",
    )(middle, act, weight, reduced, bias)


def first_kernel(g_ref, w_ref, out_ref, acc_ref):
    c = pl.program_id(0)
    value = dot(g_ref[0], w_ref[0], 1, 1)

    @pl.when(c == 0)
    def _():
        acc_ref[...] = value

    @pl.when(c > 0)
    def _():
        acc_ref[...] += value

    @pl.when(c == pl.num_programs(0) - 1)
    def _():
        out_ref[...] = acc_ref[...].astype(out_ref.dtype)


def first_rows(grad, weight, part, rows, dtype):
    kinds, model, width = weight.shape
    return pl.pallas_call(
        first_kernel,
        grid=(kinds,),
        in_specs=[
            pl.BlockSpec((1, rows, width), lambda c: (c, part, 0)),
            pl.BlockSpec((1, model, width), lambda c: (c, 0, 0)),
        ],
        out_specs=fixed((rows, model)),
        out_shape=jax.ShapeDtypeStruct((rows, model), dtype),
        scratch_shapes=[pltpu.VMEM((rows, model), F32)],
        cost_estimate=cost(2 * kinds * rows * width * model, 2 * (grad.size + weight.size) + 4 * rows * model),
        name="first_rows",
    )(grad, weight)


def back_kernel(a_ref, b_ref, source_ref, add_ref, gain_ref, out_ref, sums_ref):
    @pl.when(pl.program_id(0) == 0)
    def _():
        sums_ref[...] = jnp.zeros_like(sums_ref)

    def some(i, _):
        rows = pl.ds(pl.multiple_of(i * 128, 128), 128)
        normed, inverse = row_norm(source_ref[rows, :].astype(F32))
        grad = a_ref[rows, :].astype(F32) + b_ref[rows, :].astype(F32)
        add = add_ref[rows, :].astype(F32)
        scaled = grad * gain_ref[...]
        weighted = grad * normed
        mean = jnp.mean(scaled, axis=-1, keepdims=True)
        along = jnp.mean(scaled * normed, axis=-1, keepdims=True)
        out_ref[rows, :] = (add + inverse * (scaled - mean - normed * along)).astype(BF16)
        for k, value in enumerate((weighted, grad, add)):
            sums_ref[k:k + 1] += jnp.sum(value, axis=0, keepdims=True)
        return 0

    lax.fori_loop(0, source_ref.shape[0] // 128, some, 0)


def back_rows(a, b, source, add, gain):
    rows, model = a.shape
    step = 256
    block = pl.BlockSpec((step, model), lambda i: (i, 0))
    return pl.pallas_call(
        back_kernel,
        grid=(rows // step,),
        in_specs=[block] * 4 + [fixed((1, model))],
        out_specs=[block, fixed((8, model))],
        out_shape=[jax.ShapeDtypeStruct((rows, model), BF16), jax.ShapeDtypeStruct((8, model), F32)],
        cost_estimate=cost(30 * rows * model, 10 * rows * model),
        name="back_rows",
    )(a, b, source, add, gain)


def order_kernel(s_ref, a_ref, b_ref, out_ref):
    @pl.when(pl.program_id(0) == 0)
    def _():
        out_ref[...] = a_ref[...]

    @pl.when(pl.program_id(0) == 1)
    def _():
        out_ref[...] = b_ref[...]


def order_rows(core, a, b):
    rows, model = a.shape
    return pl.pallas_call(
        order_kernel,
        grid_spec=pltpu.PrefetchScalarGridSpec(
            num_scalar_prefetch=1, grid=(2,),
            in_specs=[pl.BlockSpec((rows, model), lambda g, s: (0, 0))] * 2,
            out_specs=pl.BlockSpec((rows, model), lambda g, s: (g ^ s[0], 0)),
        ),
        out_shape=jax.ShapeDtypeStruct((2 * rows, model), a.dtype),
        cost_estimate=cost(0, 8 * rows * model),
        name="order_rows",
    )(core, a, b)


def spread_kernel(put, s_ref, *refs):
    g = pl.program_id(0)
    count = put.pieces
    pieces, outs = refs[-2 * count - put.outs:-put.outs], refs[-put.outs:]
    for a in range(2):
        @pl.when(g == a)
        def _(a=a):
            def one(j, _):
                put([piece.at[j] for piece in pieces[a::2]], outs, j ^ (s_ref[0] % 2))
                return 0

            lax.fori_loop(0, 2, one, 0)


def spread(places, part, pieces, put, tail, out_specs, out_shape, given=None, name=None):
    zeros = (0,) * len(tail)

    def at(g, s):
        return (2 * g + part) ^ (s[0] // 2)

    in_specs = [pl.BlockSpec((2, *tail), lambda g, s: (0, *zeros)) for _ in pieces]
    args = list(pieces)
    aliases = {}
    if given is not None:
        in_specs = [pl.BlockSpec(memory_space=pl.ANY)] * len(given) + in_specs
        args = [*given, *args]
        aliases = {1 + k: k for k in range(len(given))}
    return pl.pallas_call(
        functools.partial(spread_kernel, put),
        grid_spec=pltpu.PrefetchScalarGridSpec(
            num_scalar_prefetch=1, grid=(2,), in_specs=in_specs, out_specs=[spec(at) for spec in out_specs],
        ),
        out_shape=out_shape,
        input_output_aliases=aliases,
        cost_estimate=cost(0, 24 * len(pieces) // 2 * math.prod(tail)),
        name=name,
    )(places, *args)


def by_rows(count, step):
    def some(i, _):
        step(pl.multiple_of(i * 64, 64))
        return 0

    lax.fori_loop(0, count // 64, some, 0)


def put_rows(pieces, outs, where):
    rows = pieces[0].shape[0]
    base = pl.multiple_of(where * rows, rows)

    def some(start):
        outs[0][pl.ds(base + start, 64), :] = pieces[0][pl.ds(start, 64), :].astype(F32)

    by_rows(rows, some)


put_rows.outs = 1
put_rows.pieces = 1


def put_columns(pieces, outs, where):
    rows, columns = pieces[0].shape
    base = pl.multiple_of(where * columns, columns)

    def some(start):
        outs[0][pl.ds(start, 64), pl.ds(base, columns)] = pieces[0][pl.ds(start, 64), :].astype(F32)

    by_rows(rows, some)


put_columns.outs = 1
put_columns.pieces = 1


def put_heads(pieces, outs, where):
    queries, values = pieces
    rows = queries.shape[1]
    base = pl.multiple_of(where * rows, rows)

    def some(start):
        here, there = pl.ds(start, 64), pl.ds(base + start, 64)
        for c in range(2):
            outs[0][c, there, :] = queries[c, here, :].astype(F32)
        outs[0][2, there, :] = values[0, here, :].astype(F32)

    by_rows(rows, some)
    outs[1][:, pl.ds(base, rows)] = values[1].astype(F32).T


put_heads.outs = 2
put_heads.pieces = 2


def normalize(values):
    return row_norm(values)


def norm_back(grad_norm, normed, inverse):
    return inverse * (
        grad_norm
        - jnp.mean(grad_norm, axis=-1, keepdims=True)
        - normed * jnp.mean(grad_norm * normed, axis=-1, keepdims=True)
    )


def gelu_back(expanded, grad_active):
    pull = jax.vjp(lambda value: jax.nn.gelu(value, approximate=True), expanded)[1]
    return pull(grad_active)[0]


def swap(x):
    return lax.ppermute(x, "mp", [(0, 1), (1, 0)])


def keep_valid(x, places, length):
    return jnp.where((places < length)[:, None], x, jnp.zeros_like(x))


def tie(x, *others):
    return lax.optimization_barrier((x, *others))[0]


class Line:
    def __init__(self):
        self.last = None

    def __call__(self, step, *args):
        if self.last is not None:
            args, _ = lax.optimization_barrier((args, self.last))
        out = step(*args)
        self.last = jax.tree.leaves(out)
        return out


def halve(stay, got):
    n = stay.shape[0] // 2
    return add_low(stay[n:], got[n:]), add_low(stay[:n], got[:n])


def join(a, b):
    return jnp.concatenate([a, b], axis=0)


class Sum:
    def __init__(self, line, stages):
        self.line, self.stages = line, stages

    def begin(self, send, stay):
        self.stay, self.got = stay, trade(send, self.stages[0])

    def first(self, *after):
        out, self.stay = self.line(halve, self.stay, self.got)
        self.got = trade(tie(out, *after) if after else out, self.stages[1])

    def second(self):
        out, self.stay = self.line(halve, self.stay, self.got)
        self.got = trade(out, self.stages[2])

    def third(self):
        self.stay = self.line(add_low, self.stay, self.got)
        self.got = trade(self.stay, self.stages[3])

    def fourth(self):
        self.done = self.line(add_low, self.stay, self.got)
        self.got = trade(self.done, self.stages[2])

    def fifth(self):
        self.near = self.line(join, self.done, self.got)
        self.far = trade(self.near, self.stages[1])
        self.near_other = trade(self.near, self.stages[0])

    def sixth(self):
        self.far_other = trade(tie(self.far, self.line.last), self.stages[0])

    def nears(self):
        return self.near, self.near_other

    def fars(self):
        return self.far, self.far_other


class Held:
    pass


def paired(
    tokens, lengths, first_gain, first_shift, heads_weight, relative_bias, mixer_weight, second_gain,
    second_shift, expand_weight, expand_bias, reduce_weight, reduce_bias, cotangent,
):
    member = lax.axis_index("mp")
    index = lax.axis_index("dp")
    core = index % 2
    length = lengths[0]
    own, model = tokens.shape
    buckets = relative_bias.shape[1]
    width = heads_weight.shape[2]
    hidden = expand_bias.shape[0]
    sp = jnp.stack([member.astype(jnp.int32), length.astype(jnp.int32)])
    at = jnp.stack([place_of(index, s).astype(jnp.int32) for s in STAGES])
    places = member * own + jnp.arange(own)
    places_other = (1 - member) * own + jnp.arange(own)
    row = lambda v: v.reshape(1, -1)
    line = Line()
    v = Held()
    reduce_sum, expand_sum = Sum(line, STAGES[0]), Sum(line, STAGES[0])
    query_sum, value_sum = Sum(line, STAGES[0]), Sum(line, STAGES[0])

    rows = bias_rows(relative_bias)
    target0 = keep_valid(cotangent, places, length)
    other = swap(tokens)

    def project_own():
        v.low0, v.projected0 = line(project, tokens, row(first_gain), row(first_shift), heads_weight)

    def project_other():
        v.low1, v.projected1 = line(project, other, row(first_gain), row(first_shift), heads_weight)

    active_grad = lambda t, w: columns_dot(t, w, 1, name="active_grad")

    def active_own():
        v.active_grad0 = line(active_grad, target0, reduce_weight)

    def send_more():
        n = width // 2
        half = lax.dynamic_slice_in_dim(mixer_weight, core * n, n, 0)
        ready = line.last
        v.cotangent_other = swap(tie(cotangent, other, *ready))
        v.mixer_half = swap(tie(half, other, *ready))

    def attend():
        v.mixed, v.logsum = line(attend_forward, sp, v.projected0, v.projected1, rows)
        v.mixed_other = swap(v.mixed)

    def active_other():
        v.target1 = line(lambda x: keep_valid(x, places_other, length), v.cotangent_other)
        v.active_grad1 = line(active_grad, v.target1, reduce_weight)

    def mixer_rest():
        v.mixer_rest = trade(tie(v.mixer_half, *line.last), 1)

    def mixer_both():
        a, b = v.mixer_half, v.mixer_rest
        v.mixer_other = line(order_rows, core.astype(jnp.int32).reshape(1), a, b)

    def mix_rows():
        v.middle, v.second = line(
            mix, tokens, other, v.mixed, v.mixed_other, mixer_weight, v.mixer_other,
            row(second_gain), row(second_shift),
        )

    def expand_other():
        v.act1, v.ge1, gs1, v.eb1 = line(
            lambda x, g, w, b: expand(x, 1, own, g, w, b, BF16),
            v.second, v.active_grad1, expand_weight, row(expand_bias),
        )
        v.gs_got = swap(gs1)

    def expand_own():
        v.act0, v.ge0, v.gs0, v.eb0 = line(
            lambda x, g, w, b: expand(x, 0, own, g, w, b, BF16),
            v.second, v.active_grad0, expand_weight, row(expand_bias),
        )

    def reduce_chunks():
        reduce_sum.begin(*line(
            lambda *xs: reduce_grad_part(at, 0, *xs), v.act0, v.act1, target0, v.target1
        ))

    def expand_chunks():
        expand_sum.begin(*line(lambda *xs: expand_grad_part(at, 0, *xs), v.second, v.ge0, v.ge1))

    def middle_back():
        v.attended0, v.second_sums = line(
            back_rows, v.gs0, v.gs_got, v.middle, target0, row(second_gain)
        )

    grad_mix = lambda a, w: dot(a, w, 1, 1).astype(BF16)

    def mixed_send():
        out = line(grad_mix, v.attended0, v.mixer_other)
        v.grad_mixed1 = swap(out)

    def mixed_own():
        v.grad_mixed0 = line(grad_mix, v.attended0, mixer_weight)

    def attended_send():
        v.attended1 = swap(tie(v.attended0, *line.last))

    def reduced_other():
        out = line(lambda a, w: columns_dot(a, w, 0, name="reduced"), v.act1, reduce_weight)
        v.reduced_got = swap(out)

    def attend_back():
        v.grad_projected, v.sums = line(
            attend_backward, sp, v.projected0, v.projected1, v.grad_mixed0, v.grad_mixed1,
            v.mixed, v.logsum, rows,
        )

    def query_chunks():
        query_sum.begin(*line(lambda *xs: heads_grad_part(at, 0, *xs), v.low0, v.low1, v.grad_projected))

    def value_chunks():
        value_sum.begin(*line(
            lambda *xs: values_grad_part(at, 0, *xs), v.low0, v.low1, v.grad_projected,
            v.attended0, v.attended1, v.mixed,
        ))

    def first_other():
        out = line(lambda g, w: first_rows(g, w, 1, own, BF16), v.grad_projected, heads_weight)
        v.first_got = swap(out)

    def first_own():
        v.first_part = line(lambda g, w: first_rows(g, w, 0, own, BF16), v.grad_projected, heads_weight)

    def first_back():
        v.tokens_grad, first_sums = line(
            back_rows, v.first_part, v.first_got, tokens, v.attended0, row(first_gain)
        )
        v.both = join(first_sums[:2], v.second_sums[:3])
        v.both_got = swap(v.both)

    def output():
        v.block_out = line(
            output_rows, v.middle, v.act0, reduce_weight, v.reduced_got, row(reduce_bias)
        )

    def pack_first():
        v.pack = line(
            lambda both, got, eb0, eb1, bias: jnp.concatenate(
                [(both + got).reshape(-1), (eb0 + eb1).reshape(-1), bias.reshape(-1)]
            ).reshape(-1, 128),
            v.both, v.both_got, v.eb0, v.eb1, bias_grad(v.sums, buckets),
        )
        v.pack_got = trade(v.pack, 1)

    def pack_next(bit):
        def step():
            v.pack = line(jnp.add, v.pack, v.pack_got)
            if bit:
                v.pack_got = trade(v.pack, bit)

        return step

    chunk = (hidden // 8, model)
    turned = (model, hidden // 8)

    piece = (2, model // 8, width)
    reduce_shape = [jax.ShapeDtypeStruct(reduce_weight.shape, F32)]
    expand_shape = [jax.ShapeDtypeStruct(expand_weight.shape, F32)]
    heads_shape = [jax.ShapeDtypeStruct(heads_weight.shape, F32), jax.ShapeDtypeStruct(mixer_weight.shape, F32)]
    reduce_spec = [lambda to: pl.BlockSpec((hidden // 4, model), lambda g, s: (to(g, s), 0))]
    expand_spec = [lambda to: pl.BlockSpec((model, hidden // 4), lambda g, s: (0, to(g, s)))]
    heads_spec = [
        lambda to: pl.BlockSpec((3, model // 4, width), lambda g, s: (0, to(g, s), 0)),
        lambda to: pl.BlockSpec((width, model // 4), lambda g, s: (0, to(g, s))),
    ]

    def reduce_near():
        v.reduce_grad = line(
            lambda *xs: spread(at, 0, xs, put_rows, chunk, reduce_spec, reduce_shape, name="reduce_near"),
            *reduce_sum.nears(),
        )

    def reduce_far():
        v.reduce_grad = line(
            lambda given, *xs: spread(at, 1, xs, put_rows, chunk, reduce_spec, reduce_shape, given, name="reduce_far"),
            v.reduce_grad, *reduce_sum.fars(),
        )

    def expand_near():
        v.expand_grad = line(
            lambda *xs: spread(at, 0, xs, put_columns, turned, expand_spec, expand_shape, name="expand_near"),
            *expand_sum.nears(),
        )

    def expand_far():
        v.expand_grad = line(
            lambda given, *xs: spread(at, 1, xs, put_columns, turned, expand_spec, expand_shape, given, name="expand_far"),
            v.expand_grad, *expand_sum.fars(),
        )

    def heads_near():
        v.heads_grad = line(
            lambda *xs: spread(at, 0, xs, put_heads, piece, heads_spec, heads_shape, name="heads_near"),
            *query_sum.nears(), *value_sum.nears(),
        )

    def heads_far():
        v.heads_grad = line(
            lambda given, *xs: spread(at, 1, xs, put_heads, piece, heads_spec, heads_shape, given, name="heads_far"),
            v.heads_grad, *query_sum.fars(), *value_sum.fars(),
        )

    order = (
        project_own, active_own, send_more, project_other, attend, mixer_rest, mixer_both, active_other,
        mix_rows, expand_other, expand_own, reduce_chunks, middle_back, mixed_send, expand_chunks,
        attended_send, mixed_own, reduce_sum.first, expand_sum.first, attend_back, reduce_sum.second,
        query_chunks, reduce_sum.third, value_chunks, first_other, expand_sum.second, reduce_sum.fourth,
        query_sum.first, value_sum.first, expand_sum.third, reduce_sum.fifth, query_sum.second,
        value_sum.second, first_own, first_back, expand_sum.fourth, pack_first, reduce_sum.sixth, pack_next(2),
        value_sum.third, expand_sum.fifth, reduced_other, query_sum.third, reduce_near, value_sum.fourth,
        reduce_far, query_sum.fourth, pack_next(4), expand_sum.sixth, value_sum.fifth, query_sum.fifth, output,
        value_sum.sixth, expand_near, expand_far, pack_next(8), query_sum.sixth, heads_near, heads_far,
        pack_next(0),
    )
    for step in order:
        step()
    pack = v.pack.reshape(-1)
    both = pack[: 5 * model].reshape(5, model)
    expand_bias_grad = pack[5 * model : 5 * model + hidden]
    bias_part = pack[5 * model + hidden :].reshape(relative_bias.shape)
    return (
        v.block_out, v.tokens_grad, both[0], both[1], v.heads_grad[0], bias_part, v.heads_grad[1], both[2], both[3],
        v.expand_grad[0], expand_bias_grad, v.reduce_grad[0], both[4],
    )


def gathered(
    tokens, lengths, first_gain, first_shift, heads_weight, relative_bias, mixer_weight, second_gain,
    second_shift, expand_weight, expand_bias, reduce_weight, reduce_bias, cotangent,
):
    def gather(x):
        return lax.all_gather(x, "mp", axis=0, tiled=True)

    def scatter(x):
        return lax.psum_scatter(x.astype(BF16), "mp", scatter_dimension=0, tiled=True).astype(F32)

    members = lax.axis_size("mp")
    length = lengths[0]
    own = tokens.shape[0]
    whole = own * members
    half = whole // 2
    buckets = relative_bias.shape[1]
    sp = jnp.stack([jnp.zeros((), jnp.int32), length.astype(jnp.int32)])
    places = lax.axis_index("mp") * own + jnp.arange(own)
    rows = bias_rows(relative_bias)
    source_all = gather(tokens)
    first_all, projected = project(source_all, first_gain.reshape(1, -1), first_shift.reshape(1, -1), heads_weight)
    projected0, projected1 = projected[:, :half], projected[:, half:]
    mixed, logsum = attend_forward(sp, projected0, projected1, rows)
    source = tokens.astype(F32)
    middle = source + scatter(dot(mixed, mixer_weight, 1, 0))
    second_norm, second_inverse = normalize(middle)
    second_all = gather((second_norm * second_gain + second_shift).astype(BF16))
    target = keep_valid(cotangent, places, length)
    target_wide = target.astype(F32)
    target_all = gather(target)
    expanded = dot(second_all, expand_weight, 1, 0) + expand_bias
    active_low = jax.nn.gelu(expanded, approximate=True).astype(BF16)
    grad_expanded = gelu_back(expanded, dot(target_all, reduce_weight, 1, 1)).astype(BF16)
    grad_second = scatter(dot(grad_expanded, expand_weight, 1, 1))
    reduced = scatter(dot(active_low, reduce_weight, 1, 0))
    reduce_grad = dot(active_low, target_all, 0, 0)
    expand_grad = dot(second_all, grad_expanded, 0, 0)
    expand_bias_grad = jnp.sum(grad_expanded.astype(F32), axis=0)
    block_out = (middle + reduced + reduce_bias).astype(BF16)
    grad_middle = target_wide + norm_back(grad_second * second_gain, second_norm, second_inverse)
    attended_all = gather(grad_middle.astype(BF16))
    mixer_grad = dot(mixed, attended_all, 0, 0)
    grad_mixed = dot(attended_all, mixer_weight, 1, 1).astype(BF16)
    grad_projected, sums = attend_backward(
        sp, projected0, projected1, grad_mixed[:half], grad_mixed[half:], mixed, logsum, rows
    )
    bias_part = bias_grad(sums, buckets)
    heads_grad = jnp.einsum("td,cte->cde", first_all, grad_projected, preferred_element_type=F32)
    grad_first = scatter(jnp.einsum("cte,cde->td", grad_projected, heads_weight, preferred_element_type=F32))
    first_norm, first_inverse = normalize(source)
    tokens_grad = (
        grad_middle + norm_back(grad_first * first_gain, first_norm, first_inverse)
    ).astype(BF16)
    first_gain_grad, first_shift_grad, second_gain_grad, second_shift_grad, reduce_bias_grad = (
        lax.psum(
            (
                jnp.sum(grad_first * first_norm, axis=0),
                jnp.sum(grad_first, axis=0),
                jnp.sum(grad_second * second_norm, axis=0),
                jnp.sum(grad_second, axis=0),
                jnp.sum(target_wide, axis=0),
            ),
            ("dp", "mp"),
        )
    )
    heads_grad, bias_part, mixer_grad, expand_grad, expand_bias_grad, reduce_grad = (
        lax.psum(x.astype(BF16), "dp").astype(F32)
        for x in (heads_grad, bias_part, mixer_grad, expand_grad, expand_bias_grad, reduce_grad)
    )
    return (
        block_out, tokens_grad, first_gain_grad, first_shift_grad, heads_grad, bias_part, mixer_grad,
        second_gain_grad, second_shift_grad, expand_grad, expand_bias_grad, reduce_grad, reduce_bias_grad,
    )


def per_device(*args):
    if lax.axis_size("mp") == 2 and lax.axis_size("dp") == 16:
        return paired(*args)
    return gathered(*args)


def solution(mesh):
    return jax.shard_map(
        per_device,
        mesh=mesh,
        in_specs=(
            P(("dp", "mp"), None),
            P("dp"),
            P(),
            P(),
            P(None, None, "mp"),
            P("mp", None),
            P("mp", None),
            P(),
            P(),
            P(None, "mp"),
            P("mp"),
            P("mp", None),
            P(),
            P(("dp", "mp"), None),
        ),
        out_specs=(
            P(("dp", "mp"), None),
            P(("dp", "mp"), None),
            P(),
            P(),
            P(None, None, "mp"),
            P("mp", None),
            P("mp", None),
            P(),
            P(),
            P(None, "mp"),
            P("mp"),
            P("mp", None),
            P(),
        ),
        check_vma=False,
    )
```
